32 devices in a mesh: seq: 2 (over y), blk: 16 (over z, x, core).
Axes of the slice: x: 2, y: 2, z: 4, core: 2. Of those that a mesh axis runs over, the one named last changes fastest.
Arguments:
- tokens: bfloat16 [16384, 768], P(('seq', 'blk')), may hold values from -6 to 6
- lengths: int32 [2, 4], P('seq'), may hold values from 1024 to 4096, as said below
- norm_gain: bfloat16 [768], P(('seq', 'blk')), may hold values from 0.25 to 1.75
- global_gain: bfloat16 [768], P(('seq', 'blk')), may hold values from 0.25 to 1.75
- w_query: bfloat16 [768, 768], P(('seq', 'blk')), may hold values from -0.0546875 to 0.0546875
- w_key: bfloat16 [768, 768], P(('seq', 'blk')), may hold values from -0.21875 to 0.21875
- w_value: bfloat16 [768, 768], P(('seq', 'blk')), may hold values from -0.21875 to 0.21875
- w_out: bfloat16 [768, 768], P(('seq', 'blk')), may hold values from -1.25 to 1.25
- ffn_gain: bfloat16 [768], P(('seq', 'blk')), may hold values from 0.25 to 1.75
- w_gate: bfloat16 [768, 2048], P(('seq', 'blk')), may hold values from -0.21875 to 0.21875
- w_up: bfloat16 [768, 2048], P(('seq', 'blk')), may hold values from -0.21875 to 0.21875
- w_down: bfloat16 [2048, 768], P(('seq', 'blk')), may hold values from -0.125 to 0.125
- cotangent: bfloat16 [16384, 768], P(('seq', 'blk')), may hold values from -6 to 6
Outputs:
- output: bfloat16 [16384, 768], P(('seq', 'blk'))
- grad_tokens: float32 [16384, 768], P(('seq', 'blk'))
- grad_norm_gain: float32 [768], P(('seq', 'blk'))
- grad_global_gain: float32 [768], P(('seq', 'blk'))
- grad_w_query: float32 [768, 768], P(('seq', 'blk'))
- grad_w_key: float32 [768, 768], P(('seq', 'blk'))
- grad_w_value: float32 [768, 768], P(('seq', 'blk'))
- grad_w_out: float32 [768, 768], P(('seq', 'blk'))
- grad_ffn_gain: float32 [768], P(('seq', 'blk'))
- grad_w_gate: float32 [768, 2048], P(('seq', 'blk'))
- grad_w_up: float32 [768, 2048], P(('seq', 'blk'))
- grad_w_down: float32 [2048, 768], P(('seq', 'blk'))
The draws below stay inside these ranges and needn't reach their ends.
Inputs may be any that keep to these rules, and one draw needn't show every extreme that they name: Row s lists the lengths in tokens of the 4 sequences of group s in order; they fill the group's 8192 tokens, are multiples of 128, and every row has one length of exactly 4096 and one of exactly 1024.
All inputs are finite; a program needn't handle non-finite values.
Results may differ from the reference program's by a relative error of at most 0.033.
Values may be sent and summed in bfloat16 or wider, within the bound.
A program may use at most 192 MiB of HBM per device.

```python
import jax
import jax.numpy as jnp
from jax import lax

D = 768
HEADS = 12
HEAD_DIM = 64
FF = 2048
GBLK = 16
BLOCK = 128
TOK_DEV = 512
MIN_LEN = 1024
INNER = 768
GROUPS = 2
GROUP_TOKENS = 8192
TOKENS = 16384
SEQS = 4
MAX_LEN = 4096
GLOBALS = 512


def draw_lengths(key, part):
    largest_blocks = MAX_LEN // BLOCK
    least_blocks = MIN_LEN // BLOCK
    extra_blocks = GROUP_TOKENS // BLOCK - largest_blocks - (SEQS - 1) * least_blocks
    others_count = SEQS - 1

    def one_group(group_key):
        weight_key, place_key = jax.random.split(group_key)
        positions = jnp.arange(others_count, dtype=jnp.int32)
        weights = jax.random.randint(weight_key, (others_count,), 1, 5, dtype=jnp.int32) * (positions > 0).astype(jnp.int32)
        shares = extra_blocks * weights // jnp.sum(weights)
        leftover = extra_blocks - jnp.sum(shares)
        shares = shares + ((positions >= 1) & (positions <= leftover)).astype(jnp.int32)
        others = least_blocks + shares
        chosen = jax.random.randint(place_key, (), 0, SEQS, dtype=jnp.int32)
        places = jnp.arange(SEQS, dtype=jnp.int32)
        before = others[jnp.clip(places, 0, others_count - 1)]
        shifted = others[jnp.clip(places - 1, 0, others_count - 1)]
        blocks = jnp.where(places < chosen, before, jnp.where(places == chosen, largest_blocks, shifted))
        return (blocks * BLOCK).astype(jnp.int32)
    return jax.vmap(one_group)(jax.random.split(key, GROUPS))


def levels(stream_key, dims, cuts, least, high):
    gain = 1.0
    for position, shards_of in cuts:
        heights = jax.random.uniform(jax.random.fold_in(jax.random.fold_in(stream_key, 6), position), (shards_of,), jnp.float32, least / len(cuts), high / len(cuts))
        gain = gain * jnp.repeat(jnp.exp(heights), dims[position] // shards_of).reshape((-1,) + (1,) * (len(dims) - 1 - position))
    return gain


def scatter_about(rng, shape, scale, most, cuts=(), kind=jnp.bfloat16):
    entries = jax.random.normal(rng, shape, jnp.float32) * scale
    if len(cuts) > 0:
        entries = levels(rng, shape, cuts, -0.22, 0.18) * entries
    return jnp.clip(entries, min=-most, max=most).astype(kind)


def setup_inputs(seed: int = 0) -> dict:
    arg_keys = jax.random.split(jax.random.key(seed), 14)
    tokens = scatter_about(arg_keys[0], (TOKENS, D), 1.0, 6.0, ((0, 32),))
    lengths = draw_lengths(jax.random.fold_in(arg_keys[13], 71), 0)
    norm_gain = jnp.clip(1.0 + 0.15 * jax.random.normal(arg_keys[2], (D,), jnp.float32), 0.25, 1.75).astype(jnp.bfloat16)
    global_gain = jnp.clip(1.0 + 0.15 * jax.random.normal(arg_keys[3], (D,), jnp.float32), 0.25, 1.75).astype(jnp.bfloat16)
    w_query = scatter_about(arg_keys[4], (D, INNER), (16 * D) ** -0.5, 0.0546875, ((0, 32),))
    w_key = scatter_about(arg_keys[5], (D, INNER), D ** -0.5, 0.21875, ((0, 32),))
    w_value = scatter_about(arg_keys[6], (D, INNER), D ** -0.5, 0.21875, ((0, 32),))
    w_out = scatter_about(arg_keys[7], (INNER, D), (INNER // 32) ** -0.5, 1.25, ((0, 32),))
    ffn_gain = jnp.clip(1.0 + 0.15 * jax.random.normal(arg_keys[8], (D,), jnp.float32), 0.25, 1.75).astype(jnp.bfloat16)
    w_gate = scatter_about(arg_keys[9], (D, FF), D ** -0.5, 0.21875, ((0, 32),))
    w_up = scatter_about(arg_keys[10], (D, FF), D ** -0.5, 0.21875, ((0, 32),))
    w_down = scatter_about(arg_keys[11], (FF, D), FF ** -0.5, 0.125, ((0, 32),))
    cotangent = scatter_about(arg_keys[12], (TOKENS, D), 1.0, 6.0, ((0, 32),))
    return dict(tokens=tokens, lengths=lengths, norm_gain=norm_gain, global_gain=global_gain, w_query=w_query, w_key=w_key, w_value=w_value, w_out=w_out, ffn_gain=ffn_gain, w_gate=w_gate, w_up=w_up, w_down=w_down, cotangent=cotangent)


@jax.custom_vjp
def low(v):
    return lax.optimization_barrier(v.astype(jnp.bfloat16)).astype(jnp.float32)

@jax.custom_vjp
def low_back(v):
    return v

def low_keep(v):
    return (low(v), None)

def low_pass(kept, grad):
    return (grad,)

def back_keep(v):
    return (v, None)

def back_low(kept, grad):
    return (low(grad),)
low.defvjp(low_keep, low_pass)
low_back.defvjp(back_keep, back_low)
EPSILON = 1e-06
MASKED = -1e+30
GELU_SCALE = 0.7978845608028654
GELU_CUBIC = 0.044715

def rounded(values):
    return low(low_back(values))

def product(left_side, right_side):
    return jnp.dot(left_side, right_side, precision=lax.Precision.HIGHEST)

def rms_norm(values, scales):
    return values * lax.rsqrt(lax.optimization_barrier(jnp.mean(values * values, axis=-1, keepdims=True)) + EPSILON) * scales

def gelu_tanh(values):
    return 0.5 * values * (1.0 + jnp.tanh(GELU_SCALE * (values + GELU_CUBIC * values * values * values)))

def sequence_of(positions, seq_ends):
    return lax.optimization_barrier(jnp.sum((positions[:, None] >= seq_ends[None, :]).astype(jnp.int32), axis=1)).astype(jnp.int32)

def group_forward(group_rows, row_lengths, weights):
    norm_gain, global_gain, w_query, w_key, w_value, w_out, ffn_gain, w_gate, w_up, w_down = weights
    normed = low(rms_norm(group_rows, norm_gain))
    query_rows = rounded(product(normed, w_query))
    key_rows = rounded(product(normed, w_key))
    value_rows = rounded(product(normed, w_value))
    summed = lax.optimization_barrier(jnp.sum(normed.reshape(GLOBALS, GBLK, D), axis=1))
    global_in = low(rms_norm(summed, global_gain))
    global_key = rounded(product(global_in, w_key))
    global_value = rounded(product(global_in, w_value))
    seq_ends = jnp.cumsum(row_lengths).astype(jnp.int32)
    positions = jnp.arange(GROUP_TOKENS, dtype=jnp.int32)
    token_seq = sequence_of(positions, seq_ends)
    global_seq = sequence_of(jnp.arange(GLOBALS, dtype=jnp.int32) * GBLK, seq_ends)
    padded_key = jnp.pad(key_rows, ((BLOCK, BLOCK), (0, 0)))
    padded_value = jnp.pad(value_rows, ((BLOCK, BLOCK), (0, 0)))
    padded_seq = jnp.pad(token_seq, (BLOCK, BLOCK), constant_values=-1)
    window = TOK_DEV + 2 * BLOCK

    @jax.checkpoint
    def attend(first_row):
        queries = lax.dynamic_slice_in_dim(query_rows, first_row, TOK_DEV, 0).reshape(TOK_DEV, HEADS, HEAD_DIM)
        near_keys = lax.dynamic_slice_in_dim(padded_key, first_row, window, 0)
        near_values = lax.dynamic_slice_in_dim(padded_value, first_row, window, 0)
        all_keys = jnp.concatenate([near_keys, global_key], axis=0).reshape(window + GLOBALS, HEADS, HEAD_DIM)
        all_values = jnp.concatenate([near_values, global_value], axis=0).reshape(window + GLOBALS, HEADS, HEAD_DIM)
        query_pos = first_row + jnp.arange(TOK_DEV, dtype=jnp.int32)
        key_pos = first_row - BLOCK + jnp.arange(window, dtype=jnp.int32)
        query_seq = lax.dynamic_slice_in_dim(token_seq, first_row, TOK_DEV, 0)
        key_seq = lax.dynamic_slice_in_dim(padded_seq, first_row, window, 0)
        near_mask = (jnp.abs(query_pos[:, None] - key_pos[None, :]) <= BLOCK - 1) & (query_seq[:, None] == key_seq[None, :])
        far_mask = query_seq[:, None] == global_seq[None, :]
        allowed = jnp.concatenate([near_mask, far_mask], axis=1)
        scores = low_back(jnp.einsum('qhd,khd->hqk', queries, all_keys, precision=lax.Precision.HIGHEST))
        scores = jnp.where(allowed[None], scores, MASKED)
        attn_probs = low(jax.nn.softmax(scores, axis=-1))
        mixed_heads = jnp.einsum('hqk,khd->qhd', attn_probs, all_values, precision=lax.Precision.HIGHEST)
        return mixed_heads.reshape(TOK_DEV, INNER)
    starts = jnp.arange(GROUP_TOKENS // TOK_DEV, dtype=jnp.int32) * TOK_DEV
    attended = rounded(lax.map(attend, starts).reshape(GROUP_TOKENS, INNER))
    middle = group_rows + low_back(product(attended, w_out))
    hidden = low(rms_norm(middle, ffn_gain))
    gate_pre = low_back(product(hidden, w_gate))
    up_pre = low_back(product(hidden, w_up))
    mixed = low(gelu_tanh(gate_pre) * up_pre)
    return middle + low_back(product(mixed, w_down))

def reference(tokens, lengths, norm_gain, global_gain, w_query, w_key, w_value, w_out, ffn_gain, w_gate, w_up, w_down, cotangent):
    weights = tuple((parameter.astype(jnp.float32) for parameter in (norm_gain, global_gain, w_query, w_key, w_value, w_out, ffn_gain, w_gate, w_up, w_down)))

    def forward(inputs, parameters):
        grouped = inputs.reshape(GROUPS, GROUP_TOKENS, D)

        def per_group(group_pair):
            return group_forward(group_pair[0], group_pair[1], parameters)
        return lax.map(per_group, (grouped, lengths)).reshape(TOKENS, D)
    output, pullback = jax.vjp(forward, tokens.astype(jnp.float32), weights)
    grad_tokens, grads = pullback(cotangent.astype(jnp.float32))
    return (output.astype(jnp.bfloat16), grad_tokens, grads[0], grads[1], grads[2], grads[3], grads[4], grads[5], grads[6], grads[7], grads[8], grads[9])
```

```python
import functools

import jax
import jax.numpy as jnp
from jax import lax
from jax.experimental import pallas as pl
from jax.experimental.pallas import tpu as pltpu
from jax.sharding import PartitionSpec as P


D = 768
HEADS = 12
HEAD_DIM = 64
GBLK = 16
BLOCK = 128
LONGEST = 16384


EPSILON = 1e-06
MASKED = -1e30
GELU_SCALE = 0.7978845608028654
GELU_CUBIC = 0.044715


def with_halo(block, sides, width):
    for axis, dim in sides:
        count = lax.axis_size(axis)
        forward = [(i, i + 1) for i in range(count - 1)]
        backward = [(target, source) for source, target in forward]
        low = lax.ppermute(
            lax.slice_in_dim(block, block.shape[dim] - width, None, axis=dim), axis, forward
        )
        high = lax.ppermute(lax.slice_in_dim(block, 0, width, axis=dim), axis, backward)
        block = jnp.concatenate([low, block, high], axis=dim)
    return block


def rms_norm(values, scales):
    return values * lax.rsqrt(jnp.mean(values * values, axis=-1, keepdims=True) + EPSILON) * scales


def gelu_tanh(values):
    return (
        0.5
        * values
        * (1.0 + jnp.tanh(GELU_SCALE * (values + GELU_CUBIC * values * values * values)))
    )


def gated(gate_part, up_part):
    return gelu_tanh(gate_part) * up_part


def sequence_of(positions, seq_ends):
    return jnp.sum((positions[:, None] >= seq_ends[None, :]).astype(jnp.int32), axis=1)


def matmul(left_side, right_side):
    return jnp.dot(left_side, right_side, preferred_element_type=jnp.float32)


def matmul_left(left_side, right_side):
    return jnp.einsum("ta,tb->ab", left_side, right_side, preferred_element_type=jnp.float32)


def matmul_right(left_side, right_side):
    return jnp.einsum("ta,ba->tb", left_side, right_side, preferred_element_type=jnp.float32)


def windows(extended, row_count):
    block_count = row_count // BLOCK
    pieces = [
        extended[offset * BLOCK : offset * BLOCK + row_count].reshape(
            block_count, BLOCK, extended.shape[-1]
        )
        for offset in range(3)
    ]
    return jnp.concatenate(pieces, axis=1)


def unwindow(window_grads, row_count):
    channels = window_grads.shape[-1]
    summed_grad = jnp.zeros((row_count + 2 * BLOCK, channels), jnp.float32)
    for offset in range(3):
        piece_grad = window_grads[:, offset * BLOCK : (offset + 1) * BLOCK].reshape(
            row_count, channels
        )
        summed_grad = summed_grad + jnp.pad(
            piece_grad, ((offset * BLOCK, (2 - offset) * BLOCK), (0, 0))
        )
    return summed_grad


def head_scores(query_head, near_keys, far_keys, near_mask, far_mask):
    block_count = near_keys.shape[0]
    query_blocks = query_head.reshape(block_count, BLOCK, HEAD_DIM)
    near_scores = jnp.einsum(
        "nqd,nkd->nqk", query_blocks, near_keys, preferred_element_type=jnp.float32
    )
    far_scores = jnp.einsum("qd,kd->qk", query_head, far_keys, preferred_element_type=jnp.float32)
    return (jnp.where(near_mask, near_scores, MASKED), jnp.where(far_mask, far_scores, MASKED))


def per_device_general(
    tokens,
    lengths,
    norm_gain,
    global_gain,
    w_query,
    w_key,
    w_value,
    w_out,
    ffn_gain,
    w_gate,
    w_up,
    w_down,
    cotangent,
):
    row_count = tokens.shape[0]
    inner_dim = HEADS * HEAD_DIM
    block_count = row_count // BLOCK
    local_globals = row_count // GBLK
    group_tokens = row_count * lax.axis_size("blk")
    global_count = group_tokens // GBLK
    longest_len = min(LONGEST, group_tokens // 2)
    span_rows = min(global_count, 2 * (longest_len // GBLK) + local_globals)
    attn_full = (
        lax.all_gather(norm_gain, ("seq", "blk"), axis=0, tiled=True),
        lax.all_gather(global_gain, ("seq", "blk"), axis=0, tiled=True),
        lax.all_gather(w_query, ("seq", "blk"), axis=0, tiled=True),
        lax.all_gather(w_key, ("seq", "blk"), axis=0, tiled=True),
        lax.all_gather(w_value, ("seq", "blk"), axis=0, tiled=True),
        lax.all_gather(w_out, ("seq", "blk"), axis=0, tiled=True),
    )
    seq_ends = jnp.cumsum(lengths[0])
    first_row = lax.axis_index("blk") * row_count
    span_start = jnp.clip(first_row // GBLK - longest_len // GBLK, 0, global_count - span_rows)
    query_pos = first_row + jnp.arange(row_count, dtype=jnp.int32)
    query_seq = sequence_of(query_pos, seq_ends)
    key_pos = first_row - BLOCK + jnp.arange(row_count + 2 * BLOCK, dtype=jnp.int32)
    inside = (key_pos >= 0) & (key_pos < group_tokens)
    key_seq = jnp.where(inside, sequence_of(key_pos, seq_ends), -1)
    global_seq = sequence_of((span_start + jnp.arange(span_rows, dtype=jnp.int32)) * GBLK, seq_ends)
    query_pos_win = query_pos.reshape(block_count, BLOCK)
    query_seq_win = query_seq.reshape(block_count, BLOCK)
    key_pos_win = windows(key_pos[:, None], row_count)[:, :, 0]
    key_seq_win = windows(key_seq[:, None], row_count)[:, :, 0]
    near_mask = (jnp.abs(query_pos_win[:, :, None] - key_pos_win[:, None, :]) <= BLOCK - 1) & (
        query_seq_win[:, :, None] == key_seq_win[:, None, :]
    )
    far_mask = query_seq[:, None] == global_seq[None, :]
    tokens_full = tokens.astype(jnp.float32)
    normed_full, normed_pull = jax.vjp(rms_norm, tokens_full, attn_full[0].astype(jnp.float32))
    normed = normed_full.astype(jnp.bfloat16)
    queries = matmul(normed, attn_full[2]).astype(jnp.bfloat16)
    key_rows = matmul(normed, attn_full[3]).astype(jnp.bfloat16)
    value_rows = matmul(normed, attn_full[4]).astype(jnp.bfloat16)
    local_kv = jnp.concatenate([key_rows, value_rows], axis=1)
    extended = with_halo(local_kv, (("blk", 0),), BLOCK)
    near_kv = windows(extended, row_count)
    summed = jnp.sum(normed.astype(jnp.float32).reshape(local_globals, GBLK, D), axis=1)
    global_full, global_pull = jax.vjp(rms_norm, summed, attn_full[1].astype(jnp.float32))
    global_in = global_full.astype(jnp.bfloat16)
    own_global = jnp.concatenate(
        [
            matmul(global_in, attn_full[3]).astype(jnp.bfloat16),
            matmul(global_in, attn_full[4]).astype(jnp.bfloat16),
        ],
        axis=1,
    )
    global_kv = lax.all_gather(own_global, "blk", axis=0, tiled=True)
    span_kv = lax.dynamic_slice_in_dim(global_kv, span_start, span_rows, 0)

    def head_slices(head_index):
        column = head_index * HEAD_DIM
        query_head = lax.dynamic_slice_in_dim(queries, column, HEAD_DIM, 1)
        near_keys = lax.dynamic_slice_in_dim(near_kv, column, HEAD_DIM, 2)
        near_values = lax.dynamic_slice_in_dim(near_kv, inner_dim + column, HEAD_DIM, 2)
        far_keys = lax.dynamic_slice_in_dim(span_kv, column, HEAD_DIM, 1)
        far_values = lax.dynamic_slice_in_dim(span_kv, inner_dim + column, HEAD_DIM, 1)
        return (column, query_head, near_keys, near_values, far_keys, far_values)

    def head_forward(head_index, carry):
        attended_rows, log_sums = carry
        column, query_head, near_keys, near_values, far_keys, far_values = head_slices(head_index)
        near_scores, far_scores = head_scores(query_head, near_keys, far_keys, near_mask, far_mask)
        highest = jnp.maximum(
            jnp.max(near_scores, axis=2).reshape(row_count), jnp.max(far_scores, axis=1)
        )
        near_exp = jnp.exp(near_scores - highest.reshape(block_count, BLOCK, 1))
        far_exp = jnp.exp(far_scores - highest[:, None])
        denominator = jnp.sum(near_exp, axis=2).reshape(row_count) + jnp.sum(far_exp, axis=1)
        near_probs = (near_exp / denominator.reshape(block_count, BLOCK, 1)).astype(jnp.bfloat16)
        far_probs = (far_exp / denominator[:, None]).astype(jnp.bfloat16)
        head_out = jnp.einsum(
            "nqk,nkd->nqd", near_probs, near_values, preferred_element_type=jnp.float32
        ).reshape(row_count, HEAD_DIM)
        head_out = head_out + jnp.einsum(
            "qk,kd->qd", far_probs, far_values, preferred_element_type=jnp.float32
        )
        attended_rows = lax.dynamic_update_slice_in_dim(attended_rows, head_out, column, 1)
        log_sums = lax.dynamic_update_index_in_dim(
            log_sums, highest + jnp.log(denominator), head_index, 0
        )
        return (attended_rows, log_sums)

    attended_rows, log_sums = lax.fori_loop(
        0,
        HEADS,
        head_forward,
        (
            jnp.zeros((row_count, inner_dim), jnp.float32),
            jnp.zeros((HEADS, row_count), jnp.float32),
        ),
    )
    attended = attended_rows.astype(jnp.bfloat16)
    middle = tokens_full + matmul(attended, attn_full[5])
    ffn_full = (
        lax.all_gather(ffn_gain, ("seq", "blk"), axis=0, tiled=True),
        lax.all_gather(w_gate, ("seq", "blk"), axis=0, tiled=True),
        lax.all_gather(w_up, ("seq", "blk"), axis=0, tiled=True),
        lax.all_gather(w_down, ("seq", "blk"), axis=0, tiled=True),
    )
    hidden_full, hidden_pull = jax.vjp(rms_norm, middle, ffn_full[0].astype(jnp.float32))
    hidden = hidden_full.astype(jnp.bfloat16)
    gate_pre = matmul(hidden, ffn_full[1])
    up_pre = matmul(hidden, ffn_full[2])
    gated_rows, gated_pull = jax.vjp(gated, gate_pre, up_pre)
    mixed = gated_rows.astype(jnp.bfloat16)
    output = (middle + matmul(mixed, ffn_full[3])).astype(jnp.bfloat16)
    ffn_back = (
        lax.all_gather(ffn_gain, ("seq", "blk"), axis=0, tiled=True),
        lax.all_gather(w_gate, ("seq", "blk"), axis=0, tiled=True),
        lax.all_gather(w_up, ("seq", "blk"), axis=0, tiled=True),
        lax.all_gather(w_down, ("seq", "blk"), axis=0, tiled=True),
    )
    grad_down = matmul_left(mixed, cotangent)
    grad_mixed = matmul_right(cotangent, ffn_back[3])
    grad_gate_full, grad_up_full = gated_pull(grad_mixed)
    grad_gate = grad_gate_full.astype(jnp.bfloat16)
    grad_up = grad_up_full.astype(jnp.bfloat16)
    grad_wgate = matmul_left(hidden, grad_gate)
    grad_wup = matmul_left(hidden, grad_up)
    grad_hidden = matmul_right(grad_gate, ffn_back[1]) + matmul_right(grad_up, ffn_back[2])
    grad_middle_norm, grad_ffn_gain = hidden_pull(grad_hidden)
    grad_middle = cotangent.astype(jnp.float32) + grad_middle_norm
    attn_back = (
        lax.all_gather(norm_gain, ("seq", "blk"), axis=0, tiled=True),
        lax.all_gather(global_gain, ("seq", "blk"), axis=0, tiled=True),
        lax.all_gather(w_query, ("seq", "blk"), axis=0, tiled=True),
        lax.all_gather(w_key, ("seq", "blk"), axis=0, tiled=True),
        lax.all_gather(w_value, ("seq", "blk"), axis=0, tiled=True),
        lax.all_gather(w_out, ("seq", "blk"), axis=0, tiled=True),
    )
    grad_branch = grad_middle.astype(jnp.bfloat16)
    grad_wout = matmul_left(attended, grad_branch)
    grad_attended = matmul_right(grad_branch, attn_back[5]).astype(jnp.bfloat16)

    def head_backward(head_index, carry):
        grad_query_rows, grad_near, grad_far = carry
        column, query_head, near_keys, near_values, far_keys, far_values = head_slices(head_index)
        near_scores, far_scores = head_scores(query_head, near_keys, far_keys, near_mask, far_mask)
        lse_head = log_sums[head_index]
        near_probs = jnp.exp(near_scores - lse_head.reshape(block_count, BLOCK, 1))
        far_probs = jnp.exp(far_scores - lse_head[:, None])
        grad_head = lax.dynamic_slice_in_dim(grad_attended, column, HEAD_DIM, 1)
        grad_blocks = grad_head.reshape(block_count, BLOCK, HEAD_DIM)
        query_blocks = query_head.reshape(block_count, BLOCK, HEAD_DIM)
        near_dprobs = jnp.einsum(
            "nqd,nkd->nqk", grad_blocks, near_values, preferred_element_type=jnp.float32
        )
        far_dprobs = jnp.einsum(
            "qd,kd->qk", grad_head, far_values, preferred_element_type=jnp.float32
        )
        delta_rows = jnp.sum(near_probs * near_dprobs, axis=2).reshape(row_count) + jnp.sum(
            far_probs * far_dprobs, axis=1
        )
        near_grad_scores = (
            near_probs * (near_dprobs - delta_rows.reshape(block_count, BLOCK, 1))
        ).astype(jnp.bfloat16)
        far_grad_scores = (far_probs * (far_dprobs - delta_rows[:, None])).astype(jnp.bfloat16)
        head_dquery = jnp.einsum(
            "nqk,nkd->nqd", near_grad_scores, near_keys, preferred_element_type=jnp.float32
        ).reshape(row_count, HEAD_DIM)
        head_dquery = head_dquery + jnp.einsum(
            "qk,kd->qd", far_grad_scores, far_keys, preferred_element_type=jnp.float32
        )
        near_dkey = jnp.einsum(
            "nqk,nqd->nkd", near_grad_scores, query_blocks, preferred_element_type=jnp.float32
        )
        near_dvalue = jnp.einsum(
            "nqk,nqd->nkd",
            near_probs.astype(jnp.bfloat16),
            grad_blocks,
            preferred_element_type=jnp.float32,
        )
        far_dkey = jnp.einsum(
            "qk,qd->kd", far_grad_scores, query_head, preferred_element_type=jnp.float32
        )
        far_dvalue = jnp.einsum(
            "qk,qd->kd",
            far_probs.astype(jnp.bfloat16),
            grad_head,
            preferred_element_type=jnp.float32,
        )
        grad_query_rows = lax.dynamic_update_slice_in_dim(grad_query_rows, head_dquery, column, 1)
        grad_near = lax.dynamic_update_slice_in_dim(grad_near, near_dkey, column, 2)
        grad_near = lax.dynamic_update_slice_in_dim(grad_near, near_dvalue, inner_dim + column, 2)
        grad_far = lax.dynamic_update_slice_in_dim(grad_far, far_dkey, column, 1)
        grad_far = lax.dynamic_update_slice_in_dim(grad_far, far_dvalue, inner_dim + column, 1)
        return (grad_query_rows, grad_near, grad_far)

    grad_query_rows, grad_near, grad_far = lax.fori_loop(
        0,
        HEADS,
        head_backward,
        (
            jnp.zeros((row_count, inner_dim), jnp.float32),
            jnp.zeros((block_count, 3 * BLOCK, 2 * inner_dim), jnp.float32),
            jnp.zeros((span_rows, 2 * inner_dim), jnp.float32),
        ),
    )
    grad_extended = unwindow(grad_near, row_count)
    rim_rows = jnp.concatenate([grad_extended[:BLOCK], grad_extended[row_count + BLOCK :]], axis=0)
    returned = with_halo(rim_rows.astype(jnp.bfloat16), (("blk", 0),), BLOCK).astype(rim_rows.dtype)
    grad_kv = grad_extended[BLOCK : row_count + BLOCK]
    grad_kv = grad_kv + jnp.pad(returned[:BLOCK], ((0, row_count - BLOCK), (0, 0)))
    grad_kv = grad_kv + jnp.pad(returned[3 * BLOCK :], ((row_count - BLOCK, 0), (0, 0)))
    grad_kv = grad_kv.astype(jnp.bfloat16)
    grad_key = grad_kv[:, :inner_dim]
    grad_value = grad_kv[:, inner_dim:]
    group_far = lax.dynamic_update_slice_in_dim(
        jnp.zeros((global_count, 2 * inner_dim), jnp.float32), grad_far, span_start, 0
    )
    own_global_grad = lax.psum_scatter(group_far, "blk", scatter_dimension=0, tiled=True).astype(
        jnp.bfloat16
    )
    grad_global_key = own_global_grad[:, :inner_dim]
    grad_global_value = own_global_grad[:, inner_dim:]
    grad_query = grad_query_rows.astype(jnp.bfloat16)
    grad_wquery = matmul_left(normed, grad_query)
    grad_wkey = matmul_left(normed, grad_key) + matmul_left(global_in, grad_global_key)
    grad_wvalue = matmul_left(normed, grad_value) + matmul_left(global_in, grad_global_value)
    grad_normed = (
        matmul_right(grad_query, attn_back[2])
        + matmul_right(grad_key, attn_back[3])
        + matmul_right(grad_value, attn_back[4])
    )
    grad_global_in = matmul_right(grad_global_key, attn_back[3]) + matmul_right(
        grad_global_value, attn_back[4]
    )
    grad_summed, grad_global_gain = global_pull(grad_global_in)
    grad_normed = (grad_normed.reshape(local_globals, GBLK, D) + grad_summed[:, None, :]).reshape(
        row_count, D
    )
    grad_tokens_norm, grad_norm_gain = normed_pull(grad_normed)
    grad_tokens = grad_middle + grad_tokens_norm
    every_grad = (
        lax.psum_scatter(grad_norm_gain, ("seq", "blk"), scatter_dimension=0, tiled=True),
        lax.psum_scatter(grad_global_gain, ("seq", "blk"), scatter_dimension=0, tiled=True),
        lax.psum_scatter(grad_wquery, ("seq", "blk"), scatter_dimension=0, tiled=True),
        lax.psum_scatter(grad_wkey, ("seq", "blk"), scatter_dimension=0, tiled=True),
        lax.psum_scatter(grad_wvalue, ("seq", "blk"), scatter_dimension=0, tiled=True),
        lax.psum_scatter(grad_wout, ("seq", "blk"), scatter_dimension=0, tiled=True),
        lax.psum_scatter(grad_ffn_gain, ("seq", "blk"), scatter_dimension=0, tiled=True),
        lax.psum_scatter(grad_wgate, ("seq", "blk"), scatter_dimension=0, tiled=True),
        lax.psum_scatter(grad_wup, ("seq", "blk"), scatter_dimension=0, tiled=True),
        lax.psum_scatter(grad_down, ("seq", "blk"), scatter_dimension=0, tiled=True),
    )
    return (
        output,
        grad_tokens,
        every_grad[0],
        every_grad[1],
        every_grad[2],
        every_grad[3],
        every_grad[4],
        every_grad[5],
        every_grad[6],
        every_grad[7],
        every_grad[8],
        every_grad[9],
    )


MESH = pl.DeviceIdType.MESH
CHIPS_Z = 4
NEVER = 1 << 20
VMEM_BYTES = 64 * 1024 * 1024 - 65536


def dot(a, b, dims, precision=None):
    return lax.dot_general(
        a, b, (dims, ((), ())), precision=precision, preferred_element_type=jnp.float32
    )


def dot_nn(a, b):
    return dot(a, b, ((1,), (0,)))


def dot_nt(a, b):
    return dot(a, b, ((1,), (1,)))


def coords():
    y = lax.axis_index("seq")
    blk = lax.axis_index("blk")
    return y, blk // 4, (blk // 2) % 2, blk % 2


def device(y, z, x, c):
    return (y, z * 4 + x * 2 + c)


def send(src, dst, send_sem, recv_sem, target):
    pltpu.make_async_remote_copy(
        src_ref=src,
        dst_ref=dst,
        send_sem=send_sem,
        recv_sem=recv_sem,
        device_id=target,
        device_id_type=MESH,
    ).start()


def wait_bytes(ref, sem):
    pltpu.make_async_copy(ref, ref, sem).wait()


def greet():
    y, z, x, c = coords()
    blk = lax.axis_index("blk")
    barrier = pltpu.get_barrier_semaphore()
    peers = [device(y, z, x, 1 - c), device(1 - y, z, x, c), device(y, z, 1 - x, c)]
    peers += [device(y, (z + k) % CHIPS_Z, x, c) for k in range(1, CHIPS_Z)]
    for peer in peers:
        pl.semaphore_signal(barrier, inc=1, device_id=peer, device_id_type=MESH)

    @pl.when(blk > 0)
    def _():
        pl.semaphore_signal(barrier, inc=1, device_id=(y, blk - 1), device_id_type=MESH)

    @pl.when(blk < 15)
    def _():
        pl.semaphore_signal(barrier, inc=1, device_id=(y, blk + 1), device_id_type=MESH)

    inner = jnp.where((blk > 0) & (blk < 15), 1, 0)
    pl.semaphore_wait(barrier, len(peers) + 1 + inner)


class Slots:
    def __init__(self, rows, half):
        self.rows, self.half = rows, half
        self.y, self.z, self.x, self.c = coords()

    def plane(self, c):
        return pl.ds(pl.multiple_of(c * self.half, 128), self.half)

    def slot_rows(self, y, z, x):
        return pl.ds(pl.multiple_of((y * 8 + z * 2 + x) * (2 * self.rows), 8), 2 * self.rows)

    def near_pair(self, j):
        return self.y * (1 - self.c) + j * self.c, self.x * self.c + j * (1 - self.c)

    def near_peer(self):
        y, z, x, c = self.y, self.z, self.x, self.c
        return device(y + c * (1 - 2 * y), z, x + (1 - c) * (1 - 2 * x), c)

    def far_peer(self):
        y, z, x, c = self.y, self.z, self.x, self.c
        return device(y + (1 - c) * (1 - 2 * y), z, x + c * (1 - 2 * x), c)


class Gather(Slots):
    def __init__(self, shard, full, recv, sent):
        super().__init__(shard.shape[0], shard.shape[1] // 2)
        self.shard, self.full, self.recv, self.sent = shard, full, recv, sent

    def span(self, rows):
        return self.full.at[pl.ds(0, rows), pl.ds(0, self.half)]

    def mine(self):
        index = self.y * 16 + self.z * 4 + self.x * 2 + self.c
        return pl.ds(pl.multiple_of(index * self.rows, 8), self.rows)

    def slot(self, y, z, x):
        return self.full.at[self.slot_rows(y, z, x), self.plane(self.c)]

    def own_copy(self):
        own = self.plane(self.c)
        return pltpu.make_async_copy(
            self.shard.at[:, own], self.full.at[self.mine(), own], self.sent.at[2]
        )

    def step(self, number):
        y, z, x, c, rows = self.y, self.z, self.x, self.c, self.rows
        if number == 0:
            other = self.plane(1 - c)
            send(
                self.shard.at[:, other],
                self.full.at[self.mine(), other],
                self.sent.at[0],
                self.recv.at[0],
                device(y, z, x, 1 - c),
            )
            self.own_copy().start()
        if number == 1:
            self.own_copy().wait()
            wait_bytes(self.span(rows), self.recv.at[0])
            block = self.slot(y, z, x)
            for k in range(1, CHIPS_Z):
                target = device(y, (z + k) % CHIPS_Z, x, c)
                send(block, block, self.sent.at[1], self.recv.at[1], target)
        if number == 2:
            wait_bytes(self.span(6 * rows), self.recv.at[1])
            for k in range(CHIPS_Z):
                block = self.slot(y, k, x)
                send(block, block, self.sent.at[1], self.recv.at[2], self.near_peer())
        if number == 3:
            wait_bytes(self.span(8 * rows), self.recv.at[2])
            for k in range(CHIPS_Z):
                for j in range(2):
                    slot_y, slot_x = self.near_pair(j)
                    block = self.slot(slot_y, k, slot_x)
                    send(block, block, self.sent.at[1], self.recv.at[3], self.far_peer())
        if number == 4:
            wait_bytes(self.span(16 * rows), self.recv.at[3])
            block = self.full.at[:, self.plane(c)]
            send(block, block, self.sent.at[1], self.recv.at[4], device(y, z, x, 1 - c))
        if number == 5:
            wait_bytes(self.span(32 * rows), self.recv.at[4])
        if number == 6:
            wait_bytes(self.span(rows), self.sent.at[0])
            wait_bytes(self.full.at[pl.ds(0, 31 * rows)], self.sent.at[1])


class Reduce(Slots):
    def __init__(self, part, out, work, near, mid, far, last, pair, recv, sent):
        super().__init__(out.shape[0], out.shape[1] // 2)
        self.part, self.out, self.work = part, out, work
        self.near, self.mid, self.far, self.last, self.pair = near, mid, far, last, pair
        self.recv, self.sent = recv, sent

    def add(self, rows, ref, index):
        size = 2 * self.rows
        start = pl.ds(pl.multiple_of(index * size, 8), size)
        total = self.work[rows, :].astype(jnp.float32) + ref[start, :].astype(jnp.float32)
        self.work[rows, :] = total.astype(self.work.dtype)

    def step(self, number):
        y, z, x, c, rows = self.y, self.z, self.x, self.c, self.rows
        size = 2 * rows
        if number == 0:
            send(
                self.part.at[:, self.plane(1 - c)],
                self.work,
                self.sent.at[0],
                self.recv.at[0],
                device(y, z, x, 1 - c),
            )
        if number == 1:
            wait_bytes(self.work, self.recv.at[0])

            @pl.loop(0, 16)
            def _(index):
                span = pl.ds(pl.multiple_of(index * size, 8), size)
                total = self.work[span, :].astype(jnp.float32)
                total = total + self.part[span, self.plane(c)].astype(jnp.float32)
                self.work[span, :] = total.astype(self.work.dtype)

            for k in range(CHIPS_Z):
                for j in range(2):
                    slot_y = (1 - y) * (1 - c) + j * c
                    slot_x = (1 - x) * c + j * (1 - c)
                    send(
                        self.work.at[self.slot_rows(slot_y, k, slot_x)],
                        self.near.at[pl.ds((k * 2 + j) * size, size)],
                        self.sent.at[1],
                        self.recv.at[1],
                        self.far_peer(),
                    )
        if number == 2:
            wait_bytes(self.near, self.recv.at[1])

            @pl.loop(0, 8)
            def _(index):
                k, j = index // 2, index % 2
                slot_y, slot_x = self.near_pair(j)
                self.add(self.slot_rows(slot_y, k, slot_x), self.near, index)

            for k in range(CHIPS_Z):
                slot_y = y * (1 - c) + (1 - y) * c
                slot_x = x * c + (1 - x) * (1 - c)
                send(
                    self.work.at[self.slot_rows(slot_y, k, slot_x)],
                    self.mid.at[pl.ds(k * size, size)],
                    self.sent.at[1],
                    self.recv.at[2],
                    self.near_peer(),
                )
        if number == 3:
            wait_bytes(self.mid, self.recv.at[2])

            @pl.loop(0, CHIPS_Z)
            def _(k):
                self.add(self.slot_rows(y, k, x), self.mid, k)

            for k in range(1, CHIPS_Z):
                to_z = (z + k) % CHIPS_Z
                send(
                    self.work.at[self.slot_rows(y, to_z, x)],
                    self.far.at[pl.ds((k - 1) * size, size)],
                    self.sent.at[1],
                    self.recv.at[3],
                    device(y, to_z, x, c),
                )
        if number == 4:
            wait_bytes(self.far, self.recv.at[3])
            total = self.work[self.slot_rows(y, z, x), :].astype(jnp.float32)
            for k in range(CHIPS_Z - 1):
                total = total + self.far[pl.ds(k * size, size), :].astype(jnp.float32)
            self.last[...] = total
            keep = pl.ds(pl.multiple_of(c * rows, 8), rows)
            give = pl.ds(pl.multiple_of((1 - c) * rows, 8), rows)
            send(
                self.last.at[give],
                self.pair,
                self.sent.at[2],
                self.recv.at[4],
                device(y, z, x, 1 - c),
            )
            self.out[:, self.plane(c)] = self.last[keep, :]
        if number == 5:
            wait_bytes(self.pair, self.recv.at[4])
            self.out[:, self.plane(1 - c)] = self.pair[...]
        if number == 6:
            wait_bytes(self.work, self.sent.at[0])
            wait_bytes(self.work.at[pl.ds(0, 30 * rows)], self.sent.at[1])
            wait_bytes(self.pair, self.sent.at[2])


def reduce_scratch(rows, half, dtype):
    return [
        pltpu.VMEM((32 * rows, half), dtype),
        pltpu.VMEM((16 * rows, half), dtype),
        pltpu.VMEM((8 * rows, half), dtype),
        pltpu.VMEM((6 * rows, half), dtype),
        pltpu.VMEM((2 * rows, half), jnp.float32),
        pltpu.VMEM((rows, half), jnp.float32),
    ]


def seq_bounds(lengths, position):
    low = jnp.zeros((1, 128), jnp.int32)
    high = jnp.full((1, 128), NEVER, jnp.int32)
    end = low
    for i in range(lengths.shape[0]):
        end = end + lengths[i : i + 1, :]
        low = jnp.maximum(low, jnp.where(end <= position, end, 0))
        high = jnp.minimum(high, jnp.where(end > position, end, NEVER))
    return low, high


class Span:
    fields = ("start", "far_low", "far_high", "no_before", "no_after", "second")

    def __init__(self, rows):
        for i, name in enumerate(self.fields):
            setattr(self, name, rows[i : i + 1, :])


def span_rows(lengths, first_row, block, far_rows, global_count):
    position = first_row + block * BLOCK
    low, high = seq_bounds(lengths, position)
    first_low, _ = seq_bounds(lengths, first_row)
    start = jnp.minimum(low >> 4, global_count - far_rows)
    rows = [
        start,
        (low >> 4) - start,
        (high >> 4) - start,
        jnp.where(position > low, 0, NEVER),
        jnp.where(position + BLOCK < high, 0, NEVER),
        jnp.where(low == first_low, 0, 1),
    ]
    return jnp.concatenate(rows + [start, start], axis=0)


def window_select(spans, blocks, far_rows, global_count):
    parts = []
    for window in range(2):
        start = Span(spans[pl.ds(8 * window * (blocks - 1), 8), :]).start
        start = jnp.concatenate([start] * (global_count // 128), axis=1)
        row = lax.broadcasted_iota(jnp.int32, (far_rows, global_count), 0)
        column = lax.broadcasted_iota(jnp.int32, (far_rows, global_count), 1)
        parts.append((column - start == row).astype(jnp.bfloat16))
    return jnp.concatenate(parts, axis=0)


def far_part(ref, lanes, span, near_rows, far_rows):
    first = ref[pl.ds(near_rows, far_rows), lanes]
    second = ref[pl.ds(near_rows + far_rows, far_rows), lanes]
    return jnp.where(span.second > 0, second, first)


def widen(row, width):
    return jnp.concatenate([row] * (width // 128), axis=1)


def head_pair(rows):
    lane = lax.broadcasted_iota(jnp.int32, rows.shape, 1)
    zero = jnp.zeros_like(rows)
    return jnp.concatenate(
        [jnp.where(lane < HEAD_DIM, rows, zero), jnp.where(lane < HEAD_DIM, zero, rows)], axis=0
    )


def attend_block(pair, block, span, query, keys, values, attended, near_rows, far_rows):
    lanes = pl.ds(pl.multiple_of(pair * 128, 128), 128)
    rows = pl.ds(pl.multiple_of(block * BLOCK, BLOCK), BLOCK)
    near = pl.ds(pl.multiple_of(block * BLOCK, BLOCK), 3 * BLOCK)
    both = head_pair(query[rows, lanes])
    near_scores = dot_nt(both, keys[near, lanes])
    far_scores = dot_nt(both, far_part(keys, lanes, span, near_rows, far_rows))
    row = lax.broadcasted_iota(jnp.int32, (2 * BLOCK, BLOCK), 0) % BLOCK
    column = lax.broadcasted_iota(jnp.int32, (2 * BLOCK, BLOCK), 1)
    edge = jnp.where(
        column > row + span.no_before,
        near_scores[:, :BLOCK],
        jnp.where(column < row - span.no_after, near_scores[:, 2 * BLOCK :], MASKED),
    )
    own = near_scores[:, BLOCK : 2 * BLOCK]
    far_column = lax.broadcasted_iota(jnp.int32, far_scores.shape, 1)
    far_scores = jnp.where(
        (far_column >= widen(span.far_low, far_rows))
        & (far_column < widen(span.far_high, far_rows)),
        far_scores,
        MASKED,
    )
    highest = jnp.maximum(
        jnp.max(jnp.maximum(edge, own), axis=1, keepdims=True),
        jnp.max(far_scores, axis=1, keepdims=True),
    )
    edge_exp = jnp.exp(edge - highest)
    own_exp = jnp.exp(own - highest)
    far_exp = jnp.exp(far_scores - highest)
    inverse = 1.0 / (
        jnp.sum(edge_exp + own_exp, axis=1, keepdims=True) + jnp.sum(far_exp, axis=1, keepdims=True)
    )
    edge_probs = edge_exp * inverse
    near_probs = jnp.concatenate(
        [
            jnp.where(column > row, edge_probs, 0.0).astype(jnp.bfloat16),
            (own_exp * inverse).astype(jnp.bfloat16),
            jnp.where(column < row, edge_probs, 0.0).astype(jnp.bfloat16),
        ],
        axis=1,
    )
    far_probs = (far_exp * inverse).astype(jnp.bfloat16)
    mixed = dot_nn(near_probs, values[near, lanes]) + dot_nn(
        far_probs, far_part(values, lanes, span, near_rows, far_rows)
    )
    lane = lax.broadcasted_iota(jnp.int32, (BLOCK, 128), 1)
    attended[rows, lanes] = jnp.where(lane < HEAD_DIM, mixed[:BLOCK], mixed[BLOCK:]).astype(
        jnp.bfloat16
    )


def attend_block_back(
    pair, block, span, query, grad, keys, keys_t, values, grad_query, grad_keys, grad_values,
    near_rows, far_rows,
):
    lanes = pl.ds(pl.multiple_of(pair * 128, 128), 128)
    rows = pl.ds(pl.multiple_of(block * BLOCK, BLOCK), BLOCK)
    near = pl.ds(pl.multiple_of(block * BLOCK, BLOCK), 3 * BLOCK)
    both = head_pair(query[rows, lanes])
    grads = head_pair(grad[rows, lanes])
    near_scores = dot_nt(keys[near, lanes], both)
    far_keys = far_part(keys, lanes, span, near_rows, far_rows)
    far_scores = dot_nt(far_keys, both)
    row = lax.broadcasted_iota(jnp.int32, (BLOCK, 2 * BLOCK), 0)
    column = lax.broadcasted_iota(jnp.int32, (BLOCK, 2 * BLOCK), 1) % BLOCK
    edge = jnp.where(
        row > column + widen(span.no_before, 2 * BLOCK),
        near_scores[:BLOCK],
        jnp.where(row < column - widen(span.no_after, 2 * BLOCK), near_scores[2 * BLOCK :], MASKED),
    )
    own = near_scores[BLOCK : 2 * BLOCK]
    far_row = lax.broadcasted_iota(jnp.int32, far_scores.shape, 0)
    far_scores = jnp.where(
        (far_row >= widen(span.far_low, 2 * BLOCK)) & (far_row < widen(span.far_high, 2 * BLOCK)),
        far_scores,
        MASKED,
    )
    highest = jnp.maximum(
        jnp.max(jnp.maximum(edge, own), axis=0, keepdims=True),
        jnp.max(far_scores, axis=0, keepdims=True),
    )
    edge_exp = jnp.exp(edge - highest)
    own_exp = jnp.exp(own - highest)
    far_exp = jnp.exp(far_scores - highest)
    inverse = 1.0 / (
        jnp.sum(edge_exp + own_exp, axis=0, keepdims=True) + jnp.sum(far_exp, axis=0, keepdims=True)
    )
    edge_probs, own_probs, far_probs = edge_exp * inverse, own_exp * inverse, far_exp * inverse
    near_dprobs = dot_nt(values[near, lanes], grads)
    far_dprobs = dot_nt(far_part(values, lanes, span, near_rows, far_rows), grads)
    edge_dprobs = jnp.where(row > column, near_dprobs[:BLOCK], near_dprobs[2 * BLOCK :])
    own_dprobs = near_dprobs[BLOCK : 2 * BLOCK]
    delta = jnp.sum(
        edge_probs * edge_dprobs + own_probs * own_dprobs, axis=0, keepdims=True
    ) + jnp.sum(far_probs * far_dprobs, axis=0, keepdims=True)
    edge_ds = edge_probs * (edge_dprobs - delta)
    own_ds = (own_probs * (own_dprobs - delta)).astype(jnp.bfloat16)
    far_ds = (far_probs * (far_dprobs - delta)).astype(jnp.bfloat16)

    def spread(edge_part, own_part):
        return jnp.concatenate(
            [
                jnp.where(row > column, edge_part, 0.0).astype(jnp.bfloat16),
                own_part.astype(jnp.bfloat16),
                jnp.where(row < column, edge_part, 0.0).astype(jnp.bfloat16),
            ],
            axis=0,
        )

    near_ds = spread(edge_ds, own_ds)
    far_keys_t = jnp.where(
        widen(span.second, far_rows) > 0,
        keys_t[lanes, pl.ds(near_rows + far_rows, far_rows)],
        keys_t[lanes, pl.ds(near_rows, far_rows)],
    )
    query_t = dot_nn(keys_t[lanes, near], near_ds) + dot_nn(far_keys_t, far_ds)
    feature = lax.broadcasted_iota(jnp.int32, (128, BLOCK), 0)
    query_t = jnp.where(feature < HEAD_DIM, query_t[:, :BLOCK], query_t[:, BLOCK:])
    grad_query[rows, lanes] = query_t.T.astype(jnp.bfloat16)
    grad_keys[near, lanes] += dot_nn(near_ds, both)
    grad_values[near, lanes] += dot_nn(spread(edge_probs, own_probs), grads)
    far_dkey = dot_nn(far_ds, both)
    far_dvalue = dot_nn(far_probs.astype(jnp.bfloat16), grads)
    for window in range(2):
        place = pl.ds(near_rows + window * far_rows, far_rows)
        here = span.second == window
        grad_keys[place, lanes] += jnp.where(here, far_dkey, 0.0)
        grad_values[place, lanes] += jnp.where(here, far_dvalue, 0.0)


def inverse_rms(values):
    return lax.rsqrt(jnp.mean(values * values, axis=-1, keepdims=True) + EPSILON)


def rms_back(values, gain, grads):
    scale = inverse_rms(values)
    scaled = grads * gain
    back = scale * scaled - values * (
        scale * scale * scale * jnp.mean(scaled * values, axis=-1, keepdims=True)
    )
    return back, jnp.sum(grads * values * scale, axis=0, keepdims=True)


def block_sums(rows, count):
    take = lax.broadcasted_iota(jnp.int32, (count, rows.shape[0]), 1) // GBLK
    which = lax.broadcasted_iota(jnp.int32, (count, rows.shape[0]), 0)
    return dot_nn((take == which).astype(jnp.bfloat16), rows)


def owner_of(column, rows):
    return (column * ((65536 + rows - 1) // rows)) >> 16


def spread_gains(packed, rows):
    width = 32 * rows
    lane = lax.broadcasted_iota(jnp.int32, (128, width), 0)
    column = lax.broadcasted_iota(jnp.int32, (128, width), 1)
    select = (column - rows * owner_of(column, rows) == lane).astype(jnp.float32)
    wide = dot(packed, select, ((1,), (0,)), precision=lax.Precision.HIGHEST)
    device_row = lax.broadcasted_iota(jnp.int32, wide.shape, 0) >> 3
    wide_column = lax.broadcasted_iota(jnp.int32, wide.shape, 1)
    wide = jnp.where(owner_of(wide_column, rows) == device_row, wide, 0.0)
    return jnp.sum(wide.reshape(32, 8, width), axis=0)


def pack_gains(wide, rows):
    width = 32 * rows
    tall = jnp.concatenate([wide] * 32, axis=0)
    device_row = lax.broadcasted_iota(jnp.int32, tall.shape, 0) >> 3
    column = lax.broadcasted_iota(jnp.int32, tall.shape, 1)
    tall = jnp.where(owner_of(column, rows) == device_row, tall, 0.0)
    lane = lax.broadcasted_iota(jnp.int32, (width, 128), 1)
    from_column = lax.broadcasted_iota(jnp.int32, (width, 128), 0)
    select = (from_column - rows * owner_of(from_column, rows) == lane).astype(jnp.float32)
    return dot(tall, select, ((1,), (0,)), precision=lax.Precision.HIGHEST)


def forward_kernel(lengths, tokens, gains, *refs):
    shards, refs = refs[:7], refs[7:]
    fulls, refs = refs[:7], refs[7:]
    rows_in_t, query, keys, keys_t, values, attended, gain_rows, group_sums = refs[:8]
    spans, rows_in, gathered, halo, global_rows, w_query, w_key, w_value = refs[8:16]
    recv, sent, halo_sem, global_sem, load_sem = refs[16:]
    y, z, x, c = coords()
    blk = lax.axis_index("blk")
    row_count = tokens.shape[0]
    local_globals = row_count // GBLK
    global_count = global_rows.shape[0]
    near_rows = row_count + 2 * BLOCK
    far_rows = (rows_in.shape[0] - near_rows) // 2
    first_row = blk * row_count
    feature_rows = gain_rows.shape[1] // 32
    blocks = row_count // BLOCK

    greet()
    gain_steps = Gather(gains, gathered, recv.at[0], sent.at[0])
    steps = [Gather(shards[i], fulls[i], recv.at[i + 1], sent.at[i + 1]) for i in range(7)]
    first, rest = [steps[1], steps[2], steps[0]], steps[3:]
    gain_steps.step(0)
    for one in first + rest:
        one.step(0)

    def halo_copy(side):
        source = pl.ds(row_count - BLOCK, BLOCK) if side == 0 else pl.ds(0, BLOCK)
        return pltpu.make_async_remote_copy(
            src_ref=tokens.at[source],
            dst_ref=halo.at[side],
            send_sem=halo_sem.at[side],
            recv_sem=halo_sem.at[2 + side],
            device_id=(y, blk + 1 - 2 * side),
            device_id_type=MESH,
        )

    pl.when(blk < 15)(lambda: halo_copy(0).start())
    pl.when(blk > 0)(lambda: halo_copy(1).start())
    gain_steps.step(1)
    for one in first + rest:
        one.step(1)
    for number in range(2, 6):
        gain_steps.step(number)
    for block in range(blocks):
        spans[pl.ds(8 * block, 8), :] = span_rows(
            lengths, first_row, block, far_rows, global_count
        )
    gain_rows[...] = spread_gains(gathered[:, :128], feature_rows)
    norm_gain = gain_rows[0:1, :]
    global_gain = gain_rows[1:2, :]

    def normed(part):
        wide = part.astype(jnp.float32)
        return (wide * inverse_rms(wide) * norm_gain).astype(jnp.bfloat16)

    own = normed(tokens[...])
    rows_in[pl.ds(BLOCK, row_count), :] = own
    summed = block_sums(own, local_globals)
    group_sums[...] = summed
    own_globals = (summed * inverse_rms(summed) * global_gain).astype(jnp.bfloat16)

    def global_slot(slot_z, slot_x, slot_c, count=1):
        index = slot_z * 4 + slot_x * 2 + slot_c
        return global_rows.at[pl.ds(pl.multiple_of(index * local_globals, 16), local_globals)]

    place = pl.ds(pl.multiple_of(blk * local_globals, 16), local_globals)
    global_rows[place, :] = own_globals
    for one in first:
        one.step(2)
    block = global_slot(z, x, c)
    for k in range(1, CHIPS_Z):
        send(block, block, global_sem.at[0], global_sem.at[1], device(y, (z + k) % CHIPS_Z, x, c))

    @pl.when(blk == 0)
    def _():
        halo[0] = jnp.zeros_like(halo[0])

    @pl.when(blk == 15)
    def _():
        halo[1] = jnp.zeros_like(halo[1])

    pl.when(blk > 0)(lambda: halo_copy(0).wait_recv())
    pl.when(blk < 15)(lambda: halo_copy(1).wait_recv())
    rows_in[pl.ds(0, BLOCK), :] = normed(halo[0])
    rows_in[pl.ds(BLOCK + row_count, BLOCK), :] = normed(halo[1])
    wait_bytes(global_rows.at[pl.ds(0, 3 * local_globals)], global_sem.at[1])
    for k in range(CHIPS_Z):
        block = global_slot(k, x, c)
        send(block, block, global_sem.at[0], global_sem.at[2], device(y, z, 1 - x, c))
    for one in first:
        one.step(3)
    wait_bytes(global_rows.at[pl.ds(0, 4 * local_globals)], global_sem.at[2])
    for k in range(CHIPS_Z):
        for j in range(2):
            block = global_slot(k, j, c)
            send(block, block, global_sem.at[0], global_sem.at[3], device(y, z, x, 1 - c))
    for one in first:
        one.step(4)
    wait_bytes(global_rows.at[pl.ds(0, 8 * local_globals)], global_sem.at[3])
    select = window_select(spans, blocks, far_rows, global_count)
    rows_in[pl.ds(near_rows, 2 * far_rows), :] = dot_nn(select, global_rows[...]).astype(
        jnp.bfloat16
    )
    for start in range(0, rows_in.shape[0], 256):
        rows_in_t[:, pl.ds(start, 256)] = rows_in[pl.ds(start, 256), :].T

    def project(one, held, index, target, start, count):
        one.step(5)
        load = pltpu.make_async_copy(one.full, held, load_sem.at[index])
        load.start()
        load.wait()

        @pl.loop(0, count // 256)
        def _(i):
            source = pl.ds(pl.multiple_of(start + i * 256, 128), 256)
            to = pl.ds(pl.multiple_of(i * 256, 256), 256)
            target[to, :] = dot_nn(rows_in[source, :], held[...]).astype(jnp.bfloat16)

    rest[0].step(2)
    project(steps[1], w_key, 1, keys, 0, rows_in.shape[0])
    rest[1].step(2)
    project(steps[2], w_value, 2, values, 0, rows_in.shape[0])
    rest[0].step(3)
    project(steps[0], w_query, 0, query, BLOCK, row_count)
    for start in range(0, rows_in.shape[0], 256):
        keys_t[:, pl.ds(start, 256)] = keys[pl.ds(start, 256), :].T
    ticks = [
        [(1, 3), (2, 2)],
        [(0, 4), (3, 2)],
        [(2, 3), (1, 4)],
        [(3, 3)],
        [(2, 4)],
        [(3, 4)],
    ]

    @pl.loop(0, HEADS // 2)
    def _(pair):
        for number, todo in enumerate(ticks):

            @pl.when(pair == number)
            def _():
                for index, step in todo:
                    rest[index].step(step)

        @pl.loop(0, blocks)
        def _(block):
            span = Span(spans[pl.ds(pl.multiple_of(block * 8, 8), 8), :])
            attend_block(
                pair, block, span, query, keys, values, attended, near_rows, far_rows
            )

    for one in rest:
        one.step(5)
    for one in [gain_steps] + steps:
        one.step(6)
    wait_bytes(global_rows.at[pl.ds(0, 15 * local_globals)], global_sem.at[0])
    pl.when(blk < 15)(lambda: halo_copy(0).wait_send())
    pl.when(blk > 0)(lambda: halo_copy(1).wait_send())


def forward(lengths, tokens, gains, shards, far_rows, global_count):
    row_count, width = tokens.shape
    all_rows = row_count + 2 * BLOCK + 2 * far_rows
    vmem = pl.BlockSpec(memory_space=pltpu.VMEM)
    anywhere = pl.BlockSpec(memory_space=pl.ANY)
    low = jnp.bfloat16

    def shape(*dims, dtype=low):
        return jax.ShapeDtypeStruct(dims, dtype)

    outs = pl.pallas_call(
        forward_kernel,
        out_shape=[shape(s.shape[0] * 32, s.shape[1]) for s in shards]
        + [
            shape(width, all_rows),
            shape(row_count, width),
            shape(all_rows, width),
            shape(width, all_rows),
            shape(all_rows, width),
            shape(row_count, width),
            shape(8, width, dtype=jnp.float32),
            shape(row_count // GBLK, width, dtype=jnp.float32),
            shape(8 * (row_count // BLOCK), 128, dtype=jnp.int32),
        ],
        in_specs=[vmem, vmem, vmem] + [anywhere] * 7,
        out_specs=[anywhere] * 7 + [vmem] * 9,
        scratch_shapes=[
            pltpu.VMEM((all_rows, width), low),
            pltpu.VMEM((256, 256), jnp.float32),
            pltpu.VMEM((2, BLOCK, width), low),
            pltpu.VMEM((global_count, width), low),
            pltpu.VMEM((width, width), low),
            pltpu.VMEM((width, width), low),
            pltpu.VMEM((width, width), low),
            pltpu.SemaphoreType.DMA((8, 5)),
            pltpu.SemaphoreType.DMA((8, 3)),
            pltpu.SemaphoreType.DMA((4,)),
            pltpu.SemaphoreType.DMA((4,)),
            pltpu.SemaphoreType.DMA((3,)),
        ],
        compiler_params=pltpu.CompilerParams(
            collective_id=0, has_side_effects=True, vmem_limit_bytes=VMEM_BYTES
        ),
        name="gather_attend",
    )(lengths, tokens, gains, *shards)
    return outs[:7], outs[7:]


def backward_kernel(spans, tokens, gain_rows, gain_ffn, grad_attended, *refs):
    group_sums, rows_in_t, query, keys, keys_t, values, w_query, w_key, w_value = refs[:9]
    parts, refs = refs[9:13], refs[13:]
    outs, gain_out, grad_tokens, refs = refs[:7], refs[7], refs[8], refs[9:]
    grad_query, grad_keys, grad_values, low_keys, low_values = refs[:5]
    halo, global_part, global_near, global_mid, global_far = refs[5:10]
    own_parts, gain_part, refs = refs[10:13], refs[13], refs[14:]
    buffers, refs = refs[:48], refs[48:]
    recv, sent, halo_sem, global_sem = refs
    y, z, x, c = coords()
    blk = lax.axis_index("blk")
    row_count = tokens.shape[0]
    local_globals = row_count // GBLK
    global_count = global_part.shape[0]
    near_rows = row_count + 2 * BLOCK
    all_rows = keys.shape[0]
    far_rows = (all_rows - near_rows) // 2
    blocks = row_count // BLOCK
    feature_rows = gain_rows.shape[1] // 32

    greet()
    every = list(own_parts) + list(parts) + [gain_part]
    steps = [
        Reduce(part, out, *buffers[6 * i : 6 * i + 6], recv.at[i], sent.at[i])
        for i, (part, out) in enumerate(zip(every, list(outs) + [gain_out]))
    ]
    early, late, gain_steps = [steps[6], steps[4], steps[5], steps[3]], steps[:3], steps[7]
    for one in early:
        one.step(0)
    grad_keys[...] = jnp.zeros_like(grad_keys)
    grad_values[...] = jnp.zeros_like(grad_values)
    ticks = [
        [(0, 1), (1, 1)],
        [(0, 2), (2, 1), (3, 1)],
        [(1, 2), (0, 3)],
        [(2, 2), (1, 3)],
        [(3, 2), (2, 3), (0, 4)],
        [(3, 3), (1, 4)],
    ]

    @pl.loop(0, HEADS // 2)
    def _(pair):
        for number, todo in enumerate(ticks):

            @pl.when(pair == number)
            def _():
                for index, step in todo:
                    early[index].step(step)

        @pl.loop(0, blocks)
        def _(block):
            span = Span(spans[pl.ds(pl.multiple_of(block * 8, 8), 8), :])
            attend_block_back(
                pair, block, span, query, grad_attended, keys, keys_t, values,
                grad_query, grad_keys, grad_values, near_rows, far_rows,
            )

    def weight_grad(target, grads, start, count):
        @pl.loop(0, 3)
        def _(i):
            part = pl.ds(pl.multiple_of(i * 256, 256), 256)
            target[part, :] = dot_nn(rows_in_t[part, pl.ds(start, count)], grads[...]).astype(
                jnp.bfloat16
            )

    weight_grad(own_parts[0], grad_query, BLOCK, row_count)
    late[0].step(0)
    low_keys[...] = grad_keys[...].astype(jnp.bfloat16)
    weight_grad(own_parts[1], low_keys, 0, all_rows)
    late[1].step(0)
    low_values[...] = grad_values[...].astype(jnp.bfloat16)
    weight_grad(own_parts[2], low_values, 0, all_rows)
    late[2].step(0)

    def grad_rows(start, count):
        part = pl.ds(start, count)
        return dot_nt(low_keys[part, :], w_key[...]) + dot_nt(low_values[part, :], w_value[...])

    halo[2] = grad_rows(0, BLOCK).astype(jnp.bfloat16)
    halo[3] = grad_rows(BLOCK + row_count, BLOCK).astype(jnp.bfloat16)
    late[0].step(1)

    def halo_copy(side):
        return pltpu.make_async_remote_copy(
            src_ref=halo.at[2 + side],
            dst_ref=halo.at[1 - side],
            send_sem=halo_sem.at[side],
            recv_sem=halo_sem.at[2 + side],
            device_id=(y, blk - 1 + 2 * side),
            device_id_type=MESH,
        )

    pl.when(blk > 0)(lambda: halo_copy(0).start())
    pl.when(blk < 15)(lambda: halo_copy(1).start())
    far_grads = grad_rows(near_rows, 2 * far_rows).astype(jnp.bfloat16)
    select = window_select(spans, blocks, far_rows, global_count)
    global_part[...] = dot(select, far_grads, ((0,), (0,))).astype(jnp.bfloat16)
    late[1].step(1)

    def global_rows(slot_z, slot_x, slot_c):
        index = slot_z * 4 + slot_x * 2 + slot_c
        return pl.ds(pl.multiple_of(index * local_globals, 16), local_globals)

    def packed(index):
        return pl.ds(pl.multiple_of(index * local_globals, 16), local_globals)

    for k in range(CHIPS_Z):
        for j in range(2):
            send(
                global_part.at[global_rows(k, j, 1 - c)],
                global_near.at[packed(k * 2 + j)],
                global_sem.at[0],
                global_sem.at[1],
                device(y, z, x, 1 - c),
            )
    late[2].step(1)
    wait_bytes(global_near, global_sem.at[1])

    def add_global(rows, ref, index):
        total = global_part[rows, :].astype(jnp.float32) + ref[packed(index), :].astype(jnp.float32)
        global_part[rows, :] = total.astype(jnp.bfloat16)

    for k in range(CHIPS_Z):
        for j in range(2):
            add_global(global_rows(k, j, c), global_near, k * 2 + j)
    for k in range(CHIPS_Z):
        send(
            global_part.at[global_rows(k, 1 - x, c)],
            global_mid.at[packed(k)],
            global_sem.at[0],
            global_sem.at[2],
            device(y, z, 1 - x, c),
        )
    late[0].step(2)
    late[1].step(2)
    wait_bytes(global_mid, global_sem.at[2])
    for k in range(CHIPS_Z):
        add_global(global_rows(k, x, c), global_mid, k)
    for k in range(1, CHIPS_Z):
        to_z = (z + k) % CHIPS_Z
        send(
            global_part.at[global_rows(to_z, x, c)],
            global_far.at[packed(k - 1)],
            global_sem.at[0],
            global_sem.at[3],
            device(y, to_z, x, c),
        )
    late[2].step(2)
    late[0].step(3)
    grad_normed = grad_rows(BLOCK, row_count) + dot_nt(grad_query[...], w_query[...])

    @pl.when(blk == 0)
    def _():
        halo[0] = jnp.zeros_like(halo[0])

    @pl.when(blk == 15)
    def _():
        halo[1] = jnp.zeros_like(halo[1])

    pl.when(blk > 0)(lambda: halo_copy(1).wait_recv())
    pl.when(blk < 15)(lambda: halo_copy(0).wait_recv())
    grad_normed = grad_normed + jnp.concatenate(
        [
            halo[0].astype(jnp.float32),
            jnp.zeros((row_count - 2 * BLOCK, halo.shape[2]), jnp.float32),
            halo[1].astype(jnp.float32),
        ],
        axis=0,
    )
    late[1].step(3)
    wait_bytes(global_far, global_sem.at[3])
    total = global_part[global_rows(z, x, c), :].astype(jnp.float32)
    for k in range(CHIPS_Z - 1):
        total = total + global_far[packed(k), :].astype(jnp.float32)
    grad_summed, grad_global_gain = rms_back(group_sums[...], gain_rows[1:2, :], total)
    width = grad_summed.shape[1]
    grad_normed = grad_normed + jnp.broadcast_to(
        grad_summed[:, None, :], (local_globals, GBLK, width)
    ).reshape(row_count, width)
    wide = tokens[...].astype(jnp.float32)
    back, grad_norm_gain = rms_back(wide, gain_rows[0:1, :], grad_normed)
    grad_tokens[...] = back
    gain_grads = jnp.concatenate(
        [grad_norm_gain, grad_global_gain, gain_ffn[...], jnp.zeros((5, width), jnp.float32)], axis=0
    )
    gain_part[:, pl.ds(0, 128)] = pack_gains(gain_grads, feature_rows)
    gain_part[:, pl.ds(128, 128)] = jnp.zeros((256, 128), jnp.float32)
    late[2].step(3)
    gain_steps.step(0)
    late[0].step(4)
    gain_steps.step(1)
    late[1].step(4)
    gain_steps.step(2)
    late[2].step(4)
    gain_steps.step(3)
    early[2].step(4)
    early[3].step(4)
    gain_steps.step(4)
    for one in early + late + [gain_steps]:
        one.step(5)
    for one in steps:
        one.step(6)
    wait_bytes(global_part.at[pl.ds(0, 15 * local_globals)], global_sem.at[0])
    pl.when(blk > 0)(lambda: halo_copy(0).wait_send())
    pl.when(blk < 15)(lambda: halo_copy(1).wait_send())


def backward(spans, tokens, gain_rows, gain_ffn, grad_attended, kept, weights, parts):
    row_count, width = tokens.shape
    all_rows = kept[1].shape[1]
    global_count = row_count * 16 // GBLK
    local_globals = row_count // GBLK
    vmem = pl.BlockSpec(memory_space=pltpu.VMEM)
    low = jnp.bfloat16
    shard_shapes = [(width // 32, width)] * 3 + [(p.shape[0] // 32, p.shape[1]) for p in parts]
    buffers = []
    for rows, columns in shard_shapes:
        buffers += reduce_scratch(rows, columns // 2, low)
    buffers += reduce_scratch(8, 128, jnp.float32)
    outs = pl.pallas_call(
        backward_kernel,
        out_shape=[jax.ShapeDtypeStruct(s, jnp.float32) for s in shard_shapes]
        + [
            jax.ShapeDtypeStruct((8, 256), jnp.float32),
            jax.ShapeDtypeStruct((row_count, width), jnp.float32),
        ],
        in_specs=[vmem] * 18,
        out_specs=[vmem] * 9,
        scratch_shapes=[
            pltpu.VMEM((row_count, width), low),
            pltpu.VMEM((all_rows, width), jnp.float32),
            pltpu.VMEM((all_rows, width), jnp.float32),
            pltpu.VMEM((all_rows, width), low),
            pltpu.VMEM((all_rows, width), low),
            pltpu.VMEM((4, BLOCK, width), low),
            pltpu.VMEM((global_count, width), low),
            pltpu.VMEM((8 * local_globals, width), low),
            pltpu.VMEM((4 * local_globals, width), low),
            pltpu.VMEM((3 * local_globals, width), low),
            pltpu.VMEM((width, width), low),
            pltpu.VMEM((width, width), low),
            pltpu.VMEM((width, width), low),
            pltpu.VMEM((256, 256), jnp.float32),
        ]
        + buffers
        + [
            pltpu.SemaphoreType.DMA((8, 5)),
            pltpu.SemaphoreType.DMA((8, 3)),
            pltpu.SemaphoreType.DMA((4,)),
            pltpu.SemaphoreType.DMA((4,)),
        ],
        compiler_params=pltpu.CompilerParams(
            collective_id=1, has_side_effects=True, vmem_limit_bytes=VMEM_BYTES
        ),
        name="attend_back_reduce",
    )(spans, tokens, gain_rows, gain_ffn, grad_attended, *kept, *weights, *parts)
    return outs[:7], outs[7], outs[8]


def per_device(
    tokens, lengths, norm_gain, global_gain, w_query, w_key, w_value, w_out,
    ffn_gain, w_gate, w_up, w_down, cotangent,
):
    row_count, width = tokens.shape
    low = jnp.bfloat16
    global_count = row_count * lax.axis_size("blk") // GBLK
    far_rows = global_count // 2
    feature_rows = norm_gain.shape[0]
    packed = jnp.stack([norm_gain, global_gain, ffn_gain]).astype(jnp.float32)
    packed = jnp.pad(packed, ((0, 5), (0, 256 - feature_rows)))
    shards = (w_query, w_key, w_value, w_out, w_gate, w_up, w_down)
    wide_lengths = jnp.broadcast_to(lengths[0][:, None], (lengths.shape[1], 128))
    full, kept = forward(wide_lengths, tokens, packed, shards, far_rows, global_count)
    rows_in_t, query, keys, keys_t, values, attended, gain_rows, group_sums, spans = kept
    tokens_full = tokens.astype(jnp.float32)
    middle = tokens_full + matmul(attended, full[3])
    gain = gain_rows[2]
    hidden_full, hidden_pull = jax.vjp(rms_norm, middle, gain)
    hidden = hidden_full.astype(low)
    gate_pre = matmul(hidden, full[4])
    up_pre = matmul(hidden, full[5])
    gated_rows, gated_pull = jax.vjp(gated, gate_pre, up_pre)
    mixed = gated_rows.astype(low)
    output = (middle + matmul(mixed, full[6])).astype(low)
    grad_down = matmul_left(mixed, cotangent).astype(low)
    grad_mixed = matmul_right(cotangent, full[6])
    grad_gate_full, grad_up_full = gated_pull(grad_mixed)
    grad_gate = grad_gate_full.astype(low)
    grad_up = grad_up_full.astype(low)
    grad_wgate = matmul_left(hidden, grad_gate).astype(low)
    grad_wup = matmul_left(hidden, grad_up).astype(low)
    grad_hidden = matmul_right(grad_gate, full[4]) + matmul_right(grad_up, full[5])
    grad_middle_norm, grad_ffn_gain = hidden_pull(grad_hidden)
    grad_middle = cotangent.astype(jnp.float32) + grad_middle_norm
    grad_branch = grad_middle.astype(low)
    grad_wout = matmul_left(attended, grad_branch).astype(low)
    grad_attended = matmul_right(grad_branch, full[3]).astype(low)
    grads, gain_grads, grad_tokens = backward(
        spans,
        tokens,
        gain_rows,
        grad_ffn_gain[None, :],
        grad_attended,
        (group_sums, rows_in_t, query, keys, keys_t, values),
        full[:3],
        (grad_wout, grad_wgate, grad_wup, grad_down),
    )
    return (
        output,
        grad_middle + grad_tokens,
        gain_grads[0, :feature_rows],
        gain_grads[1, :feature_rows],
        *grads[:4],
        gain_grads[2, :feature_rows],
        *grads[4:],
    )


def fits(mesh):
    return mesh.shape["seq"] == 2 and mesh.shape["blk"] == 16


def solution(mesh):
    return jax.shard_map(
        per_device if fits(mesh) else per_device_general,
        mesh=mesh,
        in_specs=(
            P(("seq", "blk"), None),
            P("seq", None),
            P(("seq", "blk")),
            P(("seq", "blk")),
            P(("seq", "blk"), None),
            P(("seq", "blk"), None),
            P(("seq", "blk"), None),
            P(("seq", "blk"), None),
            P(("seq", "blk")),
            P(("seq", "blk"), None),
            P(("seq", "blk"), None),
            P(("seq", "blk"), None),
            P(("seq", "blk"), None),
        ),
        out_specs=(
            P(("seq", "blk"), None),
            P(("seq", "blk"), None),
            P(("seq", "blk")),
            P(("seq", "blk")),
            P(("seq", "blk"), None),
            P(("seq", "blk"), None),
            P(("seq", "blk"), None),
            P(("seq", "blk"), None),
            P(("seq", "blk")),
            P(("seq", "blk"), None),
            P(("seq", "blk"), None),
            P(("seq", "blk"), None),
        ),
        check_vma=False,
    )
```

```python
import functools

import jax
import jax.numpy as jnp
from jax import lax
from jax.experimental import pallas as pl
from jax.experimental.pallas import tpu as pltpu
from jax.sharding import PartitionSpec as P


D = 768
HEADS = 12
HEAD_DIM = 64
GBLK = 16
BLOCK = 128
LONGEST = 16384


EPSILON = 1e-06
MASKED = -1e30
GELU_SCALE = 0.7978845608028654
GELU_CUBIC = 0.044715


def with_halo(block, sides, width):
    for axis, dim in sides:
        count = lax.axis_size(axis)
        forward = [(i, i + 1) for i in range(count - 1)]
        backward = [(target, source) for source, target in forward]
        low = lax.ppermute(
            lax.slice_in_dim(block, block.shape[dim] - width, None, axis=dim), axis, forward
        )
        high = lax.ppermute(lax.slice_in_dim(block, 0, width, axis=dim), axis, backward)
        block = jnp.concatenate([low, block, high], axis=dim)
    return block


def rms_norm(values, scales):
    return values * lax.rsqrt(jnp.mean(values * values, axis=-1, keepdims=True) + EPSILON) * scales


def gelu_tanh(values):
    return (
        0.5
        * values
        * (1.0 + jnp.tanh(GELU_SCALE * (values + GELU_CUBIC * values * values * values)))
    )


def gated(gate_part, up_part):
    return gelu_tanh(gate_part) * up_part


def sequence_of(positions, seq_ends):
    return jnp.sum((positions[:, None] >= seq_ends[None, :]).astype(jnp.int32), axis=1)


def matmul(left_side, right_side):
    return jnp.dot(left_side, right_side, preferred_element_type=jnp.float32)


def matmul_left(left_side, right_side):
    return jnp.einsum("ta,tb->ab", left_side, right_side, preferred_element_type=jnp.float32)


def matmul_right(left_side, right_side):
    return jnp.einsum("ta,ba->tb", left_side, right_side, preferred_element_type=jnp.float32)


def windows(extended, row_count):
    block_count = row_count // BLOCK
    pieces = [
        extended[offset * BLOCK : offset * BLOCK + row_count].reshape(
            block_count, BLOCK, extended.shape[-1]
        )
        for offset in range(3)
    ]
    return jnp.concatenate(pieces, axis=1)


def unwindow(window_grads, row_count):
    channels = window_grads.shape[-1]
    summed_grad = jnp.zeros((row_count + 2 * BLOCK, channels), jnp.float32)
    for offset in range(3):
        piece_grad = window_grads[:, offset * BLOCK : (offset + 1) * BLOCK].reshape(
            row_count, channels
        )
        summed_grad = summed_grad + jnp.pad(
            piece_grad, ((offset * BLOCK, (2 - offset) * BLOCK), (0, 0))
        )
    return summed_grad


def head_scores(query_head, near_keys, far_keys, near_mask, far_mask):
    block_count = near_keys.shape[0]
    query_blocks = query_head.reshape(block_count, BLOCK, HEAD_DIM)
    near_scores = jnp.einsum(
        "nqd,nkd->nqk", query_blocks, near_keys, preferred_element_type=jnp.float32
    )
    far_scores = jnp.einsum("qd,kd->qk", query_head, far_keys, preferred_element_type=jnp.float32)
    return (jnp.where(near_mask, near_scores, MASKED), jnp.where(far_mask, far_scores, MASKED))


def per_device_general(
    tokens,
    lengths,
    norm_gain,
    global_gain,
    w_query,
    w_key,
    w_value,
    w_out,
    ffn_gain,
    w_gate,
    w_up,
    w_down,
    cotangent,
):
    row_count = tokens.shape[0]
    inner_dim = HEADS * HEAD_DIM
    block_count = row_count // BLOCK
    local_globals = row_count // GBLK
    group_tokens = row_count * lax.axis_size("blk")
    global_count = group_tokens // GBLK
    longest_len = min(LONGEST, group_tokens // 2)
    span_rows = min(global_count, 2 * (longest_len // GBLK) + local_globals)
    attn_full = (
        lax.all_gather(norm_gain, ("seq", "blk"), axis=0, tiled=True),
        lax.all_gather(global_gain, ("seq", "blk"), axis=0, tiled=True),
        lax.all_gather(w_query, ("seq", "blk"), axis=0, tiled=True),
        lax.all_gather(w_key, ("seq", "blk"), axis=0, tiled=True),
        lax.all_gather(w_value, ("seq", "blk"), axis=0, tiled=True),
        lax.all_gather(w_out, ("seq", "blk"), axis=0, tiled=True),
    )
    seq_ends = jnp.cumsum(lengths[0])
    first_row = lax.axis_index("blk") * row_count
    span_start = jnp.clip(first_row // GBLK - longest_len // GBLK, 0, global_count - span_rows)
    query_pos = first_row + jnp.arange(row_count, dtype=jnp.int32)
    query_seq = sequence_of(query_pos, seq_ends)
    key_pos = first_row - BLOCK + jnp.arange(row_count + 2 * BLOCK, dtype=jnp.int32)
    inside = (key_pos >= 0) & (key_pos < group_tokens)
    key_seq = jnp.where(inside, sequence_of(key_pos, seq_ends), -1)
    global_seq = sequence_of((span_start + jnp.arange(span_rows, dtype=jnp.int32)) * GBLK, seq_ends)
    query_pos_win = query_pos.reshape(block_count, BLOCK)
    query_seq_win = query_seq.reshape(block_count, BLOCK)
    key_pos_win = windows(key_pos[:, None], row_count)[:, :, 0]
    key_seq_win = windows(key_seq[:, None], row_count)[:, :, 0]
    near_mask = (jnp.abs(query_pos_win[:, :, None] - key_pos_win[:, None, :]) <= BLOCK - 1) & (
        query_seq_win[:, :, None] == key_seq_win[:, None, :]
    )
    far_mask = query_seq[:, None] == global_seq[None, :]
    tokens_full = tokens.astype(jnp.float32)
    normed_full, normed_pull = jax.vjp(rms_norm, tokens_full, attn_full[0].astype(jnp.float32))
    normed = normed_full.astype(jnp.bfloat16)
    queries = matmul(normed, attn_full[2]).astype(jnp.bfloat16)
    key_rows = matmul(normed, attn_full[3]).astype(jnp.bfloat16)
    value_rows = matmul(normed, attn_full[4]).astype(jnp.bfloat16)
    local_kv = jnp.concatenate([key_rows, value_rows], axis=1)
    extended = with_halo(local_kv, (("blk", 0),), BLOCK)
    near_kv = windows(extended, row_count)
    summed = jnp.sum(normed.astype(jnp.float32).reshape(local_globals, GBLK, D), axis=1)
    global_full, global_pull = jax.vjp(rms_norm, summed, attn_full[1].astype(jnp.float32))
    global_in = global_full.astype(jnp.bfloat16)
    own_global = jnp.concatenate(
        [
            matmul(global_in, attn_full[3]).astype(jnp.bfloat16),
            matmul(global_in, attn_full[4]).astype(jnp.bfloat16),
        ],
        axis=1,
    )
    global_kv = lax.all_gather(own_global, "blk", axis=0, tiled=True)
    span_kv = lax.dynamic_slice_in_dim(global_kv, span_start, span_rows, 0)

    def head_slices(head_index):
        column = head_index * HEAD_DIM
        query_head = lax.dynamic_slice_in_dim(queries, column, HEAD_DIM, 1)
        near_keys = lax.dynamic_slice_in_dim(near_kv, column, HEAD_DIM, 2)
        near_values = lax.dynamic_slice_in_dim(near_kv, inner_dim + column, HEAD_DIM, 2)
        far_keys = lax.dynamic_slice_in_dim(span_kv, column, HEAD_DIM, 1)
        far_values = lax.dynamic_slice_in_dim(span_kv, inner_dim + column, HEAD_DIM, 1)
        return (column, query_head, near_keys, near_values, far_keys, far_values)

    def head_forward(head_index, carry):
        attended_rows, log_sums = carry
        column, query_head, near_keys, near_values, far_keys, far_values = head_slices(head_index)
        near_scores, far_scores = head_scores(query_head, near_keys, far_keys, near_mask, far_mask)
        highest = jnp.maximum(
            jnp.max(near_scores, axis=2).reshape(row_count), jnp.max(far_scores, axis=1)
        )
        near_exp = jnp.exp(near_scores - highest.reshape(block_count, BLOCK, 1))
        far_exp = jnp.exp(far_scores - highest[:, None])
        denominator = jnp.sum(near_exp, axis=2).reshape(row_count) + jnp.sum(far_exp, axis=1)
        near_probs = (near_exp / denominator.reshape(block_count, BLOCK, 1)).astype(jnp.bfloat16)
        far_probs = (far_exp / denominator[:, None]).astype(jnp.bfloat16)
        head_out = jnp.einsum(
            "nqk,nkd->nqd", near_probs, near_values, preferred_element_type=jnp.float32
        ).reshape(row_count, HEAD_DIM)
        head_out = head_out + jnp.einsum(
            "qk,kd->qd", far_probs, far_values, preferred_element_type=jnp.float32
        )
        attended_rows = lax.dynamic_update_slice_in_dim(attended_rows, head_out, column, 1)
        log_sums = lax.dynamic_update_index_in_dim(
            log_sums, highest + jnp.log(denominator), head_index, 0
        )
        return (attended_rows, log_sums)

    attended_rows, log_sums = lax.fori_loop(
        0,
        HEADS,
        head_forward,
        (
            jnp.zeros((row_count, inner_dim), jnp.float32),
            jnp.zeros((HEADS, row_count), jnp.float32),
        ),
    )
    attended = attended_rows.astype(jnp.bfloat16)
    middle = tokens_full + matmul(attended, attn_full[5])
    ffn_full = (
        lax.all_gather(ffn_gain, ("seq", "blk"), axis=0, tiled=True),
        lax.all_gather(w_gate, ("seq", "blk"), axis=0, tiled=True),
        lax.all_gather(w_up, ("seq", "blk"), axis=0, tiled=True),
        lax.all_gather(w_down, ("seq", "blk"), axis=0, tiled=True),
    )
    hidden_full, hidden_pull = jax.vjp(rms_norm, middle, ffn_full[0].astype(jnp.float32))
    hidden = hidden_full.astype(jnp.bfloat16)
    gate_pre = matmul(hidden, ffn_full[1])
    up_pre = matmul(hidden, ffn_full[2])
    gated_rows, gated_pull = jax.vjp(gated, gate_pre, up_pre)
    mixed = gated_rows.astype(jnp.bfloat16)
    output = (middle + matmul(mixed, ffn_full[3])).astype(jnp.bfloat16)
    ffn_back = (
        lax.all_gather(ffn_gain, ("seq", "blk"), axis=0, tiled=True),
        lax.all_gather(w_gate, ("seq", "blk"), axis=0, tiled=True),
        lax.all_gather(w_up, ("seq", "blk"), axis=0, tiled=True),
        lax.all_gather(w_down, ("seq", "blk"), axis=0, tiled=True),
    )
    grad_down = matmul_left(mixed, cotangent)
    grad_mixed = matmul_right(cotangent, ffn_back[3])
    grad_gate_full, grad_up_full = gated_pull(grad_mixed)
    grad_gate = grad_gate_full.astype(jnp.bfloat16)
    grad_up = grad_up_full.astype(jnp.bfloat16)
    grad_wgate = matmul_left(hidden, grad_gate)
    grad_wup = matmul_left(hidden, grad_up)
    grad_hidden = matmul_right(grad_gate, ffn_back[1]) + matmul_right(grad_up, ffn_back[2])
    grad_middle_norm, grad_ffn_gain = hidden_pull(grad_hidden)
    grad_middle = cotangent.astype(jnp.float32) + grad_middle_norm
    attn_back = (
        lax.all_gather(norm_gain, ("seq", "blk"), axis=0, tiled=True),
        lax.all_gather(global_gain, ("seq", "blk"), axis=0, tiled=True),
        lax.all_gather(w_query, ("seq", "blk"), axis=0, tiled=True),
        lax.all_gather(w_key, ("seq", "blk"), axis=0, tiled=True),
        lax.all_gather(w_value, ("seq", "blk"), axis=0, tiled=True),
        lax.all_gather(w_out, ("seq", "blk"), axis=0, tiled=True),
    )
    grad_branch = grad_middle.astype(jnp.bfloat16)
    grad_wout = matmul_left(attended, grad_branch)
    grad_attended = matmul_right(grad_branch, attn_back[5]).astype(jnp.bfloat16)

    def head_backward(head_index, carry):
        grad_query_rows, grad_near, grad_far = carry
        column, query_head, near_keys, near_values, far_keys, far_values = head_slices(head_index)
        near_scores, far_scores = head_scores(query_head, near_keys, far_keys, near_mask, far_mask)
        lse_head = log_sums[head_index]
        near_probs = jnp.exp(near_scores - lse_head.reshape(block_count, BLOCK, 1))
        far_probs = jnp.exp(far_scores - lse_head[:, None])
        grad_head = lax.dynamic_slice_in_dim(grad_attended, column, HEAD_DIM, 1)
        grad_blocks = grad_head.reshape(block_count, BLOCK, HEAD_DIM)
        query_blocks = query_head.reshape(block_count, BLOCK, HEAD_DIM)
        near_dprobs = jnp.einsum(
            "nqd,nkd->nqk", grad_blocks, near_values, preferred_element_type=jnp.float32
        )
        far_dprobs = jnp.einsum(
            "qd,kd->qk", grad_head, far_values, preferred_element_type=jnp.float32
        )
        delta_rows = jnp.sum(near_probs * near_dprobs, axis=2).reshape(row_count) + jnp.sum(
            far_probs * far_dprobs, axis=1
        )
        near_grad_scores = (
            near_probs * (near_dprobs - delta_rows.reshape(block_count, BLOCK, 1))
        ).astype(jnp.bfloat16)
        far_grad_scores = (far_probs * (far_dprobs - delta_rows[:, None])).astype(jnp.bfloat16)
        head_dquery = jnp.einsum(
            "nqk,nkd->nqd", near_grad_scores, near_keys, preferred_element_type=jnp.float32
        ).reshape(row_count, HEAD_DIM)
        head_dquery = head_dquery + jnp.einsum(
            "qk,kd->qd", far_grad_scores, far_keys, preferred_element_type=jnp.float32
        )
        near_dkey = jnp.einsum(
            "nqk,nqd->nkd", near_grad_scores, query_blocks, preferred_element_type=jnp.float32
        )
        near_dvalue = jnp.einsum(
            "nqk,nqd->nkd",
            near_probs.astype(jnp.bfloat16),
            grad_blocks,
            preferred_element_type=jnp.float32,
        )
        far_dkey = jnp.einsum(
            "qk,qd->kd", far_grad_scores, query_head, preferred_element_type=jnp.float32
        )
        far_dvalue = jnp.einsum(
            "qk,qd->kd",
            far_probs.astype(jnp.bfloat16),
            grad_head,
            preferred_element_type=jnp.float32,
        )
        grad_query_rows = lax.dynamic_update_slice_in_dim(grad_query_rows, head_dquery, column, 1)
        grad_near = lax.dynamic_update_slice_in_dim(grad_near, near_dkey, column, 2)
        grad_near = lax.dynamic_update_slice_in_dim(grad_near, near_dvalue, inner_dim + column, 2)
        grad_far = lax.dynamic_update_slice_in_dim(grad_far, far_dkey, column, 1)
        grad_far = lax.dynamic_update_slice_in_dim(grad_far, far_dvalue, inner_dim + column, 1)
        return (grad_query_rows, grad_near, grad_far)

    grad_query_rows, grad_near, grad_far = lax.fori_loop(
        0,
        HEADS,
        head_backward,
        (
            jnp.zeros((row_count, inner_dim), jnp.float32),
            jnp.zeros((block_count, 3 * BLOCK, 2 * inner_dim), jnp.float32),
            jnp.zeros((span_rows, 2 * inner_dim), jnp.float32),
        ),
    )
    grad_extended = unwindow(grad_near, row_count)
    rim_rows = jnp.concatenate([grad_extended[:BLOCK], grad_extended[row_count + BLOCK :]], axis=0)
    returned = with_halo(rim_rows.astype(jnp.bfloat16), (("blk", 0),), BLOCK).astype(rim_rows.dtype)
    grad_kv = grad_extended[BLOCK : row_count + BLOCK]
    grad_kv = grad_kv + jnp.pad(returned[:BLOCK], ((0, row_count - BLOCK), (0, 0)))
    grad_kv = grad_kv + jnp.pad(returned[3 * BLOCK :], ((row_count - BLOCK, 0), (0, 0)))
    grad_kv = grad_kv.astype(jnp.bfloat16)
    grad_key = grad_kv[:, :inner_dim]
    grad_value = grad_kv[:, inner_dim:]
    group_far = lax.dynamic_update_slice_in_dim(
        jnp.zeros((global_count, 2 * inner_dim), jnp.float32), grad_far, span_start, 0
    )
    own_global_grad = lax.psum_scatter(group_far, "blk", scatter_dimension=0, tiled=True).astype(
        jnp.bfloat16
    )
    grad_global_key = own_global_grad[:, :inner_dim]
    grad_global_value = own_global_grad[:, inner_dim:]
    grad_query = grad_query_rows.astype(jnp.bfloat16)
    grad_wquery = matmul_left(normed, grad_query)
    grad_wkey = matmul_left(normed, grad_key) + matmul_left(global_in, grad_global_key)
    grad_wvalue = matmul_left(normed, grad_value) + matmul_left(global_in, grad_global_value)
    grad_normed = (
        matmul_right(grad_query, attn_back[2])
        + matmul_right(grad_key, attn_back[3])
        + matmul_right(grad_value, attn_back[4])
    )
    grad_global_in = matmul_right(grad_global_key, attn_back[3]) + matmul_right(
        grad_global_value, attn_back[4]
    )
    grad_summed, grad_global_gain = global_pull(grad_global_in)
    grad_normed = (grad_normed.reshape(local_globals, GBLK, D) + grad_summed[:, None, :]).reshape(
        row_count, D
    )
    grad_tokens_norm, grad_norm_gain = normed_pull(grad_normed)
    grad_tokens = grad_middle + grad_tokens_norm
    every_grad = (
        lax.psum_scatter(grad_norm_gain, ("seq", "blk"), scatter_dimension=0, tiled=True),
        lax.psum_scatter(grad_global_gain, ("seq", "blk"), scatter_dimension=0, tiled=True),
        lax.psum_scatter(grad_wquery, ("seq", "blk"), scatter_dimension=0, tiled=True),
        lax.psum_scatter(grad_wkey, ("seq", "blk"), scatter_dimension=0, tiled=True),
        lax.psum_scatter(grad_wvalue, ("seq", "blk"), scatter_dimension=0, tiled=True),
        lax.psum_scatter(grad_wout, ("seq", "blk"), scatter_dimension=0, tiled=True),
        lax.psum_scatter(grad_ffn_gain, ("seq", "blk"), scatter_dimension=0, tiled=True),
        lax.psum_scatter(grad_wgate, ("seq", "blk"), scatter_dimension=0, tiled=True),
        lax.psum_scatter(grad_wup, ("seq", "blk"), scatter_dimension=0, tiled=True),
        lax.psum_scatter(grad_down, ("seq", "blk"), scatter_dimension=0, tiled=True),
    )
    return (
        output,
        grad_tokens,
        every_grad[0],
        every_grad[1],
        every_grad[2],
        every_grad[3],
        every_grad[4],
        every_grad[5],
        every_grad[6],
        every_grad[7],
        every_grad[8],
        every_grad[9],
    )


MESH = pl.DeviceIdType.MESH
CHIPS_Z = 4
NEVER = 1 << 20
VMEM_BYTES = 64 * 1024 * 1024 - 65536


def dot(a, b, dims, precision=None):
    return lax.dot_general(
        a, b, (dims, ((), ())), precision=precision, preferred_element_type=jnp.float32
    )


def dot_nn(a, b):
    return dot(a, b, ((1,), (0,)))


def dot_nt(a, b):
    return dot(a, b, ((1,), (1,)))


def coords():
    y = lax.axis_index("seq")
    blk = lax.axis_index("blk")
    return y, blk // 4, (blk // 2) % 2, blk % 2


def device(y, z, x, c):
    return (y, z * 4 + x * 2 + c)


def send(src, dst, send_sem, recv_sem, target):
    pltpu.make_async_remote_copy(
        src_ref=src,
        dst_ref=dst,
        send_sem=send_sem,
        recv_sem=recv_sem,
        device_id=target,
        device_id_type=MESH,
    ).start()


def wait_bytes(ref, sem):
    pltpu.make_async_copy(ref, ref, sem).wait()


def column_peers():
    y, z, x, c = coords()
    peers = [device(y, z, x, 1 - c)]
    for k in range(1, CHIPS_Z):
        peers += [device(y, (z + k) % CHIPS_Z, x, j) for j in range(2)]
    return peers


def side_peers():
    y, z, x, c = coords()
    return [device(y, z, 1 - x, c), device(1 - y, z, x, c), device(1 - y, z, 1 - x, c)]


def greet():
    y, z, x, c = coords()
    blk = lax.axis_index("blk")
    barrier = pltpu.get_barrier_semaphore()
    peers = column_peers() + side_peers()
    for peer in peers:
        pl.semaphore_signal(barrier, inc=1, device_id=peer, device_id_type=MESH)

    @pl.when(blk > 0)
    def _():
        pl.semaphore_signal(barrier, inc=1, device_id=(y, blk - 1), device_id_type=MESH)

    @pl.when(blk < 15)
    def _():
        pl.semaphore_signal(barrier, inc=1, device_id=(y, blk + 1), device_id_type=MESH)

    inner = jnp.where((blk > 0) & (blk < 15), 1, 0)
    pl.semaphore_wait(barrier, len(peers) + 1 + inner)


class Slots:
    def __init__(self, rows, half):
        self.rows, self.half = rows, half
        self.y, self.z, self.x, self.c = coords()

    def plane(self, c):
        return pl.ds(pl.multiple_of(c * self.half, 128), self.half)

    def slot_rows(self, y, z, x):
        return pl.ds(pl.multiple_of((y * 8 + z * 2 + x) * (2 * self.rows), 8), 2 * self.rows)

    def near_pair(self, j):
        return self.y * (1 - self.c) + j * self.c, self.x * self.c + j * (1 - self.c)

    def near_peer(self):
        y, z, x, c = self.y, self.z, self.x, self.c
        return device(y + c * (1 - 2 * y), z, x + (1 - c) * (1 - 2 * x), c)

    def far_peer(self):
        y, z, x, c = self.y, self.z, self.x, self.c
        return device(y + (1 - c) * (1 - 2 * y), z, x + c * (1 - 2 * x), c)


class Gather(Slots):
    def __init__(self, shard, full, recv, sent):
        super().__init__(shard.shape[0], shard.shape[1] // 2)
        self.shard, self.full, self.recv, self.sent = shard, full, recv, sent

    def span(self, rows):
        return self.full.at[pl.ds(0, rows), pl.ds(0, self.half)]

    def mine(self):
        index = self.y * 16 + self.z * 4 + self.x * 2 + self.c
        return pl.ds(pl.multiple_of(index * self.rows, 8), self.rows)

    def slot(self, y, z, x):
        return self.full.at[self.slot_rows(y, z, x), self.plane(self.c)]

    def own_copy(self):
        own = self.plane(self.c)
        return pltpu.make_async_copy(
            self.shard.at[:, own], self.full.at[self.mine(), own], self.sent.at[2]
        )

    def step(self, number):
        y, z, x, c, rows = self.y, self.z, self.x, self.c, self.rows
        if number == 0:
            other = self.plane(1 - c)
            send(
                self.shard.at[:, other],
                self.full.at[self.mine(), other],
                self.sent.at[0],
                self.recv.at[0],
                device(y, z, x, 1 - c),
            )
            self.own_copy().start()
        if number == 1:
            self.own_copy().wait()
            wait_bytes(self.span(rows), self.recv.at[0])
            block = self.slot(y, z, x)
            for k in range(1, CHIPS_Z):
                target = device(y, (z + k) % CHIPS_Z, x, c)
                send(block, block, self.sent.at[1], self.recv.at[1], target)
        if number == 2:
            wait_bytes(self.span(6 * rows), self.recv.at[1])
            for k in range(CHIPS_Z):
                block = self.slot(y, k, x)
                send(block, block, self.sent.at[1], self.recv.at[2], self.near_peer())
        if number == 3:
            wait_bytes(self.span(8 * rows), self.recv.at[2])
            for k in range(CHIPS_Z):
                for j in range(2):
                    slot_y, slot_x = self.near_pair(j)
                    block = self.slot(slot_y, k, slot_x)
                    send(block, block, self.sent.at[1], self.recv.at[3], self.far_peer())
        if number == 4:
            wait_bytes(self.span(16 * rows), self.recv.at[3])
            block = self.full.at[:, self.plane(c)]
            send(block, block, self.sent.at[1], self.recv.at[4], device(y, z, x, 1 - c))
        if number == 5:
            wait_bytes(self.span(32 * rows), self.recv.at[4])
        if number == 6:
            wait_bytes(self.span(rows), self.sent.at[0])
            wait_bytes(self.full.at[pl.ds(0, 31 * rows)], self.sent.at[1])


class Reduce(Slots):
    def __init__(self, part, out, work, near, mid, far, last, pair, recv, sent):
        super().__init__(out.shape[0], out.shape[1] // 2)
        self.part, self.out, self.work = part, out, work
        self.near, self.mid, self.far, self.last, self.pair = near, mid, far, last, pair
        self.recv, self.sent = recv, sent

    def add(self, rows, ref, index):
        size = 2 * self.rows
        start = pl.ds(pl.multiple_of(index * size, 8), size)
        total = self.work[rows, :].astype(jnp.float32) + ref[start, :].astype(jnp.float32)
        self.work[rows, :] = total.astype(self.work.dtype)

    def step(self, number):
        y, z, x, c, rows = self.y, self.z, self.x, self.c, self.rows
        size = 2 * rows
        if number == 0:
            send(
                self.part.at[:, self.plane(1 - c)],
                self.work,
                self.sent.at[0],
                self.recv.at[0],
                device(y, z, x, 1 - c),
            )
        if number == 1:
            wait_bytes(self.work, self.recv.at[0])

            @pl.loop(0, 16)
            def _(index):
                span = pl.ds(pl.multiple_of(index * size, 8), size)
                total = self.work[span, :].astype(jnp.float32)
                total = total + self.part[span, self.plane(c)].astype(jnp.float32)
                self.work[span, :] = total.astype(self.work.dtype)

            for k in range(CHIPS_Z):
                for j in range(2):
                    slot_y = (1 - y) * (1 - c) + j * c
                    slot_x = (1 - x) * c + j * (1 - c)
                    send(
                        self.work.at[self.slot_rows(slot_y, k, slot_x)],
                        self.near.at[pl.ds((k * 2 + j) * size, size)],
                        self.sent.at[1],
                        self.recv.at[1],
                        self.far_peer(),
                    )
        if number == 2:
            wait_bytes(self.near, self.recv.at[1])

            @pl.loop(0, 8)
            def _(index):
                k, j = index // 2, index % 2
                slot_y, slot_x = self.near_pair(j)
                self.add(self.slot_rows(slot_y, k, slot_x), self.near, index)

            for k in range(CHIPS_Z):
                slot_y = y * (1 - c) + (1 - y) * c
                slot_x = x * c + (1 - x) * (1 - c)
                send(
                    self.work.at[self.slot_rows(slot_y, k, slot_x)],
                    self.mid.at[pl.ds(k * size, size)],
                    self.sent.at[1],
                    self.recv.at[2],
                    self.near_peer(),
                )
        if number == 3:
            wait_bytes(self.mid, self.recv.at[2])

            @pl.loop(0, CHIPS_Z)
            def _(k):
                self.add(self.slot_rows(y, k, x), self.mid, k)

            for k in range(1, CHIPS_Z):
                to_z = (z + k) % CHIPS_Z
                send(
                    self.work.at[self.slot_rows(y, to_z, x)],
                    self.far.at[pl.ds((k - 1) * size, size)],
                    self.sent.at[1],
                    self.recv.at[3],
                    device(y, to_z, x, c),
                )
        if number == 4:
            wait_bytes(self.far, self.recv.at[3])
            total = self.work[self.slot_rows(y, z, x), :].astype(jnp.float32)
            for k in range(CHIPS_Z - 1):
                total = total + self.far[pl.ds(k * size, size), :].astype(jnp.float32)
            self.last[...] = total
            keep = pl.ds(pl.multiple_of(c * rows, 8), rows)
            give = pl.ds(pl.multiple_of((1 - c) * rows, 8), rows)
            send(
                self.last.at[give],
                self.pair,
                self.sent.at[2],
                self.recv.at[4],
                device(y, z, x, 1 - c),
            )
            self.out[:, self.plane(c)] = self.last[keep, :]
        if number == 5:
            wait_bytes(self.pair, self.recv.at[4])
            self.out[:, self.plane(1 - c)] = self.pair[...]
        if number == 6:
            wait_bytes(self.work, self.sent.at[0])
            wait_bytes(self.work.at[pl.ds(0, 30 * rows)], self.sent.at[1])
            wait_bytes(self.pair, self.sent.at[2])


def reduce_scratch(rows, half, dtype):
    return [
        pltpu.VMEM((32 * rows, half), dtype),
        pltpu.VMEM((16 * rows, half), dtype),
        pltpu.VMEM((8 * rows, half), dtype),
        pltpu.VMEM((6 * rows, half), dtype),
        pltpu.VMEM((2 * rows, half), jnp.float32),
        pltpu.VMEM((rows, half), jnp.float32),
    ]


def seq_bounds(lengths, position):
    low = jnp.zeros((1, 128), jnp.int32)
    high = jnp.full((1, 128), NEVER, jnp.int32)
    end = low
    for i in range(lengths.shape[0]):
        end = end + lengths[i : i + 1, :]
        low = jnp.maximum(low, jnp.where(end <= position, end, 0))
        high = jnp.minimum(high, jnp.where(end > position, end, NEVER))
    return low, high


class Span:
    fields = ("start", "far_low", "far_high", "no_before", "no_after", "second")

    def __init__(self, rows):
        for i, name in enumerate(self.fields):
            setattr(self, name, rows[i : i + 1, :])


def span_rows(lengths, first_row, block, far_rows, global_count):
    position = first_row + block * BLOCK
    low, high = seq_bounds(lengths, position)
    first_low, _ = seq_bounds(lengths, first_row)
    start = jnp.minimum(low >> 4, global_count - far_rows)
    rows = [
        start,
        (low >> 4) - start,
        (high >> 4) - start,
        jnp.where(position > low, 0, NEVER),
        jnp.where(position + BLOCK < high, 0, NEVER),
        jnp.where(low == first_low, 0, 1),
    ]
    return jnp.concatenate(rows + [start, start], axis=0)


def window_select(spans, window, blocks, far_rows, global_count):
    start = Span(spans[pl.ds(8 * window * (blocks - 1), 8), :]).start
    row = lax.broadcasted_iota(jnp.int32, (far_rows, global_count), 0)
    column = lax.broadcasted_iota(jnp.int32, (far_rows, global_count), 1)
    return (column - widen(start, global_count) == row).astype(jnp.bfloat16)


def far_part(ref, lanes, span, near_rows, far_rows):
    first = ref[pl.ds(near_rows, far_rows), lanes]
    second = ref[pl.ds(near_rows + far_rows, far_rows), lanes]
    return jnp.where(span.second > 0, second, first)


def widen(row, width):
    return jnp.concatenate([row] * (width // 128), axis=1)


def head_pair(rows):
    lane = lax.broadcasted_iota(jnp.int32, rows.shape, 1)
    zero = jnp.zeros_like(rows)
    return jnp.concatenate(
        [jnp.where(lane < HEAD_DIM, rows, zero), jnp.where(lane < HEAD_DIM, zero, rows)], axis=0
    )


def attend_block(pair, block, span, query, keys, values, attended, near_rows, far_rows):
    lanes = pl.ds(pl.multiple_of(pair * 128, 128), 128)
    rows = pl.ds(pl.multiple_of(block * BLOCK, BLOCK), BLOCK)
    near = pl.ds(pl.multiple_of(block * BLOCK, BLOCK), 3 * BLOCK)
    both = head_pair(query[rows, lanes])
    near_scores = dot_nt(both, keys[near, lanes])
    far_scores = dot_nt(both, far_part(keys, lanes, span, near_rows, far_rows))
    row = lax.broadcasted_iota(jnp.int32, (2 * BLOCK, BLOCK), 0) % BLOCK
    column = lax.broadcasted_iota(jnp.int32, (2 * BLOCK, BLOCK), 1)
    edge = jnp.where(
        column > row + span.no_before,
        near_scores[:, :BLOCK],
        jnp.where(column < row - span.no_after, near_scores[:, 2 * BLOCK :], MASKED),
    )
    own = near_scores[:, BLOCK : 2 * BLOCK]
    far_column = lax.broadcasted_iota(jnp.int32, far_scores.shape, 1)
    far_scores = jnp.where(
        (far_column >= widen(span.far_low, far_rows))
        & (far_column < widen(span.far_high, far_rows)),
        far_scores,
        MASKED,
    )
    highest = jnp.maximum(
        jnp.max(jnp.maximum(edge, own), axis=1, keepdims=True),
        jnp.max(far_scores, axis=1, keepdims=True),
    )
    edge_exp = jnp.exp(edge - highest)
    own_exp = jnp.exp(own - highest)
    far_exp = jnp.exp(far_scores - highest)
    inverse = 1.0 / (
        jnp.sum(edge_exp + own_exp, axis=1, keepdims=True) + jnp.sum(far_exp, axis=1, keepdims=True)
    )
    edge_probs = edge_exp * inverse
    near_probs = jnp.concatenate(
        [
            jnp.where(column > row, edge_probs, 0.0).astype(jnp.bfloat16),
            (own_exp * inverse).astype(jnp.bfloat16),
            jnp.where(column < row, edge_probs, 0.0).astype(jnp.bfloat16),
        ],
        axis=1,
    )
    far_probs = (far_exp * inverse).astype(jnp.bfloat16)
    mixed = dot_nn(near_probs, values[near, lanes]) + dot_nn(
        far_probs, far_part(values, lanes, span, near_rows, far_rows)
    )
    lane = lax.broadcasted_iota(jnp.int32, (BLOCK, 128), 1)
    attended[rows, lanes] = jnp.where(lane < HEAD_DIM, mixed[:BLOCK], mixed[BLOCK:]).astype(
        jnp.bfloat16
    )


def attend_block_back(
    pair, block, span, query, grad, keys, keys_t, values, grad_query, grad_keys, grad_values,
    near_rows, far_rows,
):
    lanes = pl.ds(pl.multiple_of(pair * 128, 128), 128)
    rows = pl.ds(pl.multiple_of(block * BLOCK, BLOCK), BLOCK)
    near = pl.ds(pl.multiple_of(block * BLOCK, BLOCK), 3 * BLOCK)
    both = head_pair(query[rows, lanes])
    grads = head_pair(grad[rows, lanes])
    near_scores = dot_nt(keys[near, lanes], both)
    far_keys = far_part(keys, lanes, span, near_rows, far_rows)
    far_scores = dot_nt(far_keys, both)
    row = lax.broadcasted_iota(jnp.int32, (BLOCK, 2 * BLOCK), 0)
    column = lax.broadcasted_iota(jnp.int32, (BLOCK, 2 * BLOCK), 1) % BLOCK
    edge = jnp.where(
        row > column + widen(span.no_before, 2 * BLOCK),
        near_scores[:BLOCK],
        jnp.where(row < column - widen(span.no_after, 2 * BLOCK), near_scores[2 * BLOCK :], MASKED),
    )
    own = near_scores[BLOCK : 2 * BLOCK]
    far_row = lax.broadcasted_iota(jnp.int32, far_scores.shape, 0)
    far_scores = jnp.where(
        (far_row >= widen(span.far_low, 2 * BLOCK)) & (far_row < widen(span.far_high, 2 * BLOCK)),
        far_scores,
        MASKED,
    )
    highest = jnp.maximum(
        jnp.max(jnp.maximum(edge, own), axis=0, keepdims=True),
        jnp.max(far_scores, axis=0, keepdims=True),
    )
    edge_exp = jnp.exp(edge - highest)
    own_exp = jnp.exp(own - highest)
    far_exp = jnp.exp(far_scores - highest)
    inverse = 1.0 / (
        jnp.sum(edge_exp + own_exp, axis=0, keepdims=True) + jnp.sum(far_exp, axis=0, keepdims=True)
    )
    edge_probs, own_probs, far_probs = edge_exp * inverse, own_exp * inverse, far_exp * inverse
    near_dprobs = dot_nt(values[near, lanes], grads)
    far_dprobs = dot_nt(far_part(values, lanes, span, near_rows, far_rows), grads)
    edge_dprobs = jnp.where(row > column, near_dprobs[:BLOCK], near_dprobs[2 * BLOCK :])
    own_dprobs = near_dprobs[BLOCK : 2 * BLOCK]
    delta = jnp.sum(
        edge_probs * edge_dprobs + own_probs * own_dprobs, axis=0, keepdims=True
    ) + jnp.sum(far_probs * far_dprobs, axis=0, keepdims=True)
    edge_ds = edge_probs * (edge_dprobs - delta)
    own_ds = (own_probs * (own_dprobs - delta)).astype(jnp.bfloat16)
    far_ds = (far_probs * (far_dprobs - delta)).astype(jnp.bfloat16)

    def spread(edge_part, own_part):
        return jnp.concatenate(
            [
                jnp.where(row > column, edge_part, 0.0).astype(jnp.bfloat16),
                own_part.astype(jnp.bfloat16),
                jnp.where(row < column, edge_part, 0.0).astype(jnp.bfloat16),
            ],
            axis=0,
        )

    near_ds = spread(edge_ds, own_ds)
    far_keys_t = jnp.where(
        widen(span.second, far_rows) > 0,
        keys_t[lanes, pl.ds(near_rows + far_rows, far_rows)],
        keys_t[lanes, pl.ds(near_rows, far_rows)],
    )
    query_t = dot_nn(keys_t[lanes, near], near_ds) + dot_nn(far_keys_t, far_ds)
    feature = lax.broadcasted_iota(jnp.int32, (128, BLOCK), 0)
    query_t = jnp.where(feature < HEAD_DIM, query_t[:, :BLOCK], query_t[:, BLOCK:])
    grad_query[rows, lanes] = query_t.T.astype(jnp.bfloat16)
    grad_keys[near, lanes] += dot_nn(near_ds, both)
    grad_values[near, lanes] += dot_nn(spread(edge_probs, own_probs), grads)
    far_dkey = dot_nn(far_ds, both)
    far_dvalue = dot_nn(far_probs.astype(jnp.bfloat16), grads)
    for window in range(2):
        place = pl.ds(near_rows + window * far_rows, far_rows)
        here = span.second == window
        grad_keys[place, lanes] += jnp.where(here, far_dkey, 0.0)
        grad_values[place, lanes] += jnp.where(here, far_dvalue, 0.0)


def inverse_rms(values):
    return lax.rsqrt(jnp.mean(values * values, axis=-1, keepdims=True) + EPSILON)


def rms_back(values, gain, grads):
    scale = inverse_rms(values)
    scaled = grads * gain
    back = scale * scaled - values * (
        scale * scale * scale * jnp.mean(scaled * values, axis=-1, keepdims=True)
    )
    return back, jnp.sum(grads * values * scale, axis=0, keepdims=True)


def block_sums(rows, count):
    take = lax.broadcasted_iota(jnp.int32, (count, rows.shape[0]), 1) // GBLK
    which = lax.broadcasted_iota(jnp.int32, (count, rows.shape[0]), 0)
    return dot_nn((take == which).astype(jnp.bfloat16), rows)


def owner_of(column, rows):
    return (column * ((65536 + rows - 1) // rows)) >> 16


def spread_gains(packed, rows):
    width = 32 * rows
    lane = lax.broadcasted_iota(jnp.int32, (128, width), 0)
    column = lax.broadcasted_iota(jnp.int32, (128, width), 1)
    select = (column - rows * owner_of(column, rows) == lane).astype(jnp.float32)
    wide = dot(packed, select, ((1,), (0,)), precision=lax.Precision.HIGHEST)
    device_row = lax.broadcasted_iota(jnp.int32, wide.shape, 0) >> 3
    wide_column = lax.broadcasted_iota(jnp.int32, wide.shape, 1)
    wide = jnp.where(owner_of(wide_column, rows) == device_row, wide, 0.0)
    return jnp.sum(wide.reshape(32, 8, width), axis=0)


def pack_gains(wide, rows):
    width = 32 * rows
    tall = jnp.concatenate([wide] * 32, axis=0)
    device_row = lax.broadcasted_iota(jnp.int32, tall.shape, 0) >> 3
    column = lax.broadcasted_iota(jnp.int32, tall.shape, 1)
    tall = jnp.where(owner_of(column, rows) == device_row, tall, 0.0)
    lane = lax.broadcasted_iota(jnp.int32, (width, 128), 1)
    from_column = lax.broadcasted_iota(jnp.int32, (width, 128), 0)
    select = (from_column - rows * owner_of(from_column, rows) == lane).astype(jnp.float32)
    return dot(tall, select, ((1,), (0,)), precision=lax.Precision.HIGHEST)


CHUNKS = 4
TILE = 256
SMALL_SEMS = 24
SCHEDULE = {
    "a0": ["k1", "v1", "q1"],
    "a2": ["k2"],
    "a3": ["v2", "k3", "o1", "d1"],
    "a4": ["q2", "v3", "k4", "f01"],
    "a5": ["o2", "q3", "v4", "f11"],
    "a6": ["d2", "o3", "q4", "f21"],
    "a7": ["f02", "f31"],
    "a8": ["d3", "o4"],
    "f0": ["f12"],
    "f3": ["f03"],
    "f5": ["d4"],
    "f7": ["f22"],
    "f9": ["f13"],
    "f11": ["f04"],
    "f13": ["f32"],
    "f16": ["f23"],
    "f19": ["f14"],
    "f22": ["f33"],
    "m0": ["f24"],
    "c0": ["f34"],
    "c2": ["r01"],
    "c3": ["r02", "r11"],
    "m1": ["r03", "r12", "r21"],
    "m2": ["r22", "r13", "r31"],
    "b0": ["r04", "rd1"],
    "b3": ["r23", "r32", "ro1"],
    "b6": ["r14", "rd2"],
    "b9": ["r33", "r24"],
    "b12": ["ro2"],
    "b15": ["rd3"],
    "b18": ["r34", "ro3"],
    "b22": ["rd4"],
    "e0": ["ro4"],
    "e2": ["rk1"],
    "e3": ["rv1", "rk2"],
    "e4": ["rq1", "rv2", "rk3"],
    "e5": ["rq2", "rv3", "rk4"],
    "e6": ["rq3", "rv4"],
    "e7": ["rq4"],
}


def tiled(count, body):
    @pl.loop(0, count // TILE)
    def _(i):
        body(pl.ds(pl.multiple_of(i * TILE, TILE), TILE))


class GlobalSlots:
    def __init__(self, count):
        self.count = count

    def at(self, z, x, c):
        return self.packed(z * 4 + x * 2 + c)

    def packed(self, index):
        return pl.ds(pl.multiple_of(index * self.count, 16), self.count)


def layer_kernel(packed, tokens, cotangent, *refs):
    shards, refs = refs[:6], refs[6:]
    output, grad_tokens, gain_out, refs = refs[0], refs[1], refs[2], refs[3:]
    grads_out, refs = refs[:9], refs[9:]
    w_query, w_key, w_value, w_out, w_down, w_ff = refs[:6]
    rows_in, rows_in_t, keys, keys_t, values, query, attended, hidden, turned = refs[6:15]
    mixed, grad_both, grad_keys, grad_values, gain_grads, part_key, part_value = refs[15:22]
    spans, gain_rows, gathered, gain_part, gain_side, gain_column, group_sums = refs[22:29]
    halo, global_rows, global_near, global_mid, global_far = refs[29:34]
    buffers, refs = refs[34:88], refs[88:]
    recv, sent, small = refs
    y, z, x, c = coords()
    blk = lax.axis_index("blk")
    me = blk + 16 * y
    row_count, width = tokens.shape
    blocks = row_count // BLOCK
    local_globals = row_count // GBLK
    global_count = global_rows.shape[0]
    near_rows = row_count + 2 * BLOCK
    all_rows = rows_in.shape[0]
    far_rows = (all_rows - near_rows) // 2
    feature_rows = width // 32
    hidden_rows = w_down.shape[0] // CHUNKS
    first_row = blk * row_count
    low = jnp.bfloat16
    slots = GlobalSlots(local_globals)
    column, sides = column_peers(), side_peers()

    part_query = rows_in.at[pl.ds(0, width)]
    steps = {}
    chunk_width = w_ff.shape[2]
    sources = [("q", shards[0], w_query), ("k", shards[1], w_key), ("v", shards[2], w_value)]
    sources += [("o", shards[3], w_out), ("d", shards[4], w_down)]
    for chunk in range(CHUNKS):
        part = shards[5].at[:, pl.ds(chunk * chunk_width, chunk_width)]
        sources.append((f"f{chunk}", part, w_ff.at[chunk]))
    for i, (name, shard, full) in enumerate(sources):
        steps[name] = Gather(shard, full, recv.at[i], sent.at[i])
    targets = [("rq", part_query), ("rk", part_key), ("rv", part_value), ("ro", w_out)]
    targets += [("rd", w_down)] + [(f"r{chunk}", w_ff.at[chunk]) for chunk in range(CHUNKS)]
    for i, (name, part) in enumerate(targets):
        held = buffers[6 * i : 6 * i + 6]
        steps[name] = Reduce(part, grads_out[i], *held, recv.at[9 + i], sent.at[9 + i])

    def run(todo):
        for name in todo:
            steps[name[:-1]].step(int(name[-1]))

    def tick(point):
        run(SCHEDULE.get(point, []))

    def loop_tick(kind, index, count):
        for number in range(count):
            todo = SCHEDULE.get(f"{kind}{number}", [])
            if todo:
                pl.when(index == number)(functools.partial(run, todo))

    greet()
    gathered[pl.ds(pl.multiple_of(me * 8, 8), 8), :] = packed[pl.ds(0, 8), :]
    own_tile = gathered.at[pl.ds(pl.multiple_of(me * 8, 8), 8)]
    for peer in column:
        send(packed.at[pl.ds(0, 8)], own_tile, small.at[1], small.at[0], peer)

    def token_halo(side):
        source = pl.ds(row_count - BLOCK, BLOCK) if side == 0 else pl.ds(0, BLOCK)
        return pltpu.make_async_remote_copy(
            src_ref=tokens.at[source],
            dst_ref=halo.at[side],
            send_sem=small.at[8 + side],
            recv_sem=small.at[10 + side],
            device_id=(y, blk + 1 - 2 * side),
            device_id_type=MESH,
        )

    run(["k0", "v0", "q0"])
    pl.when(blk < 15)(lambda: token_halo(0).start())
    pl.when(blk > 0)(lambda: token_halo(1).start())
    run([f"{name}0" for name, _, _ in sources[3:]])
    wait_bytes(gathered.at[pl.ds(0, 56)], small.at[0])
    for k in range(CHIPS_Z):
        pair = gathered.at[pl.ds(pl.multiple_of((y * 8 + k * 2 + x) * 16, 16), 16)]
        for peer in sides:
            send(pair, pair, small.at[3], small.at[2], peer)
    tick("a0")
    lengths = packed[pl.ds(8, packed.shape[0] - 8), :].astype(jnp.int32)
    for block in range(blocks):
        spans[pl.ds(8 * block, 8), :] = span_rows(
            lengths, first_row, block, far_rows, global_count
        )
    wait_bytes(gathered.at[pl.ds(0, 192)], small.at[2])
    gain_rows[...] = spread_gains(gathered[...], feature_rows)
    norm_gain, global_gain, ffn_gain = gain_rows[0:1, :], gain_rows[1:2, :], gain_rows[2:3, :]

    def normed(part):
        wide = part.astype(jnp.float32)
        return (wide * inverse_rms(wide) * norm_gain).astype(low)

    def norm_own(place):
        to = pl.ds(pl.multiple_of(place.start + BLOCK, BLOCK), TILE)
        rows_in[to, :] = normed(tokens[place, :])

    tiled(row_count, norm_own)
    summed = block_sums(rows_in[pl.ds(BLOCK, row_count), :], local_globals)
    group_sums[...] = summed
    global_rows[slots.packed(blk), :] = (summed * inverse_rms(summed) * global_gain).astype(low)
    tick("a2")
    block = global_rows.at[slots.at(z, x, c)]
    for k in range(1, CHIPS_Z):
        send(block, block, small.at[4], small.at[5], device(y, (z + k) % CHIPS_Z, x, c))
    tick("a3")

    @pl.when(blk == 0)
    def _():
        halo[0] = jnp.zeros_like(halo[0])

    @pl.when(blk == 15)
    def _():
        halo[1] = jnp.zeros_like(halo[1])

    pl.when(blk > 0)(lambda: token_halo(0).wait_recv())
    pl.when(blk < 15)(lambda: token_halo(1).wait_recv())
    rows_in[pl.ds(0, BLOCK), :] = normed(halo[0])
    rows_in[pl.ds(BLOCK + row_count, BLOCK), :] = normed(halo[1])
    tick("a4")
    wait_bytes(global_rows.at[pl.ds(0, 3 * local_globals)], small.at[5])
    for k in range(CHIPS_Z):
        block = global_rows.at[slots.at(k, x, c)]
        send(block, block, small.at[4], small.at[6], device(y, z, 1 - x, c))
    tick("a5")

    def project(weights, target, start, count, place):
        def one(part):
            source = pl.ds(pl.multiple_of(part.start + start, BLOCK), TILE)
            to = pl.ds(pl.multiple_of(part.start + place, BLOCK), TILE)
            target[to, :] = dot_nn(rows_in[source, :], weights[...]).astype(low)

        tiled(count, one)

    run(["k5"])
    project(w_key, keys, 0, near_rows, 0)
    tick("a6")
    wait_bytes(global_rows.at[pl.ds(0, 4 * local_globals)], small.at[6])
    for k in range(CHIPS_Z):
        for j in range(2):
            block = global_rows.at[slots.at(k, j, c)]
            send(block, block, small.at[4], small.at[7], device(y, z, x, 1 - c))
    run(["v5"])
    project(w_value, values, 0, near_rows, 0)
    tick("a7")
    run(["q5"])
    project(w_query, query, BLOCK, row_count, 0)
    wait_bytes(global_rows.at[pl.ds(0, 8 * local_globals)], small.at[7])
    for window in range(2):
        select = window_select(spans, window, blocks, far_rows, global_count)
        rows_in[pl.ds(near_rows + window * far_rows, far_rows), :] = dot_nn(
            select, global_rows[...]
        ).astype(low)
    project(w_key, keys, near_rows, 2 * far_rows, near_rows)
    project(w_value, values, near_rows, 2 * far_rows, near_rows)
    tick("a8")
    for start in range(0, all_rows, 256):
        rows_in_t[:, pl.ds(start, 256)] = rows_in[pl.ds(start, 256), :].T
        keys_t[:, pl.ds(start, 256)] = keys[pl.ds(start, 256), :].T
    iterations = blocks * (HEADS // 2)

    def span_of(block):
        return Span(spans[pl.ds(pl.multiple_of(block * 8, 8), 8), :])

    @pl.loop(0, iterations)
    def _(i):
        loop_tick("f", i, iterations)
        block = i % blocks
        attend_block(
            i // blocks, block, span_of(block), query, keys, values, attended, near_rows, far_rows
        )

    wait_bytes(global_rows.at[pl.ds(0, 15 * local_globals)], small.at[4])
    run(["o5"])

    def after(place):
        return pl.ds(pl.multiple_of(place.start + row_count, TILE), TILE)

    def join(place):
        middle = tokens[place, :].astype(jnp.float32) + dot_nn(attended[place, :], w_out[...])
        grad_keys[place, :] = middle
        grad_keys[after(place), :] = middle
        low_hidden = (middle * inverse_rms(middle) * ffn_gain).astype(low)
        hidden[place, :] = low_hidden
        turned[:, place] = low_hidden.T
        grad_values[place, :] = jnp.zeros((TILE, width), jnp.float32)

    tiled(row_count, join)
    tick("m0")
    run(["d5", "d6"])

    @pl.loop(0, CHUNKS)
    def _(chunk):
        for number in range(CHUNKS):
            pl.when(chunk == number)(functools.partial(run, [f"f{number}5", f"f{number}6"]))
        loop_tick("c", chunk, CHUNKS)
        half = chunk_width // 2
        rows = pl.ds(pl.multiple_of(chunk * hidden_rows, 128), hidden_rows)

        def feed(place):
            both = dot_nn(hidden[place, :], w_ff[chunk])
            gate, up = both[:, :half], both[:, half:]
            square = gate * gate
            bend = jnp.tanh(GELU_SCALE * gate * (1.0 + GELU_CUBIC * square))
            lift = 0.5 * (1.0 + bend)
            active = gate * lift
            slope = lift + 0.5 * gate * (1.0 - bend * bend) * (
                GELU_SCALE * (1.0 + 3.0 * GELU_CUBIC * square)
            )
            mixed[place, :] = (active * up).astype(low)
            grad_mixed = dot_nt(cotangent[place, :], w_down[rows, :])
            grad_both[place, pl.ds(0, half)] = (grad_mixed * up * slope).astype(low)
            grad_both[place, pl.ds(half, half)] = (grad_mixed * active).astype(low)
            grad_keys[after(place), :] += dot_nn(mixed[place, :], w_down[rows, :])
            grad_values[place, :] += dot_nt(grad_both[place, :], w_ff[chunk])

        tiled(row_count, feed)

        def gate_up_grad(place):
            w_ff[chunk, place, :] = dot_nn(turned[place, :], grad_both[...]).astype(low)

        tiled(width, gate_up_grad)
        for number in range(CHUNKS):
            pl.when(chunk == number)(functools.partial(run, [f"r{number}0"]))
        w_down[rows, :] = dot(mixed[...], cotangent[...], ((0,), (0,))).astype(low)

    run(["rd0"])
    tick("m1")
    gain_grads[...] = jnp.zeros_like(gain_grads)

    def split(place):
        output[place, :] = grad_keys[after(place), :].astype(low)
        back, gain_grad = rms_back(grad_keys[place, :], ffn_gain, grad_values[place, :])
        gain_grads[2:3, :] += gain_grad
        grad_middle = cotangent[place, :].astype(jnp.float32) + back
        grad_tokens[place, :] = grad_middle
        branch = grad_middle.astype(low)
        rows_in[place, :] = branch
        hidden[place, :] = dot_nt(branch, w_out[...]).astype(low)
        turned[:, place] = attended[place, :].T

    tiled(row_count, split)
    run(["o6"])

    def out_grad(place):
        w_out[place, :] = dot_nn(turned[place, :], rows_in[pl.ds(0, row_count), :]).astype(low)

    tiled(width, out_grad)
    run(["ro0"])

    def clear(place):
        grad_keys[place, :] = jnp.zeros((TILE, width), jnp.float32)
        grad_values[place, :] = jnp.zeros((TILE, width), jnp.float32)

    tiled(all_rows, clear)
    tick("m2")

    @pl.loop(0, iterations)
    def _(i):
        loop_tick("b", i, iterations)
        block = i % blocks
        attend_block_back(
            i // blocks, block, span_of(block), query, hidden, keys, keys_t, values,
            query, grad_keys, grad_values, near_rows, far_rows,
        )

    def lower(place):
        keys[place, :] = grad_keys[place, :].astype(low)
        values[place, :] = grad_values[place, :].astype(low)

    tiled(all_rows, lower)

    def grad_rows(start, count):
        part = pl.ds(start, count)
        return dot_nt(keys[part, :], w_key[...]) + dot_nt(values[part, :], w_value[...])

    halo[4] = grad_rows(0, BLOCK).astype(low)
    halo[5] = grad_rows(BLOCK + row_count, BLOCK).astype(low)
    for window in range(2):
        hidden[pl.ds(window * far_rows, far_rows), :] = grad_rows(
            near_rows + window * far_rows, far_rows
        ).astype(low)
    selects = [window_select(spans, w, blocks, far_rows, global_count) for w in range(2)]
    for half in range(2):
        part = slice(half * (global_count // 2), (half + 1) * (global_count // 2))
        global_rows[part, :] = sum(
            dot(selects[w][:, part], hidden[pl.ds(w * far_rows, far_rows), :], ((0,), (0,)))
            for w in range(2)
        ).astype(low)

    def grad_halo(side):
        return pltpu.make_async_remote_copy(
            src_ref=halo.at[4 + side],
            dst_ref=halo.at[3 - side],
            send_sem=small.at[20 + side],
            recv_sem=small.at[22 + side],
            device_id=(y, blk - 1 + 2 * side),
            device_id_type=MESH,
        )

    pl.when(blk > 0)(lambda: grad_halo(0).start())
    pl.when(blk < 15)(lambda: grad_halo(1).start())
    tick("e0")
    for k in range(CHIPS_Z):
        for j in range(2):
            send(
                global_rows.at[slots.at(k, j, 1 - c)],
                global_near.at[slots.packed(k * 2 + j)],
                small.at[16],
                small.at[17],
                device(y, z, x, 1 - c),
            )

    def weight_grad(target, start, grads):
        def one(part):
            wide = rows_in_t[part, pl.ds(start, grads.shape[0])]
            target[part, :] = dot_nn(wide, grads[...]).astype(low)

        tiled(width, one)

    def add_global(rows, ref, index):
        total = global_rows[rows, :].astype(jnp.float32)
        total = total + ref[slots.packed(index), :].astype(jnp.float32)
        global_rows[rows, :] = total.astype(low)

    weight_grad(part_key, 0, keys)
    run(["rk0"])
    wait_bytes(global_near, small.at[17])
    for k in range(CHIPS_Z):
        for j in range(2):
            add_global(slots.at(k, j, c), global_near, k * 2 + j)
    tick("e1")
    for k in range(CHIPS_Z):
        send(
            global_rows.at[slots.at(k, 1 - x, c)],
            global_mid.at[slots.packed(k)],
            small.at[16],
            small.at[18],
            device(y, z, 1 - x, c),
        )
    weight_grad(part_value, 0, values)
    run(["rv0"])
    tick("e2")
    wait_bytes(global_mid, small.at[18])
    for k in range(CHIPS_Z):
        add_global(slots.at(k, x, c), global_mid, k)
    weight_grad(part_query, BLOCK, query)
    run(["rq0"])
    for k in range(1, CHIPS_Z):
        to_z = (z + k) % CHIPS_Z
        send(
            global_rows.at[slots.at(to_z, x, c)],
            global_far.at[slots.packed(k - 1)],
            small.at[16],
            small.at[19],
            device(y, to_z, x, c),
        )
    tick("e3")

    def gather_grads(place):
        rows = pl.ds(pl.multiple_of(place.start + BLOCK, BLOCK), TILE)
        grad_keys[place, :] = (
            dot_nt(keys[rows, :], w_key[...])
            + dot_nt(values[rows, :], w_value[...])
            + dot_nt(query[place, :], w_query[...])
        )

    tiled(row_count, gather_grads)

    @pl.when(blk == 0)
    def _():
        halo[2] = jnp.zeros_like(halo[2])

    @pl.when(blk == 15)
    def _():
        halo[3] = jnp.zeros_like(halo[3])

    pl.when(blk > 0)(lambda: grad_halo(1).wait_recv())
    pl.when(blk < 15)(lambda: grad_halo(0).wait_recv())
    grad_keys[pl.ds(0, BLOCK), :] += halo[2].astype(jnp.float32)
    grad_keys[pl.ds(row_count - BLOCK, BLOCK), :] += halo[3].astype(jnp.float32)
    tick("e4")
    wait_bytes(global_far, small.at[19])
    total = global_rows[slots.at(z, x, c), :].astype(jnp.float32)
    for k in range(CHIPS_Z - 1):
        total = total + global_far[slots.packed(k), :].astype(jnp.float32)
    grad_summed, grad_global_gain = rms_back(group_sums[...], global_gain, total)
    gain_grads[1:2, :] = grad_global_gain
    group_sums[...] = grad_summed

    def finish(place):
        few = TILE // GBLK
        sums = group_sums[pl.ds(pl.multiple_of(place.start // GBLK, 8), few), :]
        grad_normed = grad_keys[place, :] + jnp.broadcast_to(
            sums[:, None, :], (few, GBLK, width)
        ).reshape(TILE, width)
        back, gain_grad = rms_back(tokens[place, :].astype(jnp.float32), norm_gain, grad_normed)
        gain_grads[0:1, :] += gain_grad
        grad_tokens[place, :] += back

    tiled(row_count, finish)
    gain_part[...] = pack_gains(gain_grads[...], feature_rows)

    def gain_pair(pair_y, k, pair_x):
        return pl.ds(pl.multiple_of((pair_y * 8 + k * 2 + pair_x) * 16, 16), 16)

    tick("e5")
    for index, peer in enumerate(sides):
        side_y = y if index == 0 else 1 - y
        side_x = x if index == 1 else 1 - x
        for k in range(CHIPS_Z):
            send(
                gain_part.at[gain_pair(side_y, k, side_x)],
                gain_side.at[index, pl.ds(k * 16, 16)],
                small.at[13],
                small.at[12],
                peer,
            )
    tick("e6")
    wait_bytes(gain_side, small.at[12])
    for k in range(CHIPS_Z):
        rows = gain_pair(y, k, x)
        place = pl.ds(k * 16, 16)
        gain_part[rows, :] += gain_side[0, place, :] + gain_side[1, place, :] + gain_side[2, place, :]
    place = z * 2 + c
    gain_column[pl.ds(pl.multiple_of(place * 8, 8), 8), :] = gain_part[
        pl.ds(pl.multiple_of(me * 8, 8), 8), :
    ]
    for k in range(CHIPS_Z):
        for j in range(2):
            if k == 0 and j == 0:
                peer_z, peer_c = z, 1 - c
            elif k == 0:
                continue
            else:
                peer_z, peer_c = (z + k) % CHIPS_Z, j
            peer_me = y * 16 + peer_z * 4 + x * 2 + peer_c
            send(
                gain_part.at[pl.ds(pl.multiple_of(peer_me * 8, 8), 8)],
                gain_column.at[pl.ds(pl.multiple_of(place * 8, 8), 8)],
                small.at[15],
                small.at[14],
                device(y, peer_z, x, peer_c),
            )
    tick("e7")
    wait_bytes(gain_column.at[pl.ds(0, 56)], small.at[14])
    gain_out[...] = jnp.sum(gain_column[...].reshape(8, 8, 128), axis=0)
    for name, _ in targets:
        run([f"{name}5"])
    for name, _ in targets:
        run([f"{name}6"])
    run(["q6", "k6", "v6"])
    wait_bytes(gathered.at[pl.ds(0, 56)], small.at[1])
    wait_bytes(gathered.at[pl.ds(0, 192)], small.at[3])
    wait_bytes(global_rows.at[pl.ds(0, 15 * local_globals)], small.at[16])
    wait_bytes(gathered.at[pl.ds(0, 192)], small.at[13])
    wait_bytes(gathered.at[pl.ds(0, 56)], small.at[15])
    pl.when(blk < 15)(lambda: token_halo(0).wait_send())
    pl.when(blk > 0)(lambda: token_halo(1).wait_send())
    pl.when(blk > 0)(lambda: grad_halo(0).wait_send())
    pl.when(blk < 15)(lambda: grad_halo(1).wait_send())


def layer(packed, tokens, cotangent, shards, far_rows, global_count):
    row_count, width = tokens.shape
    all_rows = row_count + 2 * BLOCK + 2 * far_rows
    local_globals = row_count // GBLK
    down_rows = shards[4].shape[0]
    chunk_width = shards[5].shape[1] // CHUNKS
    vmem = pl.BlockSpec(memory_space=pltpu.VMEM)
    anywhere = pl.BlockSpec(memory_space=pl.ANY)
    low, wide = jnp.bfloat16, jnp.float32
    shard_shapes = [(width // 32, width)] * 4 + [(down_rows, width)]
    shard_shapes += [(width // 32, chunk_width)] * CHUNKS
    buffers = []
    for rows, columns in shard_shapes:
        buffers += reduce_scratch(rows, columns // 2, low)
    return pl.pallas_call(
        layer_kernel,
        out_shape=[
            jax.ShapeDtypeStruct((row_count, width), low),
            jax.ShapeDtypeStruct((row_count, width), wide),
            jax.ShapeDtypeStruct((8, 128), wide),
        ]
        + [jax.ShapeDtypeStruct(shape, wide) for shape in shard_shapes],
        in_specs=[vmem] * 3 + [anywhere] * 6,
        out_specs=[vmem] * 12,
        scratch_shapes=[pltpu.VMEM((width, width), low)] * 4
        + [
            pltpu.VMEM((32 * down_rows, width), low),
            pltpu.VMEM((CHUNKS, width, chunk_width), low),
            pltpu.VMEM((all_rows, width), low),
            pltpu.VMEM((width, all_rows), low),
            pltpu.VMEM((all_rows, width), low),
            pltpu.VMEM((width, all_rows), low),
            pltpu.VMEM((all_rows, width), low),
            pltpu.VMEM((row_count, width), low),
            pltpu.VMEM((row_count, width), low),
            pltpu.VMEM((row_count, width), low),
            pltpu.VMEM((width, row_count), low),
            pltpu.VMEM((row_count, chunk_width // 2), low),
            pltpu.VMEM((row_count, chunk_width), low),
            pltpu.VMEM((all_rows, width), wide),
            pltpu.VMEM((all_rows, width), wide),
            pltpu.VMEM((8, width), wide),
            pltpu.VMEM((width, width), low),
            pltpu.VMEM((width, width), low),
            pltpu.VMEM((8 * row_count // BLOCK, 128), jnp.int32),
            pltpu.VMEM((8, width), wide),
            pltpu.VMEM((256, 128), wide),
            pltpu.VMEM((256, 128), wide),
            pltpu.VMEM((3, 64, 128), wide),
            pltpu.VMEM((64, 128), wide),
            pltpu.VMEM((local_globals, width), wide),
            pltpu.VMEM((6, BLOCK, width), low),
            pltpu.VMEM((global_count, width), low),
            pltpu.VMEM((8 * local_globals, width), low),
            pltpu.VMEM((4 * local_globals, width), low),
            pltpu.VMEM((3 * local_globals, width), low),
        ]
        + buffers
        + [
            pltpu.SemaphoreType.DMA((18, 5)),
            pltpu.SemaphoreType.DMA((18, 3)),
            pltpu.SemaphoreType.DMA((SMALL_SEMS,)),
        ],
        compiler_params=pltpu.CompilerParams(
            collective_id=0, has_side_effects=True, vmem_limit_bytes=VMEM_BYTES
        ),
        name="layer",
    )(packed, tokens, cotangent, *shards)


def per_device(
    tokens, lengths, norm_gain, global_gain, w_query, w_key, w_value, w_out,
    ffn_gain, w_gate, w_up, w_down, cotangent,
):
    row_count, width = tokens.shape
    global_count = row_count * lax.axis_size("blk") // GBLK
    far_rows = global_count // 2
    feature_rows = norm_gain.shape[0]
    gains = jnp.stack([norm_gain, global_gain, ffn_gain]).astype(jnp.float32)
    gains = jnp.pad(gains, ((0, 5), (0, 128 - feature_rows)))
    wide_lengths = jnp.broadcast_to(
        lengths[0].astype(jnp.float32)[:, None], (lengths.shape[1], 128)
    )
    packed = jnp.concatenate([gains, wide_lengths], axis=0)
    chunked = (w_gate.shape[0], CHUNKS, w_gate.shape[1] // CHUNKS)
    w_ff = jnp.concatenate([w_gate.reshape(chunked), w_up.reshape(chunked)], axis=2)
    w_ff = w_ff.reshape(w_gate.shape[0], -1)
    shards = (w_query, w_key, w_value, w_out, w_down, w_ff)
    outs = layer(packed, tokens, cotangent, shards, far_rows, global_count)
    output, grad_tokens, gain_grads = outs[:3]
    grads, grad_ff = outs[3:8], outs[8:]
    half = chunked[2]
    return (
        output,
        grad_tokens,
        gain_grads[0, :feature_rows],
        gain_grads[1, :feature_rows],
        *grads[:4],
        gain_grads[2, :feature_rows],
        jnp.concatenate([part[:, :half] for part in grad_ff], axis=1),
        jnp.concatenate([part[:, half:] for part in grad_ff], axis=1),
        grads[4],
    )


def fits(mesh):
    return mesh.shape["seq"] == 2 and mesh.shape["blk"] == 16


def solution(mesh):
    return jax.shard_map(
        per_device if fits(mesh) else per_device_general,
        mesh=mesh,
        in_specs=(
            P(("seq", "blk"), None),
            P("seq", None),
            P(("seq", "blk")),
            P(("seq", "blk")),
            P(("seq", "blk"), None),
            P(("seq", "blk"), None),
            P(("seq", "blk"), None),
            P(("seq", "blk"), None),
            P(("seq", "blk")),
            P(("seq", "blk"), None),
            P(("seq", "blk"), None),
            P(("seq", "blk"), None),
            P(("seq", "blk"), None),
        ),
        out_specs=(
            P(("seq", "blk"), None),
            P(("seq", "blk"), None),
            P(("seq", "blk")),
            P(("seq", "blk")),
            P(("seq", "blk"), None),
            P(("seq", "blk"), None),
            P(("seq", "blk"), None),
            P(("seq", "blk"), None),
            P(("seq", "blk")),
            P(("seq", "blk"), None),
            P(("seq", "blk"), None),
            P(("seq", "blk"), None),
        ),
        check_vma=False,
    )
```

```python
import functools

import jax
import jax.numpy as jnp
from jax import lax
from jax.experimental import pallas as pl
from jax.experimental.pallas import tpu as pltpu
from jax.sharding import PartitionSpec as P


D = 768
HEADS = 12
HEAD_DIM = 64
GBLK = 16
BLOCK = 128
LONGEST = 16384


EPSILON = 1e-06
MASKED = -1e30
GELU_SCALE = 0.7978845608028654
GELU_CUBIC = 0.044715


def with_halo(block, sides, width):
    for axis, dim in sides:
        count = lax.axis_size(axis)
        forward = [(i, i + 1) for i in range(count - 1)]
        backward = [(target, source) for source, target in forward]
        low = lax.ppermute(
            lax.slice_in_dim(block, block.shape[dim] - width, None, axis=dim), axis, forward
        )
        high = lax.ppermute(lax.slice_in_dim(block, 0, width, axis=dim), axis, backward)
        block = jnp.concatenate([low, block, high], axis=dim)
    return block


def rms_norm(values, scales):
    return values * lax.rsqrt(jnp.mean(values * values, axis=-1, keepdims=True) + EPSILON) * scales


def gelu_tanh(values):
    return (
        0.5
        * values
        * (1.0 + jnp.tanh(GELU_SCALE * (values + GELU_CUBIC * values * values * values)))
    )


def gated(gate_part, up_part):
    return gelu_tanh(gate_part) * up_part


def sequence_of(positions, seq_ends):
    return jnp.sum((positions[:, None] >= seq_ends[None, :]).astype(jnp.int32), axis=1)


def matmul(left_side, right_side):
    return jnp.dot(left_side, right_side, preferred_element_type=jnp.float32)


def matmul_left(left_side, right_side):
    return jnp.einsum("ta,tb->ab", left_side, right_side, preferred_element_type=jnp.float32)


def matmul_right(left_side, right_side):
    return jnp.einsum("ta,ba->tb", left_side, right_side, preferred_element_type=jnp.float32)


def windows(extended, row_count):
    block_count = row_count // BLOCK
    pieces = [
        extended[offset * BLOCK : offset * BLOCK + row_count].reshape(
            block_count, BLOCK, extended.shape[-1]
        )
        for offset in range(3)
    ]
    return jnp.concatenate(pieces, axis=1)


def unwindow(window_grads, row_count):
    channels = window_grads.shape[-1]
    summed_grad = jnp.zeros((row_count + 2 * BLOCK, channels), jnp.float32)
    for offset in range(3):
        piece_grad = window_grads[:, offset * BLOCK : (offset + 1) * BLOCK].reshape(
            row_count, channels
        )
        summed_grad = summed_grad + jnp.pad(
            piece_grad, ((offset * BLOCK, (2 - offset) * BLOCK), (0, 0))
        )
    return summed_grad


def head_scores(query_head, near_keys, far_keys, near_mask, far_mask):
    block_count = near_keys.shape[0]
    query_blocks = query_head.reshape(block_count, BLOCK, HEAD_DIM)
    near_scores = jnp.einsum(
        "nqd,nkd->nqk", query_blocks, near_keys, preferred_element_type=jnp.float32
    )
    far_scores = jnp.einsum("qd,kd->qk", query_head, far_keys, preferred_element_type=jnp.float32)
    return (jnp.where(near_mask, near_scores, MASKED), jnp.where(far_mask, far_scores, MASKED))


def per_device_general(
    tokens,
    lengths,
    norm_gain,
    global_gain,
    w_query,
    w_key,
    w_value,
    w_out,
    ffn_gain,
    w_gate,
    w_up,
    w_down,
    cotangent,
):
    row_count = tokens.shape[0]
    inner_dim = HEADS * HEAD_DIM
    block_count = row_count // BLOCK
    local_globals = row_count // GBLK
    group_tokens = row_count * lax.axis_size("blk")
    global_count = group_tokens // GBLK
    longest_len = min(LONGEST, group_tokens // 2)
    span_rows = min(global_count, 2 * (longest_len // GBLK) + local_globals)
    attn_full = (
        lax.all_gather(norm_gain, ("seq", "blk"), axis=0, tiled=True),
        lax.all_gather(global_gain, ("seq", "blk"), axis=0, tiled=True),
        lax.all_gather(w_query, ("seq", "blk"), axis=0, tiled=True),
        lax.all_gather(w_key, ("seq", "blk"), axis=0, tiled=True),
        lax.all_gather(w_value, ("seq", "blk"), axis=0, tiled=True),
        lax.all_gather(w_out, ("seq", "blk"), axis=0, tiled=True),
    )
    seq_ends = jnp.cumsum(lengths[0])
    first_row = lax.axis_index("blk") * row_count
    span_start = jnp.clip(first_row // GBLK - longest_len // GBLK, 0, global_count - span_rows)
    query_pos = first_row + jnp.arange(row_count, dtype=jnp.int32)
    query_seq = sequence_of(query_pos, seq_ends)
    key_pos = first_row - BLOCK + jnp.arange(row_count + 2 * BLOCK, dtype=jnp.int32)
    inside = (key_pos >= 0) & (key_pos < group_tokens)
    key_seq = jnp.where(inside, sequence_of(key_pos, seq_ends), -1)
    global_seq = sequence_of((span_start + jnp.arange(span_rows, dtype=jnp.int32)) * GBLK, seq_ends)
    query_pos_win = query_pos.reshape(block_count, BLOCK)
    query_seq_win = query_seq.reshape(block_count, BLOCK)
    key_pos_win = windows(key_pos[:, None], row_count)[:, :, 0]
    key_seq_win = windows(key_seq[:, None], row_count)[:, :, 0]
    near_mask = (jnp.abs(query_pos_win[:, :, None] - key_pos_win[:, None, :]) <= BLOCK - 1) & (
        query_seq_win[:, :, None] == key_seq_win[:, None, :]
    )
    far_mask = query_seq[:, None] == global_seq[None, :]
    tokens_full = tokens.astype(jnp.float32)
    normed_full, normed_pull = jax.vjp(rms_norm, tokens_full, attn_full[0].astype(jnp.float32))
    normed = normed_full.astype(jnp.bfloat16)
    queries = matmul(normed, attn_full[2]).astype(jnp.bfloat16)
    key_rows = matmul(normed, attn_full[3]).astype(jnp.bfloat16)
    value_rows = matmul(normed, attn_full[4]).astype(jnp.bfloat16)
    local_kv = jnp.concatenate([key_rows, value_rows], axis=1)
    extended = with_halo(local_kv, (("blk", 0),), BLOCK)
    near_kv = windows(extended, row_count)
    summed = jnp.sum(normed.astype(jnp.float32).reshape(local_globals, GBLK, D), axis=1)
    global_full, global_pull = jax.vjp(rms_norm, summed, attn_full[1].astype(jnp.float32))
    global_in = global_full.astype(jnp.bfloat16)
    own_global = jnp.concatenate(
        [
            matmul(global_in, attn_full[3]).astype(jnp.bfloat16),
            matmul(global_in, attn_full[4]).astype(jnp.bfloat16),
        ],
        axis=1,
    )
    global_kv = lax.all_gather(own_global, "blk", axis=0, tiled=True)
    span_kv = lax.dynamic_slice_in_dim(global_kv, span_start, span_rows, 0)

    def head_slices(head_index):
        column = head_index * HEAD_DIM
        query_head = lax.dynamic_slice_in_dim(queries, column, HEAD_DIM, 1)
        near_keys = lax.dynamic_slice_in_dim(near_kv, column, HEAD_DIM, 2)
        near_values = lax.dynamic_slice_in_dim(near_kv, inner_dim + column, HEAD_DIM, 2)
        far_keys = lax.dynamic_slice_in_dim(span_kv, column, HEAD_DIM, 1)
        far_values = lax.dynamic_slice_in_dim(span_kv, inner_dim + column, HEAD_DIM, 1)
        return (column, query_head, near_keys, near_values, far_keys, far_values)

    def head_forward(head_index, carry):
        attended_rows, log_sums = carry
        column, query_head, near_keys, near_values, far_keys, far_values = head_slices(head_index)
        near_scores, far_scores = head_scores(query_head, near_keys, far_keys, near_mask, far_mask)
        highest = jnp.maximum(
            jnp.max(near_scores, axis=2).reshape(row_count), jnp.max(far_scores, axis=1)
        )
        near_exp = jnp.exp(near_scores - highest.reshape(block_count, BLOCK, 1))
        far_exp = jnp.exp(far_scores - highest[:, None])
        denominator = jnp.sum(near_exp, axis=2).reshape(row_count) + jnp.sum(far_exp, axis=1)
        near_probs = (near_exp / denominator.reshape(block_count, BLOCK, 1)).astype(jnp.bfloat16)
        far_probs = (far_exp / denominator[:, None]).astype(jnp.bfloat16)
        head_out = jnp.einsum(
            "nqk,nkd->nqd", near_probs, near_values, preferred_element_type=jnp.float32
        ).reshape(row_count, HEAD_DIM)
        head_out = head_out + jnp.einsum(
            "qk,kd->qd", far_probs, far_values, preferred_element_type=jnp.float32
        )
        attended_rows = lax.dynamic_update_slice_in_dim(attended_rows, head_out, column, 1)
        log_sums = lax.dynamic_update_index_in_dim(
            log_sums, highest + jnp.log(denominator), head_index, 0
        )
        return (attended_rows, log_sums)

    attended_rows, log_sums = lax.fori_loop(
        0,
        HEADS,
        head_forward,
        (
            jnp.zeros((row_count, inner_dim), jnp.float32),
            jnp.zeros((HEADS, row_count), jnp.float32),
        ),
    )
    attended = attended_rows.astype(jnp.bfloat16)
    middle = tokens_full + matmul(attended, attn_full[5])
    ffn_full = (
        lax.all_gather(ffn_gain, ("seq", "blk"), axis=0, tiled=True),
        lax.all_gather(w_gate, ("seq", "blk"), axis=0, tiled=True),
        lax.all_gather(w_up, ("seq", "blk"), axis=0, tiled=True),
        lax.all_gather(w_down, ("seq", "blk"), axis=0, tiled=True),
    )
    hidden_full, hidden_pull = jax.vjp(rms_norm, middle, ffn_full[0].astype(jnp.float32))
    hidden = hidden_full.astype(jnp.bfloat16)
    gate_pre = matmul(hidden, ffn_full[1])
    up_pre = matmul(hidden, ffn_full[2])
    gated_rows, gated_pull = jax.vjp(gated, gate_pre, up_pre)
    mixed = gated_rows.astype(jnp.bfloat16)
    output = (middle + matmul(mixed, ffn_full[3])).astype(jnp.bfloat16)
    ffn_back = (
        lax.all_gather(ffn_gain, ("seq", "blk"), axis=0, tiled=True),
        lax.all_gather(w_gate, ("seq", "blk"), axis=0, tiled=True),
        lax.all_gather(w_up, ("seq", "blk"), axis=0, tiled=True),
        lax.all_gather(w_down, ("seq", "blk"), axis=0, tiled=True),
    )
    grad_down = matmul_left(mixed, cotangent)
    grad_mixed = matmul_right(cotangent, ffn_back[3])
    grad_gate_full, grad_up_full = gated_pull(grad_mixed)
    grad_gate = grad_gate_full.astype(jnp.bfloat16)
    grad_up = grad_up_full.astype(jnp.bfloat16)
    grad_wgate = matmul_left(hidden, grad_gate)
    grad_wup = matmul_left(hidden, grad_up)
    grad_hidden = matmul_right(grad_gate, ffn_back[1]) + matmul_right(grad_up, ffn_back[2])
    grad_middle_norm, grad_ffn_gain = hidden_pull(grad_hidden)
    grad_middle = cotangent.astype(jnp.float32) + grad_middle_norm
    attn_back = (
        lax.all_gather(norm_gain, ("seq", "blk"), axis=0, tiled=True),
        lax.all_gather(global_gain, ("seq", "blk"), axis=0, tiled=True),
        lax.all_gather(w_query, ("seq", "blk"), axis=0, tiled=True),
        lax.all_gather(w_key, ("seq", "blk"), axis=0, tiled=True),
        lax.all_gather(w_value, ("seq", "blk"), axis=0, tiled=True),
        lax.all_gather(w_out, ("seq", "blk"), axis=0, tiled=True),
    )
    grad_branch = grad_middle.astype(jnp.bfloat16)
    grad_wout = matmul_left(attended, grad_branch)
    grad_attended = matmul_right(grad_branch, attn_back[5]).astype(jnp.bfloat16)

    def head_backward(head_index, carry):
        grad_query_rows, grad_near, grad_far = carry
        column, query_head, near_keys, near_values, far_keys, far_values = head_slices(head_index)
        near_scores, far_scores = head_scores(query_head, near_keys, far_keys, near_mask, far_mask)
        lse_head = log_sums[head_index]
        near_probs = jnp.exp(near_scores - lse_head.reshape(block_count, BLOCK, 1))
        far_probs = jnp.exp(far_scores - lse_head[:, None])
        grad_head = lax.dynamic_slice_in_dim(grad_attended, column, HEAD_DIM, 1)
        grad_blocks = grad_head.reshape(block_count, BLOCK, HEAD_DIM)
        query_blocks = query_head.reshape(block_count, BLOCK, HEAD_DIM)
        near_dprobs = jnp.einsum(
            "nqd,nkd->nqk", grad_blocks, near_values, preferred_element_type=jnp.float32
        )
        far_dprobs = jnp.einsum(
            "qd,kd->qk", grad_head, far_values, preferred_element_type=jnp.float32
        )
        delta_rows = jnp.sum(near_probs * near_dprobs, axis=2).reshape(row_count) + jnp.sum(
            far_probs * far_dprobs, axis=1
        )
        near_grad_scores = (
            near_probs * (near_dprobs - delta_rows.reshape(block_count, BLOCK, 1))
        ).astype(jnp.bfloat16)
        far_grad_scores = (far_probs * (far_dprobs - delta_rows[:, None])).astype(jnp.bfloat16)
        head_dquery = jnp.einsum(
            "nqk,nkd->nqd", near_grad_scores, near_keys, preferred_element_type=jnp.float32
        ).reshape(row_count, HEAD_DIM)
        head_dquery = head_dquery + jnp.einsum(
            "qk,kd->qd", far_grad_scores, far_keys, preferred_element_type=jnp.float32
        )
        near_dkey = jnp.einsum(
            "nqk,nqd->nkd", near_grad_scores, query_blocks, preferred_element_type=jnp.float32
        )
        near_dvalue = jnp.einsum(
            "nqk,nqd->nkd",
            near_probs.astype(jnp.bfloat16),
            grad_blocks,
            preferred_element_type=jnp.float32,
        )
        far_dkey = jnp.einsum(
            "qk,qd->kd", far_grad_scores, query_head, preferred_element_type=jnp.float32
        )
        far_dvalue = jnp.einsum(
            "qk,qd->kd",
            far_probs.astype(jnp.bfloat16),
            grad_head,
            preferred_element_type=jnp.float32,
        )
        grad_query_rows = lax.dynamic_update_slice_in_dim(grad_query_rows, head_dquery, column, 1)
        grad_near = lax.dynamic_update_slice_in_dim(grad_near, near_dkey, column, 2)
        grad_near = lax.dynamic_update_slice_in_dim(grad_near, near_dvalue, inner_dim + column, 2)
        grad_far = lax.dynamic_update_slice_in_dim(grad_far, far_dkey, column, 1)
        grad_far = lax.dynamic_update_slice_in_dim(grad_far, far_dvalue, inner_dim + column, 1)
        return (grad_query_rows, grad_near, grad_far)

    grad_query_rows, grad_near, grad_far = lax.fori_loop(
        0,
        HEADS,
        head_backward,
        (
            jnp.zeros((row_count, inner_dim), jnp.float32),
            jnp.zeros((block_count, 3 * BLOCK, 2 * inner_dim), jnp.float32),
            jnp.zeros((span_rows, 2 * inner_dim), jnp.float32),
        ),
    )
    grad_extended = unwindow(grad_near, row_count)
    rim_rows = jnp.concatenate([grad_extended[:BLOCK], grad_extended[row_count + BLOCK :]], axis=0)
    returned = with_halo(rim_rows.astype(jnp.bfloat16), (("blk", 0),), BLOCK).astype(rim_rows.dtype)
    grad_kv = grad_extended[BLOCK : row_count + BLOCK]
    grad_kv = grad_kv + jnp.pad(returned[:BLOCK], ((0, row_count - BLOCK), (0, 0)))
    grad_kv = grad_kv + jnp.pad(returned[3 * BLOCK :], ((row_count - BLOCK, 0), (0, 0)))
    grad_kv = grad_kv.astype(jnp.bfloat16)
    grad_key = grad_kv[:, :inner_dim]
    grad_value = grad_kv[:, inner_dim:]
    group_far = lax.dynamic_update_slice_in_dim(
        jnp.zeros((global_count, 2 * inner_dim), jnp.float32), grad_far, span_start, 0
    )
    own_global_grad = lax.psum_scatter(group_far, "blk", scatter_dimension=0, tiled=True).astype(
        jnp.bfloat16
    )
    grad_global_key = own_global_grad[:, :inner_dim]
    grad_global_value = own_global_grad[:, inner_dim:]
    grad_query = grad_query_rows.astype(jnp.bfloat16)
    grad_wquery = matmul_left(normed, grad_query)
    grad_wkey = matmul_left(normed, grad_key) + matmul_left(global_in, grad_global_key)
    grad_wvalue = matmul_left(normed, grad_value) + matmul_left(global_in, grad_global_value)
    grad_normed = (
        matmul_right(grad_query, attn_back[2])
        + matmul_right(grad_key, attn_back[3])
        + matmul_right(grad_value, attn_back[4])
    )
    grad_global_in = matmul_right(grad_global_key, attn_back[3]) + matmul_right(
        grad_global_value, attn_back[4]
    )
    grad_summed, grad_global_gain = global_pull(grad_global_in)
    grad_normed = (grad_normed.reshape(local_globals, GBLK, D) + grad_summed[:, None, :]).reshape(
        row_count, D
    )
    grad_tokens_norm, grad_norm_gain = normed_pull(grad_normed)
    grad_tokens = grad_middle + grad_tokens_norm
    every_grad = (
        lax.psum_scatter(grad_norm_gain, ("seq", "blk"), scatter_dimension=0, tiled=True),
        lax.psum_scatter(grad_global_gain, ("seq", "blk"), scatter_dimension=0, tiled=True),
        lax.psum_scatter(grad_wquery, ("seq", "blk"), scatter_dimension=0, tiled=True),
        lax.psum_scatter(grad_wkey, ("seq", "blk"), scatter_dimension=0, tiled=True),
        lax.psum_scatter(grad_wvalue, ("seq", "blk"), scatter_dimension=0, tiled=True),
        lax.psum_scatter(grad_wout, ("seq", "blk"), scatter_dimension=0, tiled=True),
        lax.psum_scatter(grad_ffn_gain, ("seq", "blk"), scatter_dimension=0, tiled=True),
        lax.psum_scatter(grad_wgate, ("seq", "blk"), scatter_dimension=0, tiled=True),
        lax.psum_scatter(grad_wup, ("seq", "blk"), scatter_dimension=0, tiled=True),
        lax.psum_scatter(grad_down, ("seq", "blk"), scatter_dimension=0, tiled=True),
    )
    return (
        output,
        grad_tokens,
        every_grad[0],
        every_grad[1],
        every_grad[2],
        every_grad[3],
        every_grad[4],
        every_grad[5],
        every_grad[6],
        every_grad[7],
        every_grad[8],
        every_grad[9],
    )


MESH = pl.DeviceIdType.MESH
CHIPS_Z = 4
NEVER = 1 << 20
VMEM_BYTES = 64 * 1024 * 1024 - 65536


def dot(a, b, dims, precision=None):
    return lax.dot_general(
        a, b, (dims, ((), ())), precision=precision, preferred_element_type=jnp.float32
    )


def dot_nn(a, b):
    return dot(a, b, ((1,), (0,)))


def dot_nt(a, b):
    return dot(a, b, ((1,), (1,)))


def coords():
    y = lax.axis_index("seq")
    blk = lax.axis_index("blk")
    return y, blk // 4, (blk // 2) % 2, blk % 2


def device(y, z, x, c):
    return (y, z * 4 + x * 2 + c)


def send(src, dst, send_sem, recv_sem, target):
    pltpu.make_async_remote_copy(
        src_ref=src,
        dst_ref=dst,
        send_sem=send_sem,
        recv_sem=recv_sem,
        device_id=target,
        device_id_type=MESH,
    ).start()


def wait_bytes(ref, sem):
    pltpu.make_async_copy(ref, ref, sem).wait()


def column_peers():
    y, z, x, c = coords()
    peers = [device(y, z, x, 1 - c)]
    for k in range(1, CHIPS_Z):
        peers += [device(y, (z + k) % CHIPS_Z, x, j) for j in range(2)]
    return peers


def side_peers():
    y, z, x, c = coords()
    return [device(y, z, 1 - x, c), device(1 - y, z, x, c), device(1 - y, z, 1 - x, c)]


def greet():
    y, z, x, c = coords()
    blk = lax.axis_index("blk")
    barrier = pltpu.get_barrier_semaphore()
    peers = column_peers() + side_peers()
    for peer in peers:
        pl.semaphore_signal(barrier, inc=1, device_id=peer, device_id_type=MESH)

    @pl.when(blk > 0)
    def _():
        pl.semaphore_signal(barrier, inc=1, device_id=(y, blk - 1), device_id_type=MESH)

    @pl.when(blk < 15)
    def _():
        pl.semaphore_signal(barrier, inc=1, device_id=(y, blk + 1), device_id_type=MESH)

    inner = jnp.where((blk > 0) & (blk < 15), 1, 0)
    pl.semaphore_wait(barrier, len(peers) + 1 + inner)


class Slots:
    def __init__(self, rows, half, first=None):
        self.rows, self.half = rows, half
        self.y, self.z, self.x, self.c = coords()
        self.side = self.c if first is None else first

    def plane(self, c):
        return pl.ds(pl.multiple_of(c * self.half, 128), self.half)

    def slot_rows(self, y, z, x):
        return pl.ds(pl.multiple_of((y * 8 + z * 2 + x) * (2 * self.rows), 8), 2 * self.rows)

    def near_pair(self, j):
        y, x, side = self.y, self.x, self.side
        return y * (1 - side) + j * side, x * side + j * (1 - side)

    def far_pair(self, j):
        y, x, side = self.y, self.x, self.side
        return (1 - y) * (1 - side) + j * side, (1 - x) * side + j * (1 - side)

    def near_slot(self):
        y, x, side = self.y, self.x, self.side
        return y * (1 - side) + (1 - y) * side, x * side + (1 - x) * (1 - side)

    def near_peer(self):
        slot_y, slot_x = self.near_slot()
        return device(slot_y, self.z, slot_x, self.c)

    def far_peer(self):
        y, z, x, c, side = self.y, self.z, self.x, self.c, self.side
        return device(y + (1 - side) * (1 - 2 * y), z, x + side * (1 - 2 * x), c)


class Gather(Slots):
    def __init__(self, shard, full, recv, sent, first=None):
        super().__init__(shard.shape[0], shard.shape[1] // 2, first)
        self.shard, self.full, self.recv, self.sent = shard, full, recv, sent

    def span(self, rows):
        return self.full.at[pl.ds(0, rows), pl.ds(0, self.half)]

    def mine(self):
        index = self.y * 16 + self.z * 4 + self.x * 2 + self.c
        return pl.ds(pl.multiple_of(index * self.rows, 8), self.rows)

    def slot(self, y, z, x):
        return self.full.at[self.slot_rows(y, z, x), self.plane(self.c)]

    def own_copy(self):
        own = self.plane(self.c)
        return pltpu.make_async_copy(
            self.shard.at[:, own], self.full.at[self.mine(), own], self.sent.at[2]
        )

    def step(self, number):
        y, z, x, c, rows = self.y, self.z, self.x, self.c, self.rows
        if number == 0:
            other = self.plane(1 - c)
            send(
                self.shard.at[:, other],
                self.full.at[self.mine(), other],
                self.sent.at[0],
                self.recv.at[0],
                device(y, z, x, 1 - c),
            )
            self.own_copy().start()
        if number == 1:
            self.own_copy().wait()
            wait_bytes(self.span(rows), self.recv.at[0])
            block = self.slot(y, z, x)
            for k in range(1, CHIPS_Z):
                target = device(y, (z + k) % CHIPS_Z, x, c)
                send(block, block, self.sent.at[1], self.recv.at[1], target)
        if number == 2:
            wait_bytes(self.span(6 * rows), self.recv.at[1])
            for k in range(CHIPS_Z):
                block = self.slot(y, k, x)
                send(block, block, self.sent.at[1], self.recv.at[2], self.near_peer())
        if number == 3:
            wait_bytes(self.span(8 * rows), self.recv.at[2])
            for k in range(CHIPS_Z):
                for j in range(2):
                    slot_y, slot_x = self.near_pair(j)
                    block = self.slot(slot_y, k, slot_x)
                    send(block, block, self.sent.at[1], self.recv.at[3], self.far_peer())
        if number == 4:
            wait_bytes(self.span(16 * rows), self.recv.at[3])
            block = self.full.at[:, self.plane(c)]
            send(block, block, self.sent.at[1], self.recv.at[4], device(y, z, x, 1 - c))
        if number == 5:
            wait_bytes(self.span(32 * rows), self.recv.at[4])
        if number == 6:
            wait_bytes(self.span(rows), self.sent.at[0])
            wait_bytes(self.full.at[pl.ds(0, 31 * rows)], self.sent.at[1])


class GatherLate(Gather):
    def step(self, number):
        y, z, x, c, rows = self.y, self.z, self.x, self.c, self.rows
        if number == 1:
            self.own_copy().wait()
            wait_bytes(self.span(rows), self.recv.at[0])
            block = self.slot(y, z, x)
            send(block, block, self.sent.at[1], self.recv.at[1], self.near_peer())
        elif number == 2:
            wait_bytes(self.span(2 * rows), self.recv.at[1])
            for j in range(2):
                slot_y, slot_x = self.near_pair(j)
                block = self.slot(slot_y, z, slot_x)
                send(block, block, self.sent.at[1], self.recv.at[2], self.far_peer())
        elif number == 3:
            wait_bytes(self.span(4 * rows), self.recv.at[2])
            for k in range(1, CHIPS_Z):
                target = device(y, (z + k) % CHIPS_Z, x, c)
                for j in range(4):
                    block = self.slot(j // 2, z, j % 2)
                    send(block, block, self.sent.at[1], self.recv.at[3], target)
        elif number == 4:
            wait_bytes(self.span(24 * rows), self.recv.at[3])
            block = self.full.at[:, self.plane(c)]
            send(block, block, self.sent.at[1], self.recv.at[4], device(y, z, x, 1 - c))
        else:
            super().step(number)


class Reduce(Slots):
    def __init__(self, part, out, work, near, mid, far, last, pair, recv, sent, first=None):
        super().__init__(out.shape[0], out.shape[1] // 2, first)
        self.part, self.out, self.work = part, out, work
        self.near, self.mid, self.far, self.last, self.pair = near, mid, far, last, pair
        self.recv, self.sent = recv, sent

    def add(self, rows, ref, index):
        size = 2 * self.rows
        start = pl.ds(pl.multiple_of(index * size, 8), size)
        total = self.work[rows, :].astype(jnp.float32) + ref[start, :].astype(jnp.float32)
        self.work[rows, :] = total.astype(self.work.dtype)

    def start_sum(self):
        wait_bytes(self.work, self.recv.at[0])
        size = 2 * self.rows

        @pl.loop(0, 16)
        def _(index):
            span = pl.ds(pl.multiple_of(index * size, 8), size)
            total = self.work[span, :].astype(jnp.float32)
            total = total + self.part[span, self.plane(self.c)].astype(jnp.float32)
            self.work[span, :] = total.astype(self.work.dtype)

    def step(self, number):
        y, z, x, c, rows = self.y, self.z, self.x, self.c, self.rows
        size = 2 * rows
        if number == 0:
            send(
                self.part.at[:, self.plane(1 - c)],
                self.work,
                self.sent.at[0],
                self.recv.at[0],
                device(y, z, x, 1 - c),
            )
        if number == 1:
            self.start_sum()
            for k in range(CHIPS_Z):
                for j in range(2):
                    slot_y, slot_x = self.far_pair(j)
                    send(
                        self.work.at[self.slot_rows(slot_y, k, slot_x)],
                        self.near.at[pl.ds((k * 2 + j) * size, size)],
                        self.sent.at[1],
                        self.recv.at[1],
                        self.far_peer(),
                    )
        if number == 2:
            wait_bytes(self.near, self.recv.at[1])

            @pl.loop(0, 8)
            def _(index):
                k, j = index // 2, index % 2
                slot_y, slot_x = self.near_pair(j)
                self.add(self.slot_rows(slot_y, k, slot_x), self.near, index)

            for k in range(CHIPS_Z):
                slot_y, slot_x = self.near_slot()
                send(
                    self.work.at[self.slot_rows(slot_y, k, slot_x)],
                    self.mid.at[pl.ds(k * size, size)],
                    self.sent.at[1],
                    self.recv.at[2],
                    self.near_peer(),
                )
        if number == 3:
            wait_bytes(self.mid, self.recv.at[2])

            @pl.loop(0, CHIPS_Z)
            def _(k):
                self.add(self.slot_rows(y, k, x), self.mid, k)

            for k in range(1, CHIPS_Z):
                to_z = (z + k) % CHIPS_Z
                send(
                    self.work.at[self.slot_rows(y, to_z, x)],
                    self.far.at[pl.ds((k - 1) * size, size)],
                    self.sent.at[1],
                    self.recv.at[3],
                    device(y, to_z, x, c),
                )
        if number == 4:
            wait_bytes(self.far, self.recv.at[3])
            total = self.work[self.slot_rows(y, z, x), :].astype(jnp.float32)
            for k in range(self.far.shape[0] // size):
                total = total + self.far[pl.ds(k * size, size), :].astype(jnp.float32)
            self.last[...] = total
            keep = pl.ds(pl.multiple_of(c * rows, 8), rows)
            give = pl.ds(pl.multiple_of((1 - c) * rows, 8), rows)
            send(
                self.last.at[give],
                self.pair,
                self.sent.at[2],
                self.recv.at[4],
                device(y, z, x, 1 - c),
            )
            self.out[:, self.plane(c)] = self.last[keep, :]
        if number == 5:
            wait_bytes(self.pair, self.recv.at[4])
            self.out[:, self.plane(1 - c)] = self.pair[...]
        if number == 6:
            wait_bytes(self.work, self.sent.at[0])
            wait_bytes(self.work.at[pl.ds(0, 30 * rows)], self.sent.at[1])
            wait_bytes(self.pair, self.sent.at[2])


class ReduceEarly(Reduce):
    def step(self, number):
        y, z, x, c = self.y, self.z, self.x, self.c
        size = 2 * self.rows
        if number == 1:
            self.start_sum()
            for k in range(1, CHIPS_Z):
                to_z = (z + k) % CHIPS_Z
                for j in range(4):
                    send(
                        self.work.at[self.slot_rows(j // 2, to_z, j % 2)],
                        self.near.at[pl.ds((4 * (k - 1) + j) * size, size)],
                        self.sent.at[1],
                        self.recv.at[1],
                        device(y, to_z, x, c),
                    )
        elif number == 2:
            wait_bytes(self.near, self.recv.at[1])

            @pl.loop(0, 12)
            def _(index):
                j = index % 4
                self.add(self.slot_rows(j // 2, z, j % 2), self.near, index)

            for j in range(2):
                slot_y, slot_x = self.far_pair(j)
                send(
                    self.work.at[self.slot_rows(slot_y, z, slot_x)],
                    self.mid.at[pl.ds(j * size, size)],
                    self.sent.at[1],
                    self.recv.at[2],
                    self.far_peer(),
                )
        elif number == 3:
            wait_bytes(self.mid, self.recv.at[2])
            for j in range(2):
                slot_y, slot_x = self.near_pair(j)
                self.add(self.slot_rows(slot_y, z, slot_x), self.mid, j)
            slot_y, slot_x = self.near_slot()
            send(
                self.work.at[self.slot_rows(slot_y, z, slot_x)],
                self.far,
                self.sent.at[1],
                self.recv.at[3],
                self.near_peer(),
            )
        else:
            super().step(number)


def reduce_scratch(rows, half, dtype, counts=(16, 8, 6)):
    return [
        pltpu.VMEM((32 * rows, half), dtype),
        pltpu.VMEM((counts[0] * rows, half), dtype),
        pltpu.VMEM((counts[1] * rows, half), dtype),
        pltpu.VMEM((counts[2] * rows, half), dtype),
        pltpu.VMEM((2 * rows, half), jnp.float32),
        pltpu.VMEM((rows, half), jnp.float32),
    ]


def seq_bounds(lengths, position):
    low = jnp.zeros((1, 128), jnp.int32)
    high = jnp.full((1, 128), NEVER, jnp.int32)
    end = low
    for i in range(lengths.shape[0]):
        end = end + lengths[i : i + 1, :]
        low = jnp.maximum(low, jnp.where(end <= position, end, 0))
        high = jnp.minimum(high, jnp.where(end > position, end, NEVER))
    return low, high


class Span:
    fields = ("start", "far_low", "far_high", "no_before", "no_after", "second")

    def __init__(self, rows):
        for i, name in enumerate(self.fields):
            setattr(self, name, rows[i : i + 1, :])


def span_rows(lengths, first_row, block, far_rows, global_count):
    position = first_row + block * BLOCK
    low, high = seq_bounds(lengths, position)
    first_low, _ = seq_bounds(lengths, first_row)
    start = jnp.minimum(low >> 4, global_count - far_rows)
    rows = [
        start,
        (low >> 4) - start,
        (high >> 4) - start,
        jnp.where(position > low, 0, NEVER),
        jnp.where(position + BLOCK < high, 0, NEVER),
        jnp.where(low == first_low, 0, 1),
    ]
    return jnp.concatenate(rows + [start, start], axis=0)


def window_select(spans, window, blocks, far_rows, global_count):
    start = Span(spans[pl.ds(8 * window * (blocks - 1), 8), :]).start
    row = lax.broadcasted_iota(jnp.int32, (far_rows, global_count), 0)
    column = lax.broadcasted_iota(jnp.int32, (far_rows, global_count), 1)
    return (column - widen(start, global_count) == row).astype(jnp.bfloat16)


def far_part(ref, lanes, span, near_rows, far_rows):
    first = ref[pl.ds(near_rows, far_rows), lanes]
    second = ref[pl.ds(near_rows + far_rows, far_rows), lanes]
    return jnp.where(span.second > 0, second, first)


def widen(row, width):
    return jnp.concatenate([row] * (width // 128), axis=1)


def head_pair(rows):
    lane = lax.broadcasted_iota(jnp.int32, rows.shape, 1)
    zero = jnp.zeros_like(rows)
    return jnp.concatenate(
        [jnp.where(lane < HEAD_DIM, rows, zero), jnp.where(lane < HEAD_DIM, zero, rows)], axis=0
    )


def attend_block(pair, block, span, query, keys, values, attended, near_rows, far_rows):
    lanes = pl.ds(pl.multiple_of(pair * 128, 128), 128)
    rows = pl.ds(pl.multiple_of(block * BLOCK, BLOCK), BLOCK)
    near = pl.ds(pl.multiple_of(block * BLOCK, BLOCK), 3 * BLOCK)
    both = head_pair(query[rows, lanes])
    near_scores = dot_nt(both, keys[near, lanes])
    far_scores = dot_nt(both, far_part(keys, lanes, span, near_rows, far_rows))
    row = lax.broadcasted_iota(jnp.int32, (2 * BLOCK, BLOCK), 0) % BLOCK
    column = lax.broadcasted_iota(jnp.int32, (2 * BLOCK, BLOCK), 1)
    edge = jnp.where(
        column > row + span.no_before,
        near_scores[:, :BLOCK],
        jnp.where(column < row - span.no_after, near_scores[:, 2 * BLOCK :], MASKED),
    )
    own = near_scores[:, BLOCK : 2 * BLOCK]
    far_column = lax.broadcasted_iota(jnp.int32, far_scores.shape, 1)
    far_scores = jnp.where(
        (far_column >= widen(span.far_low, far_rows))
        & (far_column < widen(span.far_high, far_rows)),
        far_scores,
        MASKED,
    )
    highest = jnp.maximum(
        jnp.max(jnp.maximum(edge, own), axis=1, keepdims=True),
        jnp.max(far_scores, axis=1, keepdims=True),
    )
    edge_exp = jnp.exp(edge - highest)
    own_exp = jnp.exp(own - highest)
    far_exp = jnp.exp(far_scores - highest)
    inverse = 1.0 / (
        jnp.sum(edge_exp + own_exp, axis=1, keepdims=True) + jnp.sum(far_exp, axis=1, keepdims=True)
    )
    edge_probs = edge_exp * inverse
    near_probs = jnp.concatenate(
        [
            jnp.where(column > row, edge_probs, 0.0).astype(jnp.bfloat16),
            (own_exp * inverse).astype(jnp.bfloat16),
            jnp.where(column < row, edge_probs, 0.0).astype(jnp.bfloat16),
        ],
        axis=1,
    )
    far_probs = (far_exp * inverse).astype(jnp.bfloat16)
    mixed = dot_nn(near_probs, values[near, lanes]) + dot_nn(
        far_probs, far_part(values, lanes, span, near_rows, far_rows)
    )
    lane = lax.broadcasted_iota(jnp.int32, (BLOCK, 128), 1)
    attended[rows, lanes] = jnp.where(lane < HEAD_DIM, mixed[:BLOCK], mixed[BLOCK:]).astype(
        jnp.bfloat16
    )


def attend_block_back(
    pair, block, span, query, grad, keys, keys_t, values, grad_query, grad_keys, grad_values,
    near_rows, far_rows,
):
    lanes = pl.ds(pl.multiple_of(pair * 128, 128), 128)
    rows = pl.ds(pl.multiple_of(block * BLOCK, BLOCK), BLOCK)
    near = pl.ds(pl.multiple_of(block * BLOCK, BLOCK), 3 * BLOCK)
    both = head_pair(query[rows, lanes])
    grads = head_pair(grad[rows, lanes])
    near_scores = dot_nt(keys[near, lanes], both)
    far_keys = far_part(keys, lanes, span, near_rows, far_rows)
    far_scores = dot_nt(far_keys, both)
    row = lax.broadcasted_iota(jnp.int32, (BLOCK, 2 * BLOCK), 0)
    column = lax.broadcasted_iota(jnp.int32, (BLOCK, 2 * BLOCK), 1) % BLOCK
    edge = jnp.where(
        row > column + widen(span.no_before, 2 * BLOCK),
        near_scores[:BLOCK],
        jnp.where(row < column - widen(span.no_after, 2 * BLOCK), near_scores[2 * BLOCK :], MASKED),
    )
    own = near_scores[BLOCK : 2 * BLOCK]
    far_row = lax.broadcasted_iota(jnp.int32, far_scores.shape, 0)
    far_scores = jnp.where(
        (far_row >= widen(span.far_low, 2 * BLOCK)) & (far_row < widen(span.far_high, 2 * BLOCK)),
        far_scores,
        MASKED,
    )
    highest = jnp.maximum(
        jnp.max(jnp.maximum(edge, own), axis=0, keepdims=True),
        jnp.max(far_scores, axis=0, keepdims=True),
    )
    edge_exp = jnp.exp(edge - highest)
    own_exp = jnp.exp(own - highest)
    far_exp = jnp.exp(far_scores - highest)
    inverse = 1.0 / (
        jnp.sum(edge_exp + own_exp, axis=0, keepdims=True) + jnp.sum(far_exp, axis=0, keepdims=True)
    )
    edge_probs, own_probs, far_probs = edge_exp * inverse, own_exp * inverse, far_exp * inverse
    near_dprobs = dot_nt(values[near, lanes], grads)
    far_dprobs = dot_nt(far_part(values, lanes, span, near_rows, far_rows), grads)
    edge_dprobs = jnp.where(row > column, near_dprobs[:BLOCK], near_dprobs[2 * BLOCK :])
    own_dprobs = near_dprobs[BLOCK : 2 * BLOCK]
    delta = jnp.sum(
        edge_probs * edge_dprobs + own_probs * own_dprobs, axis=0, keepdims=True
    ) + jnp.sum(far_probs * far_dprobs, axis=0, keepdims=True)
    edge_ds = edge_probs * (edge_dprobs - delta)
    own_ds = (own_probs * (own_dprobs - delta)).astype(jnp.bfloat16)
    far_ds = (far_probs * (far_dprobs - delta)).astype(jnp.bfloat16)

    def spread(edge_part, own_part):
        return jnp.concatenate(
            [
                jnp.where(row > column, edge_part, 0.0).astype(jnp.bfloat16),
                own_part.astype(jnp.bfloat16),
                jnp.where(row < column, edge_part, 0.0).astype(jnp.bfloat16),
            ],
            axis=0,
        )

    near_ds = spread(edge_ds, own_ds)
    far_keys_t = jnp.where(
        widen(span.second, far_rows) > 0,
        keys_t[lanes, pl.ds(near_rows + far_rows, far_rows)],
        keys_t[lanes, pl.ds(near_rows, far_rows)],
    )
    query_t = dot_nn(keys_t[lanes, near], near_ds) + dot_nn(far_keys_t, far_ds)
    feature = lax.broadcasted_iota(jnp.int32, (128, BLOCK), 0)
    query_t = jnp.where(feature < HEAD_DIM, query_t[:, :BLOCK], query_t[:, BLOCK:])
    grad_query[rows, lanes] = query_t.T.astype(jnp.bfloat16)
    grad_keys[near, lanes] += dot_nn(near_ds, both)
    grad_values[near, lanes] += dot_nn(spread(edge_probs, own_probs), grads)
    far_dkey = dot_nn(far_ds, both)
    far_dvalue = dot_nn(far_probs.astype(jnp.bfloat16), grads)
    for window in range(2):
        place = pl.ds(near_rows + window * far_rows, far_rows)
        here = span.second == window
        grad_keys[place, lanes] += jnp.where(here, far_dkey, 0.0)
        grad_values[place, lanes] += jnp.where(here, far_dvalue, 0.0)


def inverse_rms(values):
    return lax.rsqrt(jnp.mean(values * values, axis=-1, keepdims=True) + EPSILON)


def rms_back(values, gain, grads):
    scale = inverse_rms(values)
    scaled = grads * gain
    back = scale * scaled - values * (
        scale * scale * scale * jnp.mean(scaled * values, axis=-1, keepdims=True)
    )
    return back, jnp.sum(grads * values * scale, axis=0, keepdims=True)


def block_sums(rows, count):
    take = lax.broadcasted_iota(jnp.int32, (count, rows.shape[0]), 1) // GBLK
    which = lax.broadcasted_iota(jnp.int32, (count, rows.shape[0]), 0)
    return dot_nn((take == which).astype(jnp.bfloat16), rows)


def owner_of(column, rows):
    return (column * ((65536 + rows - 1) // rows)) >> 16


def spread_gains(packed, rows):
    width = 32 * rows
    lane = lax.broadcasted_iota(jnp.int32, (128, width), 0)
    column = lax.broadcasted_iota(jnp.int32, (128, width), 1)
    select = (column - rows * owner_of(column, rows) == lane).astype(jnp.float32)
    wide = dot(packed, select, ((1,), (0,)), precision=lax.Precision.HIGHEST)
    device_row = lax.broadcasted_iota(jnp.int32, wide.shape, 0) >> 3
    wide_column = lax.broadcasted_iota(jnp.int32, wide.shape, 1)
    wide = jnp.where(owner_of(wide_column, rows) == device_row, wide, 0.0)
    return jnp.sum(wide.reshape(32, 8, width), axis=0)


def pack_gains(wide, rows):
    width = 32 * rows
    tall = jnp.concatenate([wide] * 32, axis=0)
    device_row = lax.broadcasted_iota(jnp.int32, tall.shape, 0) >> 3
    column = lax.broadcasted_iota(jnp.int32, tall.shape, 1)
    tall = jnp.where(owner_of(column, rows) == device_row, tall, 0.0)
    lane = lax.broadcasted_iota(jnp.int32, (width, 128), 1)
    from_column = lax.broadcasted_iota(jnp.int32, (width, 128), 0)
    select = (from_column - rows * owner_of(from_column, rows) == lane).astype(jnp.float32)
    return dot(tall, select, ((1,), (0,)), precision=lax.Precision.HIGHEST)


CHUNKS = 4
TILE = 256
SMALL_SEMS = 24
NAMES = ("g", "h", "i", "k", "v", "q", "o", "d", "f0", "f1", "f2", "f3")
NAMES += ("r0", "r1", "r2", "r3", "rd", "ro", "ra", "rb", "rc", "w", "j", "l")
Z_LAST = ("f3", "o")
Z_FIRST = ("r0", "r1")
FIRST = {}
SCHEDULE = {
    "s0": {
        0: (0, 10, 30, 40, 50, 60, 70, 80, 90, 100, 110),
    },
    "s0b": {
        0: (61, 111, 31, 41, 20, 51),
    },
    "s1": {
        0: (1, 11, 62, 2),
    },
    "s2": {
        0: (112, 32),
    },
    "s4": {
        0: (42, 33, 43, 21, 71, 81, 34, 52, 44, 53, 22, 72, 91, 23),
    },
    "s5": {
        0: (35,),
    },
    "kn": {
        2: (54, 82, 101, 63, 113),
    },
    "kt": {
        4: (73,),
    },
    "s6": {
        0: (45,),
    },
    "vn": {
        2: (92,),
        4: (83,),
    },
    "s7": {
        0: (55,),
    },
    "fa": {
        2: (102,),
        4: (93,),
        8: (103,),
        11: (74,),
    },
    "m0": {
        0: (64, 84, 65),
    },
    "m1": {
        0: (75,),
    },
    "ca": {
        0: (85,),
        1: (104, 95),
        2: (105,),
        3: (115,),
    },
    "cb": {
        0: (94,),
    },
    "cw": {
        0: (120,),
        1: (130,),
        2: (140,),
        3: (150,),
    },
    "cg": {
        3: (121,),
        6: (114, 131),
        9: (141,),
    },
    "sp": {
        0: (160,),
    },
    "m2": {
        0: (151,),
    },
    "m3": {
        0: (142, 161, 170),
    },
    "ba": {
        1: (122, 171),
        2: (143,),
        3: (152,),
        6: (153, 181),
        7: (162, 123),
        9: (144, 172, 191),
        11: (154, 163, 182, 124),
    },
    "bt": {
        0: (180,),
        1: (190,),
        2: (200,),
    },
    "wg": {
        3: (132,),
        6: (133,),
        8: (173,),
    },
    "e1": {
        0: (220,),
    },
    "e2": {
        0: (210, 183),
    },
    "gg": {
        1: (221, 134, 192, 201),
    },
    "e6": {
        0: (164, 211, 174, 184, 222, 193, 202, 223),
    },
    "e7": {
        0: (230, 203),
    },
    "e8": {
        0: (125, 135, 145, 155, 165, 175, 185, 194, 195, 231, 204, 232, 205),
    },
}


class Calls:
    def __init__(self, *actions):
        self.actions = actions

    def step(self, number):
        self.actions[number]()


def tiled(count, body, before=None):
    @pl.loop(0, count // TILE)
    def _(i):
        if before is not None:
            before(i)
        body(pl.ds(pl.multiple_of(i * TILE, TILE), TILE))


class GlobalSlots:
    def __init__(self, count):
        self.count = count

    def at(self, z, x, c):
        return self.packed(z * 4 + x * 2 + c)

    def packed(self, index):
        return pl.ds(pl.multiple_of(index * self.count, 16), self.count)


def layer_kernel(packed, tokens, cotangent, *refs):
    shards, refs = refs[:6], refs[6:]
    output, grad_tokens, gain_out, refs = refs[0], refs[1], refs[2], refs[3:]
    grads_out, refs = refs[:9], refs[9:]
    w_query, w_key, w_value, w_out, w_down, w_ff = refs[:6]
    rows_in, rows_in_t, keys, keys_t, values, query, attended, hidden, turned = refs[6:15]
    mixed, grad_both, grad_keys, grad_values, gain_grads, part_key, part_value = refs[15:22]
    spans, gain_rows, gathered, gain_part, gain_side, gain_column, group_sums = refs[22:29]
    halo, global_rows, global_near, global_mid, global_far = refs[29:34]
    buffers, refs = refs[34:88], refs[88:]
    recv, sent, small = refs
    y, z, x, c = coords()
    blk = lax.axis_index("blk")
    me = blk + 16 * y
    row_count, width = tokens.shape
    blocks = row_count // BLOCK
    local_globals = row_count // GBLK
    global_count = global_rows.shape[0]
    near_rows = row_count + 2 * BLOCK
    all_rows = rows_in.shape[0]
    far_rows = (all_rows - near_rows) // 2
    feature_rows = width // 32
    hidden_rows = w_down.shape[0] // CHUNKS
    first_row = blk * row_count
    low = jnp.bfloat16
    slots = GlobalSlots(local_globals)
    column, sides = column_peers(), side_peers()

    part_query = rows_in.at[pl.ds(0, width)]
    steps = {}
    chunk_width = w_ff.shape[2]
    sources = [("q", shards[0], w_query), ("k", shards[1], w_key), ("v", shards[2], w_value)]
    sources += [("o", shards[3], w_out), ("d", shards[4], w_down)]
    for chunk in range(CHUNKS):
        part = shards[5].at[:, pl.ds(chunk * chunk_width, chunk_width)]
        sources.append((NAMES[8 + chunk], part, w_ff.at[chunk]))
    for i, (name, shard, full) in enumerate(sources):
        kind = GatherLate if name in Z_LAST else Gather
        steps[name] = kind(shard, full, recv.at[i], sent.at[i], FIRST.get(name))
    ff_steps = [steps[name] for name in NAMES[8:12]]
    targets = [("ra", part_key), ("rb", part_value), ("rc", part_query), ("ro", w_out)]
    targets += [("rd", w_down)]
    targets += [(NAMES[12 + chunk], w_ff.at[chunk]) for chunk in range(CHUNKS)]
    for i, (name, part) in enumerate(targets):
        held = buffers[6 * i : 6 * i + 6]
        kind = ReduceEarly if name in Z_FIRST else Reduce
        steps[name] = kind(part, grads_out[i], *held, recv.at[9 + i], sent.at[9 + i], FIRST.get(name))

    def run(todo):
        for code in todo:
            steps[NAMES[code // 10]].step(code % 10)

    def tick(kind, number=0):
        run(SCHEDULE.get(kind, {}).get(number, ()))

    def loop_tick(kind, index, count):
        for number in range(count):
            todo = SCHEDULE.get(kind, {}).get(number, ())
            if todo:
                pl.when(index == number)(functools.partial(run, todo))

    def ticks(kind, count):
        return lambda index: loop_tick(kind, index, count)

    greet()
    own_tile = gathered.at[pl.ds(pl.multiple_of(me * 8, 8), 8)]

    def share_gains():
        own_tile[...] = packed[pl.ds(0, 8), :]
        for peer in column:
            send(packed.at[pl.ds(0, 8)], own_tile, small.at[1], small.at[0], peer)

    def spread_sides():
        wait_bytes(gathered.at[pl.ds(0, 56)], small.at[0])
        for k in range(CHIPS_Z):
            pair = gathered.at[pl.ds(pl.multiple_of((y * 8 + k * 2 + x) * 16, 16), 16)]
            for peer in sides:
                send(pair, pair, small.at[3], small.at[2], peer)

    def gains_here():
        wait_bytes(gathered.at[pl.ds(0, 192)], small.at[2])

    steps["g"] = Calls(share_gains, spread_sides, gains_here)

    def token_halo(side):
        source = pl.ds(row_count - BLOCK, BLOCK) if side == 0 else pl.ds(0, BLOCK)
        return pltpu.make_async_remote_copy(
            src_ref=tokens.at[source],
            dst_ref=halo.at[side],
            send_sem=small.at[8 + side],
            recv_sem=small.at[10 + side],
            device_id=(y, blk + 1 - 2 * side),
            device_id_type=MESH,
        )

    def start_halos():
        pl.when(blk < 15)(lambda: token_halo(0).start())
        pl.when(blk > 0)(lambda: token_halo(1).start())

    def end_halos():
        pl.when(blk > 0)(lambda: token_halo(0).wait_recv())
        pl.when(blk < 15)(lambda: token_halo(1).wait_recv())

    steps["h"] = Calls(start_halos, end_halos)

    def globals_z():
        block = global_rows.at[slots.at(z, x, c)]
        for k in range(1, CHIPS_Z):
            send(block, block, small.at[4], small.at[5], device(y, (z + k) % CHIPS_Z, x, c))

    def globals_x():
        wait_bytes(global_rows.at[pl.ds(0, 3 * local_globals)], small.at[5])
        for k in range(CHIPS_Z):
            block = global_rows.at[slots.at(k, x, c)]
            send(block, block, small.at[4], small.at[6], device(y, z, 1 - x, c))

    def globals_pair():
        wait_bytes(global_rows.at[pl.ds(0, 4 * local_globals)], small.at[6])
        for k in range(CHIPS_Z):
            for j in range(2):
                block = global_rows.at[slots.at(k, j, c)]
                send(block, block, small.at[4], small.at[7], device(y, z, x, 1 - c))

    def globals_here():
        wait_bytes(global_rows.at[pl.ds(0, 8 * local_globals)], small.at[7])

    steps["i"] = Calls(globals_z, globals_x, globals_pair, globals_here)
    tick("s0")

    def scale_own(place):
        wide = tokens[place, :].astype(jnp.float32)
        attended[place, :] = (wide * inverse_rms(wide)).astype(low)

    tiled(row_count, scale_own)
    global_rows[slots.packed(blk), :] = block_sums(attended[...], local_globals).astype(low)
    tick("s0b")
    lengths = packed[pl.ds(8, packed.shape[0] - 8), :].astype(jnp.int32)
    for block in range(blocks):
        spans[pl.ds(8 * block, 8), :] = span_rows(
            lengths, first_row, block, far_rows, global_count
        )
    tick("s1")
    gain_rows[...] = spread_gains(gathered[...], feature_rows)
    tick("s2")
    norm_gain, global_gain, ffn_gain = gain_rows[0:1, :], gain_rows[1:2, :], gain_rows[2:3, :]

    def normed(part):
        wide = part.astype(jnp.float32)
        return (wide * inverse_rms(wide) * norm_gain).astype(low)

    def norm_own(place):
        to = pl.ds(pl.multiple_of(place.start + BLOCK, BLOCK), TILE)
        rows_in[to, :] = normed(tokens[place, :])

    tiled(row_count, norm_own)
    tick("s2b")
    group_sums[...] = block_sums(rows_in[pl.ds(BLOCK, row_count), :], local_globals)
    tick("s3")

    @pl.when(blk == 0)
    def _():
        halo[0] = jnp.zeros_like(halo[0])

    @pl.when(blk == 15)
    def _():
        halo[1] = jnp.zeros_like(halo[1])

    rows_in[pl.ds(0, BLOCK), :] = normed(halo[0])
    rows_in[pl.ds(BLOCK + row_count, BLOCK), :] = normed(halo[1])
    def turn(source, target, start):
        target[:, pl.ds(start, TILE)] = source[pl.ds(start, TILE), :].T

    for start in range(0, near_rows, TILE):
        tick("tr", start // TILE)
        turn(rows_in, rows_in_t, start)

    def project(weights, target, start, count, place, kind):
        def one(part):
            source = pl.ds(pl.multiple_of(part.start + start, BLOCK), TILE)
            to = pl.ds(pl.multiple_of(part.start + place, BLOCK), TILE)
            target[to, :] = dot_nn(rows_in[source, :], weights[...]).astype(low)

        tiled(count, one, ticks(kind, count // TILE))

    tick("s4")

    def global_norm(place):
        summed = global_rows[place, :].astype(jnp.float32) * norm_gain
        attended[place, :] = (summed * inverse_rms(summed) * global_gain).astype(low)

    tiled(global_count, global_norm)
    for window in range(2):
        select = window_select(spans, window, blocks, far_rows, global_count)
        rows_in[pl.ds(near_rows + window * far_rows, far_rows), :] = dot_nn(
            select, attended[...]
        ).astype(low)
    for start in range(near_rows, all_rows, TILE):
        tick("trf", (start - near_rows) // TILE)
        turn(rows_in, rows_in_t, start)
    tick("s5")
    project(w_key, keys, 0, all_rows, 0, "kn")
    for start in range(0, all_rows, TILE):
        tick("kt", start // TILE)
        turn(keys, keys_t, start)
    tick("s6")
    project(w_value, values, 0, all_rows, 0, "vn")
    tick("s7")
    project(w_query, query, BLOCK, row_count, 0, "qn")
    tick("s8")
    iterations = blocks * (HEADS // 2)

    def span_of(block):
        return Span(spans[pl.ds(pl.multiple_of(block * 8, 8), 8), :])

    @pl.loop(0, iterations // 2)
    def _(i):
        loop_tick("fa", i, iterations // 2)
        for j in range(2):
            block = (2 * i + j) % blocks
            attend_block(
                (2 * i) // blocks, block, span_of(block), query, keys, values, attended,
                near_rows, far_rows,
            )

    wait_bytes(global_rows.at[pl.ds(0, 15 * local_globals)], small.at[4])
    tick("m0")

    def after(place):
        return pl.ds(pl.multiple_of(place.start + row_count, TILE), TILE)

    def join(place):
        middle = tokens[place, :].astype(jnp.float32) + dot_nn(attended[place, :], w_out[...])
        grad_keys[place, :] = middle
        grad_keys[after(place), :] = middle
        low_hidden = (middle * inverse_rms(middle) * ffn_gain).astype(low)
        hidden[place, :] = low_hidden
        turned[:, place] = low_hidden.T
        grad_values[place, :] = jnp.zeros((TILE, width), jnp.float32)

    tiled(row_count, join, ticks("jn", 2))
    tick("m1")

    @pl.loop(0, CHUNKS)
    def _(chunk):
        loop_tick("ca", chunk, CHUNKS)
        half = chunk_width // 2
        rows = pl.ds(pl.multiple_of(chunk * hidden_rows, 128), hidden_rows)

        def feed(place):
            both = dot_nn(hidden[place, :], w_ff[chunk])
            gate, up = both[:, :half], both[:, half:]
            square = gate * gate
            bend = jnp.tanh(GELU_SCALE * gate * (1.0 + GELU_CUBIC * square))
            lift = 0.5 * (1.0 + bend)
            active = gate * lift
            slope = lift + 0.5 * gate * (1.0 - bend * bend) * (
                GELU_SCALE * (1.0 + 3.0 * GELU_CUBIC * square)
            )
            mixed[place, :] = (active * up).astype(low)
            grad_mixed = dot_nt(cotangent[place, :], w_down[rows, :])
            grad_both[place, pl.ds(0, half)] = (grad_mixed * up * slope).astype(low)
            grad_both[place, pl.ds(half, half)] = (grad_mixed * active).astype(low)
            grad_keys[after(place), :] += dot_nn(mixed[place, :], w_down[rows, :])
            grad_values[place, :] += dot_nt(grad_both[place, :], w_ff[chunk])

        tiled(row_count, feed, lambda i: pl.when(i == 1)(lambda: loop_tick("cb", chunk, CHUNKS)))
        for number in range(CHUNKS):
            pl.when(chunk == number)(functools.partial(ff_steps[number].step, 6))

        def gate_up_grad(place):
            w_ff[chunk, place, :] = dot_nn(turned[place, :], grad_both[...]).astype(low)

        tiled(width, gate_up_grad, lambda i: loop_tick("cg", chunk * 3 + i, 3 * CHUNKS))
        loop_tick("cw", chunk, CHUNKS)
        pl.when(chunk == 0)(lambda: steps["d"].step(6))
        w_down[rows, :] = dot(mixed[...], cotangent[...], ((0,), (0,))).astype(low)

    gain_grads[...] = jnp.zeros_like(gain_grads)

    def split(place):
        output[place, :] = grad_keys[after(place), :].astype(low)
        back, gain_grad = rms_back(grad_keys[place, :], ffn_gain, grad_values[place, :])
        gain_grads[2:3, :] += gain_grad
        grad_middle = cotangent[place, :].astype(jnp.float32) + back
        grad_tokens[place, :] = grad_middle
        branch = grad_middle.astype(low)
        rows_in[place, :] = branch
        hidden[place, :] = dot_nt(branch, w_out[...]).astype(low)
        turned[:, place] = attended[place, :].T

    tiled(row_count, split, ticks("sp", 2))
    tick("m2")
    steps["o"].step(6)

    def out_grad(place):
        w_out[place, :] = dot_nn(turned[place, :], rows_in[pl.ds(0, row_count), :]).astype(low)

    tiled(width, out_grad)
    tick("m3")

    def clear(place):
        grad_keys[place, :] = jnp.zeros((TILE, width), jnp.float32)
        grad_values[place, :] = jnp.zeros((TILE, width), jnp.float32)

    tiled(all_rows, clear)
    part_width = width // 3
    part_rounds = iterations // 6

    def back_part(third, target):
        @pl.loop(0, part_rounds)
        def _(j):
            i = third * part_rounds + j
            for number in range(part_rounds):
                todo = SCHEDULE.get("ba", {}).get(third * part_rounds + number, ())
                if todo:
                    pl.when(j == number)(functools.partial(run, todo))
            for k in range(2):
                block = (2 * i + k) % blocks
                attend_block_back(
                    (2 * i) // blocks, block, span_of(block), query, hidden, keys, keys_t, values,
                    query, grad_keys, grad_values, near_rows, far_rows,
                )

        lanes = pl.ds(third * part_width, part_width)

        def lower(place):
            keys[place, lanes] = grad_keys[place, lanes].astype(low)
            values[place, lanes] = grad_values[place, lanes].astype(low)

        tiled(all_rows, lower)

        def weight_grad(place):
            own = rows_in_t[place, pl.ds(BLOCK, row_count)]
            target[place, pl.ds(0, part_width)] = dot_nn(own, query[:, lanes]).astype(low)
            every = rows_in_t[place, :]
            target[place, pl.ds(part_width, part_width)] = dot_nn(every, keys[:, lanes]).astype(low)
            target[place, pl.ds(2 * part_width, part_width)] = dot_nn(
                every, values[:, lanes]
            ).astype(low)

        tiled(width, weight_grad, functools.partial(tick_part, third))
        tick("bt", third)

    def tick_part(third, index):
        for number in range(3):
            todo = SCHEDULE.get("wg", {}).get(3 * third + number, ())
            if todo:
                pl.when(index == number)(functools.partial(run, todo))

    for third, target in enumerate((part_key, part_value, part_query)):
        back_part(third, target)
    tick("e0")

    def grad_rows(start, count):
        part = pl.ds(start, count)
        return dot_nt(keys[part, :], w_key[...]) + dot_nt(values[part, :], w_value[...])

    for window in range(2):
        hidden[pl.ds(window * far_rows, far_rows), :] = grad_rows(
            near_rows + window * far_rows, far_rows
        ).astype(low)
    tick("e1b")
    selects = [window_select(spans, w, blocks, far_rows, global_count) for w in range(2)]
    for half in range(2):
        part = slice(half * (global_count // 2), (half + 1) * (global_count // 2))
        global_rows[part, :] = sum(
            dot(selects[w][:, part], hidden[pl.ds(w * far_rows, far_rows), :], ((0,), (0,)))
            for w in range(2)
        ).astype(low)

    def add_global(rows, ref, index):
        total = global_rows[rows, :].astype(jnp.float32)
        total = total + ref[slots.packed(index), :].astype(jnp.float32)
        global_rows[rows, :] = total.astype(low)

    def sums_pair():
        for k in range(CHIPS_Z):
            for j in range(2):
                send(
                    global_rows.at[slots.at(k, j, 1 - c)],
                    global_near.at[slots.packed(k * 2 + j)],
                    small.at[16],
                    small.at[17],
                    device(y, z, x, 1 - c),
                )

    def sums_x():
        wait_bytes(global_near, small.at[17])
        for k in range(CHIPS_Z):
            for j in range(2):
                add_global(slots.at(k, j, c), global_near, k * 2 + j)
        for k in range(CHIPS_Z):
            send(
                global_rows.at[slots.at(k, 1 - x, c)],
                global_mid.at[slots.packed(k)],
                small.at[16],
                small.at[18],
                device(y, z, 1 - x, c),
            )

    def sums_z():
        wait_bytes(global_mid, small.at[18])
        for k in range(CHIPS_Z):
            add_global(slots.at(k, x, c), global_mid, k)
        for k in range(1, CHIPS_Z):
            to_z = (z + k) % CHIPS_Z
            send(
                global_rows.at[slots.at(to_z, x, c)],
                global_far.at[slots.packed(k - 1)],
                small.at[16],
                small.at[19],
                device(y, to_z, x, c),
            )

    def sums_here():
        wait_bytes(global_far, small.at[19])

    steps["j"] = Calls(sums_pair, sums_x, sums_z, sums_here)
    tick("e1")
    halo[4] = grad_rows(0, BLOCK).astype(low)
    halo[5] = grad_rows(BLOCK + row_count, BLOCK).astype(low)
    def grad_halo(side):
        return pltpu.make_async_remote_copy(
            src_ref=halo.at[4 + side],
            dst_ref=halo.at[3 - side],
            send_sem=small.at[20 + side],
            recv_sem=small.at[22 + side],
            device_id=(y, blk - 1 + 2 * side),
            device_id_type=MESH,
        )

    def start_grad_halos():
        pl.when(blk > 0)(lambda: grad_halo(0).start())
        pl.when(blk < 15)(lambda: grad_halo(1).start())

    def end_grad_halos():
        pl.when(blk > 0)(lambda: grad_halo(1).wait_recv())
        pl.when(blk < 15)(lambda: grad_halo(0).wait_recv())

    steps["w"] = Calls(start_grad_halos, end_grad_halos)
    tick("e2")
    def gather_grads(place):
        rows = pl.ds(pl.multiple_of(place.start + BLOCK, BLOCK), TILE)
        grad_keys[place, :] = (
            dot_nt(keys[rows, :], w_key[...])
            + dot_nt(values[rows, :], w_value[...])
            + dot_nt(query[place, :], w_query[...])
        )

    tiled(row_count, gather_grads, ticks("gg", 2))
    tick("e6")

    @pl.when(blk == 0)
    def _():
        halo[2] = jnp.zeros_like(halo[2])

    @pl.when(blk == 15)
    def _():
        halo[3] = jnp.zeros_like(halo[3])

    grad_keys[pl.ds(0, BLOCK), :] += halo[2].astype(jnp.float32)
    grad_keys[pl.ds(row_count - BLOCK, BLOCK), :] += halo[3].astype(jnp.float32)
    total = global_rows[slots.at(z, x, c), :].astype(jnp.float32)
    for k in range(CHIPS_Z - 1):
        total = total + global_far[slots.packed(k), :].astype(jnp.float32)
    grad_summed, grad_global_gain = rms_back(group_sums[...], global_gain, total)
    gain_grads[1:2, :] = grad_global_gain
    group_sums[...] = grad_summed

    def finish(place):
        few = TILE // GBLK
        sums = group_sums[pl.ds(pl.multiple_of(place.start // GBLK, 8), few), :]
        grad_normed = grad_keys[place, :] + jnp.broadcast_to(
            sums[:, None, :], (few, GBLK, width)
        ).reshape(TILE, width)
        back, gain_grad = rms_back(tokens[place, :].astype(jnp.float32), norm_gain, grad_normed)
        gain_grads[0:1, :] += gain_grad
        grad_tokens[place, :] += back

    tiled(row_count, finish, ticks("fi", 2))
    gain_part[...] = pack_gains(gain_grads[...], feature_rows)

    def gain_pair(pair_y, k, pair_x):
        return pl.ds(pl.multiple_of((pair_y * 8 + k * 2 + pair_x) * 16, 16), 16)

    def gains_sides():
        for index, peer in enumerate(sides):
            side_y = y if index == 0 else 1 - y
            side_x = x if index == 1 else 1 - x
            for k in range(CHIPS_Z):
                send(
                    gain_part.at[gain_pair(side_y, k, side_x)],
                    gain_side.at[index, pl.ds(k * 16, 16)],
                    small.at[13],
                    small.at[12],
                    peer,
                )

    def gains_column():
        wait_bytes(gain_side, small.at[12])
        for k in range(CHIPS_Z):
            rows = gain_pair(y, k, x)
            place = pl.ds(k * 16, 16)
            gain_part[rows, :] += gain_side[0, place, :] + gain_side[1, place, :] + gain_side[2, place, :]
        place = z * 2 + c
        gain_column[pl.ds(pl.multiple_of(place * 8, 8), 8), :] = gain_part[
            pl.ds(pl.multiple_of(me * 8, 8), 8), :
        ]
        for k in range(CHIPS_Z):
            for j in range(2):
                if k == 0 and j == 0:
                    peer_z, peer_c = z, 1 - c
                elif k == 0:
                    continue
                else:
                    peer_z, peer_c = (z + k) % CHIPS_Z, j
                peer_me = y * 16 + peer_z * 4 + x * 2 + peer_c
                send(
                    gain_part.at[pl.ds(pl.multiple_of(peer_me * 8, 8), 8)],
                    gain_column.at[pl.ds(pl.multiple_of(place * 8, 8), 8)],
                    small.at[15],
                    small.at[14],
                    device(y, peer_z, x, peer_c),
                )

    def gains_done():
        wait_bytes(gain_column.at[pl.ds(0, 56)], small.at[14])

    steps["l"] = Calls(gains_sides, gains_column, gains_done)
    tick("e7")
    tick("e8")
    gain_out[...] = jnp.sum(gain_column[...].reshape(8, 8, 128), axis=0)
    for name, _ in targets:
        steps[name].step(6)
    for one in [steps["q"], steps["k"], steps["v"]]:
        one.step(6)
    wait_bytes(gathered.at[pl.ds(0, 56)], small.at[1])
    wait_bytes(gathered.at[pl.ds(0, 192)], small.at[3])
    wait_bytes(global_rows.at[pl.ds(0, 15 * local_globals)], small.at[16])
    wait_bytes(gathered.at[pl.ds(0, 192)], small.at[13])
    wait_bytes(gathered.at[pl.ds(0, 56)], small.at[15])
    pl.when(blk < 15)(lambda: token_halo(0).wait_send())
    pl.when(blk > 0)(lambda: token_halo(1).wait_send())
    pl.when(blk > 0)(lambda: grad_halo(0).wait_send())
    pl.when(blk < 15)(lambda: grad_halo(1).wait_send())


def layer(packed, tokens, cotangent, shards, far_rows, global_count):
    row_count, width = tokens.shape
    all_rows = row_count + 2 * BLOCK + 2 * far_rows
    local_globals = row_count // GBLK
    down_rows = shards[4].shape[0]
    chunk_width = shards[5].shape[1] // CHUNKS
    vmem = pl.BlockSpec(memory_space=pltpu.VMEM)
    anywhere = pl.BlockSpec(memory_space=pl.ANY)
    low, wide = jnp.bfloat16, jnp.float32
    shard_shapes = [(width // 32, width)] * 4 + [(down_rows, width)]
    shard_shapes += [(width // 32, chunk_width)] * CHUNKS
    buffers = []
    names = ("ra", "rb", "rc", "ro", "rd") + NAMES[12:16]
    for name, (rows, columns) in zip(names, shard_shapes):
        counts = (24, 4, 2) if name in Z_FIRST else (16, 8, 6)
        buffers += reduce_scratch(rows, columns // 2, low, counts)
    return pl.pallas_call(
        layer_kernel,
        out_shape=[
            jax.ShapeDtypeStruct((row_count, width), low),
            jax.ShapeDtypeStruct((row_count, width), wide),
            jax.ShapeDtypeStruct((8, 128), wide),
        ]
        + [jax.ShapeDtypeStruct(shape, wide) for shape in shard_shapes],
        in_specs=[vmem] * 3 + [anywhere] * 6,
        out_specs=[vmem] * 12,
        scratch_shapes=[pltpu.VMEM((width, width), low)] * 4
        + [
            pltpu.VMEM((32 * down_rows, width), low),
            pltpu.VMEM((CHUNKS, width, chunk_width), low),
            pltpu.VMEM((all_rows, width), low),
            pltpu.VMEM((width, all_rows), low),
            pltpu.VMEM((all_rows, width), low),
            pltpu.VMEM((width, all_rows), low),
            pltpu.VMEM((all_rows, width), low),
            pltpu.VMEM((row_count, width), low),
            pltpu.VMEM((row_count, width), low),
            pltpu.VMEM((row_count, width), low),
            pltpu.VMEM((width, row_count), low),
            pltpu.VMEM((row_count, chunk_width // 2), low),
            pltpu.VMEM((row_count, chunk_width), low),
            pltpu.VMEM((all_rows, width), wide),
            pltpu.VMEM((all_rows, width), wide),
            pltpu.VMEM((8, width), wide),
            pltpu.VMEM((width, width), low),
            pltpu.VMEM((width, width), low),
            pltpu.VMEM((8 * row_count // BLOCK, 128), jnp.int32),
            pltpu.VMEM((8, width), wide),
            pltpu.VMEM((256, 128), wide),
            pltpu.VMEM((256, 128), wide),
            pltpu.VMEM((3, 64, 128), wide),
            pltpu.VMEM((64, 128), wide),
            pltpu.VMEM((local_globals, width), wide),
            pltpu.VMEM((6, BLOCK, width), low),
            pltpu.VMEM((global_count, width), low),
            pltpu.VMEM((8 * local_globals, width), low),
            pltpu.VMEM((4 * local_globals, width), low),
            pltpu.VMEM((3 * local_globals, width), low),
        ]
        + buffers
        + [
            pltpu.SemaphoreType.DMA((18, 5)),
            pltpu.SemaphoreType.DMA((18, 3)),
            pltpu.SemaphoreType.DMA((SMALL_SEMS,)),
        ],
        compiler_params=pltpu.CompilerParams(
            collective_id=0, has_side_effects=True, vmem_limit_bytes=VMEM_BYTES
        ),
        name="layer",
    )(packed, tokens, cotangent, *shards)


def per_device(
    tokens, lengths, norm_gain, global_gain, w_query, w_key, w_value, w_out,
    ffn_gain, w_gate, w_up, w_down, cotangent,
):
    row_count, width = tokens.shape
    global_count = row_count * lax.axis_size("blk") // GBLK
    far_rows = global_count // 2
    feature_rows = norm_gain.shape[0]
    gains = jnp.stack([norm_gain, global_gain, ffn_gain]).astype(jnp.float32)
    gains = jnp.pad(gains, ((0, 5), (0, 128 - feature_rows)))
    wide_lengths = jnp.broadcast_to(
        lengths[0].astype(jnp.float32)[:, None], (lengths.shape[1], 128)
    )
    packed = jnp.concatenate([gains, wide_lengths], axis=0)
    chunked = (w_gate.shape[0], CHUNKS, w_gate.shape[1] // CHUNKS)
    w_ff = jnp.concatenate([w_gate.reshape(chunked), w_up.reshape(chunked)], axis=2)
    w_ff = w_ff.reshape(w_gate.shape[0], -1)
    shards = (w_query, w_key, w_value, w_out, w_down, w_ff)
    outs = layer(packed, tokens, cotangent, shards, far_rows, global_count)
    output, grad_tokens, gain_grads = outs[:3]
    thirds, grads, grad_ff = outs[3:6], outs[6:8], outs[8:]
    half = chunked[2]
    part = width // 3
    in_grads = [
        jnp.concatenate([one[:, i * part : (i + 1) * part] for one in thirds], axis=1)
        for i in range(3)
    ]
    return (
        output,
        grad_tokens,
        gain_grads[0, :feature_rows],
        gain_grads[1, :feature_rows],
        *in_grads,
        grads[0],
        gain_grads[2, :feature_rows],
        jnp.concatenate([part[:, :half] for part in grad_ff], axis=1),
        jnp.concatenate([part[:, half:] for part in grad_ff], axis=1),
        grads[1],
    )


def fits(mesh):
    return mesh.shape["seq"] == 2 and mesh.shape["blk"] == 16


def solution(mesh):
    return jax.shard_map(
        per_device if fits(mesh) else per_device_general,
        mesh=mesh,
        in_specs=(
            P(("seq", "blk"), None),
            P("seq", None),
            P(("seq", "blk")),
            P(("seq", "blk")),
            P(("seq", "blk"), None),
            P(("seq", "blk"), None),
            P(("seq", "blk"), None),
            P(("seq", "blk"), None),
            P(("seq", "blk")),
            P(("seq", "blk"), None),
            P(("seq", "blk"), None),
            P(("seq", "blk"), None),
            P(("seq", "blk"), None),
        ),
        out_specs=(
            P(("seq", "blk"), None),
            P(("seq", "blk"), None),
            P(("seq", "blk")),
            P(("seq", "blk")),
            P(("seq", "blk"), None),
            P(("seq", "blk"), None),
            P(("seq", "blk"), None),
            P(("seq", "blk"), None),
            P(("seq", "blk")),
            P(("seq", "blk"), None),
            P(("seq", "blk"), None),
            P(("seq", "blk"), None),
        ),
        check_vma=False,
    )
```

```python
import functools

import jax
import jax.numpy as jnp
from jax import lax
from jax.experimental import pallas as pl
from jax.experimental.pallas import tpu as pltpu
from jax.sharding import PartitionSpec as P


D = 768
HEADS = 12
HEAD_DIM = 64
GBLK = 16
BLOCK = 128
LONGEST = 16384


EPSILON = 1e-06
MASKED = -1e30
GELU_SCALE = 0.7978845608028654
GELU_CUBIC = 0.044715


def with_halo(block, sides, width):
    for axis, dim in sides:
        count = lax.axis_size(axis)
        forward = [(i, i + 1) for i in range(count - 1)]
        backward = [(target, source) for source, target in forward]
        low = lax.ppermute(
            lax.slice_in_dim(block, block.shape[dim] - width, None, axis=dim), axis, forward
        )
        high = lax.ppermute(lax.slice_in_dim(block, 0, width, axis=dim), axis, backward)
        block = jnp.concatenate([low, block, high], axis=dim)
    return block


def rms_norm(values, scales):
    return values * lax.rsqrt(jnp.mean(values * values, axis=-1, keepdims=True) + EPSILON) * scales


def gelu_tanh(values):
    return (
        0.5
        * values
        * (1.0 + jnp.tanh(GELU_SCALE * (values + GELU_CUBIC * values * values * values)))
    )


def gated(gate_part, up_part):
    return gelu_tanh(gate_part) * up_part


def sequence_of(positions, seq_ends):
    return jnp.sum((positions[:, None] >= seq_ends[None, :]).astype(jnp.int32), axis=1)


def matmul(left_side, right_side):
    return jnp.dot(left_side, right_side, preferred_element_type=jnp.float32)


def matmul_left(left_side, right_side):
    return jnp.einsum("ta,tb->ab", left_side, right_side, preferred_element_type=jnp.float32)


def matmul_right(left_side, right_side):
    return jnp.einsum("ta,ba->tb", left_side, right_side, preferred_element_type=jnp.float32)


def windows(extended, row_count):
    block_count = row_count // BLOCK
    pieces = [
        extended[offset * BLOCK : offset * BLOCK + row_count].reshape(
            block_count, BLOCK, extended.shape[-1]
        )
        for offset in range(3)
    ]
    return jnp.concatenate(pieces, axis=1)


def unwindow(window_grads, row_count):
    channels = window_grads.shape[-1]
    summed_grad = jnp.zeros((row_count + 2 * BLOCK, channels), jnp.float32)
    for offset in range(3):
        piece_grad = window_grads[:, offset * BLOCK : (offset + 1) * BLOCK].reshape(
            row_count, channels
        )
        summed_grad = summed_grad + jnp.pad(
            piece_grad, ((offset * BLOCK, (2 - offset) * BLOCK), (0, 0))
        )
    return summed_grad


def head_scores(query_head, near_keys, far_keys, near_mask, far_mask):
    block_count = near_keys.shape[0]
    query_blocks = query_head.reshape(block_count, BLOCK, HEAD_DIM)
    near_scores = jnp.einsum(
        "nqd,nkd->nqk", query_blocks, near_keys, preferred_element_type=jnp.float32
    )
    far_scores = jnp.einsum("qd,kd->qk", query_head, far_keys, preferred_element_type=jnp.float32)
    return (jnp.where(near_mask, near_scores, MASKED), jnp.where(far_mask, far_scores, MASKED))


def per_device_general(
    tokens,
    lengths,
    norm_gain,
    global_gain,
    w_query,
    w_key,
    w_value,
    w_out,
    ffn_gain,
    w_gate,
    w_up,
    w_down,
    cotangent,
):
    row_count = tokens.shape[0]
    inner_dim = HEADS * HEAD_DIM
    block_count = row_count // BLOCK
    local_globals = row_count // GBLK
    group_tokens = row_count * lax.axis_size("blk")
    global_count = group_tokens // GBLK
    longest_len = min(LONGEST, group_tokens // 2)
    span_rows = min(global_count, 2 * (longest_len // GBLK) + local_globals)
    attn_full = (
        lax.all_gather(norm_gain, ("seq", "blk"), axis=0, tiled=True),
        lax.all_gather(global_gain, ("seq", "blk"), axis=0, tiled=True),
        lax.all_gather(w_query, ("seq", "blk"), axis=0, tiled=True),
        lax.all_gather(w_key, ("seq", "blk"), axis=0, tiled=True),
        lax.all_gather(w_value, ("seq", "blk"), axis=0, tiled=True),
        lax.all_gather(w_out, ("seq", "blk"), axis=0, tiled=True),
    )
    seq_ends = jnp.cumsum(lengths[0])
    first_row = lax.axis_index("blk") * row_count
    span_start = jnp.clip(first_row // GBLK - longest_len // GBLK, 0, global_count - span_rows)
    query_pos = first_row + jnp.arange(row_count, dtype=jnp.int32)
    query_seq = sequence_of(query_pos, seq_ends)
    key_pos = first_row - BLOCK + jnp.arange(row_count + 2 * BLOCK, dtype=jnp.int32)
    inside = (key_pos >= 0) & (key_pos < group_tokens)
    key_seq = jnp.where(inside, sequence_of(key_pos, seq_ends), -1)
    global_seq = sequence_of((span_start + jnp.arange(span_rows, dtype=jnp.int32)) * GBLK, seq_ends)
    query_pos_win = query_pos.reshape(block_count, BLOCK)
    query_seq_win = query_seq.reshape(block_count, BLOCK)
    key_pos_win = windows(key_pos[:, None], row_count)[:, :, 0]
    key_seq_win = windows(key_seq[:, None], row_count)[:, :, 0]
    near_mask = (jnp.abs(query_pos_win[:, :, None] - key_pos_win[:, None, :]) <= BLOCK - 1) & (
        query_seq_win[:, :, None] == key_seq_win[:, None, :]
    )
    far_mask = query_seq[:, None] == global_seq[None, :]
    tokens_full = tokens.astype(jnp.float32)
    normed_full, normed_pull = jax.vjp(rms_norm, tokens_full, attn_full[0].astype(jnp.float32))
    normed = normed_full.astype(jnp.bfloat16)
    queries = matmul(normed, attn_full[2]).astype(jnp.bfloat16)
    key_rows = matmul(normed, attn_full[3]).astype(jnp.bfloat16)
    value_rows = matmul(normed, attn_full[4]).astype(jnp.bfloat16)
    local_kv = jnp.concatenate([key_rows, value_rows], axis=1)
    extended = with_halo(local_kv, (("blk", 0),), BLOCK)
    near_kv = windows(extended, row_count)
    summed = jnp.sum(normed.astype(jnp.float32).reshape(local_globals, GBLK, D), axis=1)
    global_full, global_pull = jax.vjp(rms_norm, summed, attn_full[1].astype(jnp.float32))
    global_in = global_full.astype(jnp.bfloat16)
    own_global = jnp.concatenate(
        [
            matmul(global_in, attn_full[3]).astype(jnp.bfloat16),
            matmul(global_in, attn_full[4]).astype(jnp.bfloat16),
        ],
        axis=1,
    )
    global_kv = lax.all_gather(own_global, "blk", axis=0, tiled=True)
    span_kv = lax.dynamic_slice_in_dim(global_kv, span_start, span_rows, 0)

    def head_slices(head_index):
        column = head_index * HEAD_DIM
        query_head = lax.dynamic_slice_in_dim(queries, column, HEAD_DIM, 1)
        near_keys = lax.dynamic_slice_in_dim(near_kv, column, HEAD_DIM, 2)
        near_values = lax.dynamic_slice_in_dim(near_kv, inner_dim + column, HEAD_DIM, 2)
        far_keys = lax.dynamic_slice_in_dim(span_kv, column, HEAD_DIM, 1)
        far_values = lax.dynamic_slice_in_dim(span_kv, inner_dim + column, HEAD_DIM, 1)
        return (column, query_head, near_keys, near_values, far_keys, far_values)

    def head_forward(head_index, carry):
        attended_rows, log_sums = carry
        column, query_head, near_keys, near_values, far_keys, far_values = head_slices(head_index)
        near_scores, far_scores = head_scores(query_head, near_keys, far_keys, near_mask, far_mask)
        highest = jnp.maximum(
            jnp.max(near_scores, axis=2).reshape(row_count), jnp.max(far_scores, axis=1)
        )
        near_exp = jnp.exp(near_scores - highest.reshape(block_count, BLOCK, 1))
        far_exp = jnp.exp(far_scores - highest[:, None])
        denominator = jnp.sum(near_exp, axis=2).reshape(row_count) + jnp.sum(far_exp, axis=1)
        near_probs = (near_exp / denominator.reshape(block_count, BLOCK, 1)).astype(jnp.bfloat16)
        far_probs = (far_exp / denominator[:, None]).astype(jnp.bfloat16)
        head_out = jnp.einsum(
            "nqk,nkd->nqd", near_probs, near_values, preferred_element_type=jnp.float32
        ).reshape(row_count, HEAD_DIM)
        head_out = head_out + jnp.einsum(
            "qk,kd->qd", far_probs, far_values, preferred_element_type=jnp.float32
        )
        attended_rows = lax.dynamic_update_slice_in_dim(attended_rows, head_out, column, 1)
        log_sums = lax.dynamic_update_index_in_dim(
            log_sums, highest + jnp.log(denominator), head_index, 0
        )
        return (attended_rows, log_sums)

    attended_rows, log_sums = lax.fori_loop(
        0,
        HEADS,
        head_forward,
        (
            jnp.zeros((row_count, inner_dim), jnp.float32),
            jnp.zeros((HEADS, row_count), jnp.float32),
        ),
    )
    attended = attended_rows.astype(jnp.bfloat16)
    middle = tokens_full + matmul(attended, attn_full[5])
    ffn_full = (
        lax.all_gather(ffn_gain, ("seq", "blk"), axis=0, tiled=True),
        lax.all_gather(w_gate, ("seq", "blk"), axis=0, tiled=True),
        lax.all_gather(w_up, ("seq", "blk"), axis=0, tiled=True),
        lax.all_gather(w_down, ("seq", "blk"), axis=0, tiled=True),
    )
    hidden_full, hidden_pull = jax.vjp(rms_norm, middle, ffn_full[0].astype(jnp.float32))
    hidden = hidden_full.astype(jnp.bfloat16)
    gate_pre = matmul(hidden, ffn_full[1])
    up_pre = matmul(hidden, ffn_full[2])
    gated_rows, gated_pull = jax.vjp(gated, gate_pre, up_pre)
    mixed = gated_rows.astype(jnp.bfloat16)
    output = (middle + matmul(mixed, ffn_full[3])).astype(jnp.bfloat16)
    ffn_back = (
        lax.all_gather(ffn_gain, ("seq", "blk"), axis=0, tiled=True),
        lax.all_gather(w_gate, ("seq", "blk"), axis=0, tiled=True),
        lax.all_gather(w_up, ("seq", "blk"), axis=0, tiled=True),
        lax.all_gather(w_down, ("seq", "blk"), axis=0, tiled=True),
    )
    grad_down = matmul_left(mixed, cotangent)
    grad_mixed = matmul_right(cotangent, ffn_back[3])
    grad_gate_full, grad_up_full = gated_pull(grad_mixed)
    grad_gate = grad_gate_full.astype(jnp.bfloat16)
    grad_up = grad_up_full.astype(jnp.bfloat16)
    grad_wgate = matmul_left(hidden, grad_gate)
    grad_wup = matmul_left(hidden, grad_up)
    grad_hidden = matmul_right(grad_gate, ffn_back[1]) + matmul_right(grad_up, ffn_back[2])
    grad_middle_norm, grad_ffn_gain = hidden_pull(grad_hidden)
    grad_middle = cotangent.astype(jnp.float32) + grad_middle_norm
    attn_back = (
        lax.all_gather(norm_gain, ("seq", "blk"), axis=0, tiled=True),
        lax.all_gather(global_gain, ("seq", "blk"), axis=0, tiled=True),
        lax.all_gather(w_query, ("seq", "blk"), axis=0, tiled=True),
        lax.all_gather(w_key, ("seq", "blk"), axis=0, tiled=True),
        lax.all_gather(w_value, ("seq", "blk"), axis=0, tiled=True),
        lax.all_gather(w_out, ("seq", "blk"), axis=0, tiled=True),
    )
    grad_branch = grad_middle.astype(jnp.bfloat16)
    grad_wout = matmul_left(attended, grad_branch)
    grad_attended = matmul_right(grad_branch, attn_back[5]).astype(jnp.bfloat16)

    def head_backward(head_index, carry):
        grad_query_rows, grad_near, grad_far = carry
        column, query_head, near_keys, near_values, far_keys, far_values = head_slices(head_index)
        near_scores, far_scores = head_scores(query_head, near_keys, far_keys, near_mask, far_mask)
        lse_head = log_sums[head_index]
        near_probs = jnp.exp(near_scores - lse_head.reshape(block_count, BLOCK, 1))
        far_probs = jnp.exp(far_scores - lse_head[:, None])
        grad_head = lax.dynamic_slice_in_dim(grad_attended, column, HEAD_DIM, 1)
        grad_blocks = grad_head.reshape(block_count, BLOCK, HEAD_DIM)
        query_blocks = query_head.reshape(block_count, BLOCK, HEAD_DIM)
        near_dprobs = jnp.einsum(
            "nqd,nkd->nqk", grad_blocks, near_values, preferred_element_type=jnp.float32
        )
        far_dprobs = jnp.einsum(
            "qd,kd->qk", grad_head, far_values, preferred_element_type=jnp.float32
        )
        delta_rows = jnp.sum(near_probs * near_dprobs, axis=2).reshape(row_count) + jnp.sum(
            far_probs * far_dprobs, axis=1
        )
        near_grad_scores = (
            near_probs * (near_dprobs - delta_rows.reshape(block_count, BLOCK, 1))
        ).astype(jnp.bfloat16)
        far_grad_scores = (far_probs * (far_dprobs - delta_rows[:, None])).astype(jnp.bfloat16)
        head_dquery = jnp.einsum(
            "nqk,nkd->nqd", near_grad_scores, near_keys, preferred_element_type=jnp.float32
        ).reshape(row_count, HEAD_DIM)
        head_dquery = head_dquery + jnp.einsum(
            "qk,kd->qd", far_grad_scores, far_keys, preferred_element_type=jnp.float32
        )
        near_dkey = jnp.einsum(
            "nqk,nqd->nkd", near_grad_scores, query_blocks, preferred_element_type=jnp.float32
        )
        near_dvalue = jnp.einsum(
            "nqk,nqd->nkd",
            near_probs.astype(jnp.bfloat16),
            grad_blocks,
            preferred_element_type=jnp.float32,
        )
        far_dkey = jnp.einsum(
            "qk,qd->kd", far_grad_scores, query_head, preferred_element_type=jnp.float32
        )
        far_dvalue = jnp.einsum(
            "qk,qd->kd",
            far_probs.astype(jnp.bfloat16),
            grad_head,
            preferred_element_type=jnp.float32,
        )
        grad_query_rows = lax.dynamic_update_slice_in_dim(grad_query_rows, head_dquery, column, 1)
        grad_near = lax.dynamic_update_slice_in_dim(grad_near, near_dkey, column, 2)
        grad_near = lax.dynamic_update_slice_in_dim(grad_near, near_dvalue, inner_dim + column, 2)
        grad_far = lax.dynamic_update_slice_in_dim(grad_far, far_dkey, column, 1)
        grad_far = lax.dynamic_update_slice_in_dim(grad_far, far_dvalue, inner_dim + column, 1)
        return (grad_query_rows, grad_near, grad_far)

    grad_query_rows, grad_near, grad_far = lax.fori_loop(
        0,
        HEADS,
        head_backward,
        (
            jnp.zeros((row_count, inner_dim), jnp.float32),
            jnp.zeros((block_count, 3 * BLOCK, 2 * inner_dim), jnp.float32),
            jnp.zeros((span_rows, 2 * inner_dim), jnp.float32),
        ),
    )
    grad_extended = unwindow(grad_near, row_count)
    rim_rows = jnp.concatenate([grad_extended[:BLOCK], grad_extended[row_count + BLOCK :]], axis=0)
    returned = with_halo(rim_rows.astype(jnp.bfloat16), (("blk", 0),), BLOCK).astype(rim_rows.dtype)
    grad_kv = grad_extended[BLOCK : row_count + BLOCK]
    grad_kv = grad_kv + jnp.pad(returned[:BLOCK], ((0, row_count - BLOCK), (0, 0)))
    grad_kv = grad_kv + jnp.pad(returned[3 * BLOCK :], ((row_count - BLOCK, 0), (0, 0)))
    grad_kv = grad_kv.astype(jnp.bfloat16)
    grad_key = grad_kv[:, :inner_dim]
    grad_value = grad_kv[:, inner_dim:]
    group_far = lax.dynamic_update_slice_in_dim(
        jnp.zeros((global_count, 2 * inner_dim), jnp.float32), grad_far, span_start, 0
    )
    own_global_grad = lax.psum_scatter(group_far, "blk", scatter_dimension=0, tiled=True).astype(
        jnp.bfloat16
    )
    grad_global_key = own_global_grad[:, :inner_dim]
    grad_global_value = own_global_grad[:, inner_dim:]
    grad_query = grad_query_rows.astype(jnp.bfloat16)
    grad_wquery = matmul_left(normed, grad_query)
    grad_wkey = matmul_left(normed, grad_key) + matmul_left(global_in, grad_global_key)
    grad_wvalue = matmul_left(normed, grad_value) + matmul_left(global_in, grad_global_value)
    grad_normed = (
        matmul_right(grad_query, attn_back[2])
        + matmul_right(grad_key, attn_back[3])
        + matmul_right(grad_value, attn_back[4])
    )
    grad_global_in = matmul_right(grad_global_key, attn_back[3]) + matmul_right(
        grad_global_value, attn_back[4]
    )
    grad_summed, grad_global_gain = global_pull(grad_global_in)
    grad_normed = (grad_normed.reshape(local_globals, GBLK, D) + grad_summed[:, None, :]).reshape(
        row_count, D
    )
    grad_tokens_norm, grad_norm_gain = normed_pull(grad_normed)
    grad_tokens = grad_middle + grad_tokens_norm
    every_grad = (
        lax.psum_scatter(grad_norm_gain, ("seq", "blk"), scatter_dimension=0, tiled=True),
        lax.psum_scatter(grad_global_gain, ("seq", "blk"), scatter_dimension=0, tiled=True),
        lax.psum_scatter(grad_wquery, ("seq", "blk"), scatter_dimension=0, tiled=True),
        lax.psum_scatter(grad_wkey, ("seq", "blk"), scatter_dimension=0, tiled=True),
        lax.psum_scatter(grad_wvalue, ("seq", "blk"), scatter_dimension=0, tiled=True),
        lax.psum_scatter(grad_wout, ("seq", "blk"), scatter_dimension=0, tiled=True),
        lax.psum_scatter(grad_ffn_gain, ("seq", "blk"), scatter_dimension=0, tiled=True),
        lax.psum_scatter(grad_wgate, ("seq", "blk"), scatter_dimension=0, tiled=True),
        lax.psum_scatter(grad_wup, ("seq", "blk"), scatter_dimension=0, tiled=True),
        lax.psum_scatter(grad_down, ("seq", "blk"), scatter_dimension=0, tiled=True),
    )
    return (
        output,
        grad_tokens,
        every_grad[0],
        every_grad[1],
        every_grad[2],
        every_grad[3],
        every_grad[4],
        every_grad[5],
        every_grad[6],
        every_grad[7],
        every_grad[8],
        every_grad[9],
    )


MESH = pl.DeviceIdType.MESH
CHIPS_Z = 4
NEVER = 1 << 20
VMEM_BYTES = 64 * 1024 * 1024 - 65536


def dot(a, b, dims, precision=None):
    return lax.dot_general(
        a, b, (dims, ((), ())), precision=precision, preferred_element_type=jnp.float32
    )


def dot_nn(a, b):
    return dot(a, b, ((1,), (0,)))


def dot_nt(a, b):
    return dot(a, b, ((1,), (1,)))


def coords():
    y = lax.axis_index("seq")
    blk = lax.axis_index("blk")
    return y, blk // 4, (blk // 2) % 2, blk % 2


def device(y, z, x, c):
    return (y, z * 4 + x * 2 + c)


def send(src, dst, send_sem, recv_sem, target):
    pltpu.make_async_remote_copy(
        src_ref=src,
        dst_ref=dst,
        send_sem=send_sem,
        recv_sem=recv_sem,
        device_id=target,
        device_id_type=MESH,
    ).start()


def wait_bytes(ref, sem):
    pltpu.make_async_copy(ref, ref, sem).wait()


def column_peers():
    y, z, x, c = coords()
    peers = [device(y, z, x, 1 - c)]
    for k in range(1, CHIPS_Z):
        peers += [device(y, (z + k) % CHIPS_Z, x, j) for j in range(2)]
    return peers


def side_peers():
    y, z, x, c = coords()
    return [device(y, z, 1 - x, c), device(1 - y, z, x, c), device(1 - y, z, 1 - x, c)]


def greet():
    y, z, x, c = coords()
    blk = lax.axis_index("blk")
    barrier = pltpu.get_barrier_semaphore()
    peers = column_peers() + side_peers()
    for peer in peers:
        pl.semaphore_signal(barrier, inc=1, device_id=peer, device_id_type=MESH)

    @pl.when(blk > 0)
    def _():
        pl.semaphore_signal(barrier, inc=1, device_id=(y, blk - 1), device_id_type=MESH)

    @pl.when(blk < 15)
    def _():
        pl.semaphore_signal(barrier, inc=1, device_id=(y, blk + 1), device_id_type=MESH)

    inner = jnp.where((blk > 0) & (blk < 15), 1, 0)
    pl.semaphore_wait(barrier, len(peers) + 1 + inner)


class Slots:
    def __init__(self, rows, half, first=None):
        self.rows, self.half = rows, half
        self.y, self.z, self.x, self.c = coords()
        self.side = self.c if first is None else first

    def plane(self, c):
        return pl.ds(pl.multiple_of(c * self.half, 128), self.half)

    def slot_rows(self, y, z, x):
        return pl.ds(pl.multiple_of((y * 8 + z * 2 + x) * (2 * self.rows), 8), 2 * self.rows)

    def near_pair(self, j):
        y, x, side = self.y, self.x, self.side
        return y * (1 - side) + j * side, x * side + j * (1 - side)

    def far_pair(self, j):
        y, x, side = self.y, self.x, self.side
        return (1 - y) * (1 - side) + j * side, (1 - x) * side + j * (1 - side)

    def near_slot(self):
        y, x, side = self.y, self.x, self.side
        return y * (1 - side) + (1 - y) * side, x * side + (1 - x) * (1 - side)

    def near_peer(self):
        slot_y, slot_x = self.near_slot()
        return device(slot_y, self.z, slot_x, self.c)

    def far_peer(self):
        y, z, x, c, side = self.y, self.z, self.x, self.c, self.side
        return device(y + (1 - side) * (1 - 2 * y), z, x + side * (1 - 2 * x), c)


class Gather(Slots):
    def __init__(self, shard, full, recv, sent, first=None):
        if isinstance(shard, tuple):
            super().__init__(*shard[0].shape, first)
        else:
            super().__init__(shard.shape[0], shard.shape[1] // 2, first)
        self.shard, self.full, self.recv, self.sent = shard, full, recv, sent

    def span(self, rows):
        return self.full.at[pl.ds(0, rows), pl.ds(0, self.half)]

    def mine(self):
        index = self.y * 16 + self.z * 4 + self.x * 2 + self.c
        return pl.ds(pl.multiple_of(index * self.rows, 8), self.rows)

    def slot(self, y, z, x):
        return self.full.at[self.slot_rows(y, z, x), self.plane(self.c)]

    def open(self, own, other, c):
        y, z, x = self.y, self.z, self.x
        target = self.full.at[self.mine(), self.plane(1 - c)]
        send(other, target, self.sent.at[0], self.recv.at[0], device(y, z, x, 1 - c))
        target = self.full.at[self.mine(), self.plane(c)]
        pltpu.make_async_copy(own, target, self.sent.at[2]).start()

    def own_here(self):
        wait_bytes(self.full.at[self.mine(), self.plane(self.c)], self.sent.at[2])

    def step(self, number):
        y, z, x, c, rows = self.y, self.z, self.x, self.c, self.rows
        if number == 0 and isinstance(self.shard, tuple):
            for core in range(2):
                own, other = self.shard[core], self.shard[1 - core]
                pl.when(c == core)(functools.partial(self.open, own, other, core))
        elif number == 0:
            self.open(self.shard.at[:, self.plane(c)], self.shard.at[:, self.plane(1 - c)], c)
        if number == 1:
            self.own_here()
            wait_bytes(self.span(rows), self.recv.at[0])
            block = self.slot(y, z, x)
            for k in range(1, CHIPS_Z):
                target = device(y, (z + k) % CHIPS_Z, x, c)
                send(block, block, self.sent.at[1], self.recv.at[1], target)
        if number == 2:
            wait_bytes(self.span(6 * rows), self.recv.at[1])
            for k in range(CHIPS_Z):
                block = self.slot(y, k, x)
                send(block, block, self.sent.at[1], self.recv.at[2], self.near_peer())
        if number == 3:
            wait_bytes(self.span(8 * rows), self.recv.at[2])
            for k in range(CHIPS_Z):
                for j in range(2):
                    slot_y, slot_x = self.near_pair(j)
                    block = self.slot(slot_y, k, slot_x)
                    send(block, block, self.sent.at[1], self.recv.at[3], self.far_peer())
        if number == 4:
            wait_bytes(self.span(16 * rows), self.recv.at[3])
            block = self.full.at[:, self.plane(c)]
            send(block, block, self.sent.at[1], self.recv.at[4], device(y, z, x, 1 - c))
        if number == 5:
            wait_bytes(self.span(32 * rows), self.recv.at[4])
        if number == 6:
            wait_bytes(self.span(rows), self.sent.at[0])
            wait_bytes(self.full.at[pl.ds(0, 31 * rows)], self.sent.at[1])


class GatherLate(Gather):
    def step(self, number):
        y, z, x, c, rows = self.y, self.z, self.x, self.c, self.rows
        if number == 1:
            self.own_here()
            wait_bytes(self.span(rows), self.recv.at[0])
            block = self.slot(y, z, x)
            send(block, block, self.sent.at[1], self.recv.at[1], self.near_peer())
        elif number == 2:
            wait_bytes(self.span(2 * rows), self.recv.at[1])
            for j in range(2):
                slot_y, slot_x = self.near_pair(j)
                block = self.slot(slot_y, z, slot_x)
                send(block, block, self.sent.at[1], self.recv.at[2], self.far_peer())
        elif number == 3:
            wait_bytes(self.span(4 * rows), self.recv.at[2])
            for k in range(1, CHIPS_Z):
                target = device(y, (z + k) % CHIPS_Z, x, c)
                for j in range(4):
                    block = self.slot(j // 2, z, j % 2)
                    send(block, block, self.sent.at[1], self.recv.at[3], target)
        elif number == 4:
            wait_bytes(self.span(24 * rows), self.recv.at[3])
            block = self.full.at[:, self.plane(c)]
            send(block, block, self.sent.at[1], self.recv.at[4], device(y, z, x, 1 - c))
        else:
            super().step(number)


class Reduce(Slots):
    def __init__(self, part, out, work, near, mid, far, last, pair, recv, sent, first=None):
        super().__init__(out.shape[0], out.shape[1] // 2, first)
        self.part, self.out, self.work = part, out, work
        self.near, self.mid, self.far, self.last, self.pair = near, mid, far, last, pair
        self.recv, self.sent = recv, sent

    def add(self, rows, ref, index):
        size = 2 * self.rows
        start = pl.ds(pl.multiple_of(index * size, 8), size)
        total = self.work[rows, :].astype(jnp.float32) + ref[start, :].astype(jnp.float32)
        self.work[rows, :] = total.astype(self.work.dtype)

    def start_sum(self):
        wait_bytes(self.work, self.recv.at[0])
        size = 2 * self.rows

        @pl.loop(0, 16)
        def _(index):
            span = pl.ds(pl.multiple_of(index * size, 8), size)
            total = self.work[span, :].astype(jnp.float32)
            total = total + self.part[span, self.plane(self.c)].astype(jnp.float32)
            self.work[span, :] = total.astype(self.work.dtype)

    def step(self, number):
        y, z, x, c, rows = self.y, self.z, self.x, self.c, self.rows
        size = 2 * rows
        if number == 0:
            send(
                self.part.at[:, self.plane(1 - c)],
                self.work,
                self.sent.at[0],
                self.recv.at[0],
                device(y, z, x, 1 - c),
            )
        if number == 1:
            self.start_sum()
            for k in range(CHIPS_Z):
                for j in range(2):
                    slot_y, slot_x = self.far_pair(j)
                    send(
                        self.work.at[self.slot_rows(slot_y, k, slot_x)],
                        self.near.at[pl.ds((k * 2 + j) * size, size)],
                        self.sent.at[1],
                        self.recv.at[1],
                        self.far_peer(),
                    )
        if number == 2:
            wait_bytes(self.near, self.recv.at[1])

            @pl.loop(0, 8)
            def _(index):
                k, j = index // 2, index % 2
                slot_y, slot_x = self.near_pair(j)
                self.add(self.slot_rows(slot_y, k, slot_x), self.near, index)

            for k in range(CHIPS_Z):
                slot_y, slot_x = self.near_slot()
                send(
                    self.work.at[self.slot_rows(slot_y, k, slot_x)],
                    self.mid.at[pl.ds(k * size, size)],
                    self.sent.at[1],
                    self.recv.at[2],
                    self.near_peer(),
                )
        if number == 3:
            wait_bytes(self.mid, self.recv.at[2])

            @pl.loop(0, CHIPS_Z)
            def _(k):
                self.add(self.slot_rows(y, k, x), self.mid, k)

            for k in range(1, CHIPS_Z):
                to_z = (z + k) % CHIPS_Z
                send(
                    self.work.at[self.slot_rows(y, to_z, x)],
                    self.far.at[pl.ds((k - 1) * size, size)],
                    self.sent.at[1],
                    self.recv.at[3],
                    device(y, to_z, x, c),
                )
        if number == 4:
            wait_bytes(self.far, self.recv.at[3])
            total = self.work[self.slot_rows(y, z, x), :].astype(jnp.float32)
            for k in range(self.far.shape[0] // size):
                total = total + self.far[pl.ds(k * size, size), :].astype(jnp.float32)
            self.last[...] = total
            keep = pl.ds(pl.multiple_of(c * rows, 8), rows)
            give = pl.ds(pl.multiple_of((1 - c) * rows, 8), rows)
            send(
                self.last.at[give],
                self.pair,
                self.sent.at[2],
                self.recv.at[4],
                device(y, z, x, 1 - c),
            )
            self.out[:, self.plane(c)] = self.last[keep, :]
        if number == 5:
            wait_bytes(self.pair, self.recv.at[4])
            self.out[:, self.plane(1 - c)] = self.pair[...]
        if number == 6:
            wait_bytes(self.work, self.sent.at[0])
            wait_bytes(self.work.at[pl.ds(0, 30 * rows)], self.sent.at[1])
            wait_bytes(self.pair, self.sent.at[2])


class ReduceEarly(Reduce):
    def step(self, number):
        y, z, x, c = self.y, self.z, self.x, self.c
        size = 2 * self.rows
        if number == 1:
            self.start_sum()
            for k in range(1, CHIPS_Z):
                to_z = (z + k) % CHIPS_Z
                for j in range(4):
                    send(
                        self.work.at[self.slot_rows(j // 2, to_z, j % 2)],
                        self.near.at[pl.ds((4 * (k - 1) + j) * size, size)],
                        self.sent.at[1],
                        self.recv.at[1],
                        device(y, to_z, x, c),
                    )
        elif number == 2:
            wait_bytes(self.near, self.recv.at[1])

            @pl.loop(0, 12)
            def _(index):
                j = index % 4
                self.add(self.slot_rows(j // 2, z, j % 2), self.near, index)

            for j in range(2):
                slot_y, slot_x = self.far_pair(j)
                send(
                    self.work.at[self.slot_rows(slot_y, z, slot_x)],
                    self.mid.at[pl.ds(j * size, size)],
                    self.sent.at[1],
                    self.recv.at[2],
                    self.far_peer(),
                )
        elif number == 3:
            wait_bytes(self.mid, self.recv.at[2])
            for j in range(2):
                slot_y, slot_x = self.near_pair(j)
                self.add(self.slot_rows(slot_y, z, slot_x), self.mid, j)
            slot_y, slot_x = self.near_slot()
            send(
                self.work.at[self.slot_rows(slot_y, z, slot_x)],
                self.far,
                self.sent.at[1],
                self.recv.at[3],
                self.near_peer(),
            )
        else:
            super().step(number)


def reduce_scratch(rows, half, dtype, counts=(16, 8, 6)):
    return [
        pltpu.VMEM((32 * rows, half), dtype),
        pltpu.VMEM((counts[0] * rows, half), dtype),
        pltpu.VMEM((counts[1] * rows, half), dtype),
        pltpu.VMEM((counts[2] * rows, half), dtype),
        pltpu.VMEM((2 * rows, half), jnp.float32),
        pltpu.VMEM((rows, half), jnp.float32),
    ]


def seq_bounds(lengths, position):
    low = jnp.zeros((1, 128), jnp.int32)
    high = jnp.full((1, 128), NEVER, jnp.int32)
    end = low
    for i in range(lengths.shape[0]):
        end = end + lengths[i : i + 1, :]
        low = jnp.maximum(low, jnp.where(end <= position, end, 0))
        high = jnp.minimum(high, jnp.where(end > position, end, NEVER))
    return low, high


class Span:
    fields = ("start", "far_low", "far_high", "no_before", "no_after", "second")

    def __init__(self, rows):
        for i, name in enumerate(self.fields):
            setattr(self, name, rows[i : i + 1, :])


def span_rows(lengths, first_row, block, far_rows, global_count):
    position = first_row + block * BLOCK
    low, high = seq_bounds(lengths, position)
    first_low, _ = seq_bounds(lengths, first_row)
    start = jnp.minimum(low >> 4, global_count - far_rows)
    rows = [
        start,
        (low >> 4) - start,
        (high >> 4) - start,
        jnp.where(position > low, 0, NEVER),
        jnp.where(position + BLOCK < high, 0, NEVER),
        jnp.where(low == first_low, 0, 1),
    ]
    return jnp.concatenate(rows + [start, start], axis=0)


def window_select(spans, window, blocks, far_rows, global_count):
    start = Span(spans[pl.ds(8 * window * (blocks - 1), 8), :]).start
    row = lax.broadcasted_iota(jnp.int32, (far_rows, global_count), 0)
    column = lax.broadcasted_iota(jnp.int32, (far_rows, global_count), 1)
    return (column - widen(start, global_count) == row).astype(jnp.bfloat16)


def far_part(ref, lanes, span, near_rows, far_rows):
    first = ref[pl.ds(near_rows, far_rows), lanes]
    second = ref[pl.ds(near_rows + far_rows, far_rows), lanes]
    return jnp.where(span.second > 0, second, first)


def widen(row, width):
    return jnp.concatenate([row] * (width // 128), axis=1)


def head_pair(rows):
    lane = lax.broadcasted_iota(jnp.int32, rows.shape, 1)
    zero = jnp.zeros_like(rows)
    return jnp.concatenate(
        [jnp.where(lane < HEAD_DIM, rows, zero), jnp.where(lane < HEAD_DIM, zero, rows)], axis=0
    )


def attend_block(pair, block, span, query, keys, values, attended, near_rows, far_rows):
    lanes = pl.ds(pl.multiple_of(pair * 128, 128), 128)
    rows = pl.ds(pl.multiple_of(block * BLOCK, BLOCK), BLOCK)
    near = pl.ds(pl.multiple_of(block * BLOCK, BLOCK), 3 * BLOCK)
    both = head_pair(query[rows, lanes])
    near_scores = dot_nt(both, keys[near, lanes])
    far_scores = dot_nt(both, far_part(keys, lanes, span, near_rows, far_rows))
    row = lax.broadcasted_iota(jnp.int32, (2 * BLOCK, BLOCK), 0) % BLOCK
    column = lax.broadcasted_iota(jnp.int32, (2 * BLOCK, BLOCK), 1)
    edge = jnp.where(
        column > row + span.no_before,
        near_scores[:, :BLOCK],
        jnp.where(column < row - span.no_after, near_scores[:, 2 * BLOCK :], MASKED),
    )
    own = near_scores[:, BLOCK : 2 * BLOCK]
    far_column = lax.broadcasted_iota(jnp.int32, far_scores.shape, 1)
    far_scores = jnp.where(
        (far_column >= widen(span.far_low, far_rows))
        & (far_column < widen(span.far_high, far_rows)),
        far_scores,
        MASKED,
    )
    highest = jnp.maximum(
        jnp.max(jnp.maximum(edge, own), axis=1, keepdims=True),
        jnp.max(far_scores, axis=1, keepdims=True),
    )
    edge_exp = jnp.exp(edge - highest)
    own_exp = jnp.exp(own - highest)
    far_exp = jnp.exp(far_scores - highest)
    inverse = 1.0 / (
        jnp.sum(edge_exp + own_exp, axis=1, keepdims=True) + jnp.sum(far_exp, axis=1, keepdims=True)
    )
    edge_probs = edge_exp * inverse
    near_probs = jnp.concatenate(
        [
            jnp.where(column > row, edge_probs, 0.0).astype(jnp.bfloat16),
            (own_exp * inverse).astype(jnp.bfloat16),
            jnp.where(column < row, edge_probs, 0.0).astype(jnp.bfloat16),
        ],
        axis=1,
    )
    far_probs = (far_exp * inverse).astype(jnp.bfloat16)
    mixed = dot_nn(near_probs, values[near, lanes]) + dot_nn(
        far_probs, far_part(values, lanes, span, near_rows, far_rows)
    )
    lane = lax.broadcasted_iota(jnp.int32, (BLOCK, 128), 1)
    attended[rows, lanes] = jnp.where(lane < HEAD_DIM, mixed[:BLOCK], mixed[BLOCK:]).astype(
        jnp.bfloat16
    )


def attend_block_back(
    pair, block, span, query, grad, keys, keys_t, values, grad_query, grad_keys, grad_values,
    near_rows, far_rows,
):
    lanes = pl.ds(pl.multiple_of(pair * 128, 128), 128)
    rows = pl.ds(pl.multiple_of(block * BLOCK, BLOCK), BLOCK)
    near = pl.ds(pl.multiple_of(block * BLOCK, BLOCK), 3 * BLOCK)
    both = head_pair(query[rows, lanes])
    grads = head_pair(grad[rows, lanes])
    near_scores = dot_nt(keys[near, lanes], both)
    far_keys = far_part(keys, lanes, span, near_rows, far_rows)
    far_scores = dot_nt(far_keys, both)
    row = lax.broadcasted_iota(jnp.int32, (BLOCK, 2 * BLOCK), 0)
    column = lax.broadcasted_iota(jnp.int32, (BLOCK, 2 * BLOCK), 1) % BLOCK
    edge = jnp.where(
        row > column + widen(span.no_before, 2 * BLOCK),
        near_scores[:BLOCK],
        jnp.where(row < column - widen(span.no_after, 2 * BLOCK), near_scores[2 * BLOCK :], MASKED),
    )
    own = near_scores[BLOCK : 2 * BLOCK]
    far_row = lax.broadcasted_iota(jnp.int32, far_scores.shape, 0)
    far_scores = jnp.where(
        (far_row >= widen(span.far_low, 2 * BLOCK)) & (far_row < widen(span.far_high, 2 * BLOCK)),
        far_scores,
        MASKED,
    )
    highest = jnp.maximum(
        jnp.max(jnp.maximum(edge, own), axis=0, keepdims=True),
        jnp.max(far_scores, axis=0, keepdims=True),
    )
    edge_exp = jnp.exp(edge - highest)
    own_exp = jnp.exp(own - highest)
    far_exp = jnp.exp(far_scores - highest)
    inverse = 1.0 / (
        jnp.sum(edge_exp + own_exp, axis=0, keepdims=True) + jnp.sum(far_exp, axis=0, keepdims=True)
    )
    edge_probs, own_probs, far_probs = edge_exp * inverse, own_exp * inverse, far_exp * inverse
    near_dprobs = dot_nt(values[near, lanes], grads)
    far_dprobs = dot_nt(far_part(values, lanes, span, near_rows, far_rows), grads)
    edge_dprobs = jnp.where(row > column, near_dprobs[:BLOCK], near_dprobs[2 * BLOCK :])
    own_dprobs = near_dprobs[BLOCK : 2 * BLOCK]
    delta = jnp.sum(
        edge_probs * edge_dprobs + own_probs * own_dprobs, axis=0, keepdims=True
    ) + jnp.sum(far_probs * far_dprobs, axis=0, keepdims=True)
    edge_ds = edge_probs * (edge_dprobs - delta)
    own_ds = (own_probs * (own_dprobs - delta)).astype(jnp.bfloat16)
    far_ds = (far_probs * (far_dprobs - delta)).astype(jnp.bfloat16)

    def spread(edge_part, own_part):
        return jnp.concatenate(
            [
                jnp.where(row > column, edge_part, 0.0).astype(jnp.bfloat16),
                own_part.astype(jnp.bfloat16),
                jnp.where(row < column, edge_part, 0.0).astype(jnp.bfloat16),
            ],
            axis=0,
        )

    near_ds = spread(edge_ds, own_ds)
    far_keys_t = jnp.where(
        widen(span.second, far_rows) > 0,
        keys_t[lanes, pl.ds(near_rows + far_rows, far_rows)],
        keys_t[lanes, pl.ds(near_rows, far_rows)],
    )
    query_t = dot_nn(keys_t[lanes, near], near_ds) + dot_nn(far_keys_t, far_ds)
    feature = lax.broadcasted_iota(jnp.int32, (128, BLOCK), 0)
    query_t = jnp.where(feature < HEAD_DIM, query_t[:, :BLOCK], query_t[:, BLOCK:])
    grad_query[rows, lanes] = query_t.T.astype(jnp.bfloat16)
    grad_keys[near, lanes] += dot_nn(near_ds, both)
    grad_values[near, lanes] += dot_nn(spread(edge_probs, own_probs), grads)
    far_dkey = dot_nn(far_ds, both)
    far_dvalue = dot_nn(far_probs.astype(jnp.bfloat16), grads)
    for window in range(2):
        place = pl.ds(near_rows + window * far_rows, far_rows)
        here = span.second == window
        grad_keys[place, lanes] += jnp.where(here, far_dkey, 0.0)
        grad_values[place, lanes] += jnp.where(here, far_dvalue, 0.0)


def inverse_rms(values):
    return lax.rsqrt(jnp.mean(values * values, axis=-1, keepdims=True) + EPSILON)


def rms_back(values, gain, grads):
    scale = inverse_rms(values)
    scaled = grads * gain
    back = scale * scaled - values * (
        scale * scale * scale * jnp.mean(scaled * values, axis=-1, keepdims=True)
    )
    return back, jnp.sum(grads * values * scale, axis=0, keepdims=True)


def block_sums(rows, count):
    take = lax.broadcasted_iota(jnp.int32, (count, rows.shape[0]), 1) // GBLK
    which = lax.broadcasted_iota(jnp.int32, (count, rows.shape[0]), 0)
    return dot_nn((take == which).astype(jnp.bfloat16), rows)


def owner_of(column, rows):
    return (column * ((65536 + rows - 1) // rows)) >> 16


def spread_gains(packed, rows):
    width = 32 * rows
    lane = lax.broadcasted_iota(jnp.int32, (128, width), 0)
    column = lax.broadcasted_iota(jnp.int32, (128, width), 1)
    select = (column - rows * owner_of(column, rows) == lane).astype(jnp.float32)
    wide = dot(packed, select, ((1,), (0,)), precision=lax.Precision.HIGHEST)
    device_row = lax.broadcasted_iota(jnp.int32, wide.shape, 0) >> 3
    wide_column = lax.broadcasted_iota(jnp.int32, wide.shape, 1)
    wide = jnp.where(owner_of(wide_column, rows) == device_row, wide, 0.0)
    return jnp.sum(wide.reshape(32, 8, width), axis=0)


def pack_gains(wide, rows):
    width = 32 * rows
    tall = jnp.concatenate([wide] * 32, axis=0)
    device_row = lax.broadcasted_iota(jnp.int32, tall.shape, 0) >> 3
    column = lax.broadcasted_iota(jnp.int32, tall.shape, 1)
    tall = jnp.where(owner_of(column, rows) == device_row, tall, 0.0)
    lane = lax.broadcasted_iota(jnp.int32, (width, 128), 1)
    from_column = lax.broadcasted_iota(jnp.int32, (width, 128), 0)
    select = (from_column - rows * owner_of(from_column, rows) == lane).astype(jnp.float32)
    return dot(tall, select, ((1,), (0,)), precision=lax.Precision.HIGHEST)


CHUNKS = 4
TILE = 256
SMALL_SEMS = 24
NAMES = ("g", "h", "i", "k", "v", "q", "o", "d", "f0", "f1", "f2", "f3")
NAMES += ("r0", "r1", "r2", "r3", "rd", "ro", "ra", "rb", "rc", "w", "j", "l")
Z_LAST = ("f3", "o")
Z_FIRST = ("r0", "r1")
FIRST = {}
SCHEDULE = {
    "s0": {
        0: (0, 10, 30, 40, 50, 60, 70, 80, 90, 100, 110),
    },
    "s0b": {
        0: (61, 111, 31, 41, 20, 51),
    },
    "s1": {
        0: (1, 11, 62, 2),
    },
    "s2": {
        0: (112, 32),
    },
    "s4": {
        0: (42, 33, 43, 21, 71, 81, 34, 52, 44, 53, 22, 72, 91, 23),
    },
    "s5": {
        0: (35,),
    },
    "kn": {
        2: (54, 82, 101, 63, 113),
    },
    "kt": {
        4: (73,),
    },
    "s6": {
        0: (45,),
    },
    "vn": {
        2: (92,),
        4: (83,),
    },
    "s7": {
        0: (55,),
    },
    "fa": {
        2: (102,),
        4: (93,),
        8: (103,),
        11: (74,),
    },
    "m0": {
        0: (64, 84, 65),
    },
    "m1": {
        0: (75,),
    },
    "ca": {
        0: (85,),
        1: (104, 95),
        2: (105,),
        3: (115,),
    },
    "cb": {
        0: (94,),
    },
    "cw": {
        0: (120,),
        1: (130,),
        2: (140,),
        3: (150,),
    },
    "cg": {
        3: (121,),
        6: (114, 131),
        9: (141,),
    },
    "sp": {
        0: (160,),
    },
    "m2": {
        0: (151,),
    },
    "m3": {
        0: (142, 161, 170),
    },
    "ba": {
        1: (122, 171),
        2: (143,),
        3: (152,),
        6: (153, 181),
        7: (162, 123),
        9: (144, 172, 191),
        11: (154, 163, 182, 124),
    },
    "bt": {
        0: (180,),
        1: (190,),
        2: (200,),
    },
    "wg": {
        3: (132,),
        6: (133,),
        8: (173,),
    },
    "e1": {
        0: (220,),
    },
    "e2": {
        0: (210, 183),
    },
    "gg": {
        1: (221, 134, 192, 201),
    },
    "e6": {
        0: (164, 211, 174, 184, 222, 193, 202, 223),
    },
    "e7": {
        0: (230, 203),
    },
    "e8": {
        0: (125, 135, 145, 155, 165, 175, 185, 194, 195, 231, 204, 232, 205),
    },
}


class Calls:
    def __init__(self, *actions):
        self.actions = actions

    def step(self, number):
        self.actions[number]()


def tiled(count, body, before=None):
    @pl.loop(0, count // TILE)
    def _(i):
        if before is not None:
            before(i)
        body(pl.ds(pl.multiple_of(i * TILE, TILE), TILE))


class GlobalSlots:
    def __init__(self, count):
        self.count = count

    def at(self, z, x, c):
        return self.packed(z * 4 + x * 2 + c)

    def packed(self, index):
        return pl.ds(pl.multiple_of(index * self.count, 16), self.count)


def layer_kernel(lengths, first_gain, second_gain, third_gain, tokens, cotangent, *refs):
    shards, refs = refs[:7], refs[7:]
    packed, refs = refs[-1], refs[:-1]
    output, grad_tokens, gain_out, refs = refs[0], refs[1], refs[2], refs[3:]
    grads_out, refs = refs[:9], refs[9:]
    w_query, w_key, w_value, w_out, w_down, w_ff = refs[:6]
    rows_in, rows_in_t, keys, keys_t, values, query, attended, hidden, turned = refs[6:15]
    mixed, grad_both, grad_keys, grad_values, gain_grads, part_key, part_value = refs[15:22]
    spans, gain_rows, gathered, gain_part, gain_side, gain_column, group_sums = refs[22:29]
    halo, global_rows, global_near, global_mid, global_far = refs[29:34]
    buffers, refs = refs[34:88], refs[88:]
    recv, sent, small = refs
    y, z, x, c = coords()
    blk = lax.axis_index("blk")
    me = blk + 16 * y
    row_count, width = tokens.shape
    blocks = row_count // BLOCK
    local_globals = row_count // GBLK
    global_count = global_rows.shape[0]
    near_rows = row_count + 2 * BLOCK
    all_rows = rows_in.shape[0]
    far_rows = (all_rows - near_rows) // 2
    feature_rows = width // 32
    hidden_rows = w_down.shape[0] // CHUNKS
    first_row = blk * row_count
    low = jnp.bfloat16
    slots = GlobalSlots(local_globals)
    column, sides = column_peers(), side_peers()

    part_query = rows_in.at[pl.ds(0, width)]
    steps = {}
    chunk_width = w_ff.shape[2]
    sources = [("q", shards[0], w_query), ("k", shards[1], w_key), ("v", shards[2], w_value)]
    sources += [("o", shards[3], w_out), ("d", shards[4], w_down)]
    for chunk in range(CHUNKS):
        part = pl.ds(chunk * chunk_width // 2, chunk_width // 2)
        pair = (shards[5].at[:, part], shards[6].at[:, part])
        sources.append((NAMES[8 + chunk], pair, w_ff.at[chunk]))
    for i, (name, shard, full) in enumerate(sources):
        kind = GatherLate if name in Z_LAST else Gather
        steps[name] = kind(shard, full, recv.at[i], sent.at[i], FIRST.get(name))
    ff_steps = [steps[name] for name in NAMES[8:12]]
    targets = [("ra", part_key), ("rb", part_value), ("rc", part_query), ("ro", w_out)]
    targets += [("rd", w_down)]
    targets += [(NAMES[12 + chunk], w_ff.at[chunk]) for chunk in range(CHUNKS)]
    for i, (name, part) in enumerate(targets):
        held = buffers[6 * i : 6 * i + 6]
        kind = ReduceEarly if name in Z_FIRST else Reduce
        steps[name] = kind(part, grads_out[i], *held, recv.at[9 + i], sent.at[9 + i], FIRST.get(name))

    def run(todo):
        for code in todo:
            steps[NAMES[code // 10]].step(code % 10)

    def tick(kind, number=0):
        run(SCHEDULE.get(kind, {}).get(number, ()))

    def loop_tick(kind, index, count):
        for number in range(count):
            todo = SCHEDULE.get(kind, {}).get(number, ())
            if todo:
                pl.when(index == number)(functools.partial(run, todo))

    def ticks(kind, count):
        return lambda index: loop_tick(kind, index, count)

    packed[...] = jnp.zeros_like(packed)
    for i, gain in enumerate((first_gain, second_gain, third_gain)):
        packed[i : i + 1, pl.ds(0, feature_rows)] = gain[...].astype(jnp.float32).reshape(
            1, feature_rows
        )
    greet()
    own_tile = gathered.at[pl.ds(pl.multiple_of(me * 8, 8), 8)]

    def share_gains():
        own_tile[...] = packed[...]
        for peer in column:
            send(packed, own_tile, small.at[1], small.at[0], peer)

    def spread_sides():
        wait_bytes(gathered.at[pl.ds(0, 56)], small.at[0])
        for k in range(CHIPS_Z):
            pair = gathered.at[pl.ds(pl.multiple_of((y * 8 + k * 2 + x) * 16, 16), 16)]
            for peer in sides:
                send(pair, pair, small.at[3], small.at[2], peer)

    def gains_here():
        wait_bytes(gathered.at[pl.ds(0, 192)], small.at[2])

    steps["g"] = Calls(share_gains, spread_sides, gains_here)

    def token_halo(side):
        source = pl.ds(row_count - BLOCK, BLOCK) if side == 0 else pl.ds(0, BLOCK)
        return pltpu.make_async_remote_copy(
            src_ref=tokens.at[source],
            dst_ref=halo.at[side],
            send_sem=small.at[8 + side],
            recv_sem=small.at[10 + side],
            device_id=(y, blk + 1 - 2 * side),
            device_id_type=MESH,
        )

    def start_halos():
        pl.when(blk < 15)(lambda: token_halo(0).start())
        pl.when(blk > 0)(lambda: token_halo(1).start())

    def end_halos():
        pl.when(blk > 0)(lambda: token_halo(0).wait_recv())
        pl.when(blk < 15)(lambda: token_halo(1).wait_recv())

    steps["h"] = Calls(start_halos, end_halos)

    def globals_z():
        block = global_rows.at[slots.at(z, x, c)]
        for k in range(1, CHIPS_Z):
            send(block, block, small.at[4], small.at[5], device(y, (z + k) % CHIPS_Z, x, c))

    def globals_x():
        wait_bytes(global_rows.at[pl.ds(0, 3 * local_globals)], small.at[5])
        for k in range(CHIPS_Z):
            block = global_rows.at[slots.at(k, x, c)]
            send(block, block, small.at[4], small.at[6], device(y, z, 1 - x, c))

    def globals_pair():
        wait_bytes(global_rows.at[pl.ds(0, 4 * local_globals)], small.at[6])
        for k in range(CHIPS_Z):
            for j in range(2):
                block = global_rows.at[slots.at(k, j, c)]
                send(block, block, small.at[4], small.at[7], device(y, z, x, 1 - c))

    def globals_here():
        wait_bytes(global_rows.at[pl.ds(0, 8 * local_globals)], small.at[7])

    steps["i"] = Calls(globals_z, globals_x, globals_pair, globals_here)
    tick("s0")

    def scale_own(place):
        wide = tokens[place, :].astype(jnp.float32)
        attended[place, :] = (wide * inverse_rms(wide)).astype(low)

    tiled(row_count, scale_own)
    global_rows[slots.packed(blk), :] = block_sums(attended[...], local_globals).astype(low)
    tick("s0b")
    wide_lengths = jnp.concatenate(
        [
            jnp.broadcast_to(lengths[0:1, i : i + 1], (1, 128))
            for i in range(lengths.shape[1])
        ],
        axis=0,
    )
    for block in range(blocks):
        spans[pl.ds(8 * block, 8), :] = span_rows(
            wide_lengths, first_row, block, far_rows, global_count
        )
    tick("s1")
    gain_rows[...] = spread_gains(gathered[...], feature_rows)
    tick("s2")
    norm_gain, global_gain, ffn_gain = gain_rows[0:1, :], gain_rows[1:2, :], gain_rows[2:3, :]

    def normed(part):
        wide = part.astype(jnp.float32)
        return (wide * inverse_rms(wide) * norm_gain).astype(low)

    def norm_own(place):
        to = pl.ds(pl.multiple_of(place.start + BLOCK, BLOCK), TILE)
        rows_in[to, :] = normed(tokens[place, :])

    tiled(row_count, norm_own)
    tick("s2b")
    group_sums[...] = block_sums(rows_in[pl.ds(BLOCK, row_count), :], local_globals)
    tick("s3")

    @pl.when(blk == 0)
    def _():
        halo[0] = jnp.zeros_like(halo[0])

    @pl.when(blk == 15)
    def _():
        halo[1] = jnp.zeros_like(halo[1])

    rows_in[pl.ds(0, BLOCK), :] = normed(halo[0])
    rows_in[pl.ds(BLOCK + row_count, BLOCK), :] = normed(halo[1])
    def turn(source, target, start):
        target[:, pl.ds(start, TILE)] = source[pl.ds(start, TILE), :].T

    for start in range(0, near_rows, TILE):
        tick("tr", start // TILE)
        turn(rows_in, rows_in_t, start)

    def project(weights, target, start, count, place, kind):
        def one(part):
            source = pl.ds(pl.multiple_of(part.start + start, BLOCK), TILE)
            to = pl.ds(pl.multiple_of(part.start + place, BLOCK), TILE)
            target[to, :] = dot_nn(rows_in[source, :], weights[...]).astype(low)

        tiled(count, one, ticks(kind, count // TILE))

    tick("s4")

    def global_norm(place):
        summed = global_rows[place, :].astype(jnp.float32) * norm_gain
        attended[place, :] = (summed * inverse_rms(summed) * global_gain).astype(low)

    tiled(global_count, global_norm)
    for window in range(2):
        select = window_select(spans, window, blocks, far_rows, global_count)
        rows_in[pl.ds(near_rows + window * far_rows, far_rows), :] = dot_nn(
            select, attended[...]
        ).astype(low)
    for start in range(near_rows, all_rows, TILE):
        tick("trf", (start - near_rows) // TILE)
        turn(rows_in, rows_in_t, start)
    tick("s5")
    project(w_key, keys, 0, all_rows, 0, "kn")
    for start in range(0, all_rows, TILE):
        tick("kt", start // TILE)
        turn(keys, keys_t, start)
    tick("s6")
    project(w_value, values, 0, all_rows, 0, "vn")
    tick("s7")
    project(w_query, query, BLOCK, row_count, 0, "qn")
    tick("s8")
    iterations = blocks * (HEADS // 2)

    def span_of(block):
        return Span(spans[pl.ds(pl.multiple_of(block * 8, 8), 8), :])

    @pl.loop(0, iterations // 2)
    def _(i):
        loop_tick("fa", i, iterations // 2)
        for j in range(2):
            block = (2 * i + j) % blocks
            attend_block(
                (2 * i) // blocks, block, span_of(block), query, keys, values, attended,
                near_rows, far_rows,
            )

    wait_bytes(global_rows.at[pl.ds(0, 15 * local_globals)], small.at[4])
    tick("m0")

    def after(place):
        return pl.ds(pl.multiple_of(place.start + row_count, TILE), TILE)

    def join(place):
        middle = tokens[place, :].astype(jnp.float32) + dot_nn(attended[place, :], w_out[...])
        grad_keys[place, :] = middle
        grad_keys[after(place), :] = middle
        low_hidden = (middle * inverse_rms(middle) * ffn_gain).astype(low)
        hidden[place, :] = low_hidden
        turned[:, place] = low_hidden.T
        grad_values[place, :] = jnp.zeros((TILE, width), jnp.float32)

    tiled(row_count, join, ticks("jn", 2))
    tick("m1")

    @pl.loop(0, CHUNKS)
    def _(chunk):
        loop_tick("ca", chunk, CHUNKS)
        half = chunk_width // 2
        rows = pl.ds(pl.multiple_of(chunk * hidden_rows, 128), hidden_rows)

        def feed(place):
            both = dot_nn(hidden[place, :], w_ff[chunk])
            gate, up = both[:, :half], both[:, half:]
            square = gate * gate
            bend = jnp.tanh(GELU_SCALE * gate * (1.0 + GELU_CUBIC * square))
            lift = 0.5 * (1.0 + bend)
            active = gate * lift
            slope = lift + 0.5 * gate * (1.0 - bend * bend) * (
                GELU_SCALE * (1.0 + 3.0 * GELU_CUBIC * square)
            )
            mixed[place, :] = (active * up).astype(low)
            grad_mixed = dot_nt(cotangent[place, :], w_down[rows, :])
            grad_both[place, pl.ds(0, half)] = (grad_mixed * up * slope).astype(low)
            grad_both[place, pl.ds(half, half)] = (grad_mixed * active).astype(low)
            grad_keys[after(place), :] += dot_nn(mixed[place, :], w_down[rows, :])
            grad_values[place, :] += dot_nt(grad_both[place, :], w_ff[chunk])

        tiled(row_count, feed, lambda i: pl.when(i == 1)(lambda: loop_tick("cb", chunk, CHUNKS)))
        for number in range(CHUNKS):
            pl.when(chunk == number)(functools.partial(ff_steps[number].step, 6))

        def gate_up_grad(place):
            w_ff[chunk, place, :] = dot_nn(turned[place, :], grad_both[...]).astype(low)

        tiled(width, gate_up_grad, lambda i: loop_tick("cg", chunk * 3 + i, 3 * CHUNKS))
        loop_tick("cw", chunk, CHUNKS)
        pl.when(chunk == 0)(lambda: steps["d"].step(6))
        w_down[rows, :] = dot(mixed[...], cotangent[...], ((0,), (0,))).astype(low)

    gain_grads[...] = jnp.zeros_like(gain_grads)

    def split(place):
        output[place, :] = grad_keys[after(place), :].astype(low)
        back, gain_grad = rms_back(grad_keys[place, :], ffn_gain, grad_values[place, :])
        gain_grads[2:3, :] += gain_grad
        grad_middle = cotangent[place, :].astype(jnp.float32) + back
        grad_tokens[place, :] = grad_middle
        branch = grad_middle.astype(low)
        rows_in[place, :] = branch
        hidden[place, :] = dot_nt(branch, w_out[...]).astype(low)
        turned[:, place] = attended[place, :].T

    tiled(row_count, split, ticks("sp", 2))
    tick("m2")
    steps["o"].step(6)

    def out_grad(place):
        w_out[place, :] = dot_nn(turned[place, :], rows_in[pl.ds(0, row_count), :]).astype(low)

    tiled(width, out_grad)
    tick("m3")

    def clear(place):
        grad_keys[place, :] = jnp.zeros((TILE, width), jnp.float32)
        grad_values[place, :] = jnp.zeros((TILE, width), jnp.float32)

    tiled(all_rows, clear)
    part_width = width // 3
    part_rounds = iterations // 6

    def back_part(third, target):
        @pl.loop(0, part_rounds)
        def _(j):
            i = third * part_rounds + j
            for number in range(part_rounds):
                todo = SCHEDULE.get("ba", {}).get(third * part_rounds + number, ())
                if todo:
                    pl.when(j == number)(functools.partial(run, todo))
            for k in range(2):
                block = (2 * i + k) % blocks
                attend_block_back(
                    (2 * i) // blocks, block, span_of(block), query, hidden, keys, keys_t, values,
                    query, grad_keys, grad_values, near_rows, far_rows,
                )

        lanes = pl.ds(third * part_width, part_width)

        def lower(place):
            keys[place, lanes] = grad_keys[place, lanes].astype(low)
            values[place, lanes] = grad_values[place, lanes].astype(low)

        tiled(all_rows, lower)

        def weight_grad(place):
            own = rows_in_t[place, pl.ds(BLOCK, row_count)]
            target[place, pl.ds(0, part_width)] = dot_nn(own, query[:, lanes]).astype(low)
            every = rows_in_t[place, :]
            target[place, pl.ds(part_width, part_width)] = dot_nn(every, keys[:, lanes]).astype(low)
            target[place, pl.ds(2 * part_width, part_width)] = dot_nn(
                every, values[:, lanes]
            ).astype(low)

        tiled(width, weight_grad, functools.partial(tick_part, third))
        tick("bt", third)

    def tick_part(third, index):
        for number in range(3):
            todo = SCHEDULE.get("wg", {}).get(3 * third + number, ())
            if todo:
                pl.when(index == number)(functools.partial(run, todo))

    for third, target in enumerate((part_key, part_value, part_query)):
        back_part(third, target)
    tick("e0")

    def grad_rows(start, count):
        part = pl.ds(start, count)
        return dot_nt(keys[part, :], w_key[...]) + dot_nt(values[part, :], w_value[...])

    for window in range(2):
        hidden[pl.ds(window * far_rows, far_rows), :] = grad_rows(
            near_rows + window * far_rows, far_rows
        ).astype(low)
    tick("e1b")
    selects = [window_select(spans, w, blocks, far_rows, global_count) for w in range(2)]
    for half in range(2):
        part = slice(half * (global_count // 2), (half + 1) * (global_count // 2))
        global_rows[part, :] = sum(
            dot(selects[w][:, part], hidden[pl.ds(w * far_rows, far_rows), :], ((0,), (0,)))
            for w in range(2)
        ).astype(low)

    def add_global(rows, ref, index):
        total = global_rows[rows, :].astype(jnp.float32)
        total = total + ref[slots.packed(index), :].astype(jnp.float32)
        global_rows[rows, :] = total.astype(low)

    def sums_pair():
        for k in range(CHIPS_Z):
            for j in range(2):
                send(
                    global_rows.at[slots.at(k, j, 1 - c)],
                    global_near.at[slots.packed(k * 2 + j)],
                    small.at[16],
                    small.at[17],
                    device(y, z, x, 1 - c),
                )

    def sums_x():
        wait_bytes(global_near, small.at[17])
        for k in range(CHIPS_Z):
            for j in range(2):
                add_global(slots.at(k, j, c), global_near, k * 2 + j)
        for k in range(CHIPS_Z):
            send(
                global_rows.at[slots.at(k, 1 - x, c)],
                global_mid.at[slots.packed(k)],
                small.at[16],
                small.at[18],
                device(y, z, 1 - x, c),
            )

    def sums_z():
        wait_bytes(global_mid, small.at[18])
        for k in range(CHIPS_Z):
            add_global(slots.at(k, x, c), global_mid, k)
        for k in range(1, CHIPS_Z):
            to_z = (z + k) % CHIPS_Z
            send(
                global_rows.at[slots.at(to_z, x, c)],
                global_far.at[slots.packed(k - 1)],
                small.at[16],
                small.at[19],
                device(y, to_z, x, c),
            )

    def sums_here():
        wait_bytes(global_far, small.at[19])

    steps["j"] = Calls(sums_pair, sums_x, sums_z, sums_here)
    tick("e1")
    halo[4] = grad_rows(0, BLOCK).astype(low)
    halo[5] = grad_rows(BLOCK + row_count, BLOCK).astype(low)
    def grad_halo(side):
        return pltpu.make_async_remote_copy(
            src_ref=halo.at[4 + side],
            dst_ref=halo.at[3 - side],
            send_sem=small.at[20 + side],
            recv_sem=small.at[22 + side],
            device_id=(y, blk - 1 + 2 * side),
            device_id_type=MESH,
        )

    def start_grad_halos():
        pl.when(blk > 0)(lambda: grad_halo(0).start())
        pl.when(blk < 15)(lambda: grad_halo(1).start())

    def end_grad_halos():
        pl.when(blk > 0)(lambda: grad_halo(1).wait_recv())
        pl.when(blk < 15)(lambda: grad_halo(0).wait_recv())

    steps["w"] = Calls(start_grad_halos, end_grad_halos)
    tick("e2")
    def gather_grads(place):
        rows = pl.ds(pl.multiple_of(place.start + BLOCK, BLOCK), TILE)
        grad_keys[place, :] = (
            dot_nt(keys[rows, :], w_key[...])
            + dot_nt(values[rows, :], w_value[...])
            + dot_nt(query[place, :], w_query[...])
        )

    tiled(row_count, gather_grads, ticks("gg", 2))
    tick("e6")

    @pl.when(blk == 0)
    def _():
        halo[2] = jnp.zeros_like(halo[2])

    @pl.when(blk == 15)
    def _():
        halo[3] = jnp.zeros_like(halo[3])

    grad_keys[pl.ds(0, BLOCK), :] += halo[2].astype(jnp.float32)
    grad_keys[pl.ds(row_count - BLOCK, BLOCK), :] += halo[3].astype(jnp.float32)
    total = global_rows[slots.at(z, x, c), :].astype(jnp.float32)
    for k in range(CHIPS_Z - 1):
        total = total + global_far[slots.packed(k), :].astype(jnp.float32)
    grad_summed, grad_global_gain = rms_back(group_sums[...], global_gain, total)
    gain_grads[1:2, :] = grad_global_gain
    group_sums[...] = grad_summed

    def finish(place):
        few = TILE // GBLK
        sums = group_sums[pl.ds(pl.multiple_of(place.start // GBLK, 8), few), :]
        grad_normed = grad_keys[place, :] + jnp.broadcast_to(
            sums[:, None, :], (few, GBLK, width)
        ).reshape(TILE, width)
        back, gain_grad = rms_back(tokens[place, :].astype(jnp.float32), norm_gain, grad_normed)
        gain_grads[0:1, :] += gain_grad
        grad_tokens[place, :] += back

    tiled(row_count, finish, ticks("fi", 2))
    gain_part[...] = pack_gains(gain_grads[...], feature_rows)

    def gain_pair(pair_y, k, pair_x):
        return pl.ds(pl.multiple_of((pair_y * 8 + k * 2 + pair_x) * 16, 16), 16)

    def gains_sides():
        for index, peer in enumerate(sides):
            side_y = y if index == 0 else 1 - y
            side_x = x if index == 1 else 1 - x
            for k in range(CHIPS_Z):
                send(
                    gain_part.at[gain_pair(side_y, k, side_x)],
                    gain_side.at[index, pl.ds(k * 16, 16)],
                    small.at[13],
                    small.at[12],
                    peer,
                )

    def gains_column():
        wait_bytes(gain_side, small.at[12])
        for k in range(CHIPS_Z):
            rows = gain_pair(y, k, x)
            place = pl.ds(k * 16, 16)
            gain_part[rows, :] += gain_side[0, place, :] + gain_side[1, place, :] + gain_side[2, place, :]
        place = z * 2 + c
        gain_column[pl.ds(pl.multiple_of(place * 8, 8), 8), :] = gain_part[
            pl.ds(pl.multiple_of(me * 8, 8), 8), :
        ]
        for k in range(CHIPS_Z):
            for j in range(2):
                if k == 0 and j == 0:
                    peer_z, peer_c = z, 1 - c
                elif k == 0:
                    continue
                else:
                    peer_z, peer_c = (z + k) % CHIPS_Z, j
                peer_me = y * 16 + peer_z * 4 + x * 2 + peer_c
                send(
                    gain_part.at[pl.ds(pl.multiple_of(peer_me * 8, 8), 8)],
                    gain_column.at[pl.ds(pl.multiple_of(place * 8, 8), 8)],
                    small.at[15],
                    small.at[14],
                    device(y, peer_z, x, peer_c),
                )

    def gains_done():
        wait_bytes(gain_column.at[pl.ds(0, 56)], small.at[14])

    steps["l"] = Calls(gains_sides, gains_column, gains_done)
    tick("e7")
    tick("e8")
    gain_out[...] = jnp.sum(gain_column[...].reshape(8, 8, 128), axis=0)
    for name, _ in targets:
        steps[name].step(6)
    for one in [steps["q"], steps["k"], steps["v"]]:
        one.step(6)
    wait_bytes(gathered.at[pl.ds(0, 56)], small.at[1])
    wait_bytes(gathered.at[pl.ds(0, 192)], small.at[3])
    wait_bytes(global_rows.at[pl.ds(0, 15 * local_globals)], small.at[16])
    wait_bytes(gathered.at[pl.ds(0, 192)], small.at[13])
    wait_bytes(gathered.at[pl.ds(0, 56)], small.at[15])
    pl.when(blk < 15)(lambda: token_halo(0).wait_send())
    pl.when(blk > 0)(lambda: token_halo(1).wait_send())
    pl.when(blk > 0)(lambda: grad_halo(0).wait_send())
    pl.when(blk < 15)(lambda: grad_halo(1).wait_send())


def layer(lengths, gains, tokens, cotangent, shards, far_rows, global_count):
    row_count, width = tokens.shape
    all_rows = row_count + 2 * BLOCK + 2 * far_rows
    local_globals = row_count // GBLK
    down_rows = shards[4].shape[0]
    chunk_width = 2 * shards[5].shape[1] // CHUNKS
    vmem = pl.BlockSpec(memory_space=pltpu.VMEM)
    anywhere = pl.BlockSpec(memory_space=pl.ANY)
    low, wide = jnp.bfloat16, jnp.float32
    shard_shapes = [(width // 32, width)] * 4 + [(down_rows, width)]
    shard_shapes += [(width // 32, chunk_width)] * CHUNKS
    buffers = []
    names = ("ra", "rb", "rc", "ro", "rd") + NAMES[12:16]
    for name, (rows, columns) in zip(names, shard_shapes):
        counts = (24, 4, 2) if name in Z_FIRST else (16, 8, 6)
        buffers += reduce_scratch(rows, columns // 2, low, counts)
    return pl.pallas_call(
        layer_kernel,
        out_shape=[
            jax.ShapeDtypeStruct((row_count, width), low),
            jax.ShapeDtypeStruct((row_count, width), wide),
            jax.ShapeDtypeStruct((8, 128), wide),
        ]
        + [jax.ShapeDtypeStruct(shape, wide) for shape in shard_shapes],
        in_specs=[vmem] * 6 + [anywhere] * 7,
        out_specs=[vmem] * 12,
        scratch_shapes=[pltpu.VMEM((width, width), low)] * 4
        + [
            pltpu.VMEM((32 * down_rows, width), low),
            pltpu.VMEM((CHUNKS, width, chunk_width), low),
            pltpu.VMEM((all_rows, width), low),
            pltpu.VMEM((width, all_rows), low),
            pltpu.VMEM((all_rows, width), low),
            pltpu.VMEM((width, all_rows), low),
            pltpu.VMEM((all_rows, width), low),
            pltpu.VMEM((row_count, width), low),
            pltpu.VMEM((row_count, width), low),
            pltpu.VMEM((row_count, width), low),
            pltpu.VMEM((width, row_count), low),
            pltpu.VMEM((row_count, chunk_width // 2), low),
            pltpu.VMEM((row_count, chunk_width), low),
            pltpu.VMEM((all_rows, width), wide),
            pltpu.VMEM((all_rows, width), wide),
            pltpu.VMEM((8, width), wide),
            pltpu.VMEM((width, width), low),
            pltpu.VMEM((width, width), low),
            pltpu.VMEM((8 * row_count // BLOCK, 128), jnp.int32),
            pltpu.VMEM((8, width), wide),
            pltpu.VMEM((256, 128), wide),
            pltpu.VMEM((256, 128), wide),
            pltpu.VMEM((3, 64, 128), wide),
            pltpu.VMEM((64, 128), wide),
            pltpu.VMEM((local_globals, width), wide),
            pltpu.VMEM((6, BLOCK, width), low),
            pltpu.VMEM((global_count, width), low),
            pltpu.VMEM((8 * local_globals, width), low),
            pltpu.VMEM((4 * local_globals, width), low),
            pltpu.VMEM((3 * local_globals, width), low),
        ]
        + buffers
        + [
            pltpu.SemaphoreType.DMA((18, 5)),
            pltpu.SemaphoreType.DMA((18, 3)),
            pltpu.SemaphoreType.DMA((SMALL_SEMS,)),
            pltpu.VMEM((8, 128), wide),
        ],
        compiler_params=pltpu.CompilerParams(
            collective_id=0, has_side_effects=True, vmem_limit_bytes=VMEM_BYTES
        ),
        name="layer",
    )(lengths, *gains, tokens, cotangent, *shards)


def settle_kernel(*refs):
    ins, outs = refs[:12], refs[12:]
    outs[0][...] = ins[0][...]
    outs[1][...] = ins[1][...]
    rows = outs[2].shape[0]
    for i in range(3):
        outs[2 + i][...] = ins[2][i, pl.ds(0, rows)]
    thirds, chunks = ins[3:6], ins[8:12]
    part = thirds[0].shape[1] // 3
    for i in range(3):
        for third, ref in enumerate(thirds):
            outs[5 + i][:, pl.ds(third * part, part)] = ref[:, pl.ds(i * part, part)]
    outs[8][...] = ins[6][...]
    outs[9][...] = ins[7][...]
    half = chunks[0].shape[1] // 2
    for i in range(2):
        for chunk, ref in enumerate(chunks):
            outs[10 + i][:, pl.ds(chunk * half, half)] = ref[:, pl.ds(i * half, half)]


def settle(outs, rows):
    vmem = pl.BlockSpec(memory_space=pltpu.VMEM)
    wide = jnp.float32
    width = outs[0].shape[1]
    ff_width = outs[8].shape[1] // 2 * CHUNKS
    return pl.pallas_call(
        settle_kernel,
        out_shape=[jax.ShapeDtypeStruct(one.shape, one.dtype) for one in outs[:2]]
        + [jax.ShapeDtypeStruct((rows,), wide)] * 3
        + [jax.ShapeDtypeStruct((rows, width), wide)] * 4
        + [jax.ShapeDtypeStruct(outs[7].shape, wide)]
        + [jax.ShapeDtypeStruct((rows, ff_width), wide)] * 2,
        in_specs=[vmem] * 12,
        out_specs=[vmem] * 12,
        name="settle",
    )(*outs)


def per_device(
    tokens, lengths, norm_gain, global_gain, w_query, w_key, w_value, w_out,
    ffn_gain, w_gate, w_up, w_down, cotangent,
):
    global_count = tokens.shape[0] * lax.axis_size("blk") // GBLK
    gains = (norm_gain, global_gain, ffn_gain)
    shards = (w_query, w_key, w_value, w_out, w_down, w_gate, w_up)
    outs = layer(lengths, gains, tokens, cotangent, shards, global_count // 2, global_count)
    settled = settle(outs, norm_gain.shape[0])
    output, grad_tokens, first, second, third = settled[:5]
    return (output, grad_tokens, first, second, *settled[5:9], third, *settled[10:], settled[9])


def fits(mesh):
    return mesh.shape["seq"] == 2 and mesh.shape["blk"] == 16


def solution(mesh):
    return jax.shard_map(
        per_device if fits(mesh) else per_device_general,
        mesh=mesh,
        in_specs=(
            P(("seq", "blk"), None),
            P("seq", None),
            P(("seq", "blk")),
            P(("seq", "blk")),
            P(("seq", "blk"), None),
            P(("seq", "blk"), None),
            P(("seq", "blk"), None),
            P(("seq", "blk"), None),
            P(("seq", "blk")),
            P(("seq", "blk"), None),
            P(("seq", "blk"), None),
            P(("seq", "blk"), None),
            P(("seq", "blk"), None),
        ),
        out_specs=(
            P(("seq", "blk"), None),
            P(("seq", "blk"), None),
            P(("seq", "blk")),
            P(("seq", "blk")),
            P(("seq", "blk"), None),
            P(("seq", "blk"), None),
            P(("seq", "blk"), None),
            P(("seq", "blk"), None),
            P(("seq", "blk")),
            P(("seq", "blk"), None),
            P(("seq", "blk"), None),
            P(("seq", "blk"), None),
        ),
        check_vma=False,
    )
```

```python
import functools

import jax
import jax.numpy as jnp
from jax import lax
from jax.experimental import pallas as pl
from jax.experimental.pallas import tpu as pltpu
from jax.sharding import PartitionSpec as P


D = 768
HEADS = 12
HEAD_DIM = 64
GBLK = 16
BLOCK = 128
LONGEST = 16384


EPSILON = 1e-06
MASKED = -1e30
GELU_SCALE = 0.7978845608028654
GELU_CUBIC = 0.044715


def with_halo(block, sides, width):
    for axis, dim in sides:
        count = lax.axis_size(axis)
        forward = [(i, i + 1) for i in range(count - 1)]
        backward = [(target, source) for source, target in forward]
        low = lax.ppermute(
            lax.slice_in_dim(block, block.shape[dim] - width, None, axis=dim), axis, forward
        )
        high = lax.ppermute(lax.slice_in_dim(block, 0, width, axis=dim), axis, backward)
        block = jnp.concatenate([low, block, high], axis=dim)
    return block


def rms_norm(values, scales):
    return values * lax.rsqrt(jnp.mean(values * values, axis=-1, keepdims=True) + EPSILON) * scales


def gelu_tanh(values):
    return (
        0.5
        * values
        * (1.0 + jnp.tanh(GELU_SCALE * (values + GELU_CUBIC * values * values * values)))
    )


def gated(gate_part, up_part):
    return gelu_tanh(gate_part) * up_part


def sequence_of(positions, seq_ends):
    return jnp.sum((positions[:, None] >= seq_ends[None, :]).astype(jnp.int32), axis=1)


def matmul(left_side, right_side):
    return jnp.dot(left_side, right_side, preferred_element_type=jnp.float32)


def matmul_left(left_side, right_side):
    return jnp.einsum("ta,tb->ab", left_side, right_side, preferred_element_type=jnp.float32)


def matmul_right(left_side, right_side):
    return jnp.einsum("ta,ba->tb", left_side, right_side, preferred_element_type=jnp.float32)


def windows(extended, row_count):
    block_count = row_count // BLOCK
    pieces = [
        extended[offset * BLOCK : offset * BLOCK + row_count].reshape(
            block_count, BLOCK, extended.shape[-1]
        )
        for offset in range(3)
    ]
    return jnp.concatenate(pieces, axis=1)


def unwindow(window_grads, row_count):
    channels = window_grads.shape[-1]
    summed_grad = jnp.zeros((row_count + 2 * BLOCK, channels), jnp.float32)
    for offset in range(3):
        piece_grad = window_grads[:, offset * BLOCK : (offset + 1) * BLOCK].reshape(
            row_count, channels
        )
        summed_grad = summed_grad + jnp.pad(
            piece_grad, ((offset * BLOCK, (2 - offset) * BLOCK), (0, 0))
        )
    return summed_grad


def head_scores(query_head, near_keys, far_keys, near_mask, far_mask):
    block_count = near_keys.shape[0]
    query_blocks = query_head.reshape(block_count, BLOCK, HEAD_DIM)
    near_scores = jnp.einsum(
        "nqd,nkd->nqk", query_blocks, near_keys, preferred_element_type=jnp.float32
    )
    far_scores = jnp.einsum("qd,kd->qk", query_head, far_keys, preferred_element_type=jnp.float32)
    return (jnp.where(near_mask, near_scores, MASKED), jnp.where(far_mask, far_scores, MASKED))


def per_device_general(
    tokens,
    lengths,
    norm_gain,
    global_gain,
    w_query,
    w_key,
    w_value,
    w_out,
    ffn_gain,
    w_gate,
    w_up,
    w_down,
    cotangent,
):
    row_count = tokens.shape[0]
    inner_dim = HEADS * HEAD_DIM
    block_count = row_count // BLOCK
    local_globals = row_count // GBLK
    group_tokens = row_count * lax.axis_size("blk")
    global_count = group_tokens // GBLK
    longest_len = min(LONGEST, group_tokens // 2)
    span_rows = min(global_count, 2 * (longest_len // GBLK) + local_globals)
    attn_full = (
        lax.all_gather(norm_gain, ("seq", "blk"), axis=0, tiled=True),
        lax.all_gather(global_gain, ("seq", "blk"), axis=0, tiled=True),
        lax.all_gather(w_query, ("seq", "blk"), axis=0, tiled=True),
        lax.all_gather(w_key, ("seq", "blk"), axis=0, tiled=True),
        lax.all_gather(w_value, ("seq", "blk"), axis=0, tiled=True),
        lax.all_gather(w_out, ("seq", "blk"), axis=0, tiled=True),
    )
    seq_ends = jnp.cumsum(lengths[0])
    first_row = lax.axis_index("blk") * row_count
    span_start = jnp.clip(first_row // GBLK - longest_len // GBLK, 0, global_count - span_rows)
    query_pos = first_row + jnp.arange(row_count, dtype=jnp.int32)
    query_seq = sequence_of(query_pos, seq_ends)
    key_pos = first_row - BLOCK + jnp.arange(row_count + 2 * BLOCK, dtype=jnp.int32)
    inside = (key_pos >= 0) & (key_pos < group_tokens)
    key_seq = jnp.where(inside, sequence_of(key_pos, seq_ends), -1)
    global_seq = sequence_of((span_start + jnp.arange(span_rows, dtype=jnp.int32)) * GBLK, seq_ends)
    query_pos_win = query_pos.reshape(block_count, BLOCK)
    query_seq_win = query_seq.reshape(block_count, BLOCK)
    key_pos_win = windows(key_pos[:, None], row_count)[:, :, 0]
    key_seq_win = windows(key_seq[:, None], row_count)[:, :, 0]
    near_mask = (jnp.abs(query_pos_win[:, :, None] - key_pos_win[:, None, :]) <= BLOCK - 1) & (
        query_seq_win[:, :, None] == key_seq_win[:, None, :]
    )
    far_mask = query_seq[:, None] == global_seq[None, :]
    tokens_full = tokens.astype(jnp.float32)
    normed_full, normed_pull = jax.vjp(rms_norm, tokens_full, attn_full[0].astype(jnp.float32))
    normed = normed_full.astype(jnp.bfloat16)
    queries = matmul(normed, attn_full[2]).astype(jnp.bfloat16)
    key_rows = matmul(normed, attn_full[3]).astype(jnp.bfloat16)
    value_rows = matmul(normed, attn_full[4]).astype(jnp.bfloat16)
    local_kv = jnp.concatenate([key_rows, value_rows], axis=1)
    extended = with_halo(local_kv, (("blk", 0),), BLOCK)
    near_kv = windows(extended, row_count)
    summed = jnp.sum(normed.astype(jnp.float32).reshape(local_globals, GBLK, D), axis=1)
    global_full, global_pull = jax.vjp(rms_norm, summed, attn_full[1].astype(jnp.float32))
    global_in = global_full.astype(jnp.bfloat16)
    own_global = jnp.concatenate(
        [
            matmul(global_in, attn_full[3]).astype(jnp.bfloat16),
            matmul(global_in, attn_full[4]).astype(jnp.bfloat16),
        ],
        axis=1,
    )
    global_kv = lax.all_gather(own_global, "blk", axis=0, tiled=True)
    span_kv = lax.dynamic_slice_in_dim(global_kv, span_start, span_rows, 0)

    def head_slices(head_index):
        column = head_index * HEAD_DIM
        query_head = lax.dynamic_slice_in_dim(queries, column, HEAD_DIM, 1)
        near_keys = lax.dynamic_slice_in_dim(near_kv, column, HEAD_DIM, 2)
        near_values = lax.dynamic_slice_in_dim(near_kv, inner_dim + column, HEAD_DIM, 2)
        far_keys = lax.dynamic_slice_in_dim(span_kv, column, HEAD_DIM, 1)
        far_values = lax.dynamic_slice_in_dim(span_kv, inner_dim + column, HEAD_DIM, 1)
        return (column, query_head, near_keys, near_values, far_keys, far_values)

    def head_forward(head_index, carry):
        attended_rows, log_sums = carry
        column, query_head, near_keys, near_values, far_keys, far_values = head_slices(head_index)
        near_scores, far_scores = head_scores(query_head, near_keys, far_keys, near_mask, far_mask)
        highest = jnp.maximum(
            jnp.max(near_scores, axis=2).reshape(row_count), jnp.max(far_scores, axis=1)
        )
        near_exp = jnp.exp(near_scores - highest.reshape(block_count, BLOCK, 1))
        far_exp = jnp.exp(far_scores - highest[:, None])
        denominator = jnp.sum(near_exp, axis=2).reshape(row_count) + jnp.sum(far_exp, axis=1)
        near_probs = (near_exp / denominator.reshape(block_count, BLOCK, 1)).astype(jnp.bfloat16)
        far_probs = (far_exp / denominator[:, None]).astype(jnp.bfloat16)
        head_out = jnp.einsum(
            "nqk,nkd->nqd", near_probs, near_values, preferred_element_type=jnp.float32
        ).reshape(row_count, HEAD_DIM)
        head_out = head_out + jnp.einsum(
            "qk,kd->qd", far_probs, far_values, preferred_element_type=jnp.float32
        )
        attended_rows = lax.dynamic_update_slice_in_dim(attended_rows, head_out, column, 1)
        log_sums = lax.dynamic_update_index_in_dim(
            log_sums, highest + jnp.log(denominator), head_index, 0
        )
        return (attended_rows, log_sums)

    attended_rows, log_sums = lax.fori_loop(
        0,
        HEADS,
        head_forward,
        (
            jnp.zeros((row_count, inner_dim), jnp.float32),
            jnp.zeros((HEADS, row_count), jnp.float32),
        ),
    )
    attended = attended_rows.astype(jnp.bfloat16)
    middle = tokens_full + matmul(attended, attn_full[5])
    ffn_full = (
        lax.all_gather(ffn_gain, ("seq", "blk"), axis=0, tiled=True),
        lax.all_gather(w_gate, ("seq", "blk"), axis=0, tiled=True),
        lax.all_gather(w_up, ("seq", "blk"), axis=0, tiled=True),
        lax.all_gather(w_down, ("seq", "blk"), axis=0, tiled=True),
    )
    hidden_full, hidden_pull = jax.vjp(rms_norm, middle, ffn_full[0].astype(jnp.float32))
    hidden = hidden_full.astype(jnp.bfloat16)
    gate_pre = matmul(hidden, ffn_full[1])
    up_pre = matmul(hidden, ffn_full[2])
    gated_rows, gated_pull = jax.vjp(gated, gate_pre, up_pre)
    mixed = gated_rows.astype(jnp.bfloat16)
    output = (middle + matmul(mixed, ffn_full[3])).astype(jnp.bfloat16)
    ffn_back = (
        lax.all_gather(ffn_gain, ("seq", "blk"), axis=0, tiled=True),
        lax.all_gather(w_gate, ("seq", "blk"), axis=0, tiled=True),
        lax.all_gather(w_up, ("seq", "blk"), axis=0, tiled=True),
        lax.all_gather(w_down, ("seq", "blk"), axis=0, tiled=True),
    )
    grad_down = matmul_left(mixed, cotangent)
    grad_mixed = matmul_right(cotangent, ffn_back[3])
    grad_gate_full, grad_up_full = gated_pull(grad_mixed)
    grad_gate = grad_gate_full.astype(jnp.bfloat16)
    grad_up = grad_up_full.astype(jnp.bfloat16)
    grad_wgate = matmul_left(hidden, grad_gate)
    grad_wup = matmul_left(hidden, grad_up)
    grad_hidden = matmul_right(grad_gate, ffn_back[1]) + matmul_right(grad_up, ffn_back[2])
    grad_middle_norm, grad_ffn_gain = hidden_pull(grad_hidden)
    grad_middle = cotangent.astype(jnp.float32) + grad_middle_norm
    attn_back = (
        lax.all_gather(norm_gain, ("seq", "blk"), axis=0, tiled=True),
        lax.all_gather(global_gain, ("seq", "blk"), axis=0, tiled=True),
        lax.all_gather(w_query, ("seq", "blk"), axis=0, tiled=True),
        lax.all_gather(w_key, ("seq", "blk"), axis=0, tiled=True),
        lax.all_gather(w_value, ("seq", "blk"), axis=0, tiled=True),
        lax.all_gather(w_out, ("seq", "blk"), axis=0, tiled=True),
    )
    grad_branch = grad_middle.astype(jnp.bfloat16)
    grad_wout = matmul_left(attended, grad_branch)
    grad_attended = matmul_right(grad_branch, attn_back[5]).astype(jnp.bfloat16)

    def head_backward(head_index, carry):
        grad_query_rows, grad_near, grad_far = carry
        column, query_head, near_keys, near_values, far_keys, far_values = head_slices(head_index)
        near_scores, far_scores = head_scores(query_head, near_keys, far_keys, near_mask, far_mask)
        lse_head = log_sums[head_index]
        near_probs = jnp.exp(near_scores - lse_head.reshape(block_count, BLOCK, 1))
        far_probs = jnp.exp(far_scores - lse_head[:, None])
        grad_head = lax.dynamic_slice_in_dim(grad_attended, column, HEAD_DIM, 1)
        grad_blocks = grad_head.reshape(block_count, BLOCK, HEAD_DIM)
        query_blocks = query_head.reshape(block_count, BLOCK, HEAD_DIM)
        near_dprobs = jnp.einsum(
            "nqd,nkd->nqk", grad_blocks, near_values, preferred_element_type=jnp.float32
        )
        far_dprobs = jnp.einsum(
            "qd,kd->qk", grad_head, far_values, preferred_element_type=jnp.float32
        )
        delta_rows = jnp.sum(near_probs * near_dprobs, axis=2).reshape(row_count) + jnp.sum(
            far_probs * far_dprobs, axis=1
        )
        near_grad_scores = (
            near_probs * (near_dprobs - delta_rows.reshape(block_count, BLOCK, 1))
        ).astype(jnp.bfloat16)
        far_grad_scores = (far_probs * (far_dprobs - delta_rows[:, None])).astype(jnp.bfloat16)
        head_dquery = jnp.einsum(
            "nqk,nkd->nqd", near_grad_scores, near_keys, preferred_element_type=jnp.float32
        ).reshape(row_count, HEAD_DIM)
        head_dquery = head_dquery + jnp.einsum(
            "qk,kd->qd", far_grad_scores, far_keys, preferred_element_type=jnp.float32
        )
        near_dkey = jnp.einsum(
            "nqk,nqd->nkd", near_grad_scores, query_blocks, preferred_element_type=jnp.float32
        )
        near_dvalue = jnp.einsum(
            "nqk,nqd->nkd",
            near_probs.astype(jnp.bfloat16),
            grad_blocks,
            preferred_element_type=jnp.float32,
        )
        far_dkey = jnp.einsum(
            "qk,qd->kd", far_grad_scores, query_head, preferred_element_type=jnp.float32
        )
        far_dvalue = jnp.einsum(
            "qk,qd->kd",
            far_probs.astype(jnp.bfloat16),
            grad_head,
            preferred_element_type=jnp.float32,
        )
        grad_query_rows = lax.dynamic_update_slice_in_dim(grad_query_rows, head_dquery, column, 1)
        grad_near = lax.dynamic_update_slice_in_dim(grad_near, near_dkey, column, 2)
        grad_near = lax.dynamic_update_slice_in_dim(grad_near, near_dvalue, inner_dim + column, 2)
        grad_far = lax.dynamic_update_slice_in_dim(grad_far, far_dkey, column, 1)
        grad_far = lax.dynamic_update_slice_in_dim(grad_far, far_dvalue, inner_dim + column, 1)
        return (grad_query_rows, grad_near, grad_far)

    grad_query_rows, grad_near, grad_far = lax.fori_loop(
        0,
        HEADS,
        head_backward,
        (
            jnp.zeros((row_count, inner_dim), jnp.float32),
            jnp.zeros((block_count, 3 * BLOCK, 2 * inner_dim), jnp.float32),
            jnp.zeros((span_rows, 2 * inner_dim), jnp.float32),
        ),
    )
    grad_extended = unwindow(grad_near, row_count)
    rim_rows = jnp.concatenate([grad_extended[:BLOCK], grad_extended[row_count + BLOCK :]], axis=0)
    returned = with_halo(rim_rows.astype(jnp.bfloat16), (("blk", 0),), BLOCK).astype(rim_rows.dtype)
    grad_kv = grad_extended[BLOCK : row_count + BLOCK]
    grad_kv = grad_kv + jnp.pad(returned[:BLOCK], ((0, row_count - BLOCK), (0, 0)))
    grad_kv = grad_kv + jnp.pad(returned[3 * BLOCK :], ((row_count - BLOCK, 0), (0, 0)))
    grad_kv = grad_kv.astype(jnp.bfloat16)
    grad_key = grad_kv[:, :inner_dim]
    grad_value = grad_kv[:, inner_dim:]
    group_far = lax.dynamic_update_slice_in_dim(
        jnp.zeros((global_count, 2 * inner_dim), jnp.float32), grad_far, span_start, 0
    )
    own_global_grad = lax.psum_scatter(group_far, "blk", scatter_dimension=0, tiled=True).astype(
        jnp.bfloat16
    )
    grad_global_key = own_global_grad[:, :inner_dim]
    grad_global_value = own_global_grad[:, inner_dim:]
    grad_query = grad_query_rows.astype(jnp.bfloat16)
    grad_wquery = matmul_left(normed, grad_query)
    grad_wkey = matmul_left(normed, grad_key) + matmul_left(global_in, grad_global_key)
    grad_wvalue = matmul_left(normed, grad_value) + matmul_left(global_in, grad_global_value)
    grad_normed = (
        matmul_right(grad_query, attn_back[2])
        + matmul_right(grad_key, attn_back[3])
        + matmul_right(grad_value, attn_back[4])
    )
    grad_global_in = matmul_right(grad_global_key, attn_back[3]) + matmul_right(
        grad_global_value, attn_back[4]
    )
    grad_summed, grad_global_gain = global_pull(grad_global_in)
    grad_normed = (grad_normed.reshape(local_globals, GBLK, D) + grad_summed[:, None, :]).reshape(
        row_count, D
    )
    grad_tokens_norm, grad_norm_gain = normed_pull(grad_normed)
    grad_tokens = grad_middle + grad_tokens_norm
    every_grad = (
        lax.psum_scatter(grad_norm_gain, ("seq", "blk"), scatter_dimension=0, tiled=True),
        lax.psum_scatter(grad_global_gain, ("seq", "blk"), scatter_dimension=0, tiled=True),
        lax.psum_scatter(grad_wquery, ("seq", "blk"), scatter_dimension=0, tiled=True),
        lax.psum_scatter(grad_wkey, ("seq", "blk"), scatter_dimension=0, tiled=True),
        lax.psum_scatter(grad_wvalue, ("seq", "blk"), scatter_dimension=0, tiled=True),
        lax.psum_scatter(grad_wout, ("seq", "blk"), scatter_dimension=0, tiled=True),
        lax.psum_scatter(grad_ffn_gain, ("seq", "blk"), scatter_dimension=0, tiled=True),
        lax.psum_scatter(grad_wgate, ("seq", "blk"), scatter_dimension=0, tiled=True),
        lax.psum_scatter(grad_wup, ("seq", "blk"), scatter_dimension=0, tiled=True),
        lax.psum_scatter(grad_down, ("seq", "blk"), scatter_dimension=0, tiled=True),
    )
    return (
        output,
        grad_tokens,
        every_grad[0],
        every_grad[1],
        every_grad[2],
        every_grad[3],
        every_grad[4],
        every_grad[5],
        every_grad[6],
        every_grad[7],
        every_grad[8],
        every_grad[9],
    )


MESH = pl.DeviceIdType.MESH
CHIPS_Z = 4
NEVER = 1 << 20
VMEM_BYTES = 64 * 1024 * 1024 - 65536


def dot(a, b, dims, precision=None):
    return lax.dot_general(
        a, b, (dims, ((), ())), precision=precision, preferred_element_type=jnp.float32
    )


def dot_nn(a, b):
    return dot(a, b, ((1,), (0,)))


def dot_nt(a, b):
    return dot(a, b, ((1,), (1,)))


def coords():
    y = lax.axis_index("seq")
    blk = lax.axis_index("blk")
    return y, blk // 4, (blk // 2) % 2, blk % 2


def device(y, z, x, c):
    return (y, z * 4 + x * 2 + c)


def send(src, dst, send_sem, recv_sem, target):
    pltpu.make_async_remote_copy(
        src_ref=src,
        dst_ref=dst,
        send_sem=send_sem,
        recv_sem=recv_sem,
        device_id=target,
        device_id_type=MESH,
    ).start()


def wait_bytes(ref, sem):
    pltpu.make_async_copy(ref, ref, sem).wait()


def column_peers():
    y, z, x, c = coords()
    peers = [device(y, z, x, 1 - c)]
    for k in range(1, CHIPS_Z):
        peers += [device(y, (z + k) % CHIPS_Z, x, j) for j in range(2)]
    return peers


def side_peers():
    y, z, x, c = coords()
    return [device(y, z, 1 - x, c), device(1 - y, z, x, c), device(1 - y, z, 1 - x, c)]


def greet():
    y, z, x, c = coords()
    blk = lax.axis_index("blk")
    barrier = pltpu.get_barrier_semaphore()
    peers = column_peers() + side_peers()
    for peer in peers:
        pl.semaphore_signal(barrier, inc=1, device_id=peer, device_id_type=MESH)

    @pl.when(blk > 0)
    def _():
        pl.semaphore_signal(barrier, inc=1, device_id=(y, blk - 1), device_id_type=MESH)

    @pl.when(blk < 15)
    def _():
        pl.semaphore_signal(barrier, inc=1, device_id=(y, blk + 1), device_id_type=MESH)

    inner = jnp.where((blk > 0) & (blk < 15), 1, 0)
    pl.semaphore_wait(barrier, len(peers) + 1 + inner)


class Slots:
    def __init__(self, rows, half, first=None):
        self.rows, self.half = rows, half
        self.y, self.z, self.x, self.c = coords()
        self.side = self.c if first is None else first

    def plane(self, c):
        return pl.ds(pl.multiple_of(c * self.half, 128), self.half)

    def slot_rows(self, y, z, x):
        return pl.ds(pl.multiple_of((y * 8 + z * 2 + x) * (2 * self.rows), 8), 2 * self.rows)

    def near_pair(self, j):
        y, x, side = self.y, self.x, self.side
        return y * (1 - side) + j * side, x * side + j * (1 - side)

    def far_pair(self, j):
        y, x, side = self.y, self.x, self.side
        return (1 - y) * (1 - side) + j * side, (1 - x) * side + j * (1 - side)

    def near_slot(self):
        y, x, side = self.y, self.x, self.side
        return y * (1 - side) + (1 - y) * side, x * side + (1 - x) * (1 - side)

    def near_peer(self):
        slot_y, slot_x = self.near_slot()
        return device(slot_y, self.z, slot_x, self.c)

    def far_peer(self):
        y, z, x, c, side = self.y, self.z, self.x, self.c, self.side
        return device(y + (1 - side) * (1 - 2 * y), z, x + side * (1 - 2 * x), c)


class Gather(Slots):
    def __init__(self, shard, full, recv, sent, first=None):
        if isinstance(shard, tuple):
            super().__init__(*shard[0].shape, first)
        else:
            super().__init__(shard.shape[0], shard.shape[1] // 2, first)
        self.shard, self.full, self.recv, self.sent = shard, full, recv, sent

    def span(self, rows):
        return self.full.at[pl.ds(0, rows), pl.ds(0, self.half)]

    def mine(self):
        index = self.y * 16 + self.z * 4 + self.x * 2 + self.c
        return pl.ds(pl.multiple_of(index * self.rows, 8), self.rows)

    def slot(self, y, z, x):
        return self.full.at[self.slot_rows(y, z, x), self.plane(self.c)]

    def open(self, own, other, c):
        y, z, x = self.y, self.z, self.x
        target = self.full.at[self.mine(), self.plane(1 - c)]
        send(other, target, self.sent.at[0], self.recv.at[0], device(y, z, x, 1 - c))
        target = self.full.at[self.mine(), self.plane(c)]
        pltpu.make_async_copy(own, target, self.sent.at[2]).start()

    def own_here(self):
        wait_bytes(self.full.at[self.mine(), self.plane(self.c)], self.sent.at[2])

    def step(self, number):
        y, z, x, c, rows = self.y, self.z, self.x, self.c, self.rows
        if number == 0 and isinstance(self.shard, tuple):
            for core in range(2):
                own, other = self.shard[core], self.shard[1 - core]
                pl.when(c == core)(functools.partial(self.open, own, other, core))
        elif number == 0:
            self.open(self.shard.at[:, self.plane(c)], self.shard.at[:, self.plane(1 - c)], c)
        if number == 1:
            self.own_here()
            wait_bytes(self.span(rows), self.recv.at[0])
            block = self.slot(y, z, x)
            for k in range(1, CHIPS_Z):
                target = device(y, (z + k) % CHIPS_Z, x, c)
                send(block, block, self.sent.at[1], self.recv.at[1], target)
        if number == 2:
            wait_bytes(self.span(6 * rows), self.recv.at[1])
            for k in range(CHIPS_Z):
                block = self.slot(y, k, x)
                send(block, block, self.sent.at[1], self.recv.at[2], self.near_peer())
        if number == 3:
            wait_bytes(self.span(8 * rows), self.recv.at[2])
            for k in range(CHIPS_Z):
                for j in range(2):
                    slot_y, slot_x = self.near_pair(j)
                    block = self.slot(slot_y, k, slot_x)
                    send(block, block, self.sent.at[1], self.recv.at[3], self.far_peer())
        if number == 4:
            wait_bytes(self.span(16 * rows), self.recv.at[3])
            block = self.full.at[:, self.plane(c)]
            send(block, block, self.sent.at[1], self.recv.at[4], device(y, z, x, 1 - c))
        if number == 5:
            wait_bytes(self.span(32 * rows), self.recv.at[4])
        if number == 6:
            wait_bytes(self.span(rows), self.sent.at[0])
            wait_bytes(self.full.at[pl.ds(0, 31 * rows)], self.sent.at[1])


class GatherLate(Gather):
    def step(self, number):
        y, z, x, c, rows = self.y, self.z, self.x, self.c, self.rows
        if number == 1:
            self.own_here()
            wait_bytes(self.span(rows), self.recv.at[0])
            block = self.slot(y, z, x)
            send(block, block, self.sent.at[1], self.recv.at[1], self.near_peer())
        elif number == 2:
            wait_bytes(self.span(2 * rows), self.recv.at[1])
            for j in range(2):
                slot_y, slot_x = self.near_pair(j)
                block = self.slot(slot_y, z, slot_x)
                send(block, block, self.sent.at[1], self.recv.at[2], self.far_peer())
        elif number == 3:
            wait_bytes(self.span(4 * rows), self.recv.at[2])
            for k in range(1, CHIPS_Z):
                target = device(y, (z + k) % CHIPS_Z, x, c)
                for j in range(4):
                    block = self.slot(j // 2, z, j % 2)
                    send(block, block, self.sent.at[1], self.recv.at[3], target)
        elif number == 4:
            wait_bytes(self.span(24 * rows), self.recv.at[3])
            block = self.full.at[:, self.plane(c)]
            send(block, block, self.sent.at[1], self.recv.at[4], device(y, z, x, 1 - c))
        else:
            super().step(number)


class Reduce(Slots):
    def __init__(self, part, out, work, near, mid, far, last, pair, recv, sent, first=None):
        super().__init__(out.shape[0], out.shape[1] // 2, first)
        self.part, self.out, self.work = part, out, work
        self.near, self.mid, self.far, self.last, self.pair = near, mid, far, last, pair
        self.recv, self.sent = recv, sent

    def add(self, rows, ref, index):
        size = 2 * self.rows
        start = pl.ds(pl.multiple_of(index * size, 8), size)
        self.work[rows, :] += ref[start, :]

    def start_sum(self):
        wait_bytes(self.work, self.recv.at[0])
        size = 2 * self.rows

        @pl.loop(0, 16)
        def _(index):
            span = pl.ds(pl.multiple_of(index * size, 8), size)
            self.work[span, :] += self.part[span, self.plane(self.c)]

    def step(self, number):
        y, z, x, c, rows = self.y, self.z, self.x, self.c, self.rows
        size = 2 * rows
        if number == 0:
            send(
                self.part.at[:, self.plane(1 - c)],
                self.work,
                self.sent.at[0],
                self.recv.at[0],
                device(y, z, x, 1 - c),
            )
        if number == 1:
            self.start_sum()
            for k in range(CHIPS_Z):
                for j in range(2):
                    slot_y, slot_x = self.far_pair(j)
                    send(
                        self.work.at[self.slot_rows(slot_y, k, slot_x)],
                        self.near.at[pl.ds((k * 2 + j) * size, size)],
                        self.sent.at[1],
                        self.recv.at[1],
                        self.far_peer(),
                    )
        if number == 2:
            wait_bytes(self.near, self.recv.at[1])

            @pl.loop(0, 8)
            def _(index):
                k, j = index // 2, index % 2
                slot_y, slot_x = self.near_pair(j)
                self.add(self.slot_rows(slot_y, k, slot_x), self.near, index)

            for k in range(CHIPS_Z):
                slot_y, slot_x = self.near_slot()
                send(
                    self.work.at[self.slot_rows(slot_y, k, slot_x)],
                    self.mid.at[pl.ds(k * size, size)],
                    self.sent.at[1],
                    self.recv.at[2],
                    self.near_peer(),
                )
        if number == 3:
            wait_bytes(self.mid, self.recv.at[2])

            @pl.loop(0, CHIPS_Z)
            def _(k):
                self.add(self.slot_rows(y, k, x), self.mid, k)

            for k in range(1, CHIPS_Z):
                to_z = (z + k) % CHIPS_Z
                send(
                    self.work.at[self.slot_rows(y, to_z, x)],
                    self.far.at[pl.ds((k - 1) * size, size)],
                    self.sent.at[1],
                    self.recv.at[3],
                    device(y, to_z, x, c),
                )
        if number == 4:
            wait_bytes(self.far, self.recv.at[3])
            total = self.work[self.slot_rows(y, z, x), :].astype(jnp.float32)
            for k in range(self.far.shape[0] // size):
                total = total + self.far[pl.ds(k * size, size), :].astype(jnp.float32)
            self.last[...] = total
            keep = pl.ds(pl.multiple_of(c * rows, 8), rows)
            give = pl.ds(pl.multiple_of((1 - c) * rows, 8), rows)
            send(
                self.last.at[give],
                self.pair,
                self.sent.at[2],
                self.recv.at[4],
                device(y, z, x, 1 - c),
            )
            self.out[:, self.plane(c)] = self.last[keep, :]
        if number == 5:
            wait_bytes(self.pair, self.recv.at[4])
            self.out[:, self.plane(1 - c)] = self.pair[...]
        if number == 6:
            wait_bytes(self.work, self.sent.at[0])
            wait_bytes(self.work.at[pl.ds(0, 30 * rows)], self.sent.at[1])
            wait_bytes(self.pair, self.sent.at[2])


class ReduceEarly(Reduce):
    def step(self, number):
        y, z, x, c = self.y, self.z, self.x, self.c
        size = 2 * self.rows
        if number == 1:
            self.start_sum()
            for k in range(1, CHIPS_Z):
                to_z = (z + k) % CHIPS_Z
                for j in range(4):
                    send(
                        self.work.at[self.slot_rows(j // 2, to_z, j % 2)],
                        self.near.at[pl.ds((4 * (k - 1) + j) * size, size)],
                        self.sent.at[1],
                        self.recv.at[1],
                        device(y, to_z, x, c),
                    )
        elif number == 2:
            wait_bytes(self.near, self.recv.at[1])

            @pl.loop(0, 12)
            def _(index):
                j = index % 4
                self.add(self.slot_rows(j // 2, z, j % 2), self.near, index)

            for j in range(2):
                slot_y, slot_x = self.far_pair(j)
                send(
                    self.work.at[self.slot_rows(slot_y, z, slot_x)],
                    self.mid.at[pl.ds(j * size, size)],
                    self.sent.at[1],
                    self.recv.at[2],
                    self.far_peer(),
                )
        elif number == 3:
            wait_bytes(self.mid, self.recv.at[2])
            for j in range(2):
                slot_y, slot_x = self.near_pair(j)
                self.add(self.slot_rows(slot_y, z, slot_x), self.mid, j)
            slot_y, slot_x = self.near_slot()
            send(
                self.work.at[self.slot_rows(slot_y, z, slot_x)],
                self.far,
                self.sent.at[1],
                self.recv.at[3],
                self.near_peer(),
            )
        else:
            super().step(number)


def reduce_scratch(rows, half, dtype, counts=(16, 8, 6)):
    return [
        pltpu.VMEM((32 * rows, half), dtype),
        pltpu.VMEM((counts[0] * rows, half), dtype),
        pltpu.VMEM((counts[1] * rows, half), dtype),
        pltpu.VMEM((counts[2] * rows, half), dtype),
        pltpu.VMEM((2 * rows, half), jnp.float32),
        pltpu.VMEM((rows, half), jnp.float32),
    ]


def seq_bounds(lengths, position):
    low = jnp.zeros((1, 128), jnp.int32)
    high = jnp.full((1, 128), NEVER, jnp.int32)
    end = low
    for i in range(lengths.shape[0]):
        end = end + lengths[i : i + 1, :]
        low = jnp.maximum(low, jnp.where(end <= position, end, 0))
        high = jnp.minimum(high, jnp.where(end > position, end, NEVER))
    return low, high


class Span:
    fields = ("start", "far_low", "far_high", "no_before", "no_after", "second")

    def __init__(self, rows):
        for i, name in enumerate(self.fields):
            setattr(self, name, rows[i : i + 1, :])


def span_rows(lengths, first_row, block, far_rows, global_count):
    position = first_row + block * BLOCK
    low, high = seq_bounds(lengths, position)
    first_low, _ = seq_bounds(lengths, first_row)
    start = jnp.minimum(low >> 4, global_count - far_rows)
    rows = [
        start,
        (low >> 4) - start,
        (high >> 4) - start,
        jnp.where(position > low, 0, NEVER),
        jnp.where(position + BLOCK < high, 0, NEVER),
        jnp.where(low == first_low, 0, 1),
    ]
    return jnp.concatenate(rows + [start, start], axis=0)


def window_select(spans, window, blocks, far_rows, global_count):
    start = Span(spans[pl.ds(8 * window * (blocks - 1), 8), :]).start
    row = lax.broadcasted_iota(jnp.int32, (far_rows, global_count), 0)
    column = lax.broadcasted_iota(jnp.int32, (far_rows, global_count), 1)
    return (column - widen(start, global_count) == row).astype(jnp.bfloat16)


def far_part(ref, lanes, span, near_rows, far_rows):
    first = ref[pl.ds(near_rows, far_rows), lanes]
    second = ref[pl.ds(near_rows + far_rows, far_rows), lanes]
    return jnp.where(span.second > 0, second, first)


def widen(row, width):
    return jnp.concatenate([row] * (width // 128), axis=1)


def head_pair(rows):
    lane = lax.broadcasted_iota(jnp.int32, rows.shape, 1)
    zero = jnp.zeros_like(rows)
    return jnp.concatenate(
        [jnp.where(lane < HEAD_DIM, rows, zero), jnp.where(lane < HEAD_DIM, zero, rows)], axis=0
    )


def attend_block(pair, block, span, query, keys, values, attended, near_rows, far_rows):
    lanes = pl.ds(pl.multiple_of(pair * 128, 128), 128)
    rows = pl.ds(pl.multiple_of(block * BLOCK, BLOCK), BLOCK)
    near = pl.ds(pl.multiple_of(block * BLOCK, BLOCK), 3 * BLOCK)
    both = head_pair(query[rows, lanes])
    near_scores = dot_nt(both, keys[near, lanes])
    far_scores = dot_nt(both, far_part(keys, lanes, span, near_rows, far_rows))
    row = lax.broadcasted_iota(jnp.int32, (2 * BLOCK, BLOCK), 0) % BLOCK
    column = lax.broadcasted_iota(jnp.int32, (2 * BLOCK, BLOCK), 1)
    edge = jnp.where(
        column > row + span.no_before,
        near_scores[:, :BLOCK],
        jnp.where(column < row - span.no_after, near_scores[:, 2 * BLOCK :], MASKED),
    )
    own = near_scores[:, BLOCK : 2 * BLOCK]
    far_column = lax.broadcasted_iota(jnp.int32, far_scores.shape, 1)
    far_scores = jnp.where(
        (far_column >= widen(span.far_low, far_rows))
        & (far_column < widen(span.far_high, far_rows)),
        far_scores,
        MASKED,
    )
    highest = jnp.maximum(
        jnp.max(jnp.maximum(edge, own), axis=1, keepdims=True),
        jnp.max(far_scores, axis=1, keepdims=True),
    )
    edge_exp = jnp.exp(edge - highest)
    own_exp = jnp.exp(own - highest)
    far_exp = jnp.exp(far_scores - highest)
    inverse = 1.0 / (
        jnp.sum(edge_exp + own_exp, axis=1, keepdims=True) + jnp.sum(far_exp, axis=1, keepdims=True)
    )
    edge_probs = edge_exp * inverse
    near_probs = jnp.concatenate(
        [
            jnp.where(column > row, edge_probs, 0.0).astype(jnp.bfloat16),
            (own_exp * inverse).astype(jnp.bfloat16),
            jnp.where(column < row, edge_probs, 0.0).astype(jnp.bfloat16),
        ],
        axis=1,
    )
    far_probs = (far_exp * inverse).astype(jnp.bfloat16)
    mixed = dot_nn(near_probs, values[near, lanes]) + dot_nn(
        far_probs, far_part(values, lanes, span, near_rows, far_rows)
    )
    lane = lax.broadcasted_iota(jnp.int32, (BLOCK, 128), 1)
    attended[rows, lanes] = jnp.where(lane < HEAD_DIM, mixed[:BLOCK], mixed[BLOCK:]).astype(
        jnp.bfloat16
    )


def attend_block_back(
    pair, block, span, query, grad, keys, keys_t, values, grad_query, grad_keys, grad_values,
    near_rows, far_rows,
):
    lanes = pl.ds(pl.multiple_of(pair * 128, 128), 128)
    rows = pl.ds(pl.multiple_of(block * BLOCK, BLOCK), BLOCK)
    near = pl.ds(pl.multiple_of(block * BLOCK, BLOCK), 3 * BLOCK)
    both = head_pair(query[rows, lanes])
    grads = head_pair(grad[rows, lanes])
    near_scores = dot_nt(keys[near, lanes], both)
    far_keys = far_part(keys, lanes, span, near_rows, far_rows)
    far_scores = dot_nt(far_keys, both)
    row = lax.broadcasted_iota(jnp.int32, (BLOCK, 2 * BLOCK), 0)
    column = lax.broadcasted_iota(jnp.int32, (BLOCK, 2 * BLOCK), 1) % BLOCK
    edge = jnp.where(
        row > column + widen(span.no_before, 2 * BLOCK),
        near_scores[:BLOCK],
        jnp.where(row < column - widen(span.no_after, 2 * BLOCK), near_scores[2 * BLOCK :], MASKED),
    )
    own = near_scores[BLOCK : 2 * BLOCK]
    far_row = lax.broadcasted_iota(jnp.int32, far_scores.shape, 0)
    far_scores = jnp.where(
        (far_row >= widen(span.far_low, 2 * BLOCK)) & (far_row < widen(span.far_high, 2 * BLOCK)),
        far_scores,
        MASKED,
    )
    highest = jnp.maximum(
        jnp.max(jnp.maximum(edge, own), axis=0, keepdims=True),
        jnp.max(far_scores, axis=0, keepdims=True),
    )
    edge_exp = jnp.exp(edge - highest)
    own_exp = jnp.exp(own - highest)
    far_exp = jnp.exp(far_scores - highest)
    inverse = 1.0 / (
        jnp.sum(edge_exp + own_exp, axis=0, keepdims=True) + jnp.sum(far_exp, axis=0, keepdims=True)
    )
    edge_probs, own_probs, far_probs = edge_exp * inverse, own_exp * inverse, far_exp * inverse
    near_dprobs = dot_nt(values[near, lanes], grads)
    far_dprobs = dot_nt(far_part(values, lanes, span, near_rows, far_rows), grads)
    edge_dprobs = jnp.where(row > column, near_dprobs[:BLOCK], near_dprobs[2 * BLOCK :])
    own_dprobs = near_dprobs[BLOCK : 2 * BLOCK]
    delta = jnp.sum(
        edge_probs * edge_dprobs + own_probs * own_dprobs, axis=0, keepdims=True
    ) + jnp.sum(far_probs * far_dprobs, axis=0, keepdims=True)
    edge_ds = edge_probs * (edge_dprobs - delta)
    own_ds = (own_probs * (own_dprobs - delta)).astype(jnp.bfloat16)
    far_ds = (far_probs * (far_dprobs - delta)).astype(jnp.bfloat16)

    def spread(edge_part, own_part):
        return jnp.concatenate(
            [
                jnp.where(row > column, edge_part, 0.0).astype(jnp.bfloat16),
                own_part.astype(jnp.bfloat16),
                jnp.where(row < column, edge_part, 0.0).astype(jnp.bfloat16),
            ],
            axis=0,
        )

    near_ds = spread(edge_ds, own_ds)
    far_keys_t = jnp.where(
        widen(span.second, far_rows) > 0,
        keys_t[lanes, pl.ds(near_rows + far_rows, far_rows)],
        keys_t[lanes, pl.ds(near_rows, far_rows)],
    )
    query_t = dot_nn(keys_t[lanes, near], near_ds) + dot_nn(far_keys_t, far_ds)
    feature = lax.broadcasted_iota(jnp.int32, (128, BLOCK), 0)
    query_t = jnp.where(feature < HEAD_DIM, query_t[:, :BLOCK], query_t[:, BLOCK:])
    grad_query[rows, lanes] = query_t.T.astype(jnp.bfloat16)
    grad_keys[near, lanes] += dot_nn(near_ds, both)
    grad_values[near, lanes] += dot_nn(spread(edge_probs, own_probs), grads)
    far_dkey = dot_nn(far_ds, both)
    far_dvalue = dot_nn(far_probs.astype(jnp.bfloat16), grads)
    for window in range(2):
        place = pl.ds(near_rows + window * far_rows, far_rows)
        here = span.second == window
        grad_keys[place, lanes] += jnp.where(here, far_dkey, 0.0)
        grad_values[place, lanes] += jnp.where(here, far_dvalue, 0.0)


def inverse_rms(values):
    return lax.rsqrt(jnp.mean(values * values, axis=-1, keepdims=True) + EPSILON)


def rms_back(values, gain, grads):
    scale = inverse_rms(values)
    scaled = grads * gain
    back = scale * scaled - values * (
        scale * scale * scale * jnp.mean(scaled * values, axis=-1, keepdims=True)
    )
    return back, jnp.sum(grads * values * scale, axis=0, keepdims=True)


def block_sums(rows, count):
    take = lax.broadcasted_iota(jnp.int32, (count, rows.shape[0]), 1) // GBLK
    which = lax.broadcasted_iota(jnp.int32, (count, rows.shape[0]), 0)
    return dot_nn((take == which).astype(jnp.bfloat16), rows)


def owner_of(column, rows):
    return (column * ((65536 + rows - 1) // rows)) >> 16


def spread_gains(packed, rows):
    width = 32 * rows
    lane = lax.broadcasted_iota(jnp.int32, (128, width), 0)
    column = lax.broadcasted_iota(jnp.int32, (128, width), 1)
    select = (column - rows * owner_of(column, rows) == lane).astype(jnp.float32)
    wide = dot(packed, select, ((1,), (0,)), precision=lax.Precision.HIGHEST)
    device_row = lax.broadcasted_iota(jnp.int32, wide.shape, 0) >> 3
    wide_column = lax.broadcasted_iota(jnp.int32, wide.shape, 1)
    wide = jnp.where(owner_of(wide_column, rows) == device_row, wide, 0.0)
    return jnp.sum(wide.reshape(32, 8, width), axis=0)


def pack_gains(wide, rows):
    width = 32 * rows
    tall = jnp.concatenate([wide] * 32, axis=0)
    device_row = lax.broadcasted_iota(jnp.int32, tall.shape, 0) >> 3
    column = lax.broadcasted_iota(jnp.int32, tall.shape, 1)
    tall = jnp.where(owner_of(column, rows) == device_row, tall, 0.0)
    lane = lax.broadcasted_iota(jnp.int32, (width, 128), 1)
    from_column = lax.broadcasted_iota(jnp.int32, (width, 128), 0)
    select = (from_column - rows * owner_of(from_column, rows) == lane).astype(jnp.float32)
    return dot(tall, select, ((1,), (0,)), precision=lax.Precision.HIGHEST)


CHUNKS = 4
TILE = 256
SMALL_SEMS = 24
NAMES = ("g", "h", "i", "k", "v", "q", "o", "d", "f0", "f1", "f2", "f3")
NAMES += ("r0", "r1", "r2", "r3", "rd", "ro", "ra", "rb", "rc", "w", "j", "l")
Z_LAST = ("f3", "o")
Z_FIRST = ("r1",)
FIRST = {}
SCHEDULE = {
    "s0": {
        0: (0, 10, 30, 40, 50, 60, 70, 80, 90, 100, 110),
    },
    "s0b": {
        0: (61, 111, 31, 41, 20, 51),
    },
    "s1": {
        0: (1, 11, 62, 2),
    },
    "s2": {
        0: (112, 32),
    },
    "s4": {
        0: (42, 33, 43, 21, 71, 81, 34, 52, 44, 53, 22, 72, 91, 23),
    },
    "s5": {
        0: (35,),
    },
    "kn": {
        2: (54, 82, 101, 63, 113),
    },
    "kt": {
        4: (73,),
    },
    "s6": {
        0: (45,),
    },
    "vn": {
        2: (92,),
        4: (83,),
    },
    "s7": {
        0: (55,),
    },
    "fa": {
        2: (102,),
        4: (93,),
        8: (103,),
        11: (74,),
    },
    "m0": {
        0: (64, 84, 65),
    },
    "m1": {
        0: (75,),
    },
    "ca": {
        0: (85,),
        1: (104, 95),
        2: (105,),
        3: (115,),
    },
    "cb": {
        0: (94,),
    },
    "cw": {
        0: (120,),
        1: (130,),
        2: (140,),
        3: (150,),
    },
    "cg": {
        3: (121,),
        6: (114, 131),
        7: (122,),
        9: (123, 141),
    },
    "sp": {
        0: (160,),
    },
    "m2": {
        0: (151,),
    },
    "m3": {
        0: (142, 170),
    },
    "ba": {
        0: (161,),
        1: (171,),
        3: (132, 143, 152),
        6: (153, 181, 144),
        7: (162,),
        9: (154, 172, 191, 133),
    },
    "bt": {
        0: (180, 124),
        1: (190,),
        2: (200, 173),
    },
    "wg": {
        6: (163,),
        7: (182,),
    },
    "e1b": {
        0: (134,),
    },
    "e1": {
        0: (220,),
    },
    "e2": {
        0: (210,),
    },
    "gg": {
        1: (221, 183, 201, 192),
    },
    "e6": {
        0: (211,),
    },
    "e6b": {
        0: (164, 174, 222, 184, 193, 202, 223),
    },
    "e7": {
        0: (230,),
    },
    "fi": {
        1: (203,),
    },
    "e8": {
        0: (125, 135, 145, 155, 165, 175, 185, 194, 231, 195, 204, 232, 205),
    },
}


class Calls:
    def __init__(self, *actions):
        self.actions = actions

    def step(self, number):
        self.actions[number]()


def tiled(count, body, before=None):
    @pl.loop(0, count // TILE)
    def _(i):
        if before is not None:
            before(i)
        body(pl.ds(pl.multiple_of(i * TILE, TILE), TILE))


class GlobalSlots:
    def __init__(self, count):
        self.count = count

    def at(self, z, x, c):
        return self.packed(z * 4 + x * 2 + c)

    def packed(self, index):
        return pl.ds(pl.multiple_of(index * self.count, 16), self.count)


def layer_kernel(lengths, first_gain, second_gain, third_gain, tokens, cotangent, *refs):
    shards, refs = refs[:7], refs[7:]
    packed, raw_sums, refs = refs[-2], refs[-1], refs[:-2]
    output, grad_tokens, gain_out, refs = refs[0], refs[1], refs[2], refs[3:]
    grads_out, refs = refs[:9], refs[9:]
    w_query, w_key, w_value, w_out, w_down, w_ff = refs[:6]
    rows_in, rows_in_t, keys, keys_t, values, query, attended, hidden, turned = refs[6:15]
    mixed, grad_both, grad_keys, grad_values, gain_grads, part_key, part_value = refs[15:22]
    spans, gain_rows, gathered, gain_part, gain_side, gain_column, group_sums = refs[22:29]
    halo, global_rows, global_near, global_mid, global_far = refs[29:34]
    buffers, refs = refs[34:88], refs[88:]
    recv, sent, small = refs
    y, z, x, c = coords()
    blk = lax.axis_index("blk")
    me = blk + 16 * y
    row_count, width = tokens.shape
    blocks = row_count // BLOCK
    local_globals = row_count // GBLK
    global_count = global_rows.shape[0]
    near_rows = row_count + 2 * BLOCK
    all_rows = rows_in.shape[0]
    far_rows = (all_rows - near_rows) // 2
    feature_rows = width // 32
    hidden_rows = w_down.shape[0] // CHUNKS
    first_row = blk * row_count
    low = jnp.bfloat16
    slots = GlobalSlots(local_globals)
    column, sides = column_peers(), side_peers()

    part_query = rows_in.at[pl.ds(0, width)]
    steps = {}
    chunk_width = w_ff.shape[2]
    sources = [("q", shards[0], w_query), ("k", shards[1], w_key), ("v", shards[2], w_value)]
    sources += [("o", shards[3], w_out), ("d", shards[4], w_down)]
    for chunk in range(CHUNKS):
        part = pl.ds(chunk * chunk_width // 2, chunk_width // 2)
        pair = (shards[5].at[:, part], shards[6].at[:, part])
        sources.append((NAMES[8 + chunk], pair, w_ff.at[chunk]))
    for i, (name, shard, full) in enumerate(sources):
        kind = GatherLate if name in Z_LAST else Gather
        steps[name] = kind(shard, full, recv.at[i], sent.at[i], FIRST.get(name))
    ff_steps = [steps[name] for name in NAMES[8:12]]
    targets = [("ra", part_key), ("rb", part_value), ("rc", part_query), ("ro", w_out)]
    targets += [("rd", w_down)]
    targets += [(NAMES[12 + chunk], w_ff.at[chunk]) for chunk in range(CHUNKS)]
    for i, (name, part) in enumerate(targets):
        held = buffers[6 * i : 6 * i + 6]
        kind = ReduceEarly if name in Z_FIRST else Reduce
        steps[name] = kind(part, grads_out[i], *held, recv.at[9 + i], sent.at[9 + i], FIRST.get(name))

    def run(todo):
        for code in todo:
            steps[NAMES[code // 10]].step(code % 10)

    def tick(kind, number=0):
        run(SCHEDULE.get(kind, {}).get(number, ()))

    def loop_tick(kind, index, count):
        for number in range(count):
            todo = SCHEDULE.get(kind, {}).get(number, ())
            if todo:
                pl.when(index == number)(functools.partial(run, todo))

    def ticks(kind, count):
        return lambda index: loop_tick(kind, index, count)

    packed[...] = jnp.zeros_like(packed)
    for i, gain in enumerate((first_gain, second_gain, third_gain)):
        packed[i : i + 1, pl.ds(0, feature_rows)] = gain[...].astype(jnp.float32).reshape(
            1, feature_rows
        )
    greet()
    own_tile = gathered.at[pl.ds(pl.multiple_of(me * 8, 8), 8)]

    def share_gains():
        own_tile[...] = packed[...]
        for peer in column:
            send(packed, own_tile, small.at[1], small.at[0], peer)

    def spread_sides():
        wait_bytes(gathered.at[pl.ds(0, 56)], small.at[0])
        for k in range(CHIPS_Z):
            pair = gathered.at[pl.ds(pl.multiple_of((y * 8 + k * 2 + x) * 16, 16), 16)]
            for peer in sides:
                send(pair, pair, small.at[3], small.at[2], peer)

    def gains_here():
        wait_bytes(gathered.at[pl.ds(0, 192)], small.at[2])

    steps["g"] = Calls(share_gains, spread_sides, gains_here)

    def token_halo(side):
        source = pl.ds(row_count - BLOCK, BLOCK) if side == 0 else pl.ds(0, BLOCK)
        return pltpu.make_async_remote_copy(
            src_ref=tokens.at[source],
            dst_ref=halo.at[side],
            send_sem=small.at[8 + side],
            recv_sem=small.at[10 + side],
            device_id=(y, blk + 1 - 2 * side),
            device_id_type=MESH,
        )

    def start_halos():
        pl.when(blk < 15)(lambda: token_halo(0).start())
        pl.when(blk > 0)(lambda: token_halo(1).start())

    def end_halos():
        pl.when(blk > 0)(lambda: token_halo(0).wait_recv())
        pl.when(blk < 15)(lambda: token_halo(1).wait_recv())

    steps["h"] = Calls(start_halos, end_halos)

    def globals_z():
        block = global_rows.at[slots.at(z, x, c)]
        for k in range(1, CHIPS_Z):
            send(block, block, small.at[4], small.at[5], device(y, (z + k) % CHIPS_Z, x, c))

    def globals_x():
        wait_bytes(global_rows.at[pl.ds(0, 3 * local_globals)], small.at[5])
        for k in range(CHIPS_Z):
            block = global_rows.at[slots.at(k, x, c)]
            send(block, block, small.at[4], small.at[6], device(y, z, 1 - x, c))

    def globals_pair():
        wait_bytes(global_rows.at[pl.ds(0, 4 * local_globals)], small.at[6])
        for k in range(CHIPS_Z):
            for j in range(2):
                block = global_rows.at[slots.at(k, j, c)]
                send(block, block, small.at[4], small.at[7], device(y, z, x, 1 - c))

    def globals_here():
        wait_bytes(global_rows.at[pl.ds(0, 8 * local_globals)], small.at[7])

    steps["i"] = Calls(globals_z, globals_x, globals_pair, globals_here)
    tick("s0")

    def scale_own(place):
        wide = tokens[place, :].astype(jnp.float32)
        attended[place, :] = (wide * inverse_rms(wide)).astype(low)

    tiled(row_count, scale_own)
    raw_sums[...] = block_sums(attended[...], local_globals)
    global_rows[slots.packed(blk), :] = raw_sums[...].astype(low)
    tick("s0b")
    wide_lengths = jnp.concatenate(
        [
            jnp.broadcast_to(lengths[0:1, i : i + 1], (1, 128))
            for i in range(lengths.shape[1])
        ],
        axis=0,
    )
    for block in range(blocks):
        spans[pl.ds(8 * block, 8), :] = span_rows(
            wide_lengths, first_row, block, far_rows, global_count
        )
    tick("s1")
    gain_rows[...] = spread_gains(gathered[...], feature_rows)
    tick("s2")
    norm_gain, global_gain, ffn_gain = gain_rows[0:1, :], gain_rows[1:2, :], gain_rows[2:3, :]

    def normed(part):
        wide = part.astype(jnp.float32)
        return (wide * inverse_rms(wide) * norm_gain).astype(low)

    def norm_own(place):
        to = pl.ds(pl.multiple_of(place.start + BLOCK, BLOCK), TILE)
        rows_in[to, :] = normed(tokens[place, :])

    tiled(row_count, norm_own)
    tick("s2b")
    group_sums[...] = block_sums(rows_in[pl.ds(BLOCK, row_count), :], local_globals)
    tick("s3")

    @pl.when(blk == 0)
    def _():
        halo[0] = jnp.zeros_like(halo[0])

    @pl.when(blk == 15)
    def _():
        halo[1] = jnp.zeros_like(halo[1])

    rows_in[pl.ds(0, BLOCK), :] = normed(halo[0])
    rows_in[pl.ds(BLOCK + row_count, BLOCK), :] = normed(halo[1])
    def turn(source, target, start):
        target[:, pl.ds(start, TILE)] = source[pl.ds(start, TILE), :].T

    for start in range(0, near_rows, TILE):
        tick("tr", start // TILE)
        turn(rows_in, rows_in_t, start)

    def project(weights, target, start, count, place, kind):
        def one(part):
            source = pl.ds(pl.multiple_of(part.start + start, BLOCK), TILE)
            to = pl.ds(pl.multiple_of(part.start + place, BLOCK), TILE)
            target[to, :] = dot_nn(rows_in[source, :], weights[...]).astype(low)

        tiled(count, one, ticks(kind, count // TILE))

    tick("s4")

    def global_norm(place):
        summed = global_rows[place, :].astype(jnp.float32) * norm_gain
        attended[place, :] = (summed * inverse_rms(summed) * global_gain).astype(low)

    tiled(global_count, global_norm)
    for window in range(2):
        select = window_select(spans, window, blocks, far_rows, global_count)
        rows_in[pl.ds(near_rows + window * far_rows, far_rows), :] = dot_nn(
            select, attended[...]
        ).astype(low)
    for start in range(near_rows, all_rows, TILE):
        tick("trf", (start - near_rows) // TILE)
        turn(rows_in, rows_in_t, start)
    tick("s5")
    project(w_key, keys, 0, all_rows, 0, "kn")
    for start in range(0, all_rows, TILE):
        tick("kt", start // TILE)
        turn(keys, keys_t, start)
    tick("s6")
    project(w_value, values, 0, all_rows, 0, "vn")
    tick("s7")
    project(w_query, query, BLOCK, row_count, 0, "qn")
    tick("s8")
    iterations = blocks * (HEADS // 2)

    def span_of(block):
        return Span(spans[pl.ds(pl.multiple_of(block * 8, 8), 8), :])

    @pl.loop(0, iterations // 2)
    def _(i):
        loop_tick("fa", i, iterations // 2)
        for j in range(2):
            block = (2 * i + j) % blocks
            attend_block(
                (2 * i) // blocks, block, span_of(block), query, keys, values, attended,
                near_rows, far_rows,
            )

    wait_bytes(global_rows.at[pl.ds(0, 15 * local_globals)], small.at[4])
    tick("m0")

    def after(place):
        return pl.ds(pl.multiple_of(place.start + row_count, TILE), TILE)

    def join(place):
        middle = tokens[place, :].astype(jnp.float32) + dot_nn(attended[place, :], w_out[...])
        grad_keys[place, :] = middle
        grad_keys[after(place), :] = middle
        low_hidden = (middle * inverse_rms(middle) * ffn_gain).astype(low)
        hidden[place, :] = low_hidden
        turned[:, place] = low_hidden.T
        grad_values[place, :] = jnp.zeros((TILE, width), jnp.float32)

    tiled(row_count, join, ticks("jn", 2))
    tick("m1")

    @pl.loop(0, CHUNKS)
    def _(chunk):
        loop_tick("ca", chunk, CHUNKS)
        half = chunk_width // 2
        rows = pl.ds(pl.multiple_of(chunk * hidden_rows, 128), hidden_rows)

        def feed(place):
            both = dot_nn(hidden[place, :], w_ff[chunk])
            gate, up = both[:, :half], both[:, half:]
            square = gate * gate
            bend = jnp.tanh(GELU_SCALE * gate * (1.0 + GELU_CUBIC * square))
            lift = 0.5 * (1.0 + bend)
            active = gate * lift
            slope = lift + 0.5 * gate * (1.0 - bend * bend) * (
                GELU_SCALE * (1.0 + 3.0 * GELU_CUBIC * square)
            )
            mixed[place, :] = (active * up).astype(low)
            grad_mixed = dot_nt(cotangent[place, :], w_down[rows, :])
            grad_both[place, pl.ds(0, half)] = (grad_mixed * up * slope).astype(low)
            grad_both[place, pl.ds(half, half)] = (grad_mixed * active).astype(low)
            grad_keys[after(place), :] += dot_nn(mixed[place, :], w_down[rows, :])
            grad_values[place, :] += dot_nt(grad_both[place, :], w_ff[chunk])

        tiled(row_count, feed, lambda i: pl.when(i == 1)(lambda: loop_tick("cb", chunk, CHUNKS)))
        for number in range(CHUNKS):
            pl.when(chunk == number)(functools.partial(ff_steps[number].step, 6))

        def gate_up_grad(place):
            w_ff[chunk, place, :] = dot_nn(turned[place, :], grad_both[...]).astype(low)

        tiled(width, gate_up_grad, lambda i: loop_tick("cg", chunk * 3 + i, 3 * CHUNKS))
        loop_tick("cw", chunk, CHUNKS)
        pl.when(chunk == 0)(lambda: steps["d"].step(6))
        w_down[rows, :] = dot(mixed[...], cotangent[...], ((0,), (0,))).astype(low)

    gain_grads[...] = jnp.zeros_like(gain_grads)

    def split(place):
        output[place, :] = grad_keys[after(place), :].astype(low)
        back, gain_grad = rms_back(grad_keys[place, :], ffn_gain, grad_values[place, :])
        gain_grads[2:3, :] += gain_grad
        grad_middle = cotangent[place, :].astype(jnp.float32) + back
        grad_tokens[place, :] = grad_middle
        branch = grad_middle.astype(low)
        rows_in[place, :] = branch
        hidden[place, :] = dot_nt(branch, w_out[...]).astype(low)
        turned[:, place] = attended[place, :].T

    tiled(row_count, split, ticks("sp", 2))
    tick("m2")
    steps["o"].step(6)

    def out_grad(place):
        w_out[place, :] = dot_nn(turned[place, :], rows_in[pl.ds(0, row_count), :]).astype(low)

    tiled(width, out_grad)
    tick("m3")

    def clear(place):
        grad_keys[place, :] = jnp.zeros((TILE, width), jnp.float32)
        grad_values[place, :] = jnp.zeros((TILE, width), jnp.float32)

    tiled(all_rows, clear)
    part_width = width // 3
    part_rounds = iterations // 6

    def back_part(third, target):
        @pl.loop(0, part_rounds)
        def _(j):
            i = third * part_rounds + j
            for number in range(part_rounds):
                todo = SCHEDULE.get("ba", {}).get(third * part_rounds + number, ())
                if todo:
                    pl.when(j == number)(functools.partial(run, todo))
            for k in range(2):
                block = (2 * i + k) % blocks
                attend_block_back(
                    (2 * i) // blocks, block, span_of(block), query, hidden, keys, keys_t, values,
                    query, grad_keys, grad_values, near_rows, far_rows,
                )

        lanes = pl.ds(third * part_width, part_width)

        def lower(place):
            keys[place, lanes] = grad_keys[place, lanes].astype(low)
            values[place, lanes] = grad_values[place, lanes].astype(low)

        tiled(all_rows, lower)

        def weight_grad(place):
            own = rows_in_t[place, pl.ds(BLOCK, row_count)]
            target[place, pl.ds(0, part_width)] = dot_nn(own, query[:, lanes]).astype(low)
            every = rows_in_t[place, :]
            target[place, pl.ds(part_width, part_width)] = dot_nn(every, keys[:, lanes]).astype(low)
            target[place, pl.ds(2 * part_width, part_width)] = dot_nn(
                every, values[:, lanes]
            ).astype(low)

        tiled(width, weight_grad, functools.partial(tick_part, third))
        tick("bt", third)

    def tick_part(third, index):
        for number in range(3):
            todo = SCHEDULE.get("wg", {}).get(3 * third + number, ())
            if todo:
                pl.when(index == number)(functools.partial(run, todo))

    for third, target in enumerate((part_key, part_value, part_query)):
        back_part(third, target)
    tick("e0")

    def grad_rows(start, count):
        part = pl.ds(start, count)
        return dot_nt(keys[part, :], w_key[...]) + dot_nt(values[part, :], w_value[...])

    for window in range(2):
        hidden[pl.ds(window * far_rows, far_rows), :] = grad_rows(
            near_rows + window * far_rows, far_rows
        ).astype(low)
    tick("e1b")
    selects = [window_select(spans, w, blocks, far_rows, global_count) for w in range(2)]
    for half in range(2):
        part = slice(half * (global_count // 2), (half + 1) * (global_count // 2))
        global_rows[part, :] = sum(
            dot(selects[w][:, part], hidden[pl.ds(w * far_rows, far_rows), :], ((0,), (0,)))
            for w in range(2)
        ).astype(low)

    def add_global(rows, ref, index):
        total = global_rows[rows, :].astype(jnp.float32)
        total = total + ref[slots.packed(index), :].astype(jnp.float32)
        global_rows[rows, :] = total.astype(low)

    def sums_pair():
        for k in range(CHIPS_Z):
            for j in range(2):
                send(
                    global_rows.at[slots.at(k, j, 1 - c)],
                    global_near.at[slots.packed(k * 2 + j)],
                    small.at[16],
                    small.at[17],
                    device(y, z, x, 1 - c),
                )

    def sums_x():
        wait_bytes(global_near, small.at[17])
        for k in range(CHIPS_Z):
            for j in range(2):
                add_global(slots.at(k, j, c), global_near, k * 2 + j)
        for k in range(CHIPS_Z):
            send(
                global_rows.at[slots.at(k, 1 - x, c)],
                global_mid.at[slots.packed(k)],
                small.at[16],
                small.at[18],
                device(y, z, 1 - x, c),
            )

    def sums_z():
        wait_bytes(global_mid, small.at[18])
        for k in range(CHIPS_Z):
            add_global(slots.at(k, x, c), global_mid, k)
        for k in range(1, CHIPS_Z):
            to_z = (z + k) % CHIPS_Z
            send(
                global_rows.at[slots.at(to_z, x, c)],
                global_far.at[slots.packed(k - 1)],
                small.at[16],
                small.at[19],
                device(y, to_z, x, c),
            )

    def sums_here():
        wait_bytes(global_far, small.at[19])

    steps["j"] = Calls(sums_pair, sums_x, sums_z, sums_here)
    tick("e1")
    halo[4] = grad_rows(0, BLOCK).astype(low)
    halo[5] = grad_rows(BLOCK + row_count, BLOCK).astype(low)
    def grad_halo(side):
        return pltpu.make_async_remote_copy(
            src_ref=halo.at[4 + side],
            dst_ref=halo.at[3 - side],
            send_sem=small.at[20 + side],
            recv_sem=small.at[22 + side],
            device_id=(y, blk - 1 + 2 * side),
            device_id_type=MESH,
        )

    def start_grad_halos():
        pl.when(blk > 0)(lambda: grad_halo(0).start())
        pl.when(blk < 15)(lambda: grad_halo(1).start())

    def end_grad_halos():
        pl.when(blk > 0)(lambda: grad_halo(1).wait_recv())
        pl.when(blk < 15)(lambda: grad_halo(0).wait_recv())

    steps["w"] = Calls(start_grad_halos, end_grad_halos)
    tick("e2")
    def gather_grads(place):
        rows = pl.ds(pl.multiple_of(place.start + BLOCK, BLOCK), TILE)
        grad_keys[place, :] = (
            dot_nt(keys[rows, :], w_key[...])
            + dot_nt(values[rows, :], w_value[...])
            + dot_nt(query[place, :], w_query[...])
        )

    tiled(row_count, gather_grads, ticks("gg", 2))
    tick("e6")

    @pl.when(blk == 0)
    def _():
        halo[2] = jnp.zeros_like(halo[2])

    @pl.when(blk == 15)
    def _():
        halo[3] = jnp.zeros_like(halo[3])

    grad_keys[pl.ds(0, BLOCK), :] += halo[2].astype(jnp.float32)
    grad_keys[pl.ds(row_count - BLOCK, BLOCK), :] += halo[3].astype(jnp.float32)

    def gain_sum(place):
        wide = tokens[place, :].astype(jnp.float32)
        gain_grads[0:1, :] += jnp.sum(
            grad_keys[place, :] * wide * inverse_rms(wide), axis=0, keepdims=True
        )

    tiled(row_count, gain_sum)
    tick("e6b")
    total = global_rows[slots.at(z, x, c), :].astype(jnp.float32)
    for k in range(CHIPS_Z - 1):
        total = total + global_far[slots.packed(k), :].astype(jnp.float32)
    grad_summed, grad_global_gain = rms_back(group_sums[...], global_gain, total)
    gain_grads[1:2, :] = grad_global_gain
    gain_grads[0:1, :] += jnp.sum(grad_summed * raw_sums[...], axis=0, keepdims=True)
    group_sums[...] = grad_summed
    gain_part[...] = pack_gains(gain_grads[...], feature_rows)

    def finish(place):
        few = TILE // GBLK
        sums = group_sums[pl.ds(pl.multiple_of(place.start // GBLK, 8), few), :]
        grad_normed = grad_keys[place, :] + jnp.broadcast_to(
            sums[:, None, :], (few, GBLK, width)
        ).reshape(TILE, width)
        grad_tokens[place, :] += rms_back(
            tokens[place, :].astype(jnp.float32), norm_gain, grad_normed
        )[0]

    def gain_pair(pair_y, k, pair_x):
        return pl.ds(pl.multiple_of((pair_y * 8 + k * 2 + pair_x) * 16, 16), 16)

    def gains_sides():
        for index, peer in enumerate(sides):
            side_y = y if index == 0 else 1 - y
            side_x = x if index == 1 else 1 - x
            for k in range(CHIPS_Z):
                send(
                    gain_part.at[gain_pair(side_y, k, side_x)],
                    gain_side.at[index, pl.ds(k * 16, 16)],
                    small.at[13],
                    small.at[12],
                    peer,
                )

    def gains_column():
        wait_bytes(gain_side, small.at[12])
        for k in range(CHIPS_Z):
            rows = gain_pair(y, k, x)
            place = pl.ds(k * 16, 16)
            gain_part[rows, :] += gain_side[0, place, :] + gain_side[1, place, :] + gain_side[2, place, :]
        place = z * 2 + c
        gain_column[pl.ds(pl.multiple_of(place * 8, 8), 8), :] = gain_part[
            pl.ds(pl.multiple_of(me * 8, 8), 8), :
        ]
        for k in range(CHIPS_Z):
            for j in range(2):
                if k == 0 and j == 0:
                    peer_z, peer_c = z, 1 - c
                elif k == 0:
                    continue
                else:
                    peer_z, peer_c = (z + k) % CHIPS_Z, j
                peer_me = y * 16 + peer_z * 4 + x * 2 + peer_c
                send(
                    gain_part.at[pl.ds(pl.multiple_of(peer_me * 8, 8), 8)],
                    gain_column.at[pl.ds(pl.multiple_of(place * 8, 8), 8)],
                    small.at[15],
                    small.at[14],
                    device(y, peer_z, x, peer_c),
                )

    def gains_done():
        wait_bytes(gain_column.at[pl.ds(0, 56)], small.at[14])

    steps["l"] = Calls(gains_sides, gains_column, gains_done)
    tick("e7")
    tiled(row_count, finish, ticks("fi", 2))
    tick("e8")
    gain_out[...] = jnp.sum(gain_column[...].reshape(8, 8, 128), axis=0)
    for name, _ in targets:
        steps[name].step(6)
    for one in [steps["q"], steps["k"], steps["v"]]:
        one.step(6)
    wait_bytes(gathered.at[pl.ds(0, 56)], small.at[1])
    wait_bytes(gathered.at[pl.ds(0, 192)], small.at[3])
    wait_bytes(global_rows.at[pl.ds(0, 15 * local_globals)], small.at[16])
    wait_bytes(gathered.at[pl.ds(0, 192)], small.at[13])
    wait_bytes(gathered.at[pl.ds(0, 56)], small.at[15])
    pl.when(blk < 15)(lambda: token_halo(0).wait_send())
    pl.when(blk > 0)(lambda: token_halo(1).wait_send())
    pl.when(blk > 0)(lambda: grad_halo(0).wait_send())
    pl.when(blk < 15)(lambda: grad_halo(1).wait_send())


def layer(lengths, gains, tokens, cotangent, shards, far_rows, global_count):
    row_count, width = tokens.shape
    all_rows = row_count + 2 * BLOCK + 2 * far_rows
    local_globals = row_count // GBLK
    down_rows = shards[4].shape[0]
    chunk_width = 2 * shards[5].shape[1] // CHUNKS
    vmem = pl.BlockSpec(memory_space=pltpu.VMEM)
    anywhere = pl.BlockSpec(memory_space=pl.ANY)
    low, wide = jnp.bfloat16, jnp.float32
    shard_shapes = [(width // 32, width)] * 4 + [(down_rows, width)]
    shard_shapes += [(width // 32, chunk_width)] * CHUNKS
    buffers = []
    names = ("ra", "rb", "rc", "ro", "rd") + NAMES[12:16]
    for name, (rows, columns) in zip(names, shard_shapes):
        counts = (24, 4, 2) if name in Z_FIRST else (16, 8, 6)
        buffers += reduce_scratch(rows, columns // 2, low, counts)
    return pl.pallas_call(
        layer_kernel,
        out_shape=[
            jax.ShapeDtypeStruct((row_count, width), low),
            jax.ShapeDtypeStruct((row_count, width), wide),
            jax.ShapeDtypeStruct((8, 128), wide),
        ]
        + [jax.ShapeDtypeStruct(shape, wide) for shape in shard_shapes],
        in_specs=[vmem] * 6 + [anywhere] * 7,
        out_specs=[vmem] * 12,
        scratch_shapes=[pltpu.VMEM((width, width), low)] * 4
        + [
            pltpu.VMEM((32 * down_rows, width), low),
            pltpu.VMEM((CHUNKS, width, chunk_width), low),
            pltpu.VMEM((all_rows, width), low),
            pltpu.VMEM((width, all_rows), low),
            pltpu.VMEM((all_rows, width), low),
            pltpu.VMEM((width, all_rows), low),
            pltpu.VMEM((all_rows, width), low),
            pltpu.VMEM((row_count, width), low),
            pltpu.VMEM((row_count, width), low),
            pltpu.VMEM((row_count, width), low),
            pltpu.VMEM((width, row_count), low),
            pltpu.VMEM((row_count, chunk_width // 2), low),
            pltpu.VMEM((row_count, chunk_width), low),
            pltpu.VMEM((all_rows, width), wide),
            pltpu.VMEM((all_rows, width), wide),
            pltpu.VMEM((8, width), wide),
            pltpu.VMEM((width, width), low),
            pltpu.VMEM((width, width), low),
            pltpu.VMEM((8 * row_count // BLOCK, 128), jnp.int32),
            pltpu.VMEM((8, width), wide),
            pltpu.VMEM((256, 128), wide),
            pltpu.VMEM((256, 128), wide),
            pltpu.VMEM((3, 64, 128), wide),
            pltpu.VMEM((64, 128), wide),
            pltpu.VMEM((local_globals, width), wide),
            pltpu.VMEM((6, BLOCK, width), low),
            pltpu.VMEM((global_count, width), low),
            pltpu.VMEM((8 * local_globals, width), low),
            pltpu.VMEM((4 * local_globals, width), low),
            pltpu.VMEM((3 * local_globals, width), low),
        ]
        + buffers
        + [
            pltpu.SemaphoreType.DMA((18, 5)),
            pltpu.SemaphoreType.DMA((18, 3)),
            pltpu.SemaphoreType.DMA((SMALL_SEMS,)),
            pltpu.VMEM((8, 128), wide),
            pltpu.VMEM((local_globals, width), wide),
        ],
        compiler_params=pltpu.CompilerParams(
            collective_id=0, has_side_effects=True, vmem_limit_bytes=VMEM_BYTES
        ),
        name="layer",
    )(lengths, *gains, tokens, cotangent, *shards)


def settle_kernel(*refs):
    ins, outs = refs[:12], refs[12:]
    outs[0][...] = ins[0][...]
    outs[1][...] = ins[1][...]
    rows = outs[2].shape[0]
    for i in range(3):
        outs[2 + i][...] = ins[2][i, pl.ds(0, rows)]
    thirds, chunks = ins[3:6], ins[8:12]
    part = thirds[0].shape[1] // 3
    for i in range(3):
        for third, ref in enumerate(thirds):
            outs[5 + i][:, pl.ds(third * part, part)] = ref[:, pl.ds(i * part, part)]
    outs[8][...] = ins[6][...]
    outs[9][...] = ins[7][...]
    half = chunks[0].shape[1] // 2
    for i in range(2):
        for chunk, ref in enumerate(chunks):
            outs[10 + i][:, pl.ds(chunk * half, half)] = ref[:, pl.ds(i * half, half)]


def settle(outs, rows):
    vmem = pl.BlockSpec(memory_space=pltpu.VMEM)
    wide = jnp.float32
    width = outs[0].shape[1]
    ff_width = outs[8].shape[1] // 2 * CHUNKS
    return pl.pallas_call(
        settle_kernel,
        out_shape=[jax.ShapeDtypeStruct(one.shape, one.dtype) for one in outs[:2]]
        + [jax.ShapeDtypeStruct((rows,), wide)] * 3
        + [jax.ShapeDtypeStruct((rows, width), wide)] * 4
        + [jax.ShapeDtypeStruct(outs[7].shape, wide)]
        + [jax.ShapeDtypeStruct((rows, ff_width), wide)] * 2,
        in_specs=[vmem] * 12,
        out_specs=[vmem] * 12,
        name="settle",
    )(*outs)


def per_device(
    tokens, lengths, norm_gain, global_gain, w_query, w_key, w_value, w_out,
    ffn_gain, w_gate, w_up, w_down, cotangent,
):
    global_count = tokens.shape[0] * lax.axis_size("blk") // GBLK
    gains = (norm_gain, global_gain, ffn_gain)
    shards = (w_query, w_key, w_value, w_out, w_down, w_gate, w_up)
    outs = layer(lengths, gains, tokens, cotangent, shards, global_count // 2, global_count)
    settled = settle(outs, norm_gain.shape[0])
    output, grad_tokens, first, second, third = settled[:5]
    return (output, grad_tokens, first, second, *settled[5:9], third, *settled[10:], settled[9])


def fits(mesh):
    return mesh.shape["seq"] == 2 and mesh.shape["blk"] == 16


def solution(mesh):
    return jax.shard_map(
        per_device if fits(mesh) else per_device_general,
        mesh=mesh,
        in_specs=(
            P(("seq", "blk"), None),
            P("seq", None),
            P(("seq", "blk")),
            P(("seq", "blk")),
            P(("seq", "blk"), None),
            P(("seq", "blk"), None),
            P(("seq", "blk"), None),
            P(("seq", "blk"), None),
            P(("seq", "blk")),
            P(("seq", "blk"), None),
            P(("seq", "blk"), None),
            P(("seq", "blk"), None),
            P(("seq", "blk"), None),
        ),
        out_specs=(
            P(("seq", "blk"), None),
            P(("seq", "blk"), None),
            P(("seq", "blk")),
            P(("seq", "blk")),
            P(("seq", "blk"), None),
            P(("seq", "blk"), None),
            P(("seq", "blk"), None),
            P(("seq", "blk"), None),
            P(("seq", "blk")),
            P(("seq", "blk"), None),
            P(("seq", "blk"), None),
            P(("seq", "blk"), None),
        ),
        check_vma=False,
    )
```

```python
import functools

import jax
import jax.numpy as jnp
from jax import lax
from jax.experimental import pallas as pl
from jax.experimental.pallas import tpu as pltpu
from jax.sharding import PartitionSpec as P


D = 768
HEADS = 12
HEAD_DIM = 64
GBLK = 16
BLOCK = 128
LONGEST = 16384


EPSILON = 1e-06
MASKED = -1e30
GELU_SCALE = 0.7978845608028654
GELU_CUBIC = 0.044715


def with_halo(block, sides, width):
    for axis, dim in sides:
        count = lax.axis_size(axis)
        forward = [(i, i + 1) for i in range(count - 1)]
        backward = [(target, source) for source, target in forward]
        low = lax.ppermute(
            lax.slice_in_dim(block, block.shape[dim] - width, None, axis=dim), axis, forward
        )
        high = lax.ppermute(lax.slice_in_dim(block, 0, width, axis=dim), axis, backward)
        block = jnp.concatenate([low, block, high], axis=dim)
    return block


def rms_norm(values, scales):
    return values * lax.rsqrt(jnp.mean(values * values, axis=-1, keepdims=True) + EPSILON) * scales


def gelu_tanh(values):
    return (
        0.5
        * values
        * (1.0 + jnp.tanh(GELU_SCALE * (values + GELU_CUBIC * values * values * values)))
    )


def gated(gate_part, up_part):
    return gelu_tanh(gate_part) * up_part


def sequence_of(positions, seq_ends):
    return jnp.sum((positions[:, None] >= seq_ends[None, :]).astype(jnp.int32), axis=1)


def matmul(left_side, right_side):
    return jnp.dot(left_side, right_side, preferred_element_type=jnp.float32)


def matmul_left(left_side, right_side):
    return jnp.einsum("ta,tb->ab", left_side, right_side, preferred_element_type=jnp.float32)


def matmul_right(left_side, right_side):
    return jnp.einsum("ta,ba->tb", left_side, right_side, preferred_element_type=jnp.float32)


def windows(extended, row_count):
    block_count = row_count // BLOCK
    pieces = [
        extended[offset * BLOCK : offset * BLOCK + row_count].reshape(
            block_count, BLOCK, extended.shape[-1]
        )
        for offset in range(3)
    ]
    return jnp.concatenate(pieces, axis=1)


def unwindow(window_grads, row_count):
    channels = window_grads.shape[-1]
    summed_grad = jnp.zeros((row_count + 2 * BLOCK, channels), jnp.float32)
    for offset in range(3):
        piece_grad = window_grads[:, offset * BLOCK : (offset + 1) * BLOCK].reshape(
            row_count, channels
        )
        summed_grad = summed_grad + jnp.pad(
            piece_grad, ((offset * BLOCK, (2 - offset) * BLOCK), (0, 0))
        )
    return summed_grad


def head_scores(query_head, near_keys, far_keys, near_mask, far_mask):
    block_count = near_keys.shape[0]
    query_blocks = query_head.reshape(block_count, BLOCK, HEAD_DIM)
    near_scores = jnp.einsum(
        "nqd,nkd->nqk", query_blocks, near_keys, preferred_element_type=jnp.float32
    )
    far_scores = jnp.einsum("qd,kd->qk", query_head, far_keys, preferred_element_type=jnp.float32)
    return (jnp.where(near_mask, near_scores, MASKED), jnp.where(far_mask, far_scores, MASKED))


def per_device_general(
    tokens,
    lengths,
    norm_gain,
    global_gain,
    w_query,
    w_key,
    w_value,
    w_out,
    ffn_gain,
    w_gate,
    w_up,
    w_down,
    cotangent,
):
    row_count = tokens.shape[0]
    inner_dim = HEADS * HEAD_DIM
    block_count = row_count // BLOCK
    local_globals = row_count // GBLK
    group_tokens = row_count * lax.axis_size("blk")
    global_count = group_tokens // GBLK
    longest_len = min(LONGEST, group_tokens // 2)
    span_rows = min(global_count, 2 * (longest_len // GBLK) + local_globals)
    attn_full = (
        lax.all_gather(norm_gain, ("seq", "blk"), axis=0, tiled=True),
        lax.all_gather(global_gain, ("seq", "blk"), axis=0, tiled=True),
        lax.all_gather(w_query, ("seq", "blk"), axis=0, tiled=True),
        lax.all_gather(w_key, ("seq", "blk"), axis=0, tiled=True),
        lax.all_gather(w_value, ("seq", "blk"), axis=0, tiled=True),
        lax.all_gather(w_out, ("seq", "blk"), axis=0, tiled=True),
    )
    seq_ends = jnp.cumsum(lengths[0])
    first_row = lax.axis_index("blk") * row_count
    span_start = jnp.clip(first_row // GBLK - longest_len // GBLK, 0, global_count - span_rows)
    query_pos = first_row + jnp.arange(row_count, dtype=jnp.int32)
    query_seq = sequence_of(query_pos, seq_ends)
    key_pos = first_row - BLOCK + jnp.arange(row_count + 2 * BLOCK, dtype=jnp.int32)
    inside = (key_pos >= 0) & (key_pos < group_tokens)
    key_seq = jnp.where(inside, sequence_of(key_pos, seq_ends), -1)
    global_seq = sequence_of((span_start + jnp.arange(span_rows, dtype=jnp.int32)) * GBLK, seq_ends)
    query_pos_win = query_pos.reshape(block_count, BLOCK)
    query_seq_win = query_seq.reshape(block_count, BLOCK)
    key_pos_win = windows(key_pos[:, None], row_count)[:, :, 0]
    key_seq_win = windows(key_seq[:, None], row_count)[:, :, 0]
    near_mask = (jnp.abs(query_pos_win[:, :, None] - key_pos_win[:, None, :]) <= BLOCK - 1) & (
        query_seq_win[:, :, None] == key_seq_win[:, None, :]
    )
    far_mask = query_seq[:, None] == global_seq[None, :]
    tokens_full = tokens.astype(jnp.float32)
    normed_full, normed_pull = jax.vjp(rms_norm, tokens_full, attn_full[0].astype(jnp.float32))
    normed = normed_full.astype(jnp.bfloat16)
    queries = matmul(normed, attn_full[2]).astype(jnp.bfloat16)
    key_rows = matmul(normed, attn_full[3]).astype(jnp.bfloat16)
    value_rows = matmul(normed, attn_full[4]).astype(jnp.bfloat16)
    local_kv = jnp.concatenate([key_rows, value_rows], axis=1)
    extended = with_halo(local_kv, (("blk", 0),), BLOCK)
    near_kv = windows(extended, row_count)
    summed = jnp.sum(normed.astype(jnp.float32).reshape(local_globals, GBLK, D), axis=1)
    global_full, global_pull = jax.vjp(rms_norm, summed, attn_full[1].astype(jnp.float32))
    global_in = global_full.astype(jnp.bfloat16)
    own_global = jnp.concatenate(
        [
            matmul(global_in, attn_full[3]).astype(jnp.bfloat16),
            matmul(global_in, attn_full[4]).astype(jnp.bfloat16),
        ],
        axis=1,
    )
    global_kv = lax.all_gather(own_global, "blk", axis=0, tiled=True)
    span_kv = lax.dynamic_slice_in_dim(global_kv, span_start, span_rows, 0)

    def head_slices(head_index):
        column = head_index * HEAD_DIM
        query_head = lax.dynamic_slice_in_dim(queries, column, HEAD_DIM, 1)
        near_keys = lax.dynamic_slice_in_dim(near_kv, column, HEAD_DIM, 2)
        near_values = lax.dynamic_slice_in_dim(near_kv, inner_dim + column, HEAD_DIM, 2)
        far_keys = lax.dynamic_slice_in_dim(span_kv, column, HEAD_DIM, 1)
        far_values = lax.dynamic_slice_in_dim(span_kv, inner_dim + column, HEAD_DIM, 1)
        return (column, query_head, near_keys, near_values, far_keys, far_values)

    def head_forward(head_index, carry):
        attended_rows, log_sums = carry
        column, query_head, near_keys, near_values, far_keys, far_values = head_slices(head_index)
        near_scores, far_scores = head_scores(query_head, near_keys, far_keys, near_mask, far_mask)
        highest = jnp.maximum(
            jnp.max(near_scores, axis=2).reshape(row_count), jnp.max(far_scores, axis=1)
        )
        near_exp = jnp.exp(near_scores - highest.reshape(block_count, BLOCK, 1))
        far_exp = jnp.exp(far_scores - highest[:, None])
        denominator = jnp.sum(near_exp, axis=2).reshape(row_count) + jnp.sum(far_exp, axis=1)
        near_probs = (near_exp / denominator.reshape(block_count, BLOCK, 1)).astype(jnp.bfloat16)
        far_probs = (far_exp / denominator[:, None]).astype(jnp.bfloat16)
        head_out = jnp.einsum(
            "nqk,nkd->nqd", near_probs, near_values, preferred_element_type=jnp.float32
        ).reshape(row_count, HEAD_DIM)
        head_out = head_out + jnp.einsum(
            "qk,kd->qd", far_probs, far_values, preferred_element_type=jnp.float32
        )
        attended_rows = lax.dynamic_update_slice_in_dim(attended_rows, head_out, column, 1)
        log_sums = lax.dynamic_update_index_in_dim(
            log_sums, highest + jnp.log(denominator), head_index, 0
        )
        return (attended_rows, log_sums)

    attended_rows, log_sums = lax.fori_loop(
        0,
        HEADS,
        head_forward,
        (
            jnp.zeros((row_count, inner_dim), jnp.float32),
            jnp.zeros((HEADS, row_count), jnp.float32),
        ),
    )
    attended = attended_rows.astype(jnp.bfloat16)
    middle = tokens_full + matmul(attended, attn_full[5])
    ffn_full = (
        lax.all_gather(ffn_gain, ("seq", "blk"), axis=0, tiled=True),
        lax.all_gather(w_gate, ("seq", "blk"), axis=0, tiled=True),
        lax.all_gather(w_up, ("seq", "blk"), axis=0, tiled=True),
        lax.all_gather(w_down, ("seq", "blk"), axis=0, tiled=True),
    )
    hidden_full, hidden_pull = jax.vjp(rms_norm, middle, ffn_full[0].astype(jnp.float32))
    hidden = hidden_full.astype(jnp.bfloat16)
    gate_pre = matmul(hidden, ffn_full[1])
    up_pre = matmul(hidden, ffn_full[2])
    gated_rows, gated_pull = jax.vjp(gated, gate_pre, up_pre)
    mixed = gated_rows.astype(jnp.bfloat16)
    output = (middle + matmul(mixed, ffn_full[3])).astype(jnp.bfloat16)
    ffn_back = (
        lax.all_gather(ffn_gain, ("seq", "blk"), axis=0, tiled=True),
        lax.all_gather(w_gate, ("seq", "blk"), axis=0, tiled=True),
        lax.all_gather(w_up, ("seq", "blk"), axis=0, tiled=True),
        lax.all_gather(w_down, ("seq", "blk"), axis=0, tiled=True),
    )
    grad_down = matmul_left(mixed, cotangent)
    grad_mixed = matmul_right(cotangent, ffn_back[3])
    grad_gate_full, grad_up_full = gated_pull(grad_mixed)
    grad_gate = grad_gate_full.astype(jnp.bfloat16)
    grad_up = grad_up_full.astype(jnp.bfloat16)
    grad_wgate = matmul_left(hidden, grad_gate)
    grad_wup = matmul_left(hidden, grad_up)
    grad_hidden = matmul_right(grad_gate, ffn_back[1]) + matmul_right(grad_up, ffn_back[2])
    grad_middle_norm, grad_ffn_gain = hidden_pull(grad_hidden)
    grad_middle = cotangent.astype(jnp.float32) + grad_middle_norm
    attn_back = (
        lax.all_gather(norm_gain, ("seq", "blk"), axis=0, tiled=True),
        lax.all_gather(global_gain, ("seq", "blk"), axis=0, tiled=True),
        lax.all_gather(w_query, ("seq", "blk"), axis=0, tiled=True),
        lax.all_gather(w_key, ("seq", "blk"), axis=0, tiled=True),
        lax.all_gather(w_value, ("seq", "blk"), axis=0, tiled=True),
        lax.all_gather(w_out, ("seq", "blk"), axis=0, tiled=True),
    )
    grad_branch = grad_middle.astype(jnp.bfloat16)
    grad_wout = matmul_left(attended, grad_branch)
    grad_attended = matmul_right(grad_branch, attn_back[5]).astype(jnp.bfloat16)

    def head_backward(head_index, carry):
        grad_query_rows, grad_near, grad_far = carry
        column, query_head, near_keys, near_values, far_keys, far_values = head_slices(head_index)
        near_scores, far_scores = head_scores(query_head, near_keys, far_keys, near_mask, far_mask)
        lse_head = log_sums[head_index]
        near_probs = jnp.exp(near_scores - lse_head.reshape(block_count, BLOCK, 1))
        far_probs = jnp.exp(far_scores - lse_head[:, None])
        grad_head = lax.dynamic_slice_in_dim(grad_attended, column, HEAD_DIM, 1)
        grad_blocks = grad_head.reshape(block_count, BLOCK, HEAD_DIM)
        query_blocks = query_head.reshape(block_count, BLOCK, HEAD_DIM)
        near_dprobs = jnp.einsum(
            "nqd,nkd->nqk", grad_blocks, near_values, preferred_element_type=jnp.float32
        )
        far_dprobs = jnp.einsum(
            "qd,kd->qk", grad_head, far_values, preferred_element_type=jnp.float32
        )
        delta_rows = jnp.sum(near_probs * near_dprobs, axis=2).reshape(row_count) + jnp.sum(
            far_probs * far_dprobs, axis=1
        )
        near_grad_scores = (
            near_probs * (near_dprobs - delta_rows.reshape(block_count, BLOCK, 1))
        ).astype(jnp.bfloat16)
        far_grad_scores = (far_probs * (far_dprobs - delta_rows[:, None])).astype(jnp.bfloat16)
        head_dquery = jnp.einsum(
            "nqk,nkd->nqd", near_grad_scores, near_keys, preferred_element_type=jnp.float32
        ).reshape(row_count, HEAD_DIM)
        head_dquery = head_dquery + jnp.einsum(
            "qk,kd->qd", far_grad_scores, far_keys, preferred_element_type=jnp.float32
        )
        near_dkey = jnp.einsum(
            "nqk,nqd->nkd", near_grad_scores, query_blocks, preferred_element_type=jnp.float32
        )
        near_dvalue = jnp.einsum(
            "nqk,nqd->nkd",
            near_probs.astype(jnp.bfloat16),
            grad_blocks,
            preferred_element_type=jnp.float32,
        )
        far_dkey = jnp.einsum(
            "qk,qd->kd", far_grad_scores, query_head, preferred_element_type=jnp.float32
        )
        far_dvalue = jnp.einsum(
            "qk,qd->kd",
            far_probs.astype(jnp.bfloat16),
            grad_head,
            preferred_element_type=jnp.float32,
        )
        grad_query_rows = lax.dynamic_update_slice_in_dim(grad_query_rows, head_dquery, column, 1)
        grad_near = lax.dynamic_update_slice_in_dim(grad_near, near_dkey, column, 2)
        grad_near = lax.dynamic_update_slice_in_dim(grad_near, near_dvalue, inner_dim + column, 2)
        grad_far = lax.dynamic_update_slice_in_dim(grad_far, far_dkey, column, 1)
        grad_far = lax.dynamic_update_slice_in_dim(grad_far, far_dvalue, inner_dim + column, 1)
        return (grad_query_rows, grad_near, grad_far)

    grad_query_rows, grad_near, grad_far = lax.fori_loop(
        0,
        HEADS,
        head_backward,
        (
            jnp.zeros((row_count, inner_dim), jnp.float32),
            jnp.zeros((block_count, 3 * BLOCK, 2 * inner_dim), jnp.float32),
            jnp.zeros((span_rows, 2 * inner_dim), jnp.float32),
        ),
    )
    grad_extended = unwindow(grad_near, row_count)
    rim_rows = jnp.concatenate([grad_extended[:BLOCK], grad_extended[row_count + BLOCK :]], axis=0)
    returned = with_halo(rim_rows.astype(jnp.bfloat16), (("blk", 0),), BLOCK).astype(rim_rows.dtype)
    grad_kv = grad_extended[BLOCK : row_count + BLOCK]
    grad_kv = grad_kv + jnp.pad(returned[:BLOCK], ((0, row_count - BLOCK), (0, 0)))
    grad_kv = grad_kv + jnp.pad(returned[3 * BLOCK :], ((row_count - BLOCK, 0), (0, 0)))
    grad_kv = grad_kv.astype(jnp.bfloat16)
    grad_key = grad_kv[:, :inner_dim]
    grad_value = grad_kv[:, inner_dim:]
    group_far = lax.dynamic_update_slice_in_dim(
        jnp.zeros((global_count, 2 * inner_dim), jnp.float32), grad_far, span_start, 0
    )
    own_global_grad = lax.psum_scatter(group_far, "blk", scatter_dimension=0, tiled=True).astype(
        jnp.bfloat16
    )
    grad_global_key = own_global_grad[:, :inner_dim]
    grad_global_value = own_global_grad[:, inner_dim:]
    grad_query = grad_query_rows.astype(jnp.bfloat16)
    grad_wquery = matmul_left(normed, grad_query)
    grad_wkey = matmul_left(normed, grad_key) + matmul_left(global_in, grad_global_key)
    grad_wvalue = matmul_left(normed, grad_value) + matmul_left(global_in, grad_global_value)
    grad_normed = (
        matmul_right(grad_query, attn_back[2])
        + matmul_right(grad_key, attn_back[3])
        + matmul_right(grad_value, attn_back[4])
    )
    grad_global_in = matmul_right(grad_global_key, attn_back[3]) + matmul_right(
        grad_global_value, attn_back[4]
    )
    grad_summed, grad_global_gain = global_pull(grad_global_in)
    grad_normed = (grad_normed.reshape(local_globals, GBLK, D) + grad_summed[:, None, :]).reshape(
        row_count, D
    )
    grad_tokens_norm, grad_norm_gain = normed_pull(grad_normed)
    grad_tokens = grad_middle + grad_tokens_norm
    every_grad = (
        lax.psum_scatter(grad_norm_gain, ("seq", "blk"), scatter_dimension=0, tiled=True),
        lax.psum_scatter(grad_global_gain, ("seq", "blk"), scatter_dimension=0, tiled=True),
        lax.psum_scatter(grad_wquery, ("seq", "blk"), scatter_dimension=0, tiled=True),
        lax.psum_scatter(grad_wkey, ("seq", "blk"), scatter_dimension=0, tiled=True),
        lax.psum_scatter(grad_wvalue, ("seq", "blk"), scatter_dimension=0, tiled=True),
        lax.psum_scatter(grad_wout, ("seq", "blk"), scatter_dimension=0, tiled=True),
        lax.psum_scatter(grad_ffn_gain, ("seq", "blk"), scatter_dimension=0, tiled=True),
        lax.psum_scatter(grad_wgate, ("seq", "blk"), scatter_dimension=0, tiled=True),
        lax.psum_scatter(grad_wup, ("seq", "blk"), scatter_dimension=0, tiled=True),
        lax.psum_scatter(grad_down, ("seq", "blk"), scatter_dimension=0, tiled=True),
    )
    return (
        output,
        grad_tokens,
        every_grad[0],
        every_grad[1],
        every_grad[2],
        every_grad[3],
        every_grad[4],
        every_grad[5],
        every_grad[6],
        every_grad[7],
        every_grad[8],
        every_grad[9],
    )


MESH = pl.DeviceIdType.MESH
CHIPS_Z = 4
NEVER = 1 << 20
VMEM_BYTES = 64 * 1024 * 1024 - 65536


def dot(a, b, dims, precision=None):
    return lax.dot_general(
        a, b, (dims, ((), ())), precision=precision, preferred_element_type=jnp.float32
    )


def dot_nn(a, b):
    return dot(a, b, ((1,), (0,)))


def dot_nt(a, b):
    return dot(a, b, ((1,), (1,)))


def coords():
    y = lax.axis_index("seq")
    blk = lax.axis_index("blk")
    return y, blk // 4, (blk // 2) % 2, blk % 2


def device(y, z, x, c):
    return (y, z * 4 + x * 2 + c)


def send(src, dst, send_sem, recv_sem, target):
    pltpu.make_async_remote_copy(
        src_ref=src,
        dst_ref=dst,
        send_sem=send_sem,
        recv_sem=recv_sem,
        device_id=target,
        device_id_type=MESH,
    ).start()


def wait_bytes(ref, sem):
    pltpu.make_async_copy(ref, ref, sem).wait()


def column_peers():
    y, z, x, c = coords()
    peers = [device(y, z, x, 1 - c)]
    for k in range(1, CHIPS_Z):
        peers += [device(y, (z + k) % CHIPS_Z, x, j) for j in range(2)]
    return peers


def side_peers():
    y, z, x, c = coords()
    return [device(y, z, 1 - x, c), device(1 - y, z, x, c), device(1 - y, z, 1 - x, c)]


def greet():
    y, z, x, c = coords()
    blk = lax.axis_index("blk")
    barrier = pltpu.get_barrier_semaphore()
    peers = column_peers() + side_peers()
    for peer in peers:
        pl.semaphore_signal(barrier, inc=1, device_id=peer, device_id_type=MESH)

    @pl.when(blk > 0)
    def _():
        pl.semaphore_signal(barrier, inc=1, device_id=(y, blk - 1), device_id_type=MESH)

    @pl.when(blk < 15)
    def _():
        pl.semaphore_signal(barrier, inc=1, device_id=(y, blk + 1), device_id_type=MESH)

    inner = jnp.where((blk > 0) & (blk < 15), 1, 0)
    pl.semaphore_wait(barrier, len(peers) + 1 + inner)


class Slots:
    def __init__(self, rows, half, first=None):
        self.rows, self.half = rows, half
        self.y, self.z, self.x, self.c = coords()
        self.side = self.c if first is None else first

    def plane(self, c):
        return pl.ds(pl.multiple_of(c * self.half, 128), self.half)

    def slot_rows(self, y, z, x):
        return pl.ds(pl.multiple_of((y * 8 + z * 2 + x) * (2 * self.rows), 8), 2 * self.rows)

    def near_pair(self, j):
        y, x, side = self.y, self.x, self.side
        return y * (1 - side) + j * side, x * side + j * (1 - side)

    def far_pair(self, j):
        y, x, side = self.y, self.x, self.side
        return (1 - y) * (1 - side) + j * side, (1 - x) * side + j * (1 - side)

    def near_slot(self):
        y, x, side = self.y, self.x, self.side
        return y * (1 - side) + (1 - y) * side, x * side + (1 - x) * (1 - side)

    def near_peer(self):
        slot_y, slot_x = self.near_slot()
        return device(slot_y, self.z, slot_x, self.c)

    def far_peer(self):
        y, z, x, c, side = self.y, self.z, self.x, self.c, self.side
        return device(y + (1 - side) * (1 - 2 * y), z, x + side * (1 - 2 * x), c)


class Gather(Slots):
    def __init__(self, shard, full, recv, sent, first=None):
        if isinstance(shard, tuple):
            super().__init__(*shard[0].shape, first)
        else:
            super().__init__(shard.shape[0], shard.shape[1] // 2, first)
        self.shard, self.full, self.recv, self.sent = shard, full, recv, sent

    def span(self, rows):
        return self.full.at[pl.ds(0, rows), pl.ds(0, self.half)]

    def mine(self):
        index = self.y * 16 + self.z * 4 + self.x * 2 + self.c
        return pl.ds(pl.multiple_of(index * self.rows, 8), self.rows)

    def slot(self, y, z, x):
        return self.full.at[self.slot_rows(y, z, x), self.plane(self.c)]

    def open(self, own, other, c):
        y, z, x = self.y, self.z, self.x
        target = self.full.at[self.mine(), self.plane(1 - c)]
        send(other, target, self.sent.at[0], self.recv.at[0], device(y, z, x, 1 - c))
        target = self.full.at[self.mine(), self.plane(c)]
        pltpu.make_async_copy(own, target, self.sent.at[2]).start()

    def own_here(self):
        wait_bytes(self.full.at[self.mine(), self.plane(self.c)], self.sent.at[2])

    def step(self, number):
        y, z, x, c, rows = self.y, self.z, self.x, self.c, self.rows
        if number == 0 and isinstance(self.shard, tuple):
            for core in range(2):
                own, other = self.shard[core], self.shard[1 - core]
                pl.when(c == core)(functools.partial(self.open, own, other, core))
        elif number == 0:
            self.open(self.shard.at[:, self.plane(c)], self.shard.at[:, self.plane(1 - c)], c)
        if number == 1:
            self.own_here()
            wait_bytes(self.span(rows), self.recv.at[0])
            block = self.slot(y, z, x)
            for k in range(1, CHIPS_Z):
                target = device(y, (z + k) % CHIPS_Z, x, c)
                send(block, block, self.sent.at[1], self.recv.at[1], target)
        if number == 2:
            wait_bytes(self.span(6 * rows), self.recv.at[1])
            for k in range(CHIPS_Z):
                block = self.slot(y, k, x)
                send(block, block, self.sent.at[1], self.recv.at[2], self.near_peer())
        if number == 3:
            wait_bytes(self.span(8 * rows), self.recv.at[2])
            for k in range(CHIPS_Z):
                for j in range(2):
                    slot_y, slot_x = self.near_pair(j)
                    block = self.slot(slot_y, k, slot_x)
                    send(block, block, self.sent.at[1], self.recv.at[3], self.far_peer())
        if number == 4:
            wait_bytes(self.span(16 * rows), self.recv.at[3])
            block = self.full.at[:, self.plane(c)]
            send(block, block, self.sent.at[1], self.recv.at[4], device(y, z, x, 1 - c))
        if number == 5:
            wait_bytes(self.span(32 * rows), self.recv.at[4])
        if number == 6:
            wait_bytes(self.span(rows), self.sent.at[0])
            wait_bytes(self.full.at[pl.ds(0, 31 * rows)], self.sent.at[1])


class GatherLate(Gather):
    def step(self, number):
        y, z, x, c, rows = self.y, self.z, self.x, self.c, self.rows
        if number == 1:
            self.own_here()
            wait_bytes(self.span(rows), self.recv.at[0])
            block = self.slot(y, z, x)
            send(block, block, self.sent.at[1], self.recv.at[1], self.near_peer())
        elif number == 2:
            wait_bytes(self.span(2 * rows), self.recv.at[1])
            for j in range(2):
                slot_y, slot_x = self.near_pair(j)
                block = self.slot(slot_y, z, slot_x)
                send(block, block, self.sent.at[1], self.recv.at[2], self.far_peer())
        elif number == 3:
            wait_bytes(self.span(4 * rows), self.recv.at[2])
            for k in range(1, CHIPS_Z):
                target = device(y, (z + k) % CHIPS_Z, x, c)
                for j in range(4):
                    block = self.slot(j // 2, z, j % 2)
                    send(block, block, self.sent.at[1], self.recv.at[3], target)
        elif number == 4:
            wait_bytes(self.span(24 * rows), self.recv.at[3])
            block = self.full.at[:, self.plane(c)]
            send(block, block, self.sent.at[1], self.recv.at[4], device(y, z, x, 1 - c))
        else:
            super().step(number)


class Reduce(Slots):
    def __init__(self, part, out, work, near, mid, far, last, pair, recv, sent, first=None):
        super().__init__(out.shape[0], out.shape[1] // 2, first)
        self.part, self.out, self.work = part, out, work
        self.near, self.mid, self.far, self.last, self.pair = near, mid, far, last, pair
        self.recv, self.sent = recv, sent

    def add(self, rows, ref, index):
        size = 2 * self.rows
        start = pl.ds(pl.multiple_of(index * size, 8), size)
        self.work[rows, :] += ref[start, :]

    def start_sum(self):
        wait_bytes(self.work, self.recv.at[0])
        size = 2 * self.rows

        @pl.loop(0, 16)
        def _(index):
            span = pl.ds(pl.multiple_of(index * size, 8), size)
            self.work[span, :] += self.part[span, self.plane(self.c)]

    def step(self, number):
        y, z, x, c, rows = self.y, self.z, self.x, self.c, self.rows
        size = 2 * rows
        if number == 0:
            send(
                self.part.at[:, self.plane(1 - c)],
                self.work,
                self.sent.at[0],
                self.recv.at[0],
                device(y, z, x, 1 - c),
            )
        if number == 1:
            self.start_sum()
            for k in range(CHIPS_Z):
                for j in range(2):
                    slot_y, slot_x = self.far_pair(j)
                    send(
                        self.work.at[self.slot_rows(slot_y, k, slot_x)],
                        self.near.at[pl.ds((k * 2 + j) * size, size)],
                        self.sent.at[1],
                        self.recv.at[1],
                        self.far_peer(),
                    )
        if number == 2:
            wait_bytes(self.near, self.recv.at[1])

            @pl.loop(0, 8)
            def _(index):
                k, j = index // 2, index % 2
                slot_y, slot_x = self.near_pair(j)
                self.add(self.slot_rows(slot_y, k, slot_x), self.near, index)

            for k in range(CHIPS_Z):
                slot_y, slot_x = self.near_slot()
                send(
                    self.work.at[self.slot_rows(slot_y, k, slot_x)],
                    self.mid.at[pl.ds(k * size, size)],
                    self.sent.at[1],
                    self.recv.at[2],
                    self.near_peer(),
                )
        if number == 3:
            wait_bytes(self.mid, self.recv.at[2])

            @pl.loop(0, CHIPS_Z)
            def _(k):
                self.add(self.slot_rows(y, k, x), self.mid, k)

            for k in range(1, CHIPS_Z):
                to_z = (z + k) % CHIPS_Z
                send(
                    self.work.at[self.slot_rows(y, to_z, x)],
                    self.far.at[pl.ds((k - 1) * size, size)],
                    self.sent.at[1],
                    self.recv.at[3],
                    device(y, to_z, x, c),
                )
        if number == 4:
            wait_bytes(self.far, self.recv.at[3])
            total = self.work[self.slot_rows(y, z, x), :].astype(jnp.float32)
            for k in range(self.far.shape[0] // size):
                total = total + self.far[pl.ds(k * size, size), :].astype(jnp.float32)
            self.last[...] = total
            keep = pl.ds(pl.multiple_of(c * rows, 8), rows)
            give = pl.ds(pl.multiple_of((1 - c) * rows, 8), rows)
            send(
                self.last.at[give],
                self.pair,
                self.sent.at[2],
                self.recv.at[4],
                device(y, z, x, 1 - c),
            )
            self.out[:, self.plane(c)] = self.last[keep, :]
        if number == 5:
            wait_bytes(self.pair, self.recv.at[4])
            self.out[:, self.plane(1 - c)] = self.pair[...]
        if number == 6:
            wait_bytes(self.work, self.sent.at[0])
            wait_bytes(self.work.at[pl.ds(0, 30 * rows)], self.sent.at[1])
            wait_bytes(self.pair, self.sent.at[2])


class ReduceEarly(Reduce):
    def step(self, number):
        y, z, x, c = self.y, self.z, self.x, self.c
        size = 2 * self.rows
        if number == 1:
            self.start_sum()
            for k in range(1, CHIPS_Z):
                to_z = (z + k) % CHIPS_Z
                for j in range(4):
                    send(
                        self.work.at[self.slot_rows(j // 2, to_z, j % 2)],
                        self.near.at[pl.ds((4 * (k - 1) + j) * size, size)],
                        self.sent.at[1],
                        self.recv.at[1],
                        device(y, to_z, x, c),
                    )
        elif number == 2:
            wait_bytes(self.near, self.recv.at[1])

            @pl.loop(0, 12)
            def _(index):
                j = index % 4
                self.add(self.slot_rows(j // 2, z, j % 2), self.near, index)

            for j in range(2):
                slot_y, slot_x = self.far_pair(j)
                send(
                    self.work.at[self.slot_rows(slot_y, z, slot_x)],
                    self.mid.at[pl.ds(j * size, size)],
                    self.sent.at[1],
                    self.recv.at[2],
                    self.far_peer(),
                )
        elif number == 3:
            wait_bytes(self.mid, self.recv.at[2])
            for j in range(2):
                slot_y, slot_x = self.near_pair(j)
                self.add(self.slot_rows(slot_y, z, slot_x), self.mid, j)
            slot_y, slot_x = self.near_slot()
            send(
                self.work.at[self.slot_rows(slot_y, z, slot_x)],
                self.far,
                self.sent.at[1],
                self.recv.at[3],
                self.near_peer(),
            )
        else:
            super().step(number)


def reduce_scratch(rows, half, dtype, counts=(16, 8, 6)):
    return [
        pltpu.VMEM((32 * rows, half), dtype),
        pltpu.VMEM((counts[0] * rows, half), dtype),
        pltpu.VMEM((counts[1] * rows, half), dtype),
        pltpu.VMEM((counts[2] * rows, half), dtype),
        pltpu.VMEM((2 * rows, half), jnp.float32),
        pltpu.VMEM((rows, half), jnp.float32),
    ]


def seq_bounds(lengths, position):
    low = jnp.zeros((1, 128), jnp.int32)
    high = jnp.full((1, 128), NEVER, jnp.int32)
    end = low
    for i in range(lengths.shape[0]):
        end = end + lengths[i : i + 1, :]
        low = jnp.maximum(low, jnp.where(end <= position, end, 0))
        high = jnp.minimum(high, jnp.where(end > position, end, NEVER))
    return low, high


class Span:
    fields = ("start", "far_low", "far_high", "no_before", "no_after", "second")

    def __init__(self, rows):
        for i, name in enumerate(self.fields):
            setattr(self, name, rows[i : i + 1, :])


def span_rows(lengths, first_row, block, far_rows, global_count):
    position = first_row + block * BLOCK
    low, high = seq_bounds(lengths, position)
    first_low, _ = seq_bounds(lengths, first_row)
    start = jnp.minimum(low >> 4, global_count - far_rows)
    rows = [
        start,
        (low >> 4) - start,
        (high >> 4) - start,
        jnp.where(position > low, 0, NEVER),
        jnp.where(position + BLOCK < high, 0, NEVER),
        jnp.where(low == first_low, 0, 1),
    ]
    return jnp.concatenate(rows + [start, start], axis=0)


def window_select(spans, window, blocks, far_rows, global_count):
    start = Span(spans[pl.ds(8 * window * (blocks - 1), 8), :]).start
    row = lax.broadcasted_iota(jnp.int32, (far_rows, global_count), 0)
    column = lax.broadcasted_iota(jnp.int32, (far_rows, global_count), 1)
    return (column - widen(start, global_count) == row).astype(jnp.bfloat16)


def far_part(ref, lanes, span, near_rows, far_rows):
    first = ref[pl.ds(near_rows, far_rows), lanes]
    second = ref[pl.ds(near_rows + far_rows, far_rows), lanes]
    return jnp.where(span.second > 0, second, first)


def widen(row, width):
    return jnp.concatenate([row] * (width // 128), axis=1)


def head_pair(rows):
    lane = lax.broadcasted_iota(jnp.int32, rows.shape, 1)
    zero = jnp.zeros_like(rows)
    return jnp.concatenate(
        [jnp.where(lane < HEAD_DIM, rows, zero), jnp.where(lane < HEAD_DIM, zero, rows)], axis=0
    )


def attend_block(pair, block, span, query, keys, values, attended, near_rows, far_rows):
    lanes = pl.ds(pl.multiple_of(pair * 128, 128), 128)
    rows = pl.ds(pl.multiple_of(block * BLOCK, BLOCK), BLOCK)
    near = pl.ds(pl.multiple_of(block * BLOCK, BLOCK), 3 * BLOCK)
    both = head_pair(query[rows, lanes])
    near_scores = dot_nt(both, keys[near, lanes])
    far_scores = dot_nt(both, far_part(keys, lanes, span, near_rows, far_rows))
    row = lax.broadcasted_iota(jnp.int32, (2 * BLOCK, BLOCK), 0) % BLOCK
    column = lax.broadcasted_iota(jnp.int32, (2 * BLOCK, BLOCK), 1)
    edge = jnp.where(
        column > row + span.no_before,
        near_scores[:, :BLOCK],
        jnp.where(column < row - span.no_after, near_scores[:, 2 * BLOCK :], MASKED),
    )
    own = near_scores[:, BLOCK : 2 * BLOCK]
    far_column = lax.broadcasted_iota(jnp.int32, far_scores.shape, 1)
    far_scores = jnp.where(
        (far_column >= widen(span.far_low, far_rows))
        & (far_column < widen(span.far_high, far_rows)),
        far_scores,
        MASKED,
    )
    highest = jnp.maximum(
        jnp.max(jnp.maximum(edge, own), axis=1, keepdims=True),
        jnp.max(far_scores, axis=1, keepdims=True),
    )
    edge_exp = jnp.exp(edge - highest)
    own_exp = jnp.exp(own - highest)
    far_exp = jnp.exp(far_scores - highest)
    inverse = 1.0 / (
        jnp.sum(edge_exp + own_exp, axis=1, keepdims=True) + jnp.sum(far_exp, axis=1, keepdims=True)
    )
    edge_probs = edge_exp * inverse
    near_probs = jnp.concatenate(
        [
            jnp.where(column > row, edge_probs, 0.0).astype(jnp.bfloat16),
            (own_exp * inverse).astype(jnp.bfloat16),
            jnp.where(column < row, edge_probs, 0.0).astype(jnp.bfloat16),
        ],
        axis=1,
    )
    far_probs = (far_exp * inverse).astype(jnp.bfloat16)
    mixed = dot_nn(near_probs, values[near, lanes]) + dot_nn(
        far_probs, far_part(values, lanes, span, near_rows, far_rows)
    )
    lane = lax.broadcasted_iota(jnp.int32, (BLOCK, 128), 1)
    attended[rows, lanes] = jnp.where(lane < HEAD_DIM, mixed[:BLOCK], mixed[BLOCK:]).astype(
        jnp.bfloat16
    )


def attend_block_back(
    pair, block, span, query, grad, keys, keys_t, values, grad_query, grad_keys, grad_values,
    near_rows, far_rows,
):
    lanes = pl.ds(pl.multiple_of(pair * 128, 128), 128)
    rows = pl.ds(pl.multiple_of(block * BLOCK, BLOCK), BLOCK)
    near = pl.ds(pl.multiple_of(block * BLOCK, BLOCK), 3 * BLOCK)
    both = head_pair(query[rows, lanes])
    grads = head_pair(grad[rows, lanes])
    near_scores = dot_nt(keys[near, lanes], both)
    far_keys = far_part(keys, lanes, span, near_rows, far_rows)
    far_scores = dot_nt(far_keys, both)
    row = lax.broadcasted_iota(jnp.int32, (BLOCK, 2 * BLOCK), 0)
    column = lax.broadcasted_iota(jnp.int32, (BLOCK, 2 * BLOCK), 1) % BLOCK
    edge = jnp.where(
        row > column + widen(span.no_before, 2 * BLOCK),
        near_scores[:BLOCK],
        jnp.where(row < column - widen(span.no_after, 2 * BLOCK), near_scores[2 * BLOCK :], MASKED),
    )
    own = near_scores[BLOCK : 2 * BLOCK]
    far_row = lax.broadcasted_iota(jnp.int32, far_scores.shape, 0)
    far_scores = jnp.where(
        (far_row >= widen(span.far_low, 2 * BLOCK)) & (far_row < widen(span.far_high, 2 * BLOCK)),
        far_scores,
        MASKED,
    )
    highest = jnp.maximum(
        jnp.max(jnp.maximum(edge, own), axis=0, keepdims=True),
        jnp.max(far_scores, axis=0, keepdims=True),
    )
    edge_exp = jnp.exp(edge - highest)
    own_exp = jnp.exp(own - highest)
    far_exp = jnp.exp(far_scores - highest)
    inverse = 1.0 / (
        jnp.sum(edge_exp + own_exp, axis=0, keepdims=True) + jnp.sum(far_exp, axis=0, keepdims=True)
    )
    edge_probs, own_probs, far_probs = edge_exp * inverse, own_exp * inverse, far_exp * inverse
    near_dprobs = dot_nt(values[near, lanes], grads)
    far_dprobs = dot_nt(far_part(values, lanes, span, near_rows, far_rows), grads)
    edge_dprobs = jnp.where(row > column, near_dprobs[:BLOCK], near_dprobs[2 * BLOCK :])
    own_dprobs = near_dprobs[BLOCK : 2 * BLOCK]
    delta = jnp.sum(
        edge_probs * edge_dprobs + own_probs * own_dprobs, axis=0, keepdims=True
    ) + jnp.sum(far_probs * far_dprobs, axis=0, keepdims=True)
    edge_ds = edge_probs * (edge_dprobs - delta)
    own_ds = (own_probs * (own_dprobs - delta)).astype(jnp.bfloat16)
    far_ds = (far_probs * (far_dprobs - delta)).astype(jnp.bfloat16)

    def spread(edge_part, own_part):
        return jnp.concatenate(
            [
                jnp.where(row > column, edge_part, 0.0).astype(jnp.bfloat16),
                own_part.astype(jnp.bfloat16),
                jnp.where(row < column, edge_part, 0.0).astype(jnp.bfloat16),
            ],
            axis=0,
        )

    near_ds = spread(edge_ds, own_ds)
    far_keys_t = jnp.where(
        widen(span.second, far_rows) > 0,
        keys_t[lanes, pl.ds(near_rows + far_rows, far_rows)],
        keys_t[lanes, pl.ds(near_rows, far_rows)],
    )
    query_t = dot_nn(keys_t[lanes, near], near_ds) + dot_nn(far_keys_t, far_ds)
    feature = lax.broadcasted_iota(jnp.int32, (128, BLOCK), 0)
    query_t = jnp.where(feature < HEAD_DIM, query_t[:, :BLOCK], query_t[:, BLOCK:])
    grad_query[rows, lanes] = query_t.T.astype(jnp.bfloat16)
    grad_keys[near, lanes] += dot_nn(near_ds, both)
    grad_values[near, lanes] += dot_nn(spread(edge_probs, own_probs), grads)
    far_dkey = dot_nn(far_ds, both)
    far_dvalue = dot_nn(far_probs.astype(jnp.bfloat16), grads)
    for window in range(2):
        place = pl.ds(near_rows + window * far_rows, far_rows)
        here = span.second == window
        grad_keys[place, lanes] += jnp.where(here, far_dkey, 0.0)
        grad_values[place, lanes] += jnp.where(here, far_dvalue, 0.0)


def inverse_rms(values):
    return lax.rsqrt(jnp.mean(values * values, axis=-1, keepdims=True) + EPSILON)


def rms_back(values, gain, grads):
    scale = inverse_rms(values)
    scaled = grads * gain
    back = scale * scaled - values * (
        scale * scale * scale * jnp.mean(scaled * values, axis=-1, keepdims=True)
    )
    return back, jnp.sum(grads * values * scale, axis=0, keepdims=True)


def block_sums(rows, count):
    take = lax.broadcasted_iota(jnp.int32, (count, rows.shape[0]), 1) // GBLK
    which = lax.broadcasted_iota(jnp.int32, (count, rows.shape[0]), 0)
    return dot_nn((take == which).astype(jnp.bfloat16), rows)


def owner_of(column, rows):
    return (column * ((65536 + rows - 1) // rows)) >> 16


def spread_gains(packed, rows):
    width = 32 * rows
    lane = lax.broadcasted_iota(jnp.int32, (128, width), 0)
    column = lax.broadcasted_iota(jnp.int32, (128, width), 1)
    select = (column - rows * owner_of(column, rows) == lane).astype(jnp.float32)
    wide = dot(packed, select, ((1,), (0,)), precision=lax.Precision.HIGHEST)
    device_row = lax.broadcasted_iota(jnp.int32, wide.shape, 0) >> 3
    wide_column = lax.broadcasted_iota(jnp.int32, wide.shape, 1)
    wide = jnp.where(owner_of(wide_column, rows) == device_row, wide, 0.0)
    return jnp.sum(wide.reshape(32, 8, width), axis=0)


def pack_gains(wide, rows):
    width = 32 * rows
    tall = jnp.concatenate([wide] * 32, axis=0)
    device_row = lax.broadcasted_iota(jnp.int32, tall.shape, 0) >> 3
    column = lax.broadcasted_iota(jnp.int32, tall.shape, 1)
    tall = jnp.where(owner_of(column, rows) == device_row, tall, 0.0)
    lane = lax.broadcasted_iota(jnp.int32, (width, 128), 1)
    from_column = lax.broadcasted_iota(jnp.int32, (width, 128), 0)
    select = (from_column - rows * owner_of(from_column, rows) == lane).astype(jnp.float32)
    return dot(tall, select, ((1,), (0,)), precision=lax.Precision.HIGHEST)


CHUNKS = 4
TILE = 256
SMALL_SEMS = 24
NAMES = ("g", "h", "i", "k", "v", "q", "o", "d", "f0", "f1", "f2", "f3")
NAMES += ("r0", "r1", "r2", "r3", "rd", "ro", "ra", "rb", "rc", "w", "j", "l")
Z_LAST = ("f3", "o")
Z_FIRST = ("r1",)
FIRST = {}
SCHEDULE = {
    "s0": {
        0: (0, 10, 30, 40, 50, 60, 70, 80, 90, 100, 110),
    },
    "s0b": {
        0: (61, 111, 31, 41, 20, 51),
    },
    "s1": {
        0: (1, 11, 62, 2),
    },
    "s2": {
        0: (112, 32),
    },
    "s4": {
        0: (42, 33, 43, 21, 71, 81, 34, 52, 44, 53, 22, 72, 91, 23),
    },
    "s5": {
        0: (35,),
    },
    "kn": {
        2: (54, 82, 101, 63, 113),
    },
    "kt": {
        4: (73,),
    },
    "s6": {
        0: (45,),
    },
    "vn": {
        2: (92,),
        4: (83,),
    },
    "s7": {
        0: (55,),
    },
    "fa": {
        2: (102,),
        4: (93,),
        8: (103,),
        11: (74,),
    },
    "m0": {
        0: (64, 84, 65),
    },
    "m1": {
        0: (75,),
    },
    "ca": {
        0: (85,),
        1: (104, 95),
        2: (105,),
        3: (115,),
    },
    "cb": {
        0: (94,),
    },
    "cw": {
        0: (120,),
        1: (130,),
        2: (140,),
        3: (150,),
    },
    "cg": {
        3: (121,),
        6: (114, 131),
        7: (122,),
        9: (123, 141),
    },
    "sp": {
        0: (160,),
    },
    "m2": {
        0: (151,),
    },
    "m3": {
        0: (142, 170),
    },
    "ba": {
        0: (161,),
        1: (171,),
        3: (132, 143, 152),
        6: (153, 181, 144),
        7: (162,),
        9: (154, 172, 191, 133),
    },
    "bt": {
        0: (180, 124),
        1: (190,),
        2: (200, 173),
    },
    "wg": {
        6: (163,),
        7: (182,),
    },
    "e1b": {
        0: (134,),
    },
    "e1": {
        0: (220,),
    },
    "e2": {
        0: (210,),
    },
    "gg": {
        1: (221, 183, 201, 192),
    },
    "e6": {
        0: (211,),
    },
    "e6b": {
        0: (164, 174, 222, 184, 193, 202, 223),
    },
    "e7": {
        0: (230,),
    },
    "fi": {
        1: (203,),
    },
    "e8": {
        0: (125, 135, 145, 155, 165, 175, 185, 194, 231, 195, 204, 232, 205),
    },
}


class Calls:
    def __init__(self, *actions):
        self.actions = actions

    def step(self, number):
        self.actions[number]()


def tiled(count, body, before=None):
    @pl.loop(0, count // TILE)
    def _(i):
        if before is not None:
            before(i)
        body(pl.ds(pl.multiple_of(i * TILE, TILE), TILE))


class GlobalSlots:
    def __init__(self, count):
        self.count = count

    def at(self, z, x, c):
        return self.packed(z * 4 + x * 2 + c)

    def packed(self, index):
        return pl.ds(pl.multiple_of(index * self.count, 16), self.count)


def layer_kernel(lengths, first_gain, second_gain, third_gain, tokens, cotangent, *refs):
    shards, refs = refs[:7], refs[7:]
    packed, raw_sums, refs = refs[-2], refs[-1], refs[:-2]
    output, grad_tokens, gain_out, refs = refs[0], refs[1], refs[2], refs[3:]
    grads_out, refs = refs[:9], refs[9:]
    w_query, w_key, w_value, w_out, w_down, w_ff = refs[:6]
    rows_in, rows_in_t, keys, keys_t, values, query, attended, hidden, turned = refs[6:15]
    mixed, grad_both, grad_keys, grad_values, gain_grads, part_key, part_value = refs[15:22]
    spans, gain_rows, gathered, gain_part, gain_side, gain_column, group_sums = refs[22:29]
    halo, global_rows, global_near, global_mid, global_far = refs[29:34]
    buffers, refs = refs[34:88], refs[88:]
    recv, sent, small = refs
    y, z, x, c = coords()
    blk = lax.axis_index("blk")
    me = blk + 16 * y
    row_count, width = tokens.shape
    blocks = row_count // BLOCK
    local_globals = row_count // GBLK
    global_count = global_rows.shape[0]
    near_rows = row_count + 2 * BLOCK
    all_rows = rows_in.shape[0]
    far_rows = (all_rows - near_rows) // 2
    feature_rows = width // 32
    hidden_rows = w_down.shape[0] // CHUNKS
    first_row = blk * row_count
    low = jnp.bfloat16
    slots = GlobalSlots(local_globals)
    column, sides = column_peers(), side_peers()

    part_query = rows_in.at[pl.ds(0, width)]
    steps = {}
    chunk_width = w_ff.shape[2]
    sources = [("q", shards[0], w_query), ("k", shards[1], w_key), ("v", shards[2], w_value)]
    sources += [("o", shards[3], w_out), ("d", shards[4], w_down)]
    for chunk in range(CHUNKS):
        part = pl.ds(chunk * chunk_width // 2, chunk_width // 2)
        pair = (shards[5].at[:, part], shards[6].at[:, part])
        sources.append((NAMES[8 + chunk], pair, w_ff.at[chunk]))
    for i, (name, shard, full) in enumerate(sources):
        kind = GatherLate if name in Z_LAST else Gather
        steps[name] = kind(shard, full, recv.at[i], sent.at[i], FIRST.get(name))
    ff_steps = [steps[name] for name in NAMES[8:12]]
    targets = [("ra", part_key), ("rb", part_value), ("rc", part_query), ("ro", w_out)]
    targets += [("rd", w_down)]
    targets += [(NAMES[12 + chunk], w_ff.at[chunk]) for chunk in range(CHUNKS)]
    for i, (name, part) in enumerate(targets):
        held = buffers[6 * i : 6 * i + 6]
        kind = ReduceEarly if name in Z_FIRST else Reduce
        steps[name] = kind(part, grads_out[i], *held, recv.at[9 + i], sent.at[9 + i], FIRST.get(name))

    def run(todo):
        for code in todo:
            steps[NAMES[code // 10]].step(code % 10)

    def tick(kind, number=0):
        run(SCHEDULE.get(kind, {}).get(number, ()))

    def loop_tick(kind, index, count):
        for number in range(count):
            todo = SCHEDULE.get(kind, {}).get(number, ())
            if todo:
                pl.when(index == number)(functools.partial(run, todo))

    def ticks(kind, count):
        return lambda index: loop_tick(kind, index, count)

    packed[...] = jnp.zeros_like(packed)
    for i, gain in enumerate((first_gain, second_gain, third_gain)):
        packed[i : i + 1, pl.ds(0, feature_rows)] = gain[...].astype(jnp.float32).reshape(
            1, feature_rows
        )
    greet()
    own_tile = gathered.at[pl.ds(pl.multiple_of(me * 8, 8), 8)]

    def share_gains():
        own_tile[...] = packed[...]
        for peer in column:
            send(packed, own_tile, small.at[1], small.at[0], peer)

    def spread_sides():
        wait_bytes(gathered.at[pl.ds(0, 56)], small.at[0])
        for k in range(CHIPS_Z):
            pair = gathered.at[pl.ds(pl.multiple_of((y * 8 + k * 2 + x) * 16, 16), 16)]
            for peer in sides:
                send(pair, pair, small.at[3], small.at[2], peer)

    def gains_here():
        wait_bytes(gathered.at[pl.ds(0, 192)], small.at[2])

    steps["g"] = Calls(share_gains, spread_sides, gains_here)

    def token_halo(side):
        source = pl.ds(row_count - BLOCK, BLOCK) if side == 0 else pl.ds(0, BLOCK)
        return pltpu.make_async_remote_copy(
            src_ref=tokens.at[source],
            dst_ref=halo.at[side],
            send_sem=small.at[8 + side],
            recv_sem=small.at[10 + side],
            device_id=(y, blk + 1 - 2 * side),
            device_id_type=MESH,
        )

    def start_halos():
        pl.when(blk < 15)(lambda: token_halo(0).start())
        pl.when(blk > 0)(lambda: token_halo(1).start())

    def end_halos():
        pl.when(blk > 0)(lambda: token_halo(0).wait_recv())
        pl.when(blk < 15)(lambda: token_halo(1).wait_recv())

    steps["h"] = Calls(start_halos, end_halos)

    def globals_z():
        block = global_rows.at[slots.at(z, x, c)]
        for k in range(1, CHIPS_Z):
            send(block, block, small.at[4], small.at[5], device(y, (z + k) % CHIPS_Z, x, c))

    def globals_x():
        wait_bytes(global_rows.at[pl.ds(0, 3 * local_globals)], small.at[5])
        for k in range(CHIPS_Z):
            block = global_rows.at[slots.at(k, x, c)]
            send(block, block, small.at[4], small.at[6], device(y, z, 1 - x, c))

    def globals_pair():
        wait_bytes(global_rows.at[pl.ds(0, 4 * local_globals)], small.at[6])
        for k in range(CHIPS_Z):
            for j in range(2):
                block = global_rows.at[slots.at(k, j, c)]
                send(block, block, small.at[4], small.at[7], device(y, z, x, 1 - c))

    def globals_here():
        wait_bytes(global_rows.at[pl.ds(0, 8 * local_globals)], small.at[7])

    steps["i"] = Calls(globals_z, globals_x, globals_pair, globals_here)
    tick("s0")

    def scale_own(place):
        wide = tokens[place, :].astype(jnp.float32)
        attended[place, :] = (wide * inverse_rms(wide)).astype(low)

    tiled(row_count, scale_own)
    raw_sums[...] = block_sums(attended[...], local_globals)
    global_rows[slots.packed(blk), :] = raw_sums[...].astype(low)
    tick("s0b")
    wide_lengths = jnp.concatenate(
        [
            jnp.broadcast_to(lengths[0:1, i : i + 1], (1, 128))
            for i in range(lengths.shape[1])
        ],
        axis=0,
    )
    for block in range(blocks):
        spans[pl.ds(8 * block, 8), :] = span_rows(
            wide_lengths, first_row, block, far_rows, global_count
        )
    tick("s1")
    gain_rows[...] = spread_gains(gathered[...], feature_rows)
    tick("s2")
    norm_gain, global_gain, ffn_gain = gain_rows[0:1, :], gain_rows[1:2, :], gain_rows[2:3, :]

    def normed(part):
        wide = part.astype(jnp.float32)
        return (wide * inverse_rms(wide) * norm_gain).astype(low)

    def norm_own(place):
        to = pl.ds(pl.multiple_of(place.start + BLOCK, BLOCK), TILE)
        rows_in[to, :] = normed(tokens[place, :])

    tiled(row_count, norm_own)
    tick("s2b")
    group_sums[...] = block_sums(rows_in[pl.ds(BLOCK, row_count), :], local_globals)
    tick("s3")

    @pl.when(blk == 0)
    def _():
        halo[0] = jnp.zeros_like(halo[0])

    @pl.when(blk == 15)
    def _():
        halo[1] = jnp.zeros_like(halo[1])

    rows_in[pl.ds(0, BLOCK), :] = normed(halo[0])
    rows_in[pl.ds(BLOCK + row_count, BLOCK), :] = normed(halo[1])
    def turn(source, target, start):
        target[:, pl.ds(start, TILE)] = source[pl.ds(start, TILE), :].T

    for start in range(0, near_rows, TILE):
        tick("tr", start // TILE)
        turn(rows_in, rows_in_t, start)

    def project(weights, target, start, count, place, kind):
        def one(part):
            source = pl.ds(pl.multiple_of(part.start + start, BLOCK), TILE)
            to = pl.ds(pl.multiple_of(part.start + place, BLOCK), TILE)
            target[to, :] = dot_nn(rows_in[source, :], weights[...]).astype(low)

        tiled(count, one, ticks(kind, count // TILE))

    tick("s4")

    def global_norm(place):
        summed = global_rows[place, :].astype(jnp.float32) * norm_gain
        attended[place, :] = (summed * inverse_rms(summed) * global_gain).astype(low)

    tiled(global_count, global_norm)
    for window in range(2):
        select = window_select(spans, window, blocks, far_rows, global_count)
        rows_in[pl.ds(near_rows + window * far_rows, far_rows), :] = dot_nn(
            select, attended[...]
        ).astype(low)
    for start in range(near_rows, all_rows, TILE):
        tick("trf", (start - near_rows) // TILE)
        turn(rows_in, rows_in_t, start)
    tick("s5")
    project(w_key, keys, 0, all_rows, 0, "kn")
    for start in range(0, all_rows, TILE):
        tick("kt", start // TILE)
        turn(keys, keys_t, start)
    tick("s6")
    project(w_value, values, 0, all_rows, 0, "vn")
    tick("s7")
    project(w_query, query, BLOCK, row_count, 0, "qn")
    tick("s8")
    iterations = blocks * (HEADS // 2)

    def span_of(block):
        return Span(spans[pl.ds(pl.multiple_of(block * 8, 8), 8), :])

    @pl.loop(0, iterations // 2)
    def _(i):
        loop_tick("fa", i, iterations // 2)
        for j in range(2):
            block = (2 * i + j) % blocks
            attend_block(
                (2 * i) // blocks, block, span_of(block), query, keys, values, attended,
                near_rows, far_rows,
            )

    wait_bytes(global_rows.at[pl.ds(0, 15 * local_globals)], small.at[4])
    tick("m0")

    def after(place):
        return pl.ds(pl.multiple_of(place.start + row_count, TILE), TILE)

    def join(place):
        middle = tokens[place, :].astype(jnp.float32) + dot_nn(attended[place, :], w_out[...])
        grad_keys[place, :] = middle
        grad_keys[after(place), :] = middle
        low_hidden = (middle * inverse_rms(middle) * ffn_gain).astype(low)
        hidden[place, :] = low_hidden
        turned[:, place] = low_hidden.T
        grad_values[place, :] = jnp.zeros((TILE, width), jnp.float32)

    tiled(row_count, join, ticks("jn", 2))
    tick("m1")

    @pl.loop(0, CHUNKS)
    def _(chunk):
        loop_tick("ca", chunk, CHUNKS)
        half = chunk_width // 2
        rows = pl.ds(pl.multiple_of(chunk * hidden_rows, 128), hidden_rows)

        def feed(place):
            both = dot_nn(hidden[place, :], w_ff[chunk])
            gate, up = both[:, :half], both[:, half:]
            square = gate * gate
            bend = jnp.tanh(GELU_SCALE * gate * (1.0 + GELU_CUBIC * square))
            lift = 0.5 * (1.0 + bend)
            active = gate * lift
            slope = lift + 0.5 * gate * (1.0 - bend * bend) * (
                GELU_SCALE * (1.0 + 3.0 * GELU_CUBIC * square)
            )
            mixed[place, :] = (active * up).astype(low)
            grad_mixed = dot_nt(cotangent[place, :], w_down[rows, :])
            grad_both[place, pl.ds(0, half)] = (grad_mixed * up * slope).astype(low)
            grad_both[place, pl.ds(half, half)] = (grad_mixed * active).astype(low)
            grad_keys[after(place), :] += dot_nn(mixed[place, :], w_down[rows, :])
            grad_values[place, :] += dot_nt(grad_both[place, :], w_ff[chunk])

        tiled(row_count, feed, lambda i: pl.when(i == 1)(lambda: loop_tick("cb", chunk, CHUNKS)))
        for number in range(CHUNKS):
            pl.when(chunk == number)(functools.partial(ff_steps[number].step, 6))

        def gate_up_grad(place):
            w_ff[chunk, place, :] = dot_nn(turned[place, :], grad_both[...]).astype(low)

        tiled(width, gate_up_grad, lambda i: loop_tick("cg", chunk * 3 + i, 3 * CHUNKS))
        loop_tick("cw", chunk, CHUNKS)
        pl.when(chunk == 0)(lambda: steps["d"].step(6))
        w_down[rows, :] = dot(mixed[...], cotangent[...], ((0,), (0,))).astype(low)

    gain_grads[...] = jnp.zeros_like(gain_grads)

    def split(place):
        output[place, :] = grad_keys[after(place), :].astype(low)
        back, gain_grad = rms_back(grad_keys[place, :], ffn_gain, grad_values[place, :])
        gain_grads[2:3, :] += gain_grad
        grad_middle = cotangent[place, :].astype(jnp.float32) + back
        grad_tokens[place, :] = grad_middle
        branch = grad_middle.astype(low)
        rows_in[place, :] = branch
        hidden[place, :] = dot_nt(branch, w_out[...]).astype(low)
        turned[:, place] = attended[place, :].T

    tiled(row_count, split, ticks("sp", 2))
    tick("m2")
    steps["o"].step(6)

    def out_grad(place):
        w_out[place, :] = dot_nn(turned[place, :], rows_in[pl.ds(0, row_count), :]).astype(low)

    tiled(width, out_grad)
    tick("m3")

    def clear(place):
        grad_keys[place, :] = jnp.zeros((TILE, width), jnp.float32)
        grad_values[place, :] = jnp.zeros((TILE, width), jnp.float32)

    tiled(all_rows, clear)
    part_width = width // 3
    part_rounds = iterations // 6

    def back_part(third, target):
        @pl.loop(0, part_rounds)
        def _(j):
            i = third * part_rounds + j
            for number in range(part_rounds):
                todo = SCHEDULE.get("ba", {}).get(third * part_rounds + number, ())
                if todo:
                    pl.when(j == number)(functools.partial(run, todo))
            for k in range(2):
                block = (2 * i + k) % blocks
                attend_block_back(
                    (2 * i) // blocks, block, span_of(block), query, hidden, keys, keys_t, values,
                    query, grad_keys, grad_values, near_rows, far_rows,
                )

        lanes = pl.ds(third * part_width, part_width)

        def lower(place):
            keys[place, lanes] = grad_keys[place, lanes].astype(low)
            values[place, lanes] = grad_values[place, lanes].astype(low)

        tiled(all_rows, lower)

        def weight_grad(place):
            own = rows_in_t[place, pl.ds(BLOCK, row_count)]
            target[place, pl.ds(0, part_width)] = dot_nn(own, query[:, lanes]).astype(low)
            every = rows_in_t[place, :]
            target[place, pl.ds(part_width, part_width)] = dot_nn(every, keys[:, lanes]).astype(low)
            target[place, pl.ds(2 * part_width, part_width)] = dot_nn(
                every, values[:, lanes]
            ).astype(low)

        tiled(width, weight_grad, functools.partial(tick_part, third))
        tick("bt", third)

    def tick_part(third, index):
        for number in range(3):
            todo = SCHEDULE.get("wg", {}).get(3 * third + number, ())
            if todo:
                pl.when(index == number)(functools.partial(run, todo))

    for third, target in enumerate((part_key, part_value, part_query)):
        back_part(third, target)
    tick("e0")

    def grad_rows(start, count):
        part = pl.ds(start, count)
        return dot_nt(keys[part, :], w_key[...]) + dot_nt(values[part, :], w_value[...])

    for window in range(2):
        hidden[pl.ds(window * far_rows, far_rows), :] = grad_rows(
            near_rows + window * far_rows, far_rows
        ).astype(low)
    tick("e1b")
    selects = [window_select(spans, w, blocks, far_rows, global_count) for w in range(2)]
    for half in range(2):
        part = slice(half * (global_count // 2), (half + 1) * (global_count // 2))
        global_rows[part, :] = sum(
            dot(selects[w][:, part], hidden[pl.ds(w * far_rows, far_rows), :], ((0,), (0,)))
            for w in range(2)
        ).astype(low)

    def add_global(rows, ref, index):
        total = global_rows[rows, :].astype(jnp.float32)
        total = total + ref[slots.packed(index), :].astype(jnp.float32)
        global_rows[rows, :] = total.astype(low)

    def sums_pair():
        for k in range(CHIPS_Z):
            for j in range(2):
                send(
                    global_rows.at[slots.at(k, j, 1 - c)],
                    global_near.at[slots.packed(k * 2 + j)],
                    small.at[16],
                    small.at[17],
                    device(y, z, x, 1 - c),
                )

    def sums_x():
        wait_bytes(global_near, small.at[17])
        for k in range(CHIPS_Z):
            for j in range(2):
                add_global(slots.at(k, j, c), global_near, k * 2 + j)
        for k in range(CHIPS_Z):
            send(
                global_rows.at[slots.at(k, 1 - x, c)],
                global_mid.at[slots.packed(k)],
                small.at[16],
                small.at[18],
                device(y, z, 1 - x, c),
            )

    def sums_z():
        wait_bytes(global_mid, small.at[18])
        for k in range(CHIPS_Z):
            add_global(slots.at(k, x, c), global_mid, k)
        for k in range(1, CHIPS_Z):
            to_z = (z + k) % CHIPS_Z
            send(
                global_rows.at[slots.at(to_z, x, c)],
                global_far.at[slots.packed(k - 1)],
                small.at[16],
                small.at[19],
                device(y, to_z, x, c),
            )

    def sums_here():
        wait_bytes(global_far, small.at[19])

    steps["j"] = Calls(sums_pair, sums_x, sums_z, sums_here)
    tick("e1")
    halo[4] = grad_rows(0, BLOCK).astype(low)
    halo[5] = grad_rows(BLOCK + row_count, BLOCK).astype(low)
    def grad_halo(side):
        return pltpu.make_async_remote_copy(
            src_ref=halo.at[4 + side],
            dst_ref=halo.at[3 - side],
            send_sem=small.at[20 + side],
            recv_sem=small.at[22 + side],
            device_id=(y, blk - 1 + 2 * side),
            device_id_type=MESH,
        )

    def start_grad_halos():
        pl.when(blk > 0)(lambda: grad_halo(0).start())
        pl.when(blk < 15)(lambda: grad_halo(1).start())

    def end_grad_halos():
        pl.when(blk > 0)(lambda: grad_halo(1).wait_recv())
        pl.when(blk < 15)(lambda: grad_halo(0).wait_recv())

    steps["w"] = Calls(start_grad_halos, end_grad_halos)
    tick("e2")
    def gather_grads(place):
        rows = pl.ds(pl.multiple_of(place.start + BLOCK, BLOCK), TILE)
        grad_keys[place, :] = (
            dot_nt(keys[rows, :], w_key[...])
            + dot_nt(values[rows, :], w_value[...])
            + dot_nt(query[place, :], w_query[...])
        )

    tiled(row_count, gather_grads, ticks("gg", 2))
    tick("e6")

    @pl.when(blk == 0)
    def _():
        halo[2] = jnp.zeros_like(halo[2])

    @pl.when(blk == 15)
    def _():
        halo[3] = jnp.zeros_like(halo[3])

    grad_keys[pl.ds(0, BLOCK), :] += halo[2].astype(jnp.float32)
    grad_keys[pl.ds(row_count - BLOCK, BLOCK), :] += halo[3].astype(jnp.float32)

    def gain_sum(place):
        wide = tokens[place, :].astype(jnp.float32)
        gain_grads[0:1, :] += jnp.sum(
            grad_keys[place, :] * wide * inverse_rms(wide), axis=0, keepdims=True
        )

    tiled(row_count, gain_sum)
    tick("e6b")
    total = global_rows[slots.at(z, x, c), :].astype(jnp.float32)
    for k in range(CHIPS_Z - 1):
        total = total + global_far[slots.packed(k), :].astype(jnp.float32)
    grad_summed, grad_global_gain = rms_back(group_sums[...], global_gain, total)
    gain_grads[1:2, :] = grad_global_gain
    gain_grads[0:1, :] += jnp.sum(grad_summed * raw_sums[...], axis=0, keepdims=True)
    group_sums[...] = grad_summed
    gain_part[...] = pack_gains(gain_grads[...], feature_rows)

    def finish(place):
        few = TILE // GBLK
        sums = group_sums[pl.ds(pl.multiple_of(place.start // GBLK, 8), few), :]
        grad_normed = grad_keys[place, :] + jnp.broadcast_to(
            sums[:, None, :], (few, GBLK, width)
        ).reshape(TILE, width)
        grad_tokens[place, :] += rms_back(
            tokens[place, :].astype(jnp.float32), norm_gain, grad_normed
        )[0]

    def gain_pair(pair_y, k, pair_x):
        return pl.ds(pl.multiple_of((pair_y * 8 + k * 2 + pair_x) * 16, 16), 16)

    def gains_sides():
        for index, peer in enumerate(sides):
            side_y = y if index == 0 else 1 - y
            side_x = x if index == 1 else 1 - x
            for k in range(CHIPS_Z):
                send(
                    gain_part.at[gain_pair(side_y, k, side_x)],
                    gain_side.at[index, pl.ds(k * 16, 16)],
                    small.at[13],
                    small.at[12],
                    peer,
                )

    def gains_column():
        wait_bytes(gain_side, small.at[12])
        for k in range(CHIPS_Z):
            rows = gain_pair(y, k, x)
            place = pl.ds(k * 16, 16)
            gain_part[rows, :] += gain_side[0, place, :] + gain_side[1, place, :] + gain_side[2, place, :]
        place = z * 2 + c
        gain_column[pl.ds(pl.multiple_of(place * 8, 8), 8), :] = gain_part[
            pl.ds(pl.multiple_of(me * 8, 8), 8), :
        ]
        for k in range(CHIPS_Z):
            for j in range(2):
                if k == 0 and j == 0:
                    peer_z, peer_c = z, 1 - c
                elif k == 0:
                    continue
                else:
                    peer_z, peer_c = (z + k) % CHIPS_Z, j
                peer_me = y * 16 + peer_z * 4 + x * 2 + peer_c
                send(
                    gain_part.at[pl.ds(pl.multiple_of(peer_me * 8, 8), 8)],
                    gain_column.at[pl.ds(pl.multiple_of(place * 8, 8), 8)],
                    small.at[15],
                    small.at[14],
                    device(y, peer_z, x, peer_c),
                )

    def gains_done():
        wait_bytes(gain_column.at[pl.ds(0, 56)], small.at[14])

    steps["l"] = Calls(gains_sides, gains_column, gains_done)
    tick("e7")
    tiled(row_count, finish, ticks("fi", 2))
    tick("e8")
    gain_out[...] = jnp.sum(gain_column[...].reshape(8, 8, 128), axis=0)
    for name, _ in targets:
        steps[name].step(6)
    for one in [steps["q"], steps["k"], steps["v"]]:
        one.step(6)
    wait_bytes(gathered.at[pl.ds(0, 56)], small.at[1])
    wait_bytes(gathered.at[pl.ds(0, 192)], small.at[3])
    wait_bytes(global_rows.at[pl.ds(0, 15 * local_globals)], small.at[16])
    wait_bytes(gathered.at[pl.ds(0, 192)], small.at[13])
    wait_bytes(gathered.at[pl.ds(0, 56)], small.at[15])
    pl.when(blk < 15)(lambda: token_halo(0).wait_send())
    pl.when(blk > 0)(lambda: token_halo(1).wait_send())
    pl.when(blk > 0)(lambda: grad_halo(0).wait_send())
    pl.when(blk < 15)(lambda: grad_halo(1).wait_send())


def layer(lengths, gains, tokens, cotangent, shards, far_rows, global_count):
    row_count, width = tokens.shape
    all_rows = row_count + 2 * BLOCK + 2 * far_rows
    local_globals = row_count // GBLK
    down_rows = shards[4].shape[0]
    chunk_width = 2 * shards[5].shape[1] // CHUNKS
    vmem = pl.BlockSpec(memory_space=pltpu.VMEM)
    anywhere = pl.BlockSpec(memory_space=pl.ANY)
    low, wide = jnp.bfloat16, jnp.float32
    shard_shapes = [(width // 32, width)] * 4 + [(down_rows, width)]
    shard_shapes += [(width // 32, chunk_width)] * CHUNKS
    buffers = []
    names = ("ra", "rb", "rc", "ro", "rd") + NAMES[12:16]
    for name, (rows, columns) in zip(names, shard_shapes):
        counts = (24, 4, 2) if name in Z_FIRST else (16, 8, 6)
        buffers += reduce_scratch(rows, columns // 2, low, counts)
    return pl.pallas_call(
        layer_kernel,
        out_shape=[
            jax.ShapeDtypeStruct((row_count, width), low),
            jax.ShapeDtypeStruct((row_count, width), wide),
            jax.ShapeDtypeStruct((8, 128), wide),
        ]
        + [jax.ShapeDtypeStruct(shape, wide) for shape in shard_shapes],
        in_specs=[vmem] * 6 + [anywhere] * 7,
        out_specs=[vmem] * 12,
        scratch_shapes=[pltpu.VMEM((width, width), low)] * 4
        + [
            pltpu.VMEM((32 * down_rows, width), low),
            pltpu.VMEM((CHUNKS, width, chunk_width), low),
            pltpu.VMEM((all_rows, width), low),
            pltpu.VMEM((width, all_rows), low),
            pltpu.VMEM((all_rows, width), low),
            pltpu.VMEM((width, all_rows), low),
            pltpu.VMEM((all_rows, width), low),
            pltpu.VMEM((row_count, width), low),
            pltpu.VMEM((row_count, width), low),
            pltpu.VMEM((row_count, width), low),
            pltpu.VMEM((width, row_count), low),
            pltpu.VMEM((row_count, chunk_width // 2), low),
            pltpu.VMEM((row_count, chunk_width), low),
            pltpu.VMEM((all_rows, width), wide),
            pltpu.VMEM((all_rows, width), wide),
            pltpu.VMEM((8, width), wide),
            pltpu.VMEM((width, width), low),
            pltpu.VMEM((width, width), low),
            pltpu.VMEM((8 * row_count // BLOCK, 128), jnp.int32),
            pltpu.VMEM((8, width), wide),
            pltpu.VMEM((256, 128), wide),
            pltpu.VMEM((256, 128), wide),
            pltpu.VMEM((3, 64, 128), wide),
            pltpu.VMEM((64, 128), wide),
            pltpu.VMEM((local_globals, width), wide),
            pltpu.VMEM((6, BLOCK, width), low),
            pltpu.VMEM((global_count, width), low),
            pltpu.VMEM((8 * local_globals, width), low),
            pltpu.VMEM((4 * local_globals, width), low),
            pltpu.VMEM((3 * local_globals, width), low),
        ]
        + buffers
        + [
            pltpu.SemaphoreType.DMA((18, 5)),
            pltpu.SemaphoreType.DMA((18, 3)),
            pltpu.SemaphoreType.DMA((SMALL_SEMS,)),
            pltpu.VMEM((8, 128), wide),
            pltpu.VMEM((local_globals, width), wide),
        ],
        compiler_params=pltpu.CompilerParams(
            collective_id=0, has_side_effects=True, vmem_limit_bytes=VMEM_BYTES
        ),
        name="layer",
    )(lengths, *gains, tokens, cotangent, *shards)


def settle_kernel(*refs):
    ins, outs, held, sems = refs[:12], refs[12:24], refs[24:26], refs[26]
    pieces = []
    for i in range(2):
        size = held[i].shape[0] // 4
        for j in range(4):
            part = pl.ds(j * size, size)
            index = 4 * i + j
            into = pltpu.make_async_copy(ins[i].at[part], held[i].at[part], sems.at[0, index])
            back = pltpu.make_async_copy(held[i].at[part], outs[i].at[part], sems.at[1, index])
            into.start()
            pieces.append((into, back))
    for into, back in pieces:
        into.wait()
        back.start()
    rows = outs[2].shape[0]
    for i in range(3):
        outs[2 + i][...] = ins[2][i, pl.ds(0, rows)]
    thirds, chunks = ins[3:6], ins[8:12]
    part = thirds[0].shape[1] // 3
    for i in range(3):
        for third, ref in enumerate(thirds):
            outs[5 + i][:, pl.ds(third * part, part)] = ref[:, pl.ds(i * part, part)]
    outs[8][...] = ins[6][...]
    outs[9][...] = ins[7][...]
    half = chunks[0].shape[1] // 2
    for i in range(2):
        for chunk, ref in enumerate(chunks):
            outs[10 + i][:, pl.ds(chunk * half, half)] = ref[:, pl.ds(i * half, half)]
    for _, back in pieces:
        back.wait()


def settle(outs, rows):
    vmem = pl.BlockSpec(memory_space=pltpu.VMEM)
    anywhere = pl.BlockSpec(memory_space=pl.ANY)
    wide = jnp.float32
    width = outs[0].shape[1]
    ff_width = outs[8].shape[1] // 2 * CHUNKS
    return pl.pallas_call(
        settle_kernel,
        out_shape=[jax.ShapeDtypeStruct(one.shape, one.dtype) for one in outs[:2]]
        + [jax.ShapeDtypeStruct((rows,), wide)] * 3
        + [jax.ShapeDtypeStruct((rows, width), wide)] * 4
        + [jax.ShapeDtypeStruct(outs[7].shape, wide)]
        + [jax.ShapeDtypeStruct((rows, ff_width), wide)] * 2,
        in_specs=[anywhere] * 2 + [vmem] * 10,
        out_specs=[anywhere] * 2 + [vmem] * 10,
        scratch_shapes=[pltpu.VMEM(one.shape, one.dtype) for one in outs[:2]]
        + [pltpu.SemaphoreType.DMA((2, 8))],
        name="settle",
    )(*outs)


def per_device(
    tokens, lengths, norm_gain, global_gain, w_query, w_key, w_value, w_out,
    ffn_gain, w_gate, w_up, w_down, cotangent,
):
    global_count = tokens.shape[0] * lax.axis_size("blk") // GBLK
    gains = (norm_gain, global_gain, ffn_gain)
    shards = (w_query, w_key, w_value, w_out, w_down, w_gate, w_up)
    outs = layer(lengths, gains, tokens, cotangent, shards, global_count // 2, global_count)
    settled = settle(outs, norm_gain.shape[0])
    output, grad_tokens, first, second, third = settled[:5]
    return (output, grad_tokens, first, second, *settled[5:9], third, *settled[10:], settled[9])


def fits(mesh):
    return mesh.shape["seq"] == 2 and mesh.shape["blk"] == 16


def solution(mesh):
    return jax.shard_map(
        per_device if fits(mesh) else per_device_general,
        mesh=mesh,
        in_specs=(
            P(("seq", "blk"), None),
            P("seq", None),
            P(("seq", "blk")),
            P(("seq", "blk")),
            P(("seq", "blk"), None),
            P(("seq", "blk"), None),
            P(("seq", "blk"), None),
            P(("seq", "blk"), None),
            P(("seq", "blk")),
            P(("seq", "blk"), None),
            P(("seq", "blk"), None),
            P(("seq", "blk"), None),
            P(("seq", "blk"), None),
        ),
        out_specs=(
            P(("seq", "blk"), None),
            P(("seq", "blk"), None),
            P(("seq", "blk")),
            P(("seq", "blk")),
            P(("seq", "blk"), None),
            P(("seq", "blk"), None),
            P(("seq", "blk"), None),
            P(("seq", "blk"), None),
            P(("seq", "blk")),
            P(("seq", "blk"), None),
            P(("seq", "blk"), None),
            P(("seq", "blk"), None),
        ),
        check_vma=False,
    )
```
